32 devices in a mesh: dp: 4 (over y, x), seq: 4 (over z), tensor: 2 (over core).
Axes of the slice: x: 2, y: 2, z: 4, core: 2. Of those that a mesh axis runs over, the one named last changes fastest.
Arguments:
- tokens: bfloat16 [8, 1024, 2048], P('dp', 'seq'), may hold values from -6 to 6
- doc_starts: int32 [8, 1024], P('dp', 'seq'), may hold values 0 or 1
- attn_gain: bfloat16 [2048], P(('dp', 'seq')), may hold values from 0.5 to 1.5
- mlp_gain: bfloat16 [2048], P(('dp', 'seq')), may hold values from 0.5 to 1.5
- query_weight: bfloat16 [2048, 256], P(('dp', 'seq'), 'tensor'), may hold values from -0.125 to 0.125
- key_weight: bfloat16 [2048, 256], P(('dp', 'seq'), 'tensor'), may hold values from -0.125 to 0.125
- value_weight: bfloat16 [2048, 2048], P(('dp', 'seq'), 'tensor'), may hold values from -0.125 to 0.125
- output_weight: bfloat16 [2048, 2048], P('tensor', ('dp', 'seq')), may hold values from -2 to 2
- gate_weight: bfloat16 [2048, 5504], P(('dp', 'seq'), 'tensor'), may hold values from -0.125 to 0.125
- up_weight: bfloat16 [2048, 5504], P(('dp', 'seq'), 'tensor'), may hold values from -0.125 to 0.125
- down_weight: bfloat16 [5504, 2048], P('tensor', ('dp', 'seq')), may hold values from -0.078125 to 0.078125
- cotangent: bfloat16 [8, 1024, 2048], P('dp', 'seq'), may hold values from -6 to 6
Outputs:
- block_out: bfloat16 [8, 1024, 2048], P('dp', 'seq')
- grad_tokens: float32 [8, 1024, 2048], P('dp', 'seq')
- grad_attn_gain: float32 [2048], P(('dp', 'seq'))
- grad_mlp_gain: float32 [2048], P(('dp', 'seq'))
- grad_query: float32 [2048, 256], P(('dp', 'seq'), 'tensor')
- grad_key: float32 [2048, 256], P(('dp', 'seq'), 'tensor')
- grad_value: float32 [2048, 2048], P(('dp', 'seq'), 'tensor')
- grad_output: float32 [2048, 2048], P('tensor', ('dp', 'seq'))
- grad_gate: float32 [2048, 5504], P(('dp', 'seq'), 'tensor')
- grad_up: float32 [2048, 5504], P(('dp', 'seq'), 'tensor')
- grad_down: float32 [5504, 2048], P('tensor', ('dp', 'seq'))
The draws below stay inside these ranges and needn't reach their ends.
All inputs are finite; a program needn't handle non-finite values. No bound on the sum of `doc_starts` on one device may be relied on, other than what follows from the above.
Results may differ from the reference program's by a relative error of at most 0.013.
Values may be sent and summed in bfloat16 or wider, within the bound.
A program may use at most 256 MiB of HBM per device.

```python
from functools import partial
import jax
import jax.numpy as jnp
from jax import lax

D = 2048
HEADS = 16
FDIM = 16
VHEAD = 128
FF = 5504
SPAN = 256
ROWS = 8
SEQ_LEN = 1024


def set_ends(values, stream_key, least, high):
    dims = values.shape
    place = [jax.random.randint(jax.random.fold_in(stream_key, axis), (), 0, dims[axis]) for axis in range(len(dims))]
    values = values.at[tuple(place)].set(least)
    longest = dims.index(max(dims))
    place[longest] = (place[longest] + 1) % dims[longest]
    return values.at[tuple(place)].set(high)


def steps_of(rng, shape, shards, low, top_value):
    level, own = 1.0, jax.random.fold_in(rng, 6)
    for dim, parts in shards:
        steps = jnp.exp(jax.random.uniform(jax.random.fold_in(own, dim), (parts,), jnp.float32, low / len(shards), top_value / len(shards)))
        level = level * jnp.repeat(steps, shape[dim] // parts).reshape([-1 if axis == dim else 1 for axis in range(len(shape))])
    return level


def normal_values(stream_key, dims, width, bound, cuts=(), dtype=jnp.bfloat16):
    drawn = jax.random.normal(stream_key, dims, jnp.float32) * width
    if len(cuts) > 0:
        drawn = steps_of(stream_key, dims, cuts, -0.22, 0.18) * drawn
    return jnp.clip(drawn, min=-bound, max=bound).astype(dtype)


def setup_inputs(seed: int = 0) -> dict:
    arg_keys = jax.random.split(jax.random.key(seed), 13)
    tokens = normal_values(arg_keys[0], (ROWS, SEQ_LEN, D), 1.0, 6.0, ((0, 4), (1, 4)))
    doc_starts = set_ends((jax.random.randint(arg_keys[1], (ROWS, SEQ_LEN), 0, 2 * SPAN) < 1).astype(jnp.int32), jax.random.fold_in(arg_keys[1], 1), 0, 1)
    attn_gain = jnp.clip(1.0 + 0.1 * jax.random.normal(arg_keys[2], (D,), jnp.float32), 0.5, 1.5).astype(jnp.bfloat16)
    mlp_gain = jnp.clip(1.0 + 0.1 * jax.random.normal(arg_keys[3], (D,), jnp.float32), 0.5, 1.5).astype(jnp.bfloat16)
    query_weight = normal_values(arg_keys[4], (D, HEADS * FDIM), D ** -0.5, 0.125, ((0, 16), (1, 2)))
    key_weight = normal_values(arg_keys[5], (D, HEADS * FDIM), D ** -0.5, 0.125, ((0, 16), (1, 2)))
    value_weight = normal_values(arg_keys[6], (D, HEADS * VHEAD), D ** -0.5, 0.125, ((0, 16), (1, 2)))
    output_weight = normal_values(arg_keys[7], (HEADS * VHEAD, D), (max(HEADS * VHEAD // 256, 1)) ** -0.5, 2.0, ((0, 2), (1, 16)))
    gate_weight = normal_values(arg_keys[8], (D, FF), D ** -0.5, 0.125, ((0, 16), (1, 2)))
    up_weight = normal_values(arg_keys[9], (D, FF), D ** -0.5, 0.125, ((0, 16), (1, 2)))
    down_weight = normal_values(arg_keys[10], (FF, D), FF ** -0.5, 0.078125, ((0, 2), (1, 16)))
    cotangent = normal_values(arg_keys[11], (ROWS, SEQ_LEN, D), 1.0, 6.0, ((0, 4), (1, 4)))
    return dict(tokens=tokens, doc_starts=doc_starts, attn_gain=attn_gain, mlp_gain=mlp_gain, query_weight=query_weight, key_weight=key_weight, value_weight=value_weight, output_weight=output_weight, gate_weight=gate_weight, up_weight=up_weight, down_weight=down_weight, cotangent=cotangent)


@jax.custom_vjp
def low(v):
    return lax.optimization_barrier(v.astype(jnp.bfloat16)).astype(jnp.float32)

@jax.custom_vjp
def low_back(v):
    return v

def low_keep(v):
    return (low(v), None)

def low_pass(kept, grad):
    return (grad,)

def back_keep(v):
    return (v, None)

def back_low(kept, grad):
    return (low(grad),)
low.defvjp(low_keep, low_pass)
low_back.defvjp(back_keep, back_low)
norm_epsilon = 1e-05
highest = lax.Precision.HIGHEST

def matmul(left_mat, right_mat):
    return jnp.dot(left_mat, right_mat, precision=highest, preferred_element_type=jnp.float32)

def rms_norm(inputs, gain_vec):
    scale_row = lax.rsqrt(lax.optimization_barrier(jnp.mean(inputs * inputs, axis=-1, keepdims=True)) + norm_epsilon)
    return inputs * scale_row * gain_vec

def row_mixer(queries, key_rows, values, segments):
    length = queries.shape[0]
    scores = jnp.einsum('thf,shf->hts', queries, key_rows, precision=highest) / 4.0
    kernel = 1.0 + scores + 0.5 * scores * scores
    position = jnp.arange(length)
    allowed = (position[None, :] <= position[:, None]) & (segments[None, :] == segments[:, None])
    kernel = jnp.where(allowed[None], kernel, 0.0)
    numerator = jnp.einsum('hts,she->the', kernel, values, precision=highest)
    denominator = lax.optimization_barrier(jnp.sum(kernel, axis=-1))
    return numerator / jnp.transpose(denominator)[:, :, None]

def forward(params, segments):
    tokens_in, attn_gain, mlp_gain, query_weight, key_weight, value_weight, output_weight, gate_weight, up_weight, down_weight = params
    row_count, length, model_width = tokens_in.shape
    flat_rows = tokens_in.reshape(-1, model_width)
    normed_one = low(rms_norm(flat_rows, attn_gain))
    queries = low_back(low(matmul(normed_one, query_weight))).reshape(row_count, length, HEADS, FDIM)
    key_rows = low_back(low(matmul(normed_one, key_weight))).reshape(row_count, length, HEADS, FDIM)
    values = low_back(low(matmul(normed_one, value_weight))).reshape(row_count, length, HEADS, VHEAD)
    mixer_fn = jax.checkpoint(row_mixer)

    def per_row(pieces):
        return mixer_fn(pieces[0], pieces[1], pieces[2], pieces[3])
    mixed_heads = lax.map(per_row, (queries, key_rows, values, segments))
    mixed_heads = low_back(low(mixed_heads.reshape(-1, HEADS * VHEAD)))
    residual = flat_rows + low_back(matmul(mixed_heads, output_weight))
    normed_two = low(rms_norm(residual, mlp_gain))
    gate_proj = low_back(matmul(normed_two, gate_weight))
    up_proj = low_back(matmul(normed_two, up_weight))
    hidden = low(jax.nn.silu(gate_proj) * up_proj)
    result_rows = residual + low_back(matmul(hidden, down_weight))
    return result_rows.reshape(row_count, length, model_width)

def reference(tokens, doc_starts, attn_gain, mlp_gain, query_weight, key_weight, value_weight, output_weight, gate_weight, up_weight, down_weight, cotangent):
    segments = jnp.cumsum(doc_starts, axis=1).astype(jnp.int32)
    float_args = (tokens.astype(jnp.float32), attn_gain.astype(jnp.float32), mlp_gain.astype(jnp.float32), query_weight.astype(jnp.float32), key_weight.astype(jnp.float32), value_weight.astype(jnp.float32), output_weight.astype(jnp.float32), gate_weight.astype(jnp.float32), up_weight.astype(jnp.float32), down_weight.astype(jnp.float32))
    block_out, pullback = jax.vjp(partial(forward, segments=segments), float_args)
    gradients = pullback(cotangent.astype(jnp.float32))[0]
    return (block_out.astype(jnp.bfloat16), gradients[0], gradients[1], gradients[2], gradients[3], gradients[4], gradients[5], gradients[6], gradients[7], gradients[8], gradients[9])
```

```python
from functools import partial

import jax
import jax.numpy as jnp
from jax import lax
from jax.sharding import PartitionSpec as P

FDIM = 16
VHEAD = 128
MICRO = 2


norm_epsilon = 1e-05
highest = lax.Precision.HIGHEST
outer_scale = 0.17677669529663687


def prefix(x, axis, combine, identity, reverse):
    size, index = (lax.axis_size(axis), lax.axis_index(axis))
    everything = jax.tree.map(lambda part: lax.all_gather(part, axis), x)
    start = jax.tree.map(
        lambda part, zero: jnp.broadcast_to(jnp.asarray(zero, part.dtype), part.shape), x, identity
    )

    def turn(k, before):
        at = size - 1 - k if reverse else k
        reached = at > index if reverse else at < index
        new = combine(before, jax.tree.map(lambda part: part[at], everything))
        return jax.tree.map(lambda a, b: jnp.where(reached, a, b), new, before)

    return lax.fori_loop(0, size, turn, start)


def features(vectors):
    ones_col = jnp.ones(vectors.shape[:-1] + (1,), jnp.float32)
    outer_terms = vectors[..., :, None] * vectors[..., None, :] * outer_scale
    outer_terms = outer_terms.reshape(vectors.shape[:-1] + (vectors.shape[-1] * vectors.shape[-1],))
    return jnp.concatenate([ones_col, 0.5 * vectors, outer_terms], axis=-1)


def mix_span(queries, key_rows, values, state_in, norm_in, segments):
    length = queries.shape[1]
    scores = jnp.einsum("rthf,rshf->rhts", queries, key_rows, precision=highest) / 4.0
    kernel = 1.0 + scores + 0.5 * scores * scores
    position = jnp.arange(length)
    causal = position[None, :] <= position[:, None]
    allowed = causal[None] & (segments[:, :, None] == segments[:, None, :])
    kernel = jnp.where(allowed[:, None], kernel, 0.0)
    numerator = jnp.einsum("rhts,rshe->rthe", kernel, values, precision=highest)
    denominator = jnp.transpose(jnp.sum(kernel, axis=-1), (0, 2, 1))
    head_part = (segments == 0).astype(jnp.float32)[:, :, None]
    lifted = features(queries)
    numerator = numerator + head_part[..., None] * jnp.einsum(
        "rthf,rhfe->rthe", lifted, state_in, precision=highest
    )
    denominator = denominator + head_part * jnp.einsum(
        "rthf,rhf->rth", lifted, norm_in, precision=highest
    )
    return numerator / denominator[..., None]


def tail_span(key_rows, values, segments):
    tail_mask = (segments == segments[:, -1:]).astype(jnp.float32)
    lifted = features(key_rows) * tail_mask[:, :, None, None]
    tail_state = jnp.einsum("rshf,rshe->rhfe", lifted, values, precision=highest)
    return (tail_state, jnp.sum(lifted, axis=1))


def combine_carry(earlier_part, later_part):
    keep_rate = 1.0 - later_part[2]
    return (
        later_part[0] + keep_rate[:, None, None, None] * earlier_part[0],
        later_part[1] + keep_rate[:, None, None] * earlier_part[1],
        jnp.maximum(earlier_part[2], later_part[2]),
    )


def inverse_rms(inputs):
    return lax.rsqrt(jnp.mean(inputs * inputs, axis=-1, keepdims=True) + norm_epsilon)


def norm_backward(inputs, scale_row, gain_vec, grad_normed):
    scaled_grad = grad_normed * gain_vec
    grad_gain = jnp.sum(grad_normed * inputs * scale_row, axis=0)
    grad_inputs = scale_row * scaled_grad - inputs * scale_row * scale_row * scale_row * jnp.mean(
        scaled_grad * inputs, axis=-1, keepdims=True
    )
    return (grad_inputs, grad_gain)


def inner_rows(left_mat, right_mat):
    return lax.dot_general(
        left_mat, right_mat, (((0,), (0,)), ((), ())), preferred_element_type=jnp.float32
    )


def by_transpose(left_mat, right_mat):
    return lax.dot_general(
        left_mat, right_mat, (((1,), (1,)), ((), ())), preferred_element_type=jnp.float32
    )


def local(
    tokens,
    doc_starts,
    attn_gain,
    mlp_gain,
    query_weight,
    key_weight,
    value_weight,
    output_weight,
    gate_weight,
    up_weight,
    down_weight,
    cotangent,
):
    micro_rows = tokens.shape[0] // MICRO
    span_len = tokens.shape[1]
    model_width = tokens.shape[2]
    head_count = query_weight.shape[1] // FDIM
    outputs_main = []
    outputs_grad = []
    totals = None
    for micro_index in range(MICRO):
        row_start = micro_index * micro_rows
        rows_in = tokens[row_start : row_start + micro_rows]
        starts_in = doc_starts[row_start : row_start + micro_rows]
        cot_in = cotangent[row_start : row_start + micro_rows].reshape(-1, model_width)
        (
            full_query,
            full_key,
            full_value,
            full_gate,
            full_up,
            full_output,
            full_down,
            gain_one,
            gain_two,
        ) = (
            lax.all_gather(query_weight, ("dp", "seq"), axis=0, tiled=True),
            lax.all_gather(key_weight, ("dp", "seq"), axis=0, tiled=True),
            lax.all_gather(value_weight, ("dp", "seq"), axis=0, tiled=True),
            lax.all_gather(gate_weight, ("dp", "seq"), axis=0, tiled=True),
            lax.all_gather(up_weight, ("dp", "seq"), axis=0, tiled=True),
            lax.all_gather(output_weight, ("dp", "seq"), axis=1, tiled=True),
            lax.all_gather(down_weight, ("dp", "seq"), axis=1, tiled=True),
            lax.all_gather(attn_gain, ("dp", "seq"), axis=0, tiled=True),
            lax.all_gather(mlp_gain, ("dp", "seq"), axis=0, tiled=True),
        )
        gain_one_f = gain_one.astype(jnp.float32)
        gain_two_f = gain_two.astype(jnp.float32)
        flat_rows = rows_in.reshape(-1, model_width).astype(jnp.float32)
        scale_one = inverse_rms(flat_rows)
        normed_one = (flat_rows * scale_one * gain_one_f).astype(jnp.bfloat16)
        query_low = jnp.dot(normed_one, full_query, preferred_element_type=jnp.float32).astype(
            jnp.bfloat16
        )
        key_low = jnp.dot(normed_one, full_key, preferred_element_type=jnp.float32).astype(
            jnp.bfloat16
        )
        value_low = jnp.dot(normed_one, full_value, preferred_element_type=jnp.float32).astype(
            jnp.bfloat16
        )
        queries = query_low.astype(jnp.float32).reshape(micro_rows, span_len, head_count, FDIM)
        key_rows = key_low.astype(jnp.float32).reshape(micro_rows, span_len, head_count, FDIM)
        values = value_low.astype(jnp.float32).reshape(micro_rows, span_len, head_count, VHEAD)
        segments = jnp.cumsum(starts_in, axis=1)
        reset_flag = (segments[:, -1] > 0).astype(jnp.float32)
        (tail_state, tail_norm), tail_pull = jax.vjp(
            partial(tail_span, segments=segments), key_rows, values
        )
        state_in, norm_in, reset_in = prefix(
            (tail_state, tail_norm, reset_flag),
            "seq",
            combine_carry,
            (jnp.zeros_like(tail_state), jnp.zeros_like(tail_norm), jnp.zeros_like(reset_flag)),
            False,
        )
        mixed_heads, mix_pull = jax.vjp(
            partial(mix_span, segments=segments), queries, key_rows, values, state_in, norm_in
        )
        mixed_low = mixed_heads.reshape(-1, head_count * VHEAD).astype(jnp.bfloat16)
        branch_one = jnp.dot(mixed_low, full_output, preferred_element_type=jnp.float32)
        residual = flat_rows + lax.psum(branch_one, "tensor")
        scale_two = inverse_rms(residual)
        normed_two = (residual * scale_two * gain_two_f).astype(jnp.bfloat16)
        gate_proj = jnp.dot(normed_two, full_gate, preferred_element_type=jnp.float32)
        up_proj = jnp.dot(normed_two, full_up, preferred_element_type=jnp.float32)
        sigmoid_gate = jax.nn.sigmoid(gate_proj)
        hidden = (gate_proj * sigmoid_gate * up_proj).astype(jnp.bfloat16)
        branch_two = jnp.dot(hidden, full_down, preferred_element_type=jnp.float32)
        block_low = (
            residual + lax.psum(branch_two.astype(jnp.bfloat16), "tensor").astype(jnp.float32)
        ).astype(jnp.bfloat16)
        outputs_main.append(block_low.reshape(micro_rows, span_len, model_width))
        grad_down = inner_rows(hidden, cot_in)
        grad_hidden = by_transpose(cot_in, full_down)
        grad_gate_low = (
            grad_hidden * up_proj * sigmoid_gate * (1.0 + gate_proj * (1.0 - sigmoid_gate))
        ).astype(jnp.bfloat16)
        grad_up_low = (grad_hidden * gate_proj * sigmoid_gate).astype(jnp.bfloat16)
        grad_gate = inner_rows(normed_two, grad_gate_low)
        grad_up = inner_rows(normed_two, grad_up_low)
        grad_normed_two = by_transpose(grad_gate_low, full_gate) + by_transpose(
            grad_up_low, full_up
        )
        grad_normed_two = lax.psum(grad_normed_two, "tensor")
        grad_resid, grad_gain_two = norm_backward(residual, scale_two, gain_two_f, grad_normed_two)
        grad_resid = grad_resid + cot_in.astype(jnp.float32)
        grad_resid_low = grad_resid.astype(jnp.bfloat16)
        grad_output = inner_rows(mixed_low, grad_resid_low)
        grad_mixed = by_transpose(grad_resid_low, full_output).astype(jnp.bfloat16)
        grad_mixed = (
            lax.optimization_barrier(grad_mixed)
            .astype(jnp.float32)
            .reshape(micro_rows, span_len, head_count, VHEAD)
        )
        grad_queries, grad_keys, grad_values, grad_state, grad_norm = mix_pull(grad_mixed)
        carried_state, carried_norm, reset_out = prefix(
            (grad_state, grad_norm, reset_flag),
            "seq",
            combine_carry,
            (jnp.zeros_like(grad_state), jnp.zeros_like(grad_norm), jnp.zeros_like(reset_flag)),
            True,
        )
        more_keys, more_values = tail_pull((carried_state, carried_norm))
        grad_query_low = grad_queries.reshape(-1, head_count * FDIM).astype(jnp.bfloat16)
        grad_key_low = (grad_keys + more_keys).reshape(-1, head_count * FDIM).astype(jnp.bfloat16)
        grad_value_low = (
            (grad_values + more_values).reshape(-1, head_count * VHEAD).astype(jnp.bfloat16)
        )
        grad_query = inner_rows(normed_one, grad_query_low)
        grad_key = inner_rows(normed_one, grad_key_low)
        grad_value = inner_rows(normed_one, grad_value_low)
        grad_normed_one = (
            by_transpose(grad_query_low, full_query)
            + by_transpose(grad_key_low, full_key)
            + by_transpose(grad_value_low, full_value)
        )
        grad_normed_one = lax.psum(grad_normed_one, "tensor")
        grad_inputs, grad_gain_one = norm_backward(
            flat_rows, scale_one, gain_one_f, grad_normed_one
        )
        outputs_grad.append((grad_resid + grad_inputs).reshape(micro_rows, span_len, model_width))
        shares = (
            grad_query,
            grad_key,
            grad_value,
            grad_gate,
            grad_up,
            grad_output,
            grad_down,
            grad_gain_one,
            grad_gain_two,
        )
        if totals is None:
            totals = shares
        else:
            totals = jax.tree.map(jnp.add, totals, shares)
    totals = (
        lax.psum_scatter(totals[0], ("dp", "seq"), scatter_dimension=0, tiled=True),
        lax.psum_scatter(totals[1], ("dp", "seq"), scatter_dimension=0, tiled=True),
        lax.psum_scatter(totals[2], ("dp", "seq"), scatter_dimension=0, tiled=True),
        lax.psum_scatter(totals[3], ("dp", "seq"), scatter_dimension=0, tiled=True),
        lax.psum_scatter(totals[4], ("dp", "seq"), scatter_dimension=0, tiled=True),
        lax.psum_scatter(totals[5], ("dp", "seq"), scatter_dimension=1, tiled=True),
        lax.psum_scatter(totals[6], ("dp", "seq"), scatter_dimension=1, tiled=True),
        lax.psum_scatter(totals[7], ("dp", "seq"), scatter_dimension=0, tiled=True),
        lax.psum_scatter(totals[8], ("dp", "seq"), scatter_dimension=0, tiled=True),
    )
    return (
        jnp.concatenate(outputs_main, axis=0),
        jnp.concatenate(outputs_grad, axis=0),
        totals[7],
        totals[8],
        totals[0],
        totals[1],
        totals[2],
        totals[5],
        totals[3],
        totals[4],
        totals[6],
    )


def nt_dot(a, b):
    return lax.dot_general(a, b, (((1,), (1,)), ((), ())), preferred_element_type=jnp.float32)


def tn_dot(a, b):
    return lax.dot_general(a, b, (((0,), (0,)), ((), ())), preferred_element_type=jnp.float32)


def nn_dot(a, b):
    return lax.dot_general(a, b, (((1,), (0,)), ((), ())), preferred_element_type=jnp.float32)


def gather_rows(own):
    return lax.all_gather(own, ("dp", "tensor"), axis=0, tiled=True)


def scatter_rows(partial_sum):
    return lax.psum_scatter(
        partial_sum.astype(jnp.bfloat16), ("dp", "tensor"), scatter_dimension=0, tiled=True
    ).astype(jnp.float32)


def swap_rows(x):
    return lax.all_to_all(x, "seq", split_axis=0, concat_axis=0, tiled=True)


def to_whole_rows(x, rows, length):
    span = lax.axis_size("seq")
    width = x.shape[-1]
    x = swap_rows(x.reshape(span * rows, length, width))
    return x.reshape(span, rows, length, width).transpose(1, 0, 2, 3).reshape(
        rows, span * length, width
    )


def from_whole_rows(x, rows, length):
    span = lax.axis_size("seq")
    width = x.shape[-1]
    x = x.reshape(rows, span, length, width).transpose(1, 0, 2, 3)
    x = swap_rows(x.reshape(span * rows, length, width))
    return x.reshape(span * rows * length, width)


def attention_forward(queries, keys, values, segments):
    length = queries.shape[1]
    scores = jnp.einsum("rthf,rshf->rhts", queries, keys, preferred_element_type=jnp.float32) / 4.0
    position = jnp.arange(length)
    allowed = (position[None, :] <= position[:, None])[None] & (
        segments[:, :, None] == segments[:, None, :]
    )
    weight = jnp.where(allowed[:, None], 1.0 + scores + 0.5 * scores * scores, 0.0)
    den = jnp.sum(weight, axis=-1)
    num = jnp.einsum(
        "rhts,rshe->rhte", weight.astype(jnp.bfloat16), values, preferred_element_type=jnp.float32
    )
    return num / den[..., None], den, weight, scores, allowed


def attention_backward(queries, keys, values, mixed, den, weight, scores, allowed, dmixed):
    dn = jnp.transpose(dmixed, (0, 2, 1, 3)).astype(jnp.float32) / den[..., None]
    dd = -jnp.sum(dn * mixed, axis=-1)
    dn_low = dn.astype(jnp.bfloat16)
    dw = jnp.einsum("rhte,rshe->rhts", dn_low, values, preferred_element_type=jnp.float32)
    dw = jnp.where(allowed[:, None], dw + dd[..., None], 0.0)
    dvalues = jnp.einsum(
        "rhts,rhte->rshe", weight.astype(jnp.bfloat16), dn_low, preferred_element_type=jnp.float32
    )
    da = (dw * (1.0 + scores) * 0.25).astype(jnp.bfloat16)
    dqueries = jnp.einsum("rhts,rshf->rthf", da, keys, preferred_element_type=jnp.float32)
    dkeys = jnp.einsum("rhts,rthf->rshf", da, queries, preferred_element_type=jnp.float32)
    return dqueries, dkeys, dvalues


def plane_local(
    tokens,
    doc_starts,
    attn_gain,
    mlp_gain,
    query_weight,
    key_weight,
    value_weight,
    output_weight,
    gate_weight,
    up_weight,
    down_weight,
    cotangent,
):
    plane, span, cores = (lax.axis_size("dp"), lax.axis_size("seq"), lax.axis_size("tensor"))
    rows, length, width = tokens.shape
    chunk = width // (plane * span)
    own = rows * length // cores
    heads = query_weight.shape[1] // FDIM // plane
    hidden_part = gate_weight.shape[1] // plane
    vcols, qcols = heads * VHEAD, heads * FDIM
    all_rows = rows * plane // span

    def seq_major(a):
        return (
            a.reshape(a.shape[:-1] + (plane, span, chunk)).swapaxes(-3, -2).reshape(a.shape)
        )

    def plane_major(a):
        return (
            a.reshape(a.shape[:-1] + (span, plane, chunk)).swapaxes(-3, -2).reshape(a.shape)
        )

    core = lax.axis_index("tensor")
    small = jnp.concatenate(
        [
            attn_gain.astype(jnp.float32)[None],
            mlp_gain.astype(jnp.float32)[None],
            doc_starts.astype(jnp.float32).reshape(-1, chunk),
        ]
    )
    small = lax.all_gather(small, ("seq", "dp"), axis=0, tiled=False)
    gain_one = small[:, 0].reshape(width)
    gain_two = small[:, 1].reshape(width)
    starts = small[:, 2:].reshape(span, plane * rows, length)
    starts = lax.dynamic_slice_in_dim(starts, lax.axis_index("seq") * all_rows, all_rows, 1)
    segments = jnp.cumsum(starts.transpose(1, 0, 2).reshape(all_rows, span * length), axis=1)

    def spread(pack):
        pack = lax.all_to_all(pack, "dp", split_axis=0, concat_axis=0, tiled=True)
        pack = lax.all_gather(pack, "seq", axis=0, tiled=False)
        return pack.transpose(2, 0, 1, 3).reshape(pack.shape[2], width)

    def collect(grads):
        part = lax.psum_scatter(
            grads.astype(jnp.bfloat16), "seq", scatter_dimension=1, tiled=True
        )
        part = part.reshape(part.shape[0], plane, chunk).transpose(1, 0, 2)
        return lax.all_to_all(part, "dp", split_axis=0, concat_axis=0, tiled=True).astype(
            jnp.float32
        )

    def split(w):
        return w.reshape(plane, -1, chunk)

    attn_pack = spread(
        jnp.concatenate(
            [split(value_weight.T), split(query_weight.T), split(key_weight.T), split(output_weight)],
            axis=1,
        )
    )
    ffn_pack = spread(
        jnp.concatenate([split(gate_weight.T), split(up_weight.T), split(down_weight)], axis=1)
    )
    qkv_rows = vcols + 2 * qcols
    w_qkv, w_out = attn_pack[:qkv_rows], attn_pack[qkv_rows:]
    w_gate_up, w_down = ffn_pack[: 2 * hidden_part], ffn_pack[2 * hidden_part :]

    def mine(a):
        a = lax.dynamic_slice_in_dim(a.reshape(rows * length, width), core * own, own, 0)
        return seq_major(a)

    x = mine(tokens).astype(jnp.float32)
    cot_own = mine(cotangent)
    scale_one = inverse_rms(x)
    normed_one = gather_rows((x * scale_one * gain_one).astype(jnp.bfloat16))
    cot = gather_rows(cot_own)
    qkv = nt_dot(normed_one, w_qkv).astype(jnp.bfloat16)
    qkv = to_whole_rows(qkv, all_rows, length)
    values = qkv[..., :vcols].reshape(all_rows, -1, heads, VHEAD)
    queries = qkv[..., vcols : vcols + qcols].reshape(all_rows, -1, heads, FDIM)
    keys = qkv[..., vcols + qcols :].reshape(all_rows, -1, heads, FDIM)
    mixed, den, weight, scores, allowed = attention_forward(queries, keys, values, segments)
    mixed_low = mixed.transpose(0, 2, 1, 3).reshape(all_rows, -1, vcols).astype(jnp.bfloat16)
    mixed_low = from_whole_rows(mixed_low, all_rows, length)
    residual = x + scatter_rows(nn_dot(mixed_low, w_out))
    scale_two = inverse_rms(residual)
    normed_two = gather_rows((residual * scale_two * gain_two).astype(jnp.bfloat16))
    gate_up = nt_dot(normed_two, w_gate_up)
    gate, up = gate_up[:, :hidden_part], gate_up[:, hidden_part:]
    sig = jax.nn.sigmoid(gate)
    hidden = (gate * sig * up).astype(jnp.bfloat16)
    block_own = (residual + scatter_rows(nn_dot(hidden, w_down))).astype(jnp.bfloat16)

    dhidden = nt_dot(cot, w_down)
    dgate = (dhidden * up * sig * (1.0 + gate * (1.0 - sig))).astype(jnp.bfloat16)
    dup = (dhidden * gate * sig).astype(jnp.bfloat16)
    dgate_up = jnp.concatenate([dgate, dup], axis=1)
    dnormed_two = scatter_rows(nn_dot(dgate_up, w_gate_up))
    ffn_grads = collect(
        jnp.concatenate([tn_dot(dgate_up, normed_two), tn_dot(hidden, cot)], axis=0)
    )
    dresid, gain_two_grad = norm_backward(residual, scale_two, gain_two, dnormed_two)
    dresid = dresid + cot_own.astype(jnp.float32)
    dresid_low = gather_rows(dresid.astype(jnp.bfloat16))
    dmixed = nt_dot(dresid_low, w_out).astype(jnp.bfloat16)
    dmixed = to_whole_rows(dmixed, all_rows, length).reshape(all_rows, -1, heads, VHEAD)
    dqueries, dkeys, dvalues = attention_backward(
        queries, keys, values, mixed, den, weight, scores, allowed, dmixed
    )
    dqkv = jnp.concatenate(
        [
            d.reshape(all_rows, span * length, -1).astype(jnp.bfloat16)
            for d in (dvalues, dqueries, dkeys)
        ],
        axis=-1,
    )
    dqkv = from_whole_rows(dqkv, all_rows, length)
    dnormed_one = scatter_rows(nn_dot(dqkv, w_qkv))
    attn_grads = collect(
        jnp.concatenate([tn_dot(dqkv, normed_one), tn_dot(mixed_low, dresid_low)], axis=0)
    )
    dtokens, gain_one_grad = norm_backward(x, scale_one, gain_one, dnormed_one)
    dtokens = dresid + dtokens
    gain_grads = lax.psum(jnp.stack([gain_one_grad, gain_two_grad]), "tensor")
    gain_grads = lax.psum_scatter(
        gain_grads, ("seq", "dp"), scatter_dimension=1, tiled=True
    )

    def whole(a):
        a = lax.all_gather(plane_major(a), "tensor", axis=0, tiled=True)
        return a.reshape(rows, length, width)

    def stacked(a, start, size):
        return a[:, start : start + size].reshape(plane * size, chunk)

    h = hidden_part
    return (
        whole(block_own),
        whole(dtokens),
        gain_grads[0],
        gain_grads[1],
        stacked(attn_grads, vcols, qcols).T,
        stacked(attn_grads, vcols + qcols, qcols).T,
        stacked(attn_grads, 0, vcols).T,
        stacked(attn_grads, qkv_rows, vcols),
        stacked(ffn_grads, 0, h).T,
        stacked(ffn_grads, h, h).T,
        stacked(ffn_grads, 2 * h, h),
    )


def fits_plane(mesh, tokens, query_weight, gate_weight):
    plane, span, cores = (mesh.shape[a] for a in ("dp", "seq", "tensor"))
    heads = query_weight.shape[1] // FDIM // cores
    return (
        plane == 4
        and cores == 2
        and heads % plane == 0
        and (gate_weight.shape[1] // cores) % (16 * plane) == 0
        and tokens.shape[0] % span == 0
    )


def solution(mesh):
    def step(*args):
        use = fits_plane(mesh, args[0], args[4], args[8])
        return sharded(mesh, plane_local if use else local)(*args)

    return step


def sharded(mesh, body):
    return jax.shard_map(
        body,
        mesh=mesh,
        in_specs=(
            P("dp", "seq", None),
            P("dp", "seq"),
            P(("dp", "seq")),
            P(("dp", "seq")),
            P(("dp", "seq"), "tensor"),
            P(("dp", "seq"), "tensor"),
            P(("dp", "seq"), "tensor"),
            P("tensor", ("dp", "seq")),
            P(("dp", "seq"), "tensor"),
            P(("dp", "seq"), "tensor"),
            P("tensor", ("dp", "seq")),
            P("dp", "seq", None),
        ),
        out_specs=(
            P("dp", "seq", None),
            P("dp", "seq", None),
            P(("dp", "seq")),
            P(("dp", "seq")),
            P(("dp", "seq"), "tensor"),
            P(("dp", "seq"), "tensor"),
            P(("dp", "seq"), "tensor"),
            P("tensor", ("dp", "seq")),
            P(("dp", "seq"), "tensor"),
            P(("dp", "seq"), "tensor"),
            P("tensor", ("dp", "seq")),
        ),
        check_vma=False,
    )
```

```python
from functools import partial

import jax
import jax.numpy as jnp
from jax import lax
from jax.experimental import pallas as pl
from jax.experimental.pallas import tpu as pltpu
from jax.sharding import PartitionSpec as P

FDIM = 16
VHEAD = 128
MICRO = 2


norm_epsilon = 1e-05
highest = lax.Precision.HIGHEST
outer_scale = 0.17677669529663687


def prefix(x, axis, combine, identity, reverse):
    size, index = (lax.axis_size(axis), lax.axis_index(axis))
    everything = jax.tree.map(lambda part: lax.all_gather(part, axis), x)
    start = jax.tree.map(
        lambda part, zero: jnp.broadcast_to(jnp.asarray(zero, part.dtype), part.shape), x, identity
    )

    def turn(k, before):
        at = size - 1 - k if reverse else k
        reached = at > index if reverse else at < index
        new = combine(before, jax.tree.map(lambda part: part[at], everything))
        return jax.tree.map(lambda a, b: jnp.where(reached, a, b), new, before)

    return lax.fori_loop(0, size, turn, start)


def features(vectors):
    ones_col = jnp.ones(vectors.shape[:-1] + (1,), jnp.float32)
    outer_terms = vectors[..., :, None] * vectors[..., None, :] * outer_scale
    outer_terms = outer_terms.reshape(vectors.shape[:-1] + (vectors.shape[-1] * vectors.shape[-1],))
    return jnp.concatenate([ones_col, 0.5 * vectors, outer_terms], axis=-1)


def mix_span(queries, key_rows, values, state_in, norm_in, segments):
    length = queries.shape[1]
    scores = jnp.einsum("rthf,rshf->rhts", queries, key_rows, precision=highest) / 4.0
    kernel = 1.0 + scores + 0.5 * scores * scores
    position = jnp.arange(length)
    causal = position[None, :] <= position[:, None]
    allowed = causal[None] & (segments[:, :, None] == segments[:, None, :])
    kernel = jnp.where(allowed[:, None], kernel, 0.0)
    numerator = jnp.einsum("rhts,rshe->rthe", kernel, values, precision=highest)
    denominator = jnp.transpose(jnp.sum(kernel, axis=-1), (0, 2, 1))
    head_part = (segments == 0).astype(jnp.float32)[:, :, None]
    lifted = features(queries)
    numerator = numerator + head_part[..., None] * jnp.einsum(
        "rthf,rhfe->rthe", lifted, state_in, precision=highest
    )
    denominator = denominator + head_part * jnp.einsum(
        "rthf,rhf->rth", lifted, norm_in, precision=highest
    )
    return numerator / denominator[..., None]


def tail_span(key_rows, values, segments):
    tail_mask = (segments == segments[:, -1:]).astype(jnp.float32)
    lifted = features(key_rows) * tail_mask[:, :, None, None]
    tail_state = jnp.einsum("rshf,rshe->rhfe", lifted, values, precision=highest)
    return (tail_state, jnp.sum(lifted, axis=1))


def combine_carry(earlier_part, later_part):
    keep_rate = 1.0 - later_part[2]
    return (
        later_part[0] + keep_rate[:, None, None, None] * earlier_part[0],
        later_part[1] + keep_rate[:, None, None] * earlier_part[1],
        jnp.maximum(earlier_part[2], later_part[2]),
    )


def inverse_rms(inputs):
    return lax.rsqrt(jnp.mean(inputs * inputs, axis=-1, keepdims=True) + norm_epsilon)


def norm_backward(inputs, scale_row, gain_vec, grad_normed):
    scaled_grad = grad_normed * gain_vec
    grad_gain = jnp.sum(grad_normed * inputs * scale_row, axis=0)
    grad_inputs = scale_row * scaled_grad - inputs * scale_row * scale_row * scale_row * jnp.mean(
        scaled_grad * inputs, axis=-1, keepdims=True
    )
    return (grad_inputs, grad_gain)


def inner_rows(left_mat, right_mat):
    return lax.dot_general(
        left_mat, right_mat, (((0,), (0,)), ((), ())), preferred_element_type=jnp.float32
    )


def by_transpose(left_mat, right_mat):
    return lax.dot_general(
        left_mat, right_mat, (((1,), (1,)), ((), ())), preferred_element_type=jnp.float32
    )


def local(
    tokens,
    doc_starts,
    attn_gain,
    mlp_gain,
    query_weight,
    key_weight,
    value_weight,
    output_weight,
    gate_weight,
    up_weight,
    down_weight,
    cotangent,
):
    micro_rows = tokens.shape[0] // MICRO
    span_len = tokens.shape[1]
    model_width = tokens.shape[2]
    head_count = query_weight.shape[1] // FDIM
    outputs_main = []
    outputs_grad = []
    totals = None
    for micro_index in range(MICRO):
        row_start = micro_index * micro_rows
        rows_in = tokens[row_start : row_start + micro_rows]
        starts_in = doc_starts[row_start : row_start + micro_rows]
        cot_in = cotangent[row_start : row_start + micro_rows].reshape(-1, model_width)
        (
            full_query,
            full_key,
            full_value,
            full_gate,
            full_up,
            full_output,
            full_down,
            gain_one,
            gain_two,
        ) = (
            lax.all_gather(query_weight, ("dp", "seq"), axis=0, tiled=True),
            lax.all_gather(key_weight, ("dp", "seq"), axis=0, tiled=True),
            lax.all_gather(value_weight, ("dp", "seq"), axis=0, tiled=True),
            lax.all_gather(gate_weight, ("dp", "seq"), axis=0, tiled=True),
            lax.all_gather(up_weight, ("dp", "seq"), axis=0, tiled=True),
            lax.all_gather(output_weight, ("dp", "seq"), axis=1, tiled=True),
            lax.all_gather(down_weight, ("dp", "seq"), axis=1, tiled=True),
            lax.all_gather(attn_gain, ("dp", "seq"), axis=0, tiled=True),
            lax.all_gather(mlp_gain, ("dp", "seq"), axis=0, tiled=True),
        )
        gain_one_f = gain_one.astype(jnp.float32)
        gain_two_f = gain_two.astype(jnp.float32)
        flat_rows = rows_in.reshape(-1, model_width).astype(jnp.float32)
        scale_one = inverse_rms(flat_rows)
        normed_one = (flat_rows * scale_one * gain_one_f).astype(jnp.bfloat16)
        query_low = jnp.dot(normed_one, full_query, preferred_element_type=jnp.float32).astype(
            jnp.bfloat16
        )
        key_low = jnp.dot(normed_one, full_key, preferred_element_type=jnp.float32).astype(
            jnp.bfloat16
        )
        value_low = jnp.dot(normed_one, full_value, preferred_element_type=jnp.float32).astype(
            jnp.bfloat16
        )
        queries = query_low.astype(jnp.float32).reshape(micro_rows, span_len, head_count, FDIM)
        key_rows = key_low.astype(jnp.float32).reshape(micro_rows, span_len, head_count, FDIM)
        values = value_low.astype(jnp.float32).reshape(micro_rows, span_len, head_count, VHEAD)
        segments = jnp.cumsum(starts_in, axis=1)
        reset_flag = (segments[:, -1] > 0).astype(jnp.float32)
        (tail_state, tail_norm), tail_pull = jax.vjp(
            partial(tail_span, segments=segments), key_rows, values
        )
        state_in, norm_in, reset_in = prefix(
            (tail_state, tail_norm, reset_flag),
            "seq",
            combine_carry,
            (jnp.zeros_like(tail_state), jnp.zeros_like(tail_norm), jnp.zeros_like(reset_flag)),
            False,
        )
        mixed_heads, mix_pull = jax.vjp(
            partial(mix_span, segments=segments), queries, key_rows, values, state_in, norm_in
        )
        mixed_low = mixed_heads.reshape(-1, head_count * VHEAD).astype(jnp.bfloat16)
        branch_one = jnp.dot(mixed_low, full_output, preferred_element_type=jnp.float32)
        residual = flat_rows + lax.psum(branch_one, "tensor")
        scale_two = inverse_rms(residual)
        normed_two = (residual * scale_two * gain_two_f).astype(jnp.bfloat16)
        gate_proj = jnp.dot(normed_two, full_gate, preferred_element_type=jnp.float32)
        up_proj = jnp.dot(normed_two, full_up, preferred_element_type=jnp.float32)
        sigmoid_gate = jax.nn.sigmoid(gate_proj)
        hidden = (gate_proj * sigmoid_gate * up_proj).astype(jnp.bfloat16)
        branch_two = jnp.dot(hidden, full_down, preferred_element_type=jnp.float32)
        block_low = (
            residual + lax.psum(branch_two.astype(jnp.bfloat16), "tensor").astype(jnp.float32)
        ).astype(jnp.bfloat16)
        outputs_main.append(block_low.reshape(micro_rows, span_len, model_width))
        grad_down = inner_rows(hidden, cot_in)
        grad_hidden = by_transpose(cot_in, full_down)
        grad_gate_low = (
            grad_hidden * up_proj * sigmoid_gate * (1.0 + gate_proj * (1.0 - sigmoid_gate))
        ).astype(jnp.bfloat16)
        grad_up_low = (grad_hidden * gate_proj * sigmoid_gate).astype(jnp.bfloat16)
        grad_gate = inner_rows(normed_two, grad_gate_low)
        grad_up = inner_rows(normed_two, grad_up_low)
        grad_normed_two = by_transpose(grad_gate_low, full_gate) + by_transpose(
            grad_up_low, full_up
        )
        grad_normed_two = lax.psum(grad_normed_two, "tensor")
        grad_resid, grad_gain_two = norm_backward(residual, scale_two, gain_two_f, grad_normed_two)
        grad_resid = grad_resid + cot_in.astype(jnp.float32)
        grad_resid_low = grad_resid.astype(jnp.bfloat16)
        grad_output = inner_rows(mixed_low, grad_resid_low)
        grad_mixed = by_transpose(grad_resid_low, full_output).astype(jnp.bfloat16)
        grad_mixed = (
            lax.optimization_barrier(grad_mixed)
            .astype(jnp.float32)
            .reshape(micro_rows, span_len, head_count, VHEAD)
        )
        grad_queries, grad_keys, grad_values, grad_state, grad_norm = mix_pull(grad_mixed)
        carried_state, carried_norm, reset_out = prefix(
            (grad_state, grad_norm, reset_flag),
            "seq",
            combine_carry,
            (jnp.zeros_like(grad_state), jnp.zeros_like(grad_norm), jnp.zeros_like(reset_flag)),
            True,
        )
        more_keys, more_values = tail_pull((carried_state, carried_norm))
        grad_query_low = grad_queries.reshape(-1, head_count * FDIM).astype(jnp.bfloat16)
        grad_key_low = (grad_keys + more_keys).reshape(-1, head_count * FDIM).astype(jnp.bfloat16)
        grad_value_low = (
            (grad_values + more_values).reshape(-1, head_count * VHEAD).astype(jnp.bfloat16)
        )
        grad_query = inner_rows(normed_one, grad_query_low)
        grad_key = inner_rows(normed_one, grad_key_low)
        grad_value = inner_rows(normed_one, grad_value_low)
        grad_normed_one = (
            by_transpose(grad_query_low, full_query)
            + by_transpose(grad_key_low, full_key)
            + by_transpose(grad_value_low, full_value)
        )
        grad_normed_one = lax.psum(grad_normed_one, "tensor")
        grad_inputs, grad_gain_one = norm_backward(
            flat_rows, scale_one, gain_one_f, grad_normed_one
        )
        outputs_grad.append((grad_resid + grad_inputs).reshape(micro_rows, span_len, model_width))
        shares = (
            grad_query,
            grad_key,
            grad_value,
            grad_gate,
            grad_up,
            grad_output,
            grad_down,
            grad_gain_one,
            grad_gain_two,
        )
        if totals is None:
            totals = shares
        else:
            totals = jax.tree.map(jnp.add, totals, shares)
    totals = (
        lax.psum_scatter(totals[0], ("dp", "seq"), scatter_dimension=0, tiled=True),
        lax.psum_scatter(totals[1], ("dp", "seq"), scatter_dimension=0, tiled=True),
        lax.psum_scatter(totals[2], ("dp", "seq"), scatter_dimension=0, tiled=True),
        lax.psum_scatter(totals[3], ("dp", "seq"), scatter_dimension=0, tiled=True),
        lax.psum_scatter(totals[4], ("dp", "seq"), scatter_dimension=0, tiled=True),
        lax.psum_scatter(totals[5], ("dp", "seq"), scatter_dimension=1, tiled=True),
        lax.psum_scatter(totals[6], ("dp", "seq"), scatter_dimension=1, tiled=True),
        lax.psum_scatter(totals[7], ("dp", "seq"), scatter_dimension=0, tiled=True),
        lax.psum_scatter(totals[8], ("dp", "seq"), scatter_dimension=0, tiled=True),
    )
    return (
        jnp.concatenate(outputs_main, axis=0),
        jnp.concatenate(outputs_grad, axis=0),
        totals[7],
        totals[8],
        totals[0],
        totals[1],
        totals[2],
        totals[5],
        totals[3],
        totals[4],
        totals[6],
    )


MESH_ID = pl.DeviceIdType.MESH
VMEM_LIMIT = 52 << 20


def nt_dot(a, b):
    return lax.dot_general(a, b, (((1,), (1,)), ((), ())), preferred_element_type=jnp.float32)


def tn_dot(a, b):
    return lax.dot_general(a, b, (((0,), (0,)), ((), ())), preferred_element_type=jnp.float32)


def nn_dot(a, b):
    return lax.dot_general(a, b, (((1,), (0,)), ((), ())), preferred_element_type=jnp.float32)


def plane_places():
    at, core = lax.axis_index("dp"), lax.axis_index("tensor")
    x_bit, y_bit = lax.rem(at, 2), at // 2
    return (
        at,
        y_bit * 2 + (1 - x_bit),
        (1 - y_bit) * 2 + x_bit,
        (1 - y_bit) * 2 + (1 - x_bit),
        core,
    )


def greet(places):
    barrier = pltpu.get_barrier_semaphore()
    for place in places:
        pl.semaphore_signal(barrier, inc=1, device_id=place, device_id_type=MESH_ID)
    pl.semaphore_wait(barrier, len(places))


class Sender:
    def __init__(self, sems):
        self.sems, self.used = sems, 0

    def __call__(self, src, dst, place):
        index = self.used
        self.used += 1
        return pltpu.make_async_remote_copy(
            src_ref=src,
            dst_ref=dst,
            send_sem=self.sems.at[0, index],
            recv_sem=self.sems.at[1, index],
            device_id=place,
            device_id_type=MESH_ID,
        )


def greet_plane():
    at, x_at, y_at, _, core = plane_places()
    greet([{"dp": x_at}, {"dp": y_at}, {"tensor": 1 - core}])


def add_rows(dst, *srcs, step=64):
    def body(i, carry):
        r = pl.ds(pl.multiple_of(i * step, step), step)
        total = srcs[0][r].astype(jnp.float32)
        for s in srcs[1:]:
            total = total + s[r].astype(jnp.float32)
        dst[r] = total.astype(dst.dtype)
        return carry

    lax.fori_loop(0, srcs[0].shape[0] // step, body, 0)


GATHER_COPIES = 13
SCATTER_COPIES = 10


def gather_steps(own_ref, out_ref, copy, local_sem):
    at, x_at, y_at, d_at, core = plane_places()
    half = own_ref.shape[0] // 2
    xp, yp, sp = {"dp": x_at}, {"dp": y_at}, {"tensor": 1 - core}
    lo, hi = pl.ds(0, half), pl.ds(half, half)
    mine = out_ref.at[at, core]
    x_lo = copy(own_ref.at[lo], mine.at[lo], xp)
    y_hi = copy(own_ref.at[hi], mine.at[hi], yp)
    x_hi = copy(own_ref.at[hi], mine.at[hi], xp)
    y_lo = copy(own_ref.at[lo], mine.at[lo], yp)
    pair = copy(own_ref, mine, sp)
    for c in (x_lo, y_hi, x_hi, y_lo, pair):
        c.start()
    local_copy = pltpu.make_async_copy(own_ref, mine, local_sem)
    local_copy.start()
    from_x, from_y, from_d = out_ref.at[x_at, core], out_ref.at[y_at, core], out_ref.at[d_at, core]
    on_y = copy(from_x.at[lo], from_x.at[lo], yp)
    on_x = copy(from_y.at[hi], from_y.at[hi], xp)
    late = [pair]

    def hand(block, rows):
        c = copy(block.at[rows], block.at[rows], sp)
        c.start()
        late.append(c)

    x_lo.wait_recv()
    on_y.start()
    hand(from_x, lo)
    y_hi.wait_recv()
    on_x.start()
    hand(from_y, hi)
    x_hi.wait_recv()
    hand(from_x, hi)
    y_lo.wait_recv()
    hand(from_y, lo)
    on_y.wait_recv()
    hand(from_d, lo)
    on_x.wait_recv()
    hand(from_d, hi)
    for c in late:
        c.wait_recv()
    for c in [x_lo, y_hi, x_hi, y_lo, on_y, on_x] + late:
        c.wait_send()
    local_copy.wait()


def gather_kernel(own_ref, out_ref, sems, local_sem):
    greet_plane()
    gather_steps(own_ref, out_ref, Sender(sems), local_sem)


def plane_gather(own, cid):
    m, width = own.shape
    out = pl.pallas_call(
        gather_kernel,
        name="plane_gather",
        out_shape=jax.ShapeDtypeStruct((4, 2, m, width), own.dtype),
        in_specs=[pl.BlockSpec(memory_space=pltpu.VMEM)],
        out_specs=pl.BlockSpec(memory_space=pl.ANY),
        scratch_shapes=[pltpu.SemaphoreType.DMA((2, GATHER_COPIES)), pltpu.SemaphoreType.DMA],
        compiler_params=pltpu.CompilerParams(collective_id=cid, has_side_effects=True),
        cost_estimate=pl.CostEstimate(flops=0, bytes_accessed=own.size * 80, transcendentals=0),
    )(own)
    return out.reshape(8 * m, width)


def scatter_steps(part_ref, out_ref, pair_ref, sum_ref, got_ref, copy):
    at, x_at, y_at, d_at, core = plane_places()
    half = part_ref.shape[2] // 2
    xp, yp, sp = {"dp": x_at}, {"dp": y_at}, {"tensor": 1 - core}
    lo, hi = pl.ds(0, half), pl.ds(half, half)
    order = (d_at, x_at, y_at, at)
    pairs = [copy(part_ref.at[to, 1 - core], pair_ref.at[j], sp) for j, to in enumerate(order)]
    for c in pairs:
        c.start()

    def total(j, rows, *more):
        add_rows(
            sum_ref.at[j, rows], part_ref.at[order[j], core, rows], pair_ref.at[j, rows], *more
        )

    def sent(j, rows, place):
        return copy(sum_ref.at[j, rows], got_ref.at[j, rows], place)

    d_lo, d_hi = sent(0, lo, xp), sent(0, hi, yp)
    x_lo, y_hi, x_hi, y_lo = sent(1, lo, xp), sent(2, hi, yp), sent(1, hi, xp), sent(2, lo, yp)
    pairs[0].wait_recv()
    total(0, lo)
    d_lo.start()
    total(0, hi)
    d_hi.start()
    pairs[1].wait_recv()
    total(1, lo)
    x_lo.start()
    pairs[2].wait_recv()
    total(2, hi)
    y_hi.start()
    d_lo.wait_recv()
    total(2, lo, got_ref.at[0, lo])
    y_lo.start()
    d_hi.wait_recv()
    total(1, hi, got_ref.at[0, hi])
    x_hi.start()
    pairs[3].wait_recv()
    for c in (x_lo, y_hi, y_lo, x_hi):
        c.wait_recv()
    add_rows(out_ref, part_ref.at[at, core], pair_ref.at[3], got_ref.at[1], got_ref.at[2])
    for c in pairs + [d_lo, d_hi, x_lo, y_hi, x_hi, y_lo]:
        c.wait_send()


def scatter_kernel(part_ref, out_ref, pair_ref, sum_ref, got_ref, sems):
    greet_plane()
    scatter_steps(part_ref, out_ref, pair_ref, sum_ref, got_ref, Sender(sems))


def plane_scatter(part, cid):
    rows, width = part.shape
    m = rows // 8
    return pl.pallas_call(
        scatter_kernel,
        name="plane_scatter",
        out_shape=jax.ShapeDtypeStruct((m, width), jnp.float32),
        in_specs=[pl.BlockSpec(memory_space=pltpu.VMEM)],
        out_specs=pl.BlockSpec(memory_space=pltpu.VMEM),
        scratch_shapes=[
            pltpu.VMEM((4, m, width), part.dtype),
            pltpu.VMEM((3, m, width), part.dtype),
            pltpu.VMEM((3, m, width), part.dtype),
            pltpu.SemaphoreType.DMA((2, SCATTER_COPIES)),
        ],
        compiler_params=pltpu.CompilerParams(
            collective_id=cid, has_side_effects=True, vmem_limit_bytes=VMEM_LIMIT
        ),
        cost_estimate=pl.CostEstimate(flops=0, bytes_accessed=part.size * 10, transcendentals=0),
    )(part.reshape(4, 2, m, width))


def exchange_kernel(axis, take, put, count, *refs):
    ins, outs, sems, local_sems = refs[:count], refs[count : 2 * count], refs[-2], refs[-1]
    size, me = lax.axis_size(axis), lax.axis_index(axis)
    peers = [lax.rem(me + k, size) for k in range(1, size)]
    greet([{axis: p} for p in peers])
    copy = Sender(sems)
    copies = [copy(take(i, p), put(o, me), {axis: p}) for i, o in zip(ins, outs) for p in peers]
    copies += [
        pltpu.make_async_copy(take(i, me), put(o, me), local_sems.at[n])
        for n, (i, o) in enumerate(zip(ins, outs))
    ]
    for c in copies:
        c.start()
    for c in copies:
        c.wait()


def block_of(ref, index):
    return ref.at[index]


def columns_of(ref, index):
    width = ref.shape[1] // lax.axis_size("dp")
    return ref.at[:, pl.ds(pl.multiple_of(index * width, width), width)]


def exchange(arrays, axis, cid, shapes, take=block_of, put=block_of):
    count, peers = len(arrays), lax.axis_size(axis) - 1
    anywhere = [pl.BlockSpec(memory_space=pl.ANY)] * count
    return pl.pallas_call(
        partial(exchange_kernel, axis, take, put, count),
        name="exchange_" + axis,
        out_shape=[jax.ShapeDtypeStruct(s, x.dtype) for s, x in zip(shapes, arrays)],
        in_specs=anywhere,
        out_specs=anywhere,
        scratch_shapes=[
            pltpu.SemaphoreType.DMA((2, count * peers)),
            pltpu.SemaphoreType.DMA((count,)),
        ],
        compiler_params=pltpu.CompilerParams(collective_id=cid, has_side_effects=True),
        cost_estimate=pl.CostEstimate(
            flops=0, bytes_accessed=60 * sum(x.size for x in arrays), transcendentals=0
        ),
    )(*arrays)


def first_kernel(pack_ref, small_ref, out_ref, all_ref, sems, small_sems, local_sems):
    plane, span = lax.axis_size("dp"), lax.axis_size("seq")
    at, z = lax.axis_index("dp"), lax.axis_index("seq")
    places = [
        {"dp": lax.rem(at + i, plane), "seq": lax.rem(z + k, span)}
        for k in range(span)
        for i in range(plane)
        if i or k
    ]
    greet(places)
    copy, copy_small = Sender(sems), Sender(small_sems)
    block = all_ref.at[z * plane + at]
    copies = [copy_small(small_ref, block, p) for p in places]
    for i in range(1, plane):
        to = lax.rem(at + i, plane)
        copies.append(copy(pack_ref.at[to], columns_of(out_ref, at), {"dp": to}))
    copies.append(pltpu.make_async_copy(small_ref, block, local_sems.at[0]))
    copies.append(
        pltpu.make_async_copy(pack_ref.at[at], columns_of(out_ref, at), local_sems.at[1])
    )
    for c in copies:
        c.start()
    for c in copies:
        c.wait()


def first_exchange(pack, small, cid):
    plane, span = lax.axis_size("dp"), lax.axis_size("seq")
    _, size, chunk = pack.shape
    anywhere = pl.BlockSpec(memory_space=pl.ANY)
    whole = pl.BlockSpec(memory_space=pltpu.VMEM)
    return pl.pallas_call(
        first_kernel,
        name="first_exchange",
        out_shape=[
            jax.ShapeDtypeStruct((size, plane * chunk), pack.dtype),
            jax.ShapeDtypeStruct((span * plane,) + small.shape, small.dtype),
        ],
        in_specs=[anywhere, whole],
        out_specs=[anywhere, whole],
        scratch_shapes=[
            pltpu.SemaphoreType.DMA((2, plane - 1)),
            pltpu.SemaphoreType.DMA((2, plane * span - 1)),
            pltpu.SemaphoreType.DMA((2,)),
        ],
        compiler_params=pltpu.CompilerParams(collective_id=cid, has_side_effects=True),
        cost_estimate=pl.CostEstimate(
            flops=0, bytes_accessed=60 * pack.size, transcendentals=0
        ),
    )(pack, small)


def ffn_kernel(normed_ref, cot_ref, w_ref, out_ref, dnormed_ref, dgate_ref, dup_ref, hidden_ref):
    parts, units, depth = w_ref.shape
    units //= 3

    def rows(k):
        return pl.ds(k * units, units)

    def cols(s):
        return pl.ds(s * depth, depth)

    def project(x_ref, k):
        total = nt_dot(x_ref[:, cols(0)], w_ref[0, rows(k)])
        for s in range(1, parts):
            total += nt_dot(x_ref[:, cols(s)], w_ref[s, rows(k)])
        return total

    gate, up, dhidden = project(normed_ref, 0), project(normed_ref, 1), project(cot_ref, 2)
    sig = jax.nn.sigmoid(gate)
    silu = gate * sig
    hidden = (silu * up).astype(jnp.bfloat16)
    dgate = (dhidden * up * sig * (1.0 + gate * (1.0 - sig))).astype(jnp.bfloat16)
    dup = (dhidden * silu).astype(jnp.bfloat16)
    hidden_ref[...], dgate_ref[...], dup_ref[...] = hidden, dgate, dup
    for s in range(parts):
        dnormed_ref[:, cols(s)] = (
            nn_dot(dgate, w_ref[s, rows(0)]) + nn_dot(dup, w_ref[s, rows(1)])
        ).astype(jnp.bfloat16)
        out_ref[:, cols(s)] = nn_dot(hidden, w_ref[s, rows(2)]).astype(jnp.bfloat16)


def ffn(normed, cot, weights, block=256):
    tokens, width = normed.shape
    units = weights.shape[1] // 3
    wide = pl.BlockSpec((block, width), lambda i: (i, 0))
    thin = pl.BlockSpec((block, units), lambda i: (i, 0))
    return pl.pallas_call(
        ffn_kernel,
        name="ffn",
        grid=(tokens // block,),
        out_shape=[jax.ShapeDtypeStruct((tokens, width), jnp.bfloat16)] * 2
        + [jax.ShapeDtypeStruct((tokens, units), jnp.bfloat16)] * 3,
        in_specs=[
            wide,
            wide,
            pl.BlockSpec(weights.shape, lambda i: (0, 0, 0), pipeline_mode=pl.Buffered(1)),
        ],
        out_specs=[wide, wide, thin, thin, thin],
        compiler_params=pltpu.CompilerParams(vmem_limit_bytes=VMEM_LIMIT),
        cost_estimate=pl.CostEstimate(
            flops=12 * tokens * width * units,
            bytes_accessed=2 * (4 * tokens * width + weights.size + 3 * tokens * units),
            transcendentals=tokens * units,
        ),
    )(normed, cot, weights)


def to_whole_rows(x, rows, length, cid):
    span = lax.axis_size("seq")
    width = x.shape[-1]
    [x] = exchange(
        [x.reshape(span, rows * length, width)], "seq", cid, [(span, rows * length, width)]
    )
    return x.reshape(span, rows, length, width).transpose(1, 0, 2, 3).reshape(
        rows, span * length, width
    )


def from_whole_rows(x, rows, length, cid):
    span = lax.axis_size("seq")
    width = x.shape[-1]
    x = x.reshape(rows, span, length, width).transpose(1, 0, 2, 3)
    [x] = exchange(
        [x.reshape(span, rows * length, width)], "seq", cid, [(span, rows * length, width)]
    )
    return x.reshape(span * rows * length, width)


def attention_forward(queries, keys, values, segments):
    length = queries.shape[1]
    scores = jnp.einsum("rthf,rshf->rhts", queries, keys, preferred_element_type=jnp.float32) / 4.0
    position = jnp.arange(length)
    allowed = (position[None, :] <= position[:, None])[None] & (
        segments[:, :, None] == segments[:, None, :]
    )
    weight = jnp.where(allowed[:, None], 1.0 + scores + 0.5 * scores * scores, 0.0)
    den = jnp.sum(weight, axis=-1)
    num = jnp.einsum(
        "rhts,rshe->rhte", weight.astype(jnp.bfloat16), values, preferred_element_type=jnp.float32
    )
    return num / den[..., None], den, weight, scores, allowed


def attention_backward(queries, keys, values, mixed, den, weight, scores, allowed, dmixed):
    dn = jnp.transpose(dmixed, (0, 2, 1, 3)).astype(jnp.float32) / den[..., None]
    dd = -jnp.sum(dn * mixed, axis=-1)
    dn_low = dn.astype(jnp.bfloat16)
    dw = jnp.einsum("rhte,rshe->rhts", dn_low, values, preferred_element_type=jnp.float32)
    dw = jnp.where(allowed[:, None], dw + dd[..., None], 0.0)
    dvalues = jnp.einsum(
        "rhts,rhte->rshe", weight.astype(jnp.bfloat16), dn_low, preferred_element_type=jnp.float32
    )
    da = (dw * (1.0 + scores) * 0.25).astype(jnp.bfloat16)
    dqueries = jnp.einsum("rhts,rshf->rthf", da, keys, preferred_element_type=jnp.float32)
    dkeys = jnp.einsum("rhts,rthf->rshf", da, queries, preferred_element_type=jnp.float32)
    return dqueries, dkeys, dvalues


def plane_local(
    tokens,
    doc_starts,
    attn_gain,
    mlp_gain,
    query_weight,
    key_weight,
    value_weight,
    output_weight,
    gate_weight,
    up_weight,
    down_weight,
    cotangent,
):
    plane, span, cores = (lax.axis_size("dp"), lax.axis_size("seq"), lax.axis_size("tensor"))
    rows, length, width = tokens.shape
    chunk = width // (plane * span)
    own = rows * length // cores
    heads = query_weight.shape[1] // FDIM // plane
    hidden_part = gate_weight.shape[1] // plane
    vcols, qcols = heads * VHEAD, heads * FDIM
    all_rows = rows * plane // span

    def seq_major(a):
        return (
            a.reshape(a.shape[:-1] + (plane, span, chunk)).swapaxes(-3, -2).reshape(a.shape)
        )

    def plane_major(a):
        return (
            a.reshape(a.shape[:-1] + (span, plane, chunk)).swapaxes(-3, -2).reshape(a.shape)
        )

    core = lax.axis_index("tensor")
    def over_seq(pack):
        return lax.all_gather(pack, "seq", axis=0, tiled=False)

    def flat(pack):
        return pack.transpose(1, 0, 2).reshape(-1, width)

    def summed(grads):
        return lax.psum_scatter(
            grads.astype(jnp.bfloat16), "seq", scatter_dimension=1, tiled=True
        )

    def collect(parts, cid):
        return exchange(
            parts, "dp", cid, [(plane, p.shape[0], chunk) for p in parts], take=columns_of
        )

    def split(w):
        return w.reshape(plane, -1, chunk)

    small = jnp.concatenate(
        [
            attn_gain.astype(jnp.float32)[None],
            mlp_gain.astype(jnp.float32)[None],
            doc_starts.astype(jnp.float32).reshape(-1, chunk),
            jnp.zeros((2, chunk), jnp.float32),
        ]
    )
    attn_pack = jnp.concatenate(
        [split(value_weight.T), split(query_weight.T), split(key_weight.T), split(output_weight)],
        axis=1,
    )
    attn_pack, small = first_exchange(attn_pack, small, 1)
    ffn_pack = jnp.concatenate([split(gate_weight.T), split(up_weight.T), split(down_weight)], axis=1)
    ffn_pack, _ = lax.optimization_barrier((ffn_pack, attn_pack))
    [ffn_pack] = exchange(
        [ffn_pack], "dp", 2, [(ffn_pack.shape[1], plane * chunk)], put=columns_of
    )
    attn_pack, ffn_pack = over_seq(attn_pack), over_seq(ffn_pack)
    gain_one = small[:, 0].reshape(width)
    gain_two = small[:, 1].reshape(width)
    starts = small[:, 2:-2].reshape(span, plane * rows, length)
    starts = lax.dynamic_slice_in_dim(starts, lax.axis_index("seq") * all_rows, all_rows, 1)
    segments = jnp.cumsum(starts.transpose(1, 0, 2).reshape(all_rows, span * length), axis=1)

    qkv_rows = vcols + 2 * qcols
    w_qkv, w_out = flat(attn_pack[:, :qkv_rows]), flat(attn_pack[:, qkv_rows:])

    def mine(a):
        a = lax.dynamic_slice_in_dim(a.reshape(rows * length, width), core * own, own, 0)
        return seq_major(a)

    x = mine(tokens).astype(jnp.float32)
    cot_own = mine(cotangent)
    scale_one = inverse_rms(x)
    normed_one = plane_gather((x * scale_one * gain_one).astype(jnp.bfloat16), 3)
    cot = plane_gather(cot_own, 4)
    qkv = nt_dot(normed_one, w_qkv).astype(jnp.bfloat16)
    qkv = to_whole_rows(qkv, all_rows, length, 5)
    values = qkv[..., :vcols].reshape(all_rows, -1, heads, VHEAD)
    queries = qkv[..., vcols : vcols + qcols].reshape(all_rows, -1, heads, FDIM)
    keys = qkv[..., vcols + qcols :].reshape(all_rows, -1, heads, FDIM)
    mixed, den, weight, scores, allowed = attention_forward(queries, keys, values, segments)
    mixed_low = mixed.transpose(0, 2, 1, 3).reshape(all_rows, -1, vcols).astype(jnp.bfloat16)
    mixed_low = from_whole_rows(mixed_low, all_rows, length, 6)
    residual = x + plane_scatter(nn_dot(mixed_low, w_out).astype(jnp.bfloat16), 7)
    scale_two = inverse_rms(residual)
    normed_two = plane_gather((residual * scale_two * gain_two).astype(jnp.bfloat16), 11)
    out_part, dnormed_part, dgate, dup, hidden = ffn(normed_two, cot, ffn_pack)
    down_grad = tn_dot(hidden, cot).astype(jnp.bfloat16)
    gate_grad = tn_dot(dgate, normed_two).astype(jnp.bfloat16)
    up_grad = tn_dot(dup, normed_two).astype(jnp.bfloat16)
    dnormed_part, gate_grad, up_grad, down_grad = lax.optimization_barrier(
        (dnormed_part, gate_grad, up_grad, down_grad)
    )
    down_grad, gate_grad, up_grad = summed(down_grad), summed(gate_grad), summed(up_grad)
    dnormed_two = plane_scatter(dnormed_part, 9)
    dresid, gain_two_grad = norm_backward(residual, scale_two, gain_two, dnormed_two)
    dresid = dresid + cot_own.astype(jnp.float32)
    dresid_low = plane_gather(dresid.astype(jnp.bfloat16), 12)
    block_own = (residual + plane_scatter(out_part, 8)).astype(jnp.bfloat16)
    dmixed = nt_dot(dresid_low, w_out).astype(jnp.bfloat16)
    dmixed = to_whole_rows(dmixed, all_rows, length, 13).reshape(all_rows, -1, heads, VHEAD)
    dqueries, dkeys, dvalues = attention_backward(
        queries, keys, values, mixed, den, weight, scores, allowed, dmixed
    )
    dqkv = jnp.concatenate(
        [
            d.reshape(all_rows, span * length, -1).astype(jnp.bfloat16)
            for d in (dvalues, dqueries, dkeys)
        ],
        axis=-1,
    )
    dqkv = from_whole_rows(dqkv, all_rows, length, 14)
    dnormed_one = plane_scatter(nn_dot(dqkv, w_qkv).astype(jnp.bfloat16), 10)
    out_grad = summed(tn_dot(mixed_low, dresid_low))
    qkv_grad = tn_dot(dqkv, normed_one)
    dtokens, gain_one_grad = norm_backward(x, scale_one, gain_one, dnormed_one)
    dtokens = dresid + dtokens
    gain_grads = jnp.stack([gain_one_grad, gain_two_grad])
    qkv_grad = summed(
        jnp.concatenate([qkv_grad, jnp.pad(gain_grads, ((0, 14), (0, 0)))], axis=0)
    )
    down_grad, gate_grad, up_grad, dtokens = lax.optimization_barrier(
        (down_grad, gate_grad, up_grad, dtokens)
    )
    down_grad, gate_grad, up_grad = collect([down_grad, gate_grad, up_grad], 15)
    out_grad, qkv_grad = collect([out_grad, qkv_grad], 16)
    gain_grads = qkv_grad[:, qkv_rows : qkv_rows + 2].astype(jnp.float32).sum(axis=0)
    gain_grads = lax.psum(gain_grads, "tensor")

    def whole(a):
        a = lax.all_gather(plane_major(a), "tensor", axis=0, tiled=True)
        return a.reshape(rows, length, width)

    def stacked(a, start, size):
        return a[:, start : start + size].reshape(plane * size, chunk).astype(jnp.float32)

    h = hidden_part
    return (
        whole(block_own),
        whole(dtokens),
        gain_grads[0],
        gain_grads[1],
        stacked(qkv_grad, vcols, qcols).T,
        stacked(qkv_grad, vcols + qcols, qcols).T,
        stacked(qkv_grad, 0, vcols).T,
        stacked(out_grad, 0, vcols),
        stacked(gate_grad, 0, h).T,
        stacked(up_grad, 0, h).T,
        stacked(down_grad, 0, h),
    )


def fits_plane(mesh, tokens, query_weight, gate_weight):
    plane, span, cores = (mesh.shape[a] for a in ("dp", "seq", "tensor"))
    heads = query_weight.shape[1] // FDIM // cores
    return (
        plane == 4
        and cores == 2
        and heads % plane == 0
        and (gate_weight.shape[1] // cores) % (16 * plane) == 0
        and tokens.shape[0] % span == 0
    )


def solution(mesh):
    def step(*args):
        use = fits_plane(mesh, args[0], args[4], args[8])
        return sharded(mesh, plane_local if use else local)(*args)

    return step


def sharded(mesh, body):
    return jax.shard_map(
        body,
        mesh=mesh,
        in_specs=(
            P("dp", "seq", None),
            P("dp", "seq"),
            P(("dp", "seq")),
            P(("dp", "seq")),
            P(("dp", "seq"), "tensor"),
            P(("dp", "seq"), "tensor"),
            P(("dp", "seq"), "tensor"),
            P("tensor", ("dp", "seq")),
            P(("dp", "seq"), "tensor"),
            P(("dp", "seq"), "tensor"),
            P("tensor", ("dp", "seq")),
            P("dp", "seq", None),
        ),
        out_specs=(
            P("dp", "seq", None),
            P("dp", "seq", None),
            P(("dp", "seq")),
            P(("dp", "seq")),
            P(("dp", "seq"), "tensor"),
            P(("dp", "seq"), "tensor"),
            P(("dp", "seq"), "tensor"),
            P("tensor", ("dp", "seq")),
            P(("dp", "seq"), "tensor"),
            P(("dp", "seq"), "tensor"),
            P("tensor", ("dp", "seq")),
        ),
        check_vma=False,
    )
```

```python
from functools import partial

import jax
import jax.numpy as jnp
from jax import lax
from jax.experimental import pallas as pl
from jax.experimental.pallas import tpu as pltpu
from jax.sharding import PartitionSpec as P

FDIM = 16
VHEAD = 128
MICRO = 2


norm_epsilon = 1e-05
highest = lax.Precision.HIGHEST
outer_scale = 0.17677669529663687


def prefix(x, axis, combine, identity, reverse):
    size, index = (lax.axis_size(axis), lax.axis_index(axis))
    everything = jax.tree.map(lambda part: lax.all_gather(part, axis), x)
    start = jax.tree.map(
        lambda part, zero: jnp.broadcast_to(jnp.asarray(zero, part.dtype), part.shape), x, identity
    )

    def turn(k, before):
        at = size - 1 - k if reverse else k
        reached = at > index if reverse else at < index
        new = combine(before, jax.tree.map(lambda part: part[at], everything))
        return jax.tree.map(lambda a, b: jnp.where(reached, a, b), new, before)

    return lax.fori_loop(0, size, turn, start)


def features(vectors):
    ones_col = jnp.ones(vectors.shape[:-1] + (1,), jnp.float32)
    outer_terms = vectors[..., :, None] * vectors[..., None, :] * outer_scale
    outer_terms = outer_terms.reshape(vectors.shape[:-1] + (vectors.shape[-1] * vectors.shape[-1],))
    return jnp.concatenate([ones_col, 0.5 * vectors, outer_terms], axis=-1)


def mix_span(queries, key_rows, values, state_in, norm_in, segments):
    length = queries.shape[1]
    scores = jnp.einsum("rthf,rshf->rhts", queries, key_rows, precision=highest) / 4.0
    kernel = 1.0 + scores + 0.5 * scores * scores
    position = jnp.arange(length)
    causal = position[None, :] <= position[:, None]
    allowed = causal[None] & (segments[:, :, None] == segments[:, None, :])
    kernel = jnp.where(allowed[:, None], kernel, 0.0)
    numerator = jnp.einsum("rhts,rshe->rthe", kernel, values, precision=highest)
    denominator = jnp.transpose(jnp.sum(kernel, axis=-1), (0, 2, 1))
    head_part = (segments == 0).astype(jnp.float32)[:, :, None]
    lifted = features(queries)
    numerator = numerator + head_part[..., None] * jnp.einsum(
        "rthf,rhfe->rthe", lifted, state_in, precision=highest
    )
    denominator = denominator + head_part * jnp.einsum(
        "rthf,rhf->rth", lifted, norm_in, precision=highest
    )
    return numerator / denominator[..., None]


def tail_span(key_rows, values, segments):
    tail_mask = (segments == segments[:, -1:]).astype(jnp.float32)
    lifted = features(key_rows) * tail_mask[:, :, None, None]
    tail_state = jnp.einsum("rshf,rshe->rhfe", lifted, values, precision=highest)
    return (tail_state, jnp.sum(lifted, axis=1))


def combine_carry(earlier_part, later_part):
    keep_rate = 1.0 - later_part[2]
    return (
        later_part[0] + keep_rate[:, None, None, None] * earlier_part[0],
        later_part[1] + keep_rate[:, None, None] * earlier_part[1],
        jnp.maximum(earlier_part[2], later_part[2]),
    )


def inverse_rms(inputs):
    return lax.rsqrt(jnp.mean(inputs * inputs, axis=-1, keepdims=True) + norm_epsilon)


def norm_backward(inputs, scale_row, gain_vec, grad_normed):
    scaled_grad = grad_normed * gain_vec
    grad_gain = jnp.sum(grad_normed * inputs * scale_row, axis=0)
    grad_inputs = scale_row * scaled_grad - inputs * scale_row * scale_row * scale_row * jnp.mean(
        scaled_grad * inputs, axis=-1, keepdims=True
    )
    return (grad_inputs, grad_gain)


def inner_rows(left_mat, right_mat):
    return lax.dot_general(
        left_mat, right_mat, (((0,), (0,)), ((), ())), preferred_element_type=jnp.float32
    )


def by_transpose(left_mat, right_mat):
    return lax.dot_general(
        left_mat, right_mat, (((1,), (1,)), ((), ())), preferred_element_type=jnp.float32
    )


def local(
    tokens,
    doc_starts,
    attn_gain,
    mlp_gain,
    query_weight,
    key_weight,
    value_weight,
    output_weight,
    gate_weight,
    up_weight,
    down_weight,
    cotangent,
):
    micro_rows = tokens.shape[0] // MICRO
    span_len = tokens.shape[1]
    model_width = tokens.shape[2]
    head_count = query_weight.shape[1] // FDIM
    outputs_main = []
    outputs_grad = []
    totals = None
    for micro_index in range(MICRO):
        row_start = micro_index * micro_rows
        rows_in = tokens[row_start : row_start + micro_rows]
        starts_in = doc_starts[row_start : row_start + micro_rows]
        cot_in = cotangent[row_start : row_start + micro_rows].reshape(-1, model_width)
        (
            full_query,
            full_key,
            full_value,
            full_gate,
            full_up,
            full_output,
            full_down,
            gain_one,
            gain_two,
        ) = (
            lax.all_gather(query_weight, ("dp", "seq"), axis=0, tiled=True),
            lax.all_gather(key_weight, ("dp", "seq"), axis=0, tiled=True),
            lax.all_gather(value_weight, ("dp", "seq"), axis=0, tiled=True),
            lax.all_gather(gate_weight, ("dp", "seq"), axis=0, tiled=True),
            lax.all_gather(up_weight, ("dp", "seq"), axis=0, tiled=True),
            lax.all_gather(output_weight, ("dp", "seq"), axis=1, tiled=True),
            lax.all_gather(down_weight, ("dp", "seq"), axis=1, tiled=True),
            lax.all_gather(attn_gain, ("dp", "seq"), axis=0, tiled=True),
            lax.all_gather(mlp_gain, ("dp", "seq"), axis=0, tiled=True),
        )
        gain_one_f = gain_one.astype(jnp.float32)
        gain_two_f = gain_two.astype(jnp.float32)
        flat_rows = rows_in.reshape(-1, model_width).astype(jnp.float32)
        scale_one = inverse_rms(flat_rows)
        normed_one = (flat_rows * scale_one * gain_one_f).astype(jnp.bfloat16)
        query_low = jnp.dot(normed_one, full_query, preferred_element_type=jnp.float32).astype(
            jnp.bfloat16
        )
        key_low = jnp.dot(normed_one, full_key, preferred_element_type=jnp.float32).astype(
            jnp.bfloat16
        )
        value_low = jnp.dot(normed_one, full_value, preferred_element_type=jnp.float32).astype(
            jnp.bfloat16
        )
        queries = query_low.astype(jnp.float32).reshape(micro_rows, span_len, head_count, FDIM)
        key_rows = key_low.astype(jnp.float32).reshape(micro_rows, span_len, head_count, FDIM)
        values = value_low.astype(jnp.float32).reshape(micro_rows, span_len, head_count, VHEAD)
        segments = jnp.cumsum(starts_in, axis=1)
        reset_flag = (segments[:, -1] > 0).astype(jnp.float32)
        (tail_state, tail_norm), tail_pull = jax.vjp(
            partial(tail_span, segments=segments), key_rows, values
        )
        state_in, norm_in, reset_in = prefix(
            (tail_state, tail_norm, reset_flag),
            "seq",
            combine_carry,
            (jnp.zeros_like(tail_state), jnp.zeros_like(tail_norm), jnp.zeros_like(reset_flag)),
            False,
        )
        mixed_heads, mix_pull = jax.vjp(
            partial(mix_span, segments=segments), queries, key_rows, values, state_in, norm_in
        )
        mixed_low = mixed_heads.reshape(-1, head_count * VHEAD).astype(jnp.bfloat16)
        branch_one = jnp.dot(mixed_low, full_output, preferred_element_type=jnp.float32)
        residual = flat_rows + lax.psum(branch_one, "tensor")
        scale_two = inverse_rms(residual)
        normed_two = (residual * scale_two * gain_two_f).astype(jnp.bfloat16)
        gate_proj = jnp.dot(normed_two, full_gate, preferred_element_type=jnp.float32)
        up_proj = jnp.dot(normed_two, full_up, preferred_element_type=jnp.float32)
        sigmoid_gate = jax.nn.sigmoid(gate_proj)
        hidden = (gate_proj * sigmoid_gate * up_proj).astype(jnp.bfloat16)
        branch_two = jnp.dot(hidden, full_down, preferred_element_type=jnp.float32)
        block_low = (
            residual + lax.psum(branch_two.astype(jnp.bfloat16), "tensor").astype(jnp.float32)
        ).astype(jnp.bfloat16)
        outputs_main.append(block_low.reshape(micro_rows, span_len, model_width))
        grad_down = inner_rows(hidden, cot_in)
        grad_hidden = by_transpose(cot_in, full_down)
        grad_gate_low = (
            grad_hidden * up_proj * sigmoid_gate * (1.0 + gate_proj * (1.0 - sigmoid_gate))
        ).astype(jnp.bfloat16)
        grad_up_low = (grad_hidden * gate_proj * sigmoid_gate).astype(jnp.bfloat16)
        grad_gate = inner_rows(normed_two, grad_gate_low)
        grad_up = inner_rows(normed_two, grad_up_low)
        grad_normed_two = by_transpose(grad_gate_low, full_gate) + by_transpose(
            grad_up_low, full_up
        )
        grad_normed_two = lax.psum(grad_normed_two, "tensor")
        grad_resid, grad_gain_two = norm_backward(residual, scale_two, gain_two_f, grad_normed_two)
        grad_resid = grad_resid + cot_in.astype(jnp.float32)
        grad_resid_low = grad_resid.astype(jnp.bfloat16)
        grad_output = inner_rows(mixed_low, grad_resid_low)
        grad_mixed = by_transpose(grad_resid_low, full_output).astype(jnp.bfloat16)
        grad_mixed = (
            lax.optimization_barrier(grad_mixed)
            .astype(jnp.float32)
            .reshape(micro_rows, span_len, head_count, VHEAD)
        )
        grad_queries, grad_keys, grad_values, grad_state, grad_norm = mix_pull(grad_mixed)
        carried_state, carried_norm, reset_out = prefix(
            (grad_state, grad_norm, reset_flag),
            "seq",
            combine_carry,
            (jnp.zeros_like(grad_state), jnp.zeros_like(grad_norm), jnp.zeros_like(reset_flag)),
            True,
        )
        more_keys, more_values = tail_pull((carried_state, carried_norm))
        grad_query_low = grad_queries.reshape(-1, head_count * FDIM).astype(jnp.bfloat16)
        grad_key_low = (grad_keys + more_keys).reshape(-1, head_count * FDIM).astype(jnp.bfloat16)
        grad_value_low = (
            (grad_values + more_values).reshape(-1, head_count * VHEAD).astype(jnp.bfloat16)
        )
        grad_query = inner_rows(normed_one, grad_query_low)
        grad_key = inner_rows(normed_one, grad_key_low)
        grad_value = inner_rows(normed_one, grad_value_low)
        grad_normed_one = (
            by_transpose(grad_query_low, full_query)
            + by_transpose(grad_key_low, full_key)
            + by_transpose(grad_value_low, full_value)
        )
        grad_normed_one = lax.psum(grad_normed_one, "tensor")
        grad_inputs, grad_gain_one = norm_backward(
            flat_rows, scale_one, gain_one_f, grad_normed_one
        )
        outputs_grad.append((grad_resid + grad_inputs).reshape(micro_rows, span_len, model_width))
        shares = (
            grad_query,
            grad_key,
            grad_value,
            grad_gate,
            grad_up,
            grad_output,
            grad_down,
            grad_gain_one,
            grad_gain_two,
        )
        if totals is None:
            totals = shares
        else:
            totals = jax.tree.map(jnp.add, totals, shares)
    totals = (
        lax.psum_scatter(totals[0], ("dp", "seq"), scatter_dimension=0, tiled=True),
        lax.psum_scatter(totals[1], ("dp", "seq"), scatter_dimension=0, tiled=True),
        lax.psum_scatter(totals[2], ("dp", "seq"), scatter_dimension=0, tiled=True),
        lax.psum_scatter(totals[3], ("dp", "seq"), scatter_dimension=0, tiled=True),
        lax.psum_scatter(totals[4], ("dp", "seq"), scatter_dimension=0, tiled=True),
        lax.psum_scatter(totals[5], ("dp", "seq"), scatter_dimension=1, tiled=True),
        lax.psum_scatter(totals[6], ("dp", "seq"), scatter_dimension=1, tiled=True),
        lax.psum_scatter(totals[7], ("dp", "seq"), scatter_dimension=0, tiled=True),
        lax.psum_scatter(totals[8], ("dp", "seq"), scatter_dimension=0, tiled=True),
    )
    return (
        jnp.concatenate(outputs_main, axis=0),
        jnp.concatenate(outputs_grad, axis=0),
        totals[7],
        totals[8],
        totals[0],
        totals[1],
        totals[2],
        totals[5],
        totals[3],
        totals[4],
        totals[6],
    )


MESH_ID = pl.DeviceIdType.MESH
VMEM_LIMIT = 58 << 20
LANES = 128
ROW_STEP = 32


def nt_dot(a, b):
    return lax.dot_general(a, b, (((1,), (1,)), ((), ())), preferred_element_type=jnp.float32)


def tn_dot(a, b):
    return lax.dot_general(a, b, (((0,), (0,)), ((), ())), preferred_element_type=jnp.float32)


def nn_dot(a, b):
    return lax.dot_general(a, b, (((1,), (0,)), ((), ())), preferred_element_type=jnp.float32)


def plane_places():
    at, core = lax.axis_index("dp"), lax.axis_index("tensor")
    x_bit, y_bit = lax.rem(at, 2), at // 2
    return (
        at,
        y_bit * 2 + (1 - x_bit),
        (1 - y_bit) * 2 + x_bit,
        (1 - y_bit) * 2 + (1 - x_bit),
        core,
    )


def greet(places):
    barrier = pltpu.get_barrier_semaphore()
    for place in places:
        pl.semaphore_signal(barrier, inc=1, device_id=place, device_id_type=MESH_ID)
    pl.semaphore_wait(barrier, len(places))


class Sender:
    def __init__(self, sems):
        self.sems, self.used = sems, 0

    def __call__(self, src, dst, place):
        index = self.used
        self.used += 1
        return pltpu.make_async_remote_copy(
            src_ref=src,
            dst_ref=dst,
            send_sem=self.sems.at[0, index],
            recv_sem=self.sems.at[1, index],
            device_id=place,
            device_id_type=MESH_ID,
        )


def greet_plane():
    at, x_at, y_at, _, core = plane_places()
    greet([{"dp": x_at}, {"dp": y_at}, {"tensor": 1 - core}])


def add_rows(dst, *srcs, step=64):
    def body(i, carry):
        r = pl.ds(pl.multiple_of(i * step, step), step)
        total = srcs[0][r].astype(jnp.float32)
        for s in srcs[1:]:
            total = total + s[r].astype(jnp.float32)
        dst[r] = total.astype(dst.dtype)
        return carry

    lax.fori_loop(0, srcs[0].shape[0] // step, body, 0)


GATHER_COPIES = 13
SCATTER_COPIES = 10


def gather_steps(own_ref, out_ref, copy, local_sem):
    at, x_at, y_at, d_at, core = plane_places()
    half = own_ref.shape[0] // 2
    xp, yp, sp = {"dp": x_at}, {"dp": y_at}, {"tensor": 1 - core}
    lo, hi = pl.ds(0, half), pl.ds(half, half)
    mine = out_ref.at[at, core]
    x_lo = copy(own_ref.at[lo], mine.at[lo], xp)
    y_hi = copy(own_ref.at[hi], mine.at[hi], yp)
    x_hi = copy(own_ref.at[hi], mine.at[hi], xp)
    y_lo = copy(own_ref.at[lo], mine.at[lo], yp)
    pair = copy(own_ref, mine, sp)
    for c in (x_lo, y_hi, x_hi, y_lo, pair):
        c.start()
    local_copy = pltpu.make_async_copy(own_ref, mine, local_sem)
    local_copy.start()
    yield
    from_x, from_y, from_d = out_ref.at[x_at, core], out_ref.at[y_at, core], out_ref.at[d_at, core]
    on_y = copy(from_x.at[lo], from_x.at[lo], yp)
    on_x = copy(from_y.at[hi], from_y.at[hi], xp)
    late = [pair]

    def hand(block, rows):
        c = copy(block.at[rows], block.at[rows], sp)
        c.start()
        late.append(c)

    x_lo.wait_recv()
    on_y.start()
    hand(from_x, lo)
    y_hi.wait_recv()
    on_x.start()
    hand(from_y, hi)
    x_hi.wait_recv()
    hand(from_x, hi)
    y_lo.wait_recv()
    hand(from_y, lo)
    on_y.wait_recv()
    hand(from_d, lo)
    on_x.wait_recv()
    hand(from_d, hi)
    for c in late:
        c.wait_recv()
    for c in [x_lo, y_hi, x_hi, y_lo, on_y, on_x] + late:
        c.wait_send()
    local_copy.wait()


def scatter_steps(part_ref, out_ref, pair_ref, sum_ref, got_ref, copy):
    at, x_at, y_at, d_at, core = plane_places()
    half = part_ref.shape[2] // 2
    xp, yp, sp = {"dp": x_at}, {"dp": y_at}, {"tensor": 1 - core}
    lo, hi = pl.ds(0, half), pl.ds(half, half)
    order = (d_at, x_at, y_at, at)
    pairs = [copy(part_ref.at[to, 1 - core], pair_ref.at[j], sp) for j, to in enumerate(order)]
    for c in pairs:
        c.start()
    yield

    def total(j, rows, *more):
        add_rows(
            sum_ref.at[j, rows], part_ref.at[order[j], core, rows], pair_ref.at[j, rows], *more
        )

    def sent(j, rows, place):
        return copy(sum_ref.at[j, rows], got_ref.at[j, rows], place)

    d_lo, d_hi = sent(0, lo, xp), sent(0, hi, yp)
    x_lo, y_hi, x_hi, y_lo = sent(1, lo, xp), sent(2, hi, yp), sent(1, hi, xp), sent(2, lo, yp)
    pairs[0].wait_recv()
    total(0, lo)
    d_lo.start()
    total(0, hi)
    d_hi.start()
    pairs[1].wait_recv()
    total(1, lo)
    x_lo.start()
    pairs[2].wait_recv()
    total(2, hi)
    y_hi.start()
    d_lo.wait_recv()
    total(2, lo, got_ref.at[0, lo])
    y_lo.start()
    d_hi.wait_recv()
    total(1, hi, got_ref.at[0, hi])
    x_hi.start()
    pairs[3].wait_recv()
    for c in (x_lo, y_hi, y_lo, x_hi):
        c.wait_recv()
    add_rows(out_ref, part_ref.at[at, core], pair_ref.at[3], got_ref.at[1], got_ref.at[2])
    for c in pairs + [d_lo, d_hi, x_lo, y_hi, x_hi, y_lo]:
        c.wait_send()


def exchange_kernel(axis, take, put, count, *refs):
    ins, outs, sems, local_sems = refs[:count], refs[count : 2 * count], refs[-2], refs[-1]
    size, me = lax.axis_size(axis), lax.axis_index(axis)
    peers = [lax.rem(me + k, size) for k in range(1, size)]
    greet([{axis: p} for p in peers])
    copy = Sender(sems)
    copies = [copy(take(i, p), put(o, me), {axis: p}) for i, o in zip(ins, outs) for p in peers]
    copies += [
        pltpu.make_async_copy(take(i, me), put(o, me), local_sems.at[n])
        for n, (i, o) in enumerate(zip(ins, outs))
    ]
    for c in copies:
        c.start()
    for c in copies:
        c.wait()


def block_of(ref, index):
    return ref.at[index]


def columns_of(ref, index):
    width = ref.shape[1] // lax.axis_size("dp")
    return ref.at[:, pl.ds(pl.multiple_of(index * width, width), width)]


def exchange(arrays, axis, cid, shapes, take=block_of, put=block_of):
    count, peers = len(arrays), lax.axis_size(axis) - 1
    anywhere = [pl.BlockSpec(memory_space=pl.ANY)] * count
    return pl.pallas_call(
        partial(exchange_kernel, axis, take, put, count),
        name="exchange_" + axis,
        out_shape=[jax.ShapeDtypeStruct(s, x.dtype) for s, x in zip(shapes, arrays)],
        in_specs=anywhere,
        out_specs=anywhere,
        scratch_shapes=[
            pltpu.SemaphoreType.DMA((2, count * peers)),
            pltpu.SemaphoreType.DMA((count,)),
        ],
        compiler_params=pltpu.CompilerParams(collective_id=cid, has_side_effects=True),
        cost_estimate=pl.CostEstimate(
            flops=0, bytes_accessed=60 * sum(x.size for x in arrays), transcendentals=0
        ),
    )(*arrays)


def first_kernel(pack_ref, small_ref, out_ref, all_ref, sems, small_sems, local_sems):
    plane, span = lax.axis_size("dp"), lax.axis_size("seq")
    at, z = lax.axis_index("dp"), lax.axis_index("seq")
    places = [
        {"dp": lax.rem(at + i, plane), "seq": lax.rem(z + k, span)}
        for k in range(span)
        for i in range(plane)
        if i or k
    ]
    greet(places)
    copy, copy_small = Sender(sems), Sender(small_sems)
    block = all_ref.at[z * plane + at]
    copies = [copy_small(small_ref, block, p) for p in places]
    for i in range(1, plane):
        to = lax.rem(at + i, plane)
        copies.append(copy(pack_ref.at[to], columns_of(out_ref, at), {"dp": to}))
    copies.append(pltpu.make_async_copy(small_ref, block, local_sems.at[0]))
    copies.append(
        pltpu.make_async_copy(pack_ref.at[at], columns_of(out_ref, at), local_sems.at[1])
    )
    for c in copies:
        c.start()
    for c in copies:
        c.wait()


def first_exchange(pack, small, cid):
    plane, span = lax.axis_size("dp"), lax.axis_size("seq")
    _, size, chunk = pack.shape
    anywhere = pl.BlockSpec(memory_space=pl.ANY)
    whole = pl.BlockSpec(memory_space=pltpu.VMEM)
    return pl.pallas_call(
        first_kernel,
        name="first_exchange",
        out_shape=[
            jax.ShapeDtypeStruct((size, plane * chunk), pack.dtype),
            jax.ShapeDtypeStruct((span * plane,) + small.shape, small.dtype),
        ],
        in_specs=[anywhere, whole],
        out_specs=[anywhere, whole],
        scratch_shapes=[
            pltpu.SemaphoreType.DMA((2, plane - 1)),
            pltpu.SemaphoreType.DMA((2, plane * span - 1)),
            pltpu.SemaphoreType.DMA((2,)),
        ],
        compiler_params=pltpu.CompilerParams(collective_id=cid, has_side_effects=True),
        cost_estimate=pl.CostEstimate(
            flops=0, bytes_accessed=60 * pack.size, transcendentals=0
        ),
    )(pack, small)


def ffn_kernel(normed_ref, cot_ref, w_ref, out_ref, dnormed_ref, dgate_ref, dup_ref, hidden_ref):
    parts, units, depth = w_ref.shape
    units //= 3

    def rows(k):
        return pl.ds(k * units, units)

    def cols(s):
        return pl.ds(s * depth, depth)

    def project(x_ref, k):
        total = nt_dot(x_ref[:, cols(0)], w_ref[0, rows(k)])
        for s in range(1, parts):
            total += nt_dot(x_ref[:, cols(s)], w_ref[s, rows(k)])
        return total

    gate, up, dhidden = project(normed_ref, 0), project(normed_ref, 1), project(cot_ref, 2)
    sig = jax.nn.sigmoid(gate)
    silu = gate * sig
    hidden = (silu * up).astype(jnp.bfloat16)
    dgate = (dhidden * up * sig * (1.0 + gate * (1.0 - sig))).astype(jnp.bfloat16)
    dup = (dhidden * silu).astype(jnp.bfloat16)
    hidden_ref[...], dgate_ref[...], dup_ref[...] = hidden, dgate, dup
    for s in range(parts):
        dnormed_ref[:, cols(s)] = (
            nn_dot(dgate, w_ref[s, rows(0)]) + nn_dot(dup, w_ref[s, rows(1)])
        ).astype(jnp.bfloat16)
        out_ref[:, cols(s)] = nn_dot(hidden, w_ref[s, rows(2)]).astype(jnp.bfloat16)


def ffn(normed, cot, weights, block=256):
    tokens, width = normed.shape
    units = weights.shape[1] // 3
    wide = pl.BlockSpec((block, width), lambda i: (i, 0))
    thin = pl.BlockSpec((block, units), lambda i: (i, 0))
    return pl.pallas_call(
        ffn_kernel,
        name="ffn",
        grid=(tokens // block,),
        out_shape=[jax.ShapeDtypeStruct((tokens, width), jnp.bfloat16)] * 2
        + [jax.ShapeDtypeStruct((tokens, units), jnp.bfloat16)] * 3,
        in_specs=[
            wide,
            wide,
            pl.BlockSpec(weights.shape, lambda i: (0, 0, 0), pipeline_mode=pl.Buffered(1)),
        ],
        out_specs=[wide, wide, thin, thin, thin],
        compiler_params=pltpu.CompilerParams(vmem_limit_bytes=VMEM_LIMIT),
        cost_estimate=pl.CostEstimate(
            flops=12 * tokens * width * units,
            bytes_accessed=2 * (4 * tokens * width + weights.size + 3 * tokens * units),
            transcendentals=tokens * units,
        ),
    )(normed, cot, weights)


def run(*steps):
    for g in steps:
        for _ in g:
            pass


def row_blocks(rows, step, body):
    def inner(i, carry):
        return body(pl.ds(pl.multiple_of(i * step, step), step), carry)

    return lambda init: lax.fori_loop(0, rows // step, inner, init)


def lanes(k):
    return pl.ds(k * LANES, LANES)


def seq_major_block(k):
    plane, span = lax.axis_size("dp"), lax.axis_size("seq")
    s, g = divmod(k, plane)
    return g * span + s


def mean_of(acc, width):
    return jnp.sum(acc, axis=1, keepdims=True) * (1.0 / width)


def kernel_call(body, name, cid, outs, ins, scratch, flops=0, moved=0):
    params = dict(has_side_effects=True, vmem_limit_bytes=VMEM_LIMIT)
    return pl.pallas_call(
        body,
        name=name,
        out_shape=[jax.ShapeDtypeStruct(s, d) for s, d, _ in outs],
        in_specs=[pl.BlockSpec(memory_space=m) for _, m in ins],
        out_specs=[pl.BlockSpec(memory_space=m) for _, _, m in outs],
        scratch_shapes=scratch,
        compiler_params=pltpu.CompilerParams(collective_id=cid, **params),
        cost_estimate=pl.CostEstimate(flops=flops, bytes_accessed=moved, transcendentals=0),
    )(*[a for a, _ in ins])


def copies(count):
    return pltpu.SemaphoreType.DMA((2, count))


def entry_kernel(
    tokens_ref, cot_ref, small_ref, all_ref, x_ref, cot_own_ref, normed_ref, sems, local_sem
):
    greet_plane()
    core = lax.axis_index("tensor")
    m, width = x_ref.shape
    blocks = width // LANES

    def body(r, carry):
        acc = jnp.zeros((ROW_STEP, LANES), jnp.float32)
        for k in range(blocks):
            source = lanes(seq_major_block(k))
            v = tokens_ref[core, r, source]
            x_ref[r, lanes(k)] = v
            cot_own_ref[r, lanes(k)] = cot_ref[core, r, source]
            v = v.astype(jnp.float32)
            acc += v * v
        scale = lax.rsqrt(mean_of(acc, width) + norm_epsilon)
        for k in range(blocks):
            v = x_ref[r, lanes(k)].astype(jnp.float32)
            normed_ref[r, lanes(k)] = (v * scale * small_ref[k, 0:1, :]).astype(jnp.bfloat16)
        return carry

    row_blocks(m, ROW_STEP, body)(0)
    run(gather_steps(normed_ref, all_ref, Sender(sems), local_sem))


def entry(tokens, cot, small, cid):
    cores, m, width = tokens.shape
    whole = pltpu.VMEM
    gathered, x, cot_own = kernel_call(
        entry_kernel,
        "entry",
        cid,
        [
            ((4, cores, m, width), jnp.bfloat16, pl.ANY),
            ((m, width), jnp.bfloat16, whole),
            ((m, width), jnp.bfloat16, whole),
        ],
        [(tokens, whole), (cot, whole), (small, whole)],
        [pltpu.VMEM((m, width), jnp.bfloat16), copies(GATHER_COPIES), pltpu.SemaphoreType.DMA],
        moved=tokens.size * 40,
    )
    return gathered.reshape(-1, width), x, cot_own


def head_mask(rows, head):
    lane = lax.broadcasted_iota(jnp.int32, (rows, LANES), 1)
    return (lane >= head * FDIM) & (lane < (head + 1) * FDIM)


def keys_in_place(qkv_ref, keys_ref, vcols, qcols):
    for j in range(qkv_ref.shape[0]):
        tile = qkv_ref[j, :, pl.ds(vcols, LANES)].astype(jnp.float32)
        keys_ref[j] = pltpu.roll(tile, LANES - qcols, axis=1).astype(jnp.bfloat16)


def masked_weights(query, key, col_ref, row_ref, r, i, j, length):
    a = nt_dot(query, key) * 0.25
    t = lax.broadcasted_iota(jnp.int32, (length, length), 0) + i * length
    s = lax.broadcasted_iota(jnp.int32, (length, length), 1) + j * length
    keep = (s <= t) & (col_ref[r, i] == row_ref[r, j])
    return a, jnp.where(keep, 1.0 + a + 0.5 * a * a, 0.0), keep


def mix_kernel(
    heads,
    normed_ref,
    pack_ref,
    col_ref,
    row_ref,
    cot_ref,
    qkv_ref,
    mixed_ref,
    exact_ref,
    den_ref,
    cot_all_ref,
    out_qkv,
    out_mixed,
    keys_ref,
    sems,
    cot_sems,
    local_sem,
):
    span, z = lax.axis_size("seq"), lax.axis_index("seq")
    parts, _, depth = pack_ref.shape
    tokens = qkv_ref.shape[1]
    rows, length = col_ref.shape[0], col_ref.shape[2]
    vcols, qcols = heads * VHEAD, heads * FDIM
    at, x_at, y_at, _, core = plane_places()
    peers = [lax.rem(z + k, span) for k in range(1, span)]
    greet([{"dp": x_at}, {"dp": y_at}, {"tensor": 1 - core}] + [{"seq": p} for p in peers])
    gather = gather_steps(cot_ref, cot_all_ref, Sender(cot_sems), local_sem)
    next(gather)
    copy = Sender(sems)

    def project(dest, out):
        x = pl.ds(pl.multiple_of(dest * tokens, tokens), tokens)
        value = jnp.zeros((tokens, vcols), jnp.float32)
        tile = jnp.zeros((tokens, LANES), jnp.float32)
        for s in range(parts):
            piece = normed_ref[x, pl.ds(s * depth, depth)]
            value += nt_dot(piece, pack_ref[s, pl.ds(0, vcols)])
            tile += nt_dot(piece, pack_ref[s, pl.ds(vcols, LANES)])
        lane = lax.broadcasted_iota(jnp.int32, (tokens, LANES), 1)
        out[:, pl.ds(0, vcols)] = value.astype(jnp.bfloat16)
        out[:, pl.ds(vcols, LANES)] = jnp.where(lane < 2 * qcols, tile, 0.0).astype(jnp.bfloat16)

    there = []
    for k, p in enumerate(peers):
        project(p, out_qkv.at[k])
        there.append(copy(out_qkv.at[k], qkv_ref.at[z], {"seq": p}))
        there[-1].start()
    project(z, qkv_ref.at[z])
    run(gather)
    for c in there:
        c.wait()
    keys_in_place(qkv_ref, keys_ref, vcols, qcols)

    def mixer(i, out):
        def one_row(r, carry):
            t = pl.ds(pl.multiple_of(r * length, length), length)
            tile = qkv_ref[i, t, pl.ds(vcols, LANES)]
            queries = [
                jnp.where(head_mask(length, h), tile, jnp.zeros_like(tile)) for h in range(heads)
            ]

            def block(j, carry):
                new = []
                for h in range(heads):
                    num, den = carry[h]
                    _, w, _ = masked_weights(
                        queries[h], keys_ref[j, t], col_ref, row_ref, r, i, j, length
                    )
                    value = qkv_ref[j, t, pl.ds(h * VHEAD, VHEAD)]
                    new.append(
                        (
                            num + nn_dot(w.astype(jnp.bfloat16), value),
                            den + jnp.sum(w, axis=1, keepdims=True),
                        )
                    )
                return tuple(new)

            zero = (
                jnp.zeros((length, VHEAD), jnp.float32),
                jnp.zeros((length, 1), jnp.float32),
            )
            done = lax.fori_loop(0, i + 1, block, (zero,) * heads)
            lane = lax.broadcasted_iota(jnp.int32, (length, LANES), 1)
            dens = jnp.zeros((length, LANES), jnp.float32)
            for h, (num, den) in enumerate(done):
                v = num / den
                exact_ref[i, t, pl.ds(h * VHEAD, VHEAD)] = v
                out[t, pl.ds(h * VHEAD, VHEAD)] = v.astype(jnp.bfloat16)
                dens = jnp.where(lane == h, den, dens)
            den_ref[i, t] = dens
            return carry

        lax.fori_loop(0, rows, one_row, 0)

    back = []
    for k, p in enumerate(peers):
        mixer(p, out_mixed.at[k])
        back.append(copy(out_mixed.at[k], mixed_ref.at[z], {"seq": p}))
        back[-1].start()
    mixer(z, mixed_ref.at[z])
    for c in back:
        c.wait()


def mix(normed, pack, seg_col, seg_row, cot_own, heads, cid):
    span = lax.axis_size("seq")
    tokens = normed.shape[0] // span
    vcols = heads * VHEAD
    m, width = cot_own.shape
    whole = pltpu.VMEM
    qkv, mixed, exact, den, cot = kernel_call(
        partial(mix_kernel, heads),
        "mix",
        cid,
        [
            ((span, tokens, vcols + LANES), jnp.bfloat16, whole),
            ((span, tokens, vcols), jnp.bfloat16, whole),
            ((span, tokens, vcols), jnp.float32, whole),
            ((span, tokens, LANES), jnp.float32, whole),
            ((4, 2, m, width), jnp.bfloat16, pl.ANY),
        ],
        [(normed, whole), (pack, whole), (seg_col, whole), (seg_row, whole), (cot_own, whole)],
        [
            pltpu.VMEM((span - 1, tokens, vcols + LANES), jnp.bfloat16),
            pltpu.VMEM((span - 1, tokens, vcols), jnp.bfloat16),
            pltpu.VMEM((span, tokens, LANES), jnp.bfloat16),
            copies(2 * (span - 1)),
            copies(GATHER_COPIES),
            pltpu.SemaphoreType.DMA,
        ],
        moved=normed.size * 40,
    )
    return qkv, mixed.reshape(-1, vcols), exact, den, cot.reshape(-1, width)


def branch_kernel(
    mixed_ref,
    pack_ref,
    x_ref,
    small_ref,
    residual_ref,
    all_ref,
    part_ref,
    pair_ref,
    sum_ref,
    got_ref,
    normed_ref,
    sems,
    gather_sems,
    local_sem,
):
    greet_plane()
    parts, _, depth = pack_ref.shape
    m, width = x_ref.shape
    vcols = mixed_ref.shape[1]
    first = pack_ref.shape[1] - vcols

    def project(b, carry):
        left = mixed_ref[pl.ds(pl.multiple_of(b * m, m), m)]
        for s in range(parts):
            part_ref[b // 2, lax.rem(b, 2), :, pl.ds(s * depth, depth)] = nn_dot(
                left, pack_ref[s, pl.ds(first, vcols)]
            ).astype(jnp.bfloat16)
        return carry

    lax.fori_loop(0, 8, project, 0)
    run(scatter_steps(part_ref, residual_ref, pair_ref, sum_ref, got_ref, Sender(sems)))

    def body(r, carry):
        acc = jnp.zeros((ROW_STEP, LANES), jnp.float32)
        for k in range(width // LANES):
            v = residual_ref[r, lanes(k)] + x_ref[r, lanes(k)].astype(jnp.float32)
            residual_ref[r, lanes(k)] = v
            acc += v * v
        scale = lax.rsqrt(mean_of(acc, width) + norm_epsilon)
        for k in range(width // LANES):
            normed_ref[r, lanes(k)] = (
                residual_ref[r, lanes(k)] * scale * small_ref[k, 1:2, :]
            ).astype(jnp.bfloat16)
        return carry

    row_blocks(m, ROW_STEP, body)(0)
    run(gather_steps(normed_ref, all_ref, Sender(gather_sems), local_sem))


def scatter_scratch(m, width):
    return [
        pltpu.VMEM((4, m, width), jnp.bfloat16),
        pltpu.VMEM((3, m, width), jnp.bfloat16),
        pltpu.VMEM((3, m, width), jnp.bfloat16),
    ]


def branch(mixed, pack, x, small, cid):
    m, width = x.shape
    whole = pltpu.VMEM
    residual, gathered = kernel_call(
        branch_kernel,
        "branch",
        cid,
        [((m, width), jnp.float32, whole), ((4, 2, m, width), jnp.bfloat16, pl.ANY)],
        [(mixed, whole), (pack, whole), (x, whole), (small, whole)],
        [pltpu.VMEM((4, 2, m, width), jnp.bfloat16)]
        + scatter_scratch(m, width)
        + [
            pltpu.VMEM((m, width), jnp.bfloat16),
            copies(SCATTER_COPIES),
            copies(GATHER_COPIES),
            pltpu.SemaphoreType.DMA,
        ],
        moved=x.size * 120,
    )
    return residual, gathered.reshape(-1, width)


def norm_gradient(r, value_at, grad_ref, gain_at, gain_grad, finish, width):
    squares = jnp.zeros((ROW_STEP, LANES), jnp.float32)
    cross = jnp.zeros((ROW_STEP, LANES), jnp.float32)
    for k in range(width // LANES):
        v = value_at(r, k)
        squares += v * v
        cross += v * grad_ref[r, lanes(k)] * gain_at(k)
    scale = lax.rsqrt(mean_of(squares, width) + norm_epsilon)
    pull = mean_of(cross, width) * scale * scale * scale
    for k in range(width // LANES):
        v, g = value_at(r, k), grad_ref[r, lanes(k)]
        gain_grad[:, lanes(k)] += jnp.sum(
            (g * v * scale).reshape(ROW_STEP // 8, 8, LANES), axis=0
        )
        finish(r, k, scale * g * gain_at(k) - v * pull)


def middle_kernel(
    part_ref,
    residual_ref,
    cot_ref,
    small_ref,
    dresid_ref,
    gain_ref,
    all_ref,
    pair_ref,
    sum_ref,
    got_ref,
    low_ref,
    sems,
    gather_sems,
    local_sem,
):
    greet_plane()
    m, width = residual_ref.shape
    run(scatter_steps(part_ref, dresid_ref, pair_ref, sum_ref, got_ref, Sender(sems)))
    gain_ref[...] = jnp.zeros_like(gain_ref)

    def finish(r, k, v):
        v += cot_ref[r, lanes(k)].astype(jnp.float32)
        dresid_ref[r, lanes(k)] = v
        low_ref[r, lanes(k)] = v.astype(jnp.bfloat16)

    def body(r, carry):
        norm_gradient(
            r,
            lambda r, k: residual_ref[r, lanes(k)],
            dresid_ref,
            lambda k: small_ref[k, 1:2, :],
            gain_ref,
            finish,
            width,
        )
        return carry

    row_blocks(m, ROW_STEP, body)(0)
    run(gather_steps(low_ref, all_ref, Sender(gather_sems), local_sem))


def middle(part, residual, cot_own, small, cid):
    m, width = residual.shape
    whole = pltpu.VMEM
    dresid, gain, gathered = kernel_call(
        middle_kernel,
        "middle",
        cid,
        [
            ((m, width), jnp.float32, whole),
            ((8, width), jnp.float32, whole),
            ((4, 2, m, width), jnp.bfloat16, pl.ANY),
        ],
        [
            (part.reshape(4, 2, m, width), whole),
            (residual, whole),
            (cot_own, whole),
            (small, whole),
        ],
        scatter_scratch(m, width)
        + [
            pltpu.VMEM((m, width), jnp.bfloat16),
            copies(SCATTER_COPIES),
            copies(GATHER_COPIES),
            pltpu.SemaphoreType.DMA,
        ],
        moved=residual.size * 120,
    )
    return dresid, gain, gathered.reshape(-1, width)


def unmix_kernel(
    heads,
    dresid_ref,
    pack_ref,
    col_ref,
    row_ref,
    qkv_ref,
    exact_ref,
    den_ref,
    part_ref,
    residual_ref,
    dqkv_ref,
    block_ref,
    out_dmixed,
    dmixed_ref,
    out_dqkv,
    keys_ref,
    dtile_ref,
    dkey_ref,
    dvalue_ref,
    total_ref,
    pair_ref,
    sum_ref,
    got_ref,
    sems,
    scatter_sems,
):
    span, z = lax.axis_size("seq"), lax.axis_index("seq")
    parts, _, depth = pack_ref.shape
    tokens = qkv_ref.shape[1]
    rows, length = col_ref.shape[0], col_ref.shape[2]
    vcols, qcols = heads * VHEAD, heads * FDIM
    first = pack_ref.shape[1] - vcols
    at, x_at, y_at, _, core = plane_places()
    peers = [lax.rem(z + k, span) for k in range(1, span)]
    greet([{"dp": x_at}, {"dp": y_at}, {"tensor": 1 - core}] + [{"seq": p} for p in peers])
    scatter = scatter_steps(part_ref, total_ref, pair_ref, sum_ref, got_ref, Sender(scatter_sems))
    next(scatter)
    copy = Sender(sems)

    def project(dest, out):
        x = pl.ds(pl.multiple_of(dest * tokens, tokens), tokens)
        total = jnp.zeros((tokens, vcols), jnp.float32)
        for s in range(parts):
            total += nt_dot(
                dresid_ref[x, pl.ds(s * depth, depth)], pack_ref[s, pl.ds(first, vcols)]
            )
        out[...] = total.astype(jnp.bfloat16)

    there = []
    for k, p in enumerate(peers):
        project(p, out_dmixed.at[k])
        there.append(copy(out_dmixed.at[k], dmixed_ref.at[z], {"seq": p}))
        there[-1].start()
    project(z, dmixed_ref.at[z])
    keys_in_place(qkv_ref, keys_ref, vcols, qcols)
    dkey_ref[...] = jnp.zeros_like(dkey_ref)
    dvalue_ref[...] = jnp.zeros_like(dvalue_ref)
    run(scatter)

    def finish(r, carry):
        block_ref[r] = (residual_ref[r] + total_ref[r]).astype(jnp.bfloat16)
        return carry

    row_blocks(block_ref.shape[0], ROW_STEP, finish)(0)
    for c in there:
        c.wait()

    def one_block(step, carry):
        r, i = step // span, lax.rem(step, span)
        t = pl.ds(pl.multiple_of(r * length, length), length)
        tile = qkv_ref[i, t, pl.ds(vcols, LANES)]
        dtile = jnp.zeros((length, LANES), jnp.float32)
        for h in range(heads):
            inside = head_mask(length, h)
            v = pl.ds(h * VHEAD, VHEAD)
            query = jnp.where(inside, tile, jnp.zeros_like(tile))
            dn = dmixed_ref[i, t, v].astype(jnp.float32) / den_ref[i, t, pl.ds(h, 1)]
            dd = -jnp.sum(dn * exact_ref[i, t, v], axis=1, keepdims=True)
            dn_low = dn.astype(jnp.bfloat16)

            def block(j, dquery, query=query, v=v, dn_low=dn_low, dd=dd, inside=inside):
                key = keys_ref[j, t]
                a, w, keep = masked_weights(query, key, col_ref, row_ref, r, i, j, length)
                dw = jnp.where(keep, nt_dot(dn_low, qkv_ref[j, t, v]) + dd, 0.0)
                da = (dw * (1.0 + a) * 0.25).astype(jnp.bfloat16)
                dvalue_ref[j, t, v] += tn_dot(w.astype(jnp.bfloat16), dn_low)
                dkey_ref[j, t] += jnp.where(inside, tn_dot(da, query), 0.0)
                return dquery + nn_dot(da, key)

            dquery = lax.fori_loop(0, i + 1, block, jnp.zeros((length, LANES), jnp.float32))
            dtile += jnp.where(inside, dquery, 0.0)
        dtile_ref[i, t] = dtile
        return carry

    lax.fori_loop(0, rows * span, one_block, 0)

    def pack(i, out):
        out[:, pl.ds(0, vcols)] = dvalue_ref[i].astype(jnp.bfloat16)
        out[:, pl.ds(vcols, LANES)] = (
            dtile_ref[i] + pltpu.roll(dkey_ref[i], qcols, axis=1)
        ).astype(jnp.bfloat16)

    back = []
    for k, p in enumerate(peers):
        pack(p, out_dqkv.at[k])
        back.append(copy(out_dqkv.at[k], dqkv_ref.at[z], {"seq": p}))
        back[-1].start()
    pack(z, dqkv_ref.at[z])
    for c in back:
        c.wait()


def unmix(dresid_low, pack, seg_col, seg_row, qkv, exact, den, part, residual, heads, cid):
    span, tokens, wide = qkv.shape
    vcols = heads * VHEAD
    m, width = residual.shape
    whole = pltpu.VMEM
    ins = (dresid_low, pack, seg_col, seg_row, qkv, exact, den, part.reshape(4, 2, m, width), residual)
    dqkv, block = kernel_call(
        partial(unmix_kernel, heads),
        "unmix",
        cid,
        [((span, tokens, wide), jnp.bfloat16, whole), ((m, width), jnp.bfloat16, whole)],
        [(a, whole) for a in ins],
        [
            pltpu.VMEM((span - 1, tokens, vcols), jnp.bfloat16),
            pltpu.VMEM((span, tokens, vcols), jnp.bfloat16),
            pltpu.VMEM((span - 1, tokens, wide), jnp.bfloat16),
            pltpu.VMEM((span, tokens, LANES), jnp.bfloat16),
            pltpu.VMEM((span, tokens, LANES), jnp.float32),
            pltpu.VMEM((span, tokens, LANES), jnp.float32),
            pltpu.VMEM((span, tokens, vcols), jnp.float32),
            pltpu.VMEM((m, width), jnp.float32),
        ]
        + scatter_scratch(m, width)
        + [copies(2 * (span - 1)), copies(SCATTER_COPIES)],
        moved=residual.size * 160,
    )
    return dqkv.reshape(-1, wide), block


def everyone():
    plane, span, cores = (lax.axis_size(a) for a in ("dp", "seq", "tensor"))
    at, z, core = (lax.axis_index(a) for a in ("dp", "seq", "tensor"))
    others = [
        {
            "dp": lax.rem(at + i, plane),
            "seq": lax.rem(z + k, span),
            "tensor": lax.rem(core + c, cores),
        }
        for k in range(span)
        for i in range(plane)
        for c in range(cores)
        if i or k or c
    ]
    return others, (at * span + z) * cores + core


def exit_kernel(
    dqkv_ref,
    pack_ref,
    x_ref,
    dresid_ref,
    block_ref,
    small_ref,
    gain_two_ref,
    grad_ref,
    out_ref,
    gains_ref,
    gain_ref,
    out_gain,
    got_gain,
    part_ref,
    total_ref,
    ordered_ref,
    low_ref,
    pair_ref,
    sum_ref,
    got_ref,
    sems,
    pair_sems,
    gain_sems,
    local_sems,
):
    others, me = everyone()
    greet(others)
    core = lax.axis_index("tensor")
    plane, span = lax.axis_size("dp"), lax.axis_size("seq")
    parts, _, depth = pack_ref.shape
    m, width = x_ref.shape
    wide = dqkv_ref.shape[1] - LANES + 2 * FDIM * ((dqkv_ref.shape[1] - LANES) // VHEAD)
    blocks = width // LANES
    copy = Sender(pair_sems)

    def project(b, carry):
        left = dqkv_ref[pl.ds(pl.multiple_of(b * m, m), m), pl.ds(0, wide)]
        for s in range(parts):
            part_ref[b // 2, lax.rem(b, 2), :, pl.ds(s * depth, depth)] = nn_dot(
                left, pack_ref[s, pl.ds(0, wide)]
            ).astype(jnp.bfloat16)
        return carry

    lax.fori_loop(0, 8, project, 0)
    scatter = scatter_steps(part_ref, total_ref, pair_ref, sum_ref, got_ref, Sender(sems))
    next(scatter)

    def order(r, carry):
        for k in range(blocks):
            low_ref[r, lanes(seq_major_block(k))] = block_ref[r, lanes(k)]
        return carry

    row_blocks(m, ROW_STEP, order)(0)
    to_pair = [copy(low_ref, out_ref.at[core], {"tensor": 1 - core})]
    local = [pltpu.make_async_copy(low_ref, out_ref.at[core], local_sems.at[0])]
    to_pair[0].start()
    local[0].start()
    run(scatter)
    gain_ref[...] = jnp.zeros_like(gain_ref)

    def finish(r, k, v):
        ordered_ref[r, lanes(seq_major_block(k))] = v + dresid_ref[r, lanes(k)]

    def body(r, carry):
        norm_gradient(
            r,
            lambda r, k: x_ref[r, lanes(k)].astype(jnp.float32),
            total_ref,
            lambda k: small_ref[k, 0:1, :],
            gain_ref,
            finish,
            width,
        )
        return carry

    row_blocks(m, ROW_STEP, body)(0)
    to_pair.append(copy(ordered_ref, grad_ref.at[core], {"tensor": 1 - core}))
    local.append(pltpu.make_async_copy(ordered_ref, grad_ref.at[core], local_sems.at[1]))
    to_pair[1].start()
    local[1].start()
    out_gain[...] = jnp.zeros_like(out_gain)
    for k in range(blocks):
        for row, ref in enumerate((gain_ref, gain_two_ref)):
            out_gain[k, row : row + 1] = jnp.sum(ref[:, lanes(k)], axis=0, keepdims=True)
    copy_gain = Sender(gain_sems)
    for p in others:
        block = out_gain.at[p["seq"] * plane + p["dp"], pl.ds(0, 8)]
        to_pair.append(copy_gain(block, got_gain.at[me], p))
        to_pair[-1].start()
    mine = lax.axis_index("seq") * plane + lax.axis_index("dp")
    got_gain[me] = out_gain[mine]
    for c in to_pair + local:
        c.wait()
    total = got_gain[0]
    for k in range(1, len(others) + 1):
        total += got_gain[k]
    gains_ref[...] = total


def leave(dqkv, pack, x, dresid, block, small, gain_two, cid):
    m, width = x.shape
    devices = lax.axis_size(("dp", "seq", "tensor"))
    whole = pltpu.VMEM
    return kernel_call(
        exit_kernel,
        "leave",
        cid,
        [
            ((2, m, width), jnp.float32, pl.ANY),
            ((2, m, width), jnp.bfloat16, pl.ANY),
            ((8, LANES), jnp.float32, whole),
        ],
        [(a, whole) for a in (dqkv, pack, x, dresid, block, small, gain_two)],
        [
            pltpu.VMEM((8, width), jnp.float32),
            pltpu.VMEM((width // LANES, 8, LANES), jnp.float32),
            pltpu.VMEM((devices, 8, LANES), jnp.float32),
            pltpu.VMEM((4, 2, m, width), jnp.bfloat16),
            pltpu.VMEM((m, width), jnp.float32),
            pltpu.VMEM((m, width), jnp.float32),
            pltpu.VMEM((m, width), jnp.bfloat16),
        ]
        + scatter_scratch(m, width)
        + [
            copies(SCATTER_COPIES),
            copies(2),
            copies(devices - 1),
            pltpu.SemaphoreType.DMA((2,)),
        ],
        moved=x.size * 120,
    )


def plane_local(
    tokens,
    doc_starts,
    attn_gain,
    mlp_gain,
    query_weight,
    key_weight,
    value_weight,
    output_weight,
    gate_weight,
    up_weight,
    down_weight,
    cotangent,
):
    plane, span, cores = (lax.axis_size("dp"), lax.axis_size("seq"), lax.axis_size("tensor"))
    rows, length, width = tokens.shape
    chunk = width // (plane * span)
    own = rows * length // cores
    heads = query_weight.shape[1] // FDIM // plane
    hidden_part = gate_weight.shape[1] // plane
    vcols, qcols = heads * VHEAD, heads * FDIM
    all_rows = rows * plane // span

    def over_seq(pack):
        return lax.all_gather(pack, "seq", axis=0, tiled=False)

    def summed(grads):
        return lax.psum_scatter(
            grads.astype(jnp.bfloat16), "seq", scatter_dimension=1, tiled=True
        )

    def collect(parts, cid):
        return exchange(
            parts, "dp", cid, [(plane, p.shape[0], chunk) for p in parts], take=columns_of
        )

    def split(w):
        return w.reshape(plane, -1, chunk)

    small = jnp.concatenate(
        [
            attn_gain.astype(jnp.float32)[None],
            mlp_gain.astype(jnp.float32)[None],
            doc_starts.astype(jnp.float32).reshape(-1, chunk),
            jnp.zeros((2, chunk), jnp.float32),
        ]
    )
    attn_pack = jnp.concatenate(
        [split(value_weight.T), split(query_weight.T), split(key_weight.T), split(output_weight)],
        axis=1,
    )
    attn_pack, small = first_exchange(attn_pack, small, 1)
    ffn_pack = jnp.concatenate([split(gate_weight.T), split(up_weight.T), split(down_weight)], axis=1)
    ffn_pack, _ = lax.optimization_barrier((ffn_pack, attn_pack))
    [ffn_pack] = exchange(
        [ffn_pack], "dp", 2, [(ffn_pack.shape[1], plane * chunk)], put=columns_of
    )
    attn_pack, ffn_pack = over_seq(attn_pack), over_seq(ffn_pack)
    starts = small[:, 2:-2].reshape(span, plane * rows, length)
    starts = lax.dynamic_slice_in_dim(starts, lax.axis_index("seq") * all_rows, all_rows, 1)
    segments = jnp.cumsum(starts.transpose(1, 0, 2).reshape(all_rows, span * length), axis=1)

    qkv_rows = vcols + 2 * qcols
    seg_col = segments.reshape(all_rows, span, length, 1)
    seg_row = segments.reshape(all_rows, span, 1, length)
    normed_one, x, cot_own = entry(
        tokens.reshape(cores, own, width), cotangent.reshape(cores, own, width), small, 3
    )
    qkv, mixed, exact, den, cot = mix(normed_one, attn_pack, seg_col, seg_row, cot_own, heads, 4)
    residual, normed_two = branch(mixed, attn_pack, x, small, 5)
    out_part, dnormed_part, dgate, dup, hidden = ffn(normed_two, cot, ffn_pack)
    down_grad = tn_dot(hidden, cot).astype(jnp.bfloat16)
    gate_grad = tn_dot(dgate, normed_two).astype(jnp.bfloat16)
    up_grad = tn_dot(dup, normed_two).astype(jnp.bfloat16)
    dnormed_part, gate_grad, up_grad, down_grad = lax.optimization_barrier(
        (dnormed_part, gate_grad, up_grad, down_grad)
    )
    down_grad, gate_grad, up_grad = summed(down_grad), summed(gate_grad), summed(up_grad)
    dresid, gain_two_grad, dresid_low = middle(dnormed_part, residual, cot_own, small, 6)
    dresid_low, down_grad = lax.optimization_barrier((dresid_low, down_grad))
    dqkv, block_own = unmix(
        dresid_low, attn_pack, seg_col, seg_row, qkv, exact, den, out_part, residual, heads, 7
    )
    out_grad = tn_dot(mixed, dresid_low).astype(jnp.bfloat16)
    qkv_grad = tn_dot(dqkv, normed_one)[:qkv_rows].astype(jnp.bfloat16)
    dqkv, out_grad, qkv_grad, gate_grad, up_grad = lax.optimization_barrier(
        (dqkv, out_grad, qkv_grad, gate_grad, up_grad)
    )
    out_grad, qkv_grad = summed(out_grad), summed(qkv_grad)
    dtokens, block_out, gain_grads = leave(
        dqkv, attn_pack, x, dresid, block_own, small, gain_two_grad, 8
    )
    down_grad, gate_grad, up_grad, dtokens = lax.optimization_barrier(
        (down_grad, gate_grad, up_grad, dtokens)
    )
    down_grad, gate_grad, up_grad = collect([down_grad, gate_grad, up_grad], 9)
    out_grad, qkv_grad = collect([out_grad, qkv_grad], 10)

    def stacked(a, start, size):
        return a[:, start : start + size].reshape(plane * size, chunk).astype(jnp.float32)

    h = hidden_part
    return (
        block_out.reshape(rows, length, width),
        dtokens.reshape(rows, length, width),
        gain_grads[0],
        gain_grads[1],
        stacked(qkv_grad, vcols, qcols).T,
        stacked(qkv_grad, vcols + qcols, qcols).T,
        stacked(qkv_grad, 0, vcols).T,
        stacked(out_grad, 0, vcols),
        stacked(gate_grad, 0, h).T,
        stacked(up_grad, 0, h).T,
        stacked(down_grad, 0, h),
    )


def fits_plane(mesh, tokens, query_weight, gate_weight):
    plane, span, cores = (mesh.shape[a] for a in ("dp", "seq", "tensor"))
    heads = query_weight.shape[1] // FDIM // cores
    return (
        plane == 4
        and cores == 2
        and heads % plane == 0
        and (gate_weight.shape[1] // cores) % (16 * plane) == 0
        and tokens.shape[0] % span == 0
    )


def solution(mesh):
    def step(*args):
        use = fits_plane(mesh, args[0], args[4], args[8])
        return sharded(mesh, plane_local if use else local)(*args)

    return step


def sharded(mesh, body):
    return jax.shard_map(
        body,
        mesh=mesh,
        in_specs=(
            P("dp", "seq", None),
            P("dp", "seq"),
            P(("dp", "seq")),
            P(("dp", "seq")),
            P(("dp", "seq"), "tensor"),
            P(("dp", "seq"), "tensor"),
            P(("dp", "seq"), "tensor"),
            P("tensor", ("dp", "seq")),
            P(("dp", "seq"), "tensor"),
            P(("dp", "seq"), "tensor"),
            P("tensor", ("dp", "seq")),
            P("dp", "seq", None),
        ),
        out_specs=(
            P("dp", "seq", None),
            P("dp", "seq", None),
            P(("dp", "seq")),
            P(("dp", "seq")),
            P(("dp", "seq"), "tensor"),
            P(("dp", "seq"), "tensor"),
            P(("dp", "seq"), "tensor"),
            P("tensor", ("dp", "seq")),
            P(("dp", "seq"), "tensor"),
            P(("dp", "seq"), "tensor"),
            P("tensor", ("dp", "seq")),
        ),
        check_vma=False,
    )
```

```python
from functools import partial

import jax
import jax.numpy as jnp
from jax import lax
from jax.experimental import pallas as pl
from jax.experimental.pallas import tpu as pltpu
from jax.sharding import PartitionSpec as P

FDIM = 16
VHEAD = 128
MICRO = 2


norm_epsilon = 1e-05
highest = lax.Precision.HIGHEST
outer_scale = 0.17677669529663687


def prefix(x, axis, combine, identity, reverse):
    size, index = (lax.axis_size(axis), lax.axis_index(axis))
    everything = jax.tree.map(lambda part: lax.all_gather(part, axis), x)
    start = jax.tree.map(
        lambda part, zero: jnp.broadcast_to(jnp.asarray(zero, part.dtype), part.shape), x, identity
    )

    def turn(k, before):
        at = size - 1 - k if reverse else k
        reached = at > index if reverse else at < index
        new = combine(before, jax.tree.map(lambda part: part[at], everything))
        return jax.tree.map(lambda a, b: jnp.where(reached, a, b), new, before)

    return lax.fori_loop(0, size, turn, start)


def features(vectors):
    ones_col = jnp.ones(vectors.shape[:-1] + (1,), jnp.float32)
    outer_terms = vectors[..., :, None] * vectors[..., None, :] * outer_scale
    outer_terms = outer_terms.reshape(vectors.shape[:-1] + (vectors.shape[-1] * vectors.shape[-1],))
    return jnp.concatenate([ones_col, 0.5 * vectors, outer_terms], axis=-1)


def mix_span(queries, key_rows, values, state_in, norm_in, segments):
    length = queries.shape[1]
    scores = jnp.einsum("rthf,rshf->rhts", queries, key_rows, precision=highest) / 4.0
    kernel = 1.0 + scores + 0.5 * scores * scores
    position = jnp.arange(length)
    causal = position[None, :] <= position[:, None]
    allowed = causal[None] & (segments[:, :, None] == segments[:, None, :])
    kernel = jnp.where(allowed[:, None], kernel, 0.0)
    numerator = jnp.einsum("rhts,rshe->rthe", kernel, values, precision=highest)
    denominator = jnp.transpose(jnp.sum(kernel, axis=-1), (0, 2, 1))
    head_part = (segments == 0).astype(jnp.float32)[:, :, None]
    lifted = features(queries)
    numerator = numerator + head_part[..., None] * jnp.einsum(
        "rthf,rhfe->rthe", lifted, state_in, precision=highest
    )
    denominator = denominator + head_part * jnp.einsum(
        "rthf,rhf->rth", lifted, norm_in, precision=highest
    )
    return numerator / denominator[..., None]


def tail_span(key_rows, values, segments):
    tail_mask = (segments == segments[:, -1:]).astype(jnp.float32)
    lifted = features(key_rows) * tail_mask[:, :, None, None]
    tail_state = jnp.einsum("rshf,rshe->rhfe", lifted, values, precision=highest)
    return (tail_state, jnp.sum(lifted, axis=1))


def combine_carry(earlier_part, later_part):
    keep_rate = 1.0 - later_part[2]
    return (
        later_part[0] + keep_rate[:, None, None, None] * earlier_part[0],
        later_part[1] + keep_rate[:, None, None] * earlier_part[1],
        jnp.maximum(earlier_part[2], later_part[2]),
    )


def inverse_rms(inputs):
    return lax.rsqrt(jnp.mean(inputs * inputs, axis=-1, keepdims=True) + norm_epsilon)


def norm_backward(inputs, scale_row, gain_vec, grad_normed):
    scaled_grad = grad_normed * gain_vec
    grad_gain = jnp.sum(grad_normed * inputs * scale_row, axis=0)
    grad_inputs = scale_row * scaled_grad - inputs * scale_row * scale_row * scale_row * jnp.mean(
        scaled_grad * inputs, axis=-1, keepdims=True
    )
    return (grad_inputs, grad_gain)


def inner_rows(left_mat, right_mat):
    return lax.dot_general(
        left_mat, right_mat, (((0,), (0,)), ((), ())), preferred_element_type=jnp.float32
    )


def by_transpose(left_mat, right_mat):
    return lax.dot_general(
        left_mat, right_mat, (((1,), (1,)), ((), ())), preferred_element_type=jnp.float32
    )


def local(
    tokens,
    doc_starts,
    attn_gain,
    mlp_gain,
    query_weight,
    key_weight,
    value_weight,
    output_weight,
    gate_weight,
    up_weight,
    down_weight,
    cotangent,
):
    micro_rows = tokens.shape[0] // MICRO
    span_len = tokens.shape[1]
    model_width = tokens.shape[2]
    head_count = query_weight.shape[1] // FDIM
    outputs_main = []
    outputs_grad = []
    totals = None
    for micro_index in range(MICRO):
        row_start = micro_index * micro_rows
        rows_in = tokens[row_start : row_start + micro_rows]
        starts_in = doc_starts[row_start : row_start + micro_rows]
        cot_in = cotangent[row_start : row_start + micro_rows].reshape(-1, model_width)
        (
            full_query,
            full_key,
            full_value,
            full_gate,
            full_up,
            full_output,
            full_down,
            gain_one,
            gain_two,
        ) = (
            lax.all_gather(query_weight, ("dp", "seq"), axis=0, tiled=True),
            lax.all_gather(key_weight, ("dp", "seq"), axis=0, tiled=True),
            lax.all_gather(value_weight, ("dp", "seq"), axis=0, tiled=True),
            lax.all_gather(gate_weight, ("dp", "seq"), axis=0, tiled=True),
            lax.all_gather(up_weight, ("dp", "seq"), axis=0, tiled=True),
            lax.all_gather(output_weight, ("dp", "seq"), axis=1, tiled=True),
            lax.all_gather(down_weight, ("dp", "seq"), axis=1, tiled=True),
            lax.all_gather(attn_gain, ("dp", "seq"), axis=0, tiled=True),
            lax.all_gather(mlp_gain, ("dp", "seq"), axis=0, tiled=True),
        )
        gain_one_f = gain_one.astype(jnp.float32)
        gain_two_f = gain_two.astype(jnp.float32)
        flat_rows = rows_in.reshape(-1, model_width).astype(jnp.float32)
        scale_one = inverse_rms(flat_rows)
        normed_one = (flat_rows * scale_one * gain_one_f).astype(jnp.bfloat16)
        query_low = jnp.dot(normed_one, full_query, preferred_element_type=jnp.float32).astype(
            jnp.bfloat16
        )
        key_low = jnp.dot(normed_one, full_key, preferred_element_type=jnp.float32).astype(
            jnp.bfloat16
        )
        value_low = jnp.dot(normed_one, full_value, preferred_element_type=jnp.float32).astype(
            jnp.bfloat16
        )
        queries = query_low.astype(jnp.float32).reshape(micro_rows, span_len, head_count, FDIM)
        key_rows = key_low.astype(jnp.float32).reshape(micro_rows, span_len, head_count, FDIM)
        values = value_low.astype(jnp.float32).reshape(micro_rows, span_len, head_count, VHEAD)
        segments = jnp.cumsum(starts_in, axis=1)
        reset_flag = (segments[:, -1] > 0).astype(jnp.float32)
        (tail_state, tail_norm), tail_pull = jax.vjp(
            partial(tail_span, segments=segments), key_rows, values
        )
        state_in, norm_in, reset_in = prefix(
            (tail_state, tail_norm, reset_flag),
            "seq",
            combine_carry,
            (jnp.zeros_like(tail_state), jnp.zeros_like(tail_norm), jnp.zeros_like(reset_flag)),
            False,
        )
        mixed_heads, mix_pull = jax.vjp(
            partial(mix_span, segments=segments), queries, key_rows, values, state_in, norm_in
        )
        mixed_low = mixed_heads.reshape(-1, head_count * VHEAD).astype(jnp.bfloat16)
        branch_one = jnp.dot(mixed_low, full_output, preferred_element_type=jnp.float32)
        residual = flat_rows + lax.psum(branch_one, "tensor")
        scale_two = inverse_rms(residual)
        normed_two = (residual * scale_two * gain_two_f).astype(jnp.bfloat16)
        gate_proj = jnp.dot(normed_two, full_gate, preferred_element_type=jnp.float32)
        up_proj = jnp.dot(normed_two, full_up, preferred_element_type=jnp.float32)
        sigmoid_gate = jax.nn.sigmoid(gate_proj)
        hidden = (gate_proj * sigmoid_gate * up_proj).astype(jnp.bfloat16)
        branch_two = jnp.dot(hidden, full_down, preferred_element_type=jnp.float32)
        block_low = (
            residual + lax.psum(branch_two.astype(jnp.bfloat16), "tensor").astype(jnp.float32)
        ).astype(jnp.bfloat16)
        outputs_main.append(block_low.reshape(micro_rows, span_len, model_width))
        grad_down = inner_rows(hidden, cot_in)
        grad_hidden = by_transpose(cot_in, full_down)
        grad_gate_low = (
            grad_hidden * up_proj * sigmoid_gate * (1.0 + gate_proj * (1.0 - sigmoid_gate))
        ).astype(jnp.bfloat16)
        grad_up_low = (grad_hidden * gate_proj * sigmoid_gate).astype(jnp.bfloat16)
        grad_gate = inner_rows(normed_two, grad_gate_low)
        grad_up = inner_rows(normed_two, grad_up_low)
        grad_normed_two = by_transpose(grad_gate_low, full_gate) + by_transpose(
            grad_up_low, full_up
        )
        grad_normed_two = lax.psum(grad_normed_two, "tensor")
        grad_resid, grad_gain_two = norm_backward(residual, scale_two, gain_two_f, grad_normed_two)
        grad_resid = grad_resid + cot_in.astype(jnp.float32)
        grad_resid_low = grad_resid.astype(jnp.bfloat16)
        grad_output = inner_rows(mixed_low, grad_resid_low)
        grad_mixed = by_transpose(grad_resid_low, full_output).astype(jnp.bfloat16)
        grad_mixed = (
            lax.optimization_barrier(grad_mixed)
            .astype(jnp.float32)
            .reshape(micro_rows, span_len, head_count, VHEAD)
        )
        grad_queries, grad_keys, grad_values, grad_state, grad_norm = mix_pull(grad_mixed)
        carried_state, carried_norm, reset_out = prefix(
            (grad_state, grad_norm, reset_flag),
            "seq",
            combine_carry,
            (jnp.zeros_like(grad_state), jnp.zeros_like(grad_norm), jnp.zeros_like(reset_flag)),
            True,
        )
        more_keys, more_values = tail_pull((carried_state, carried_norm))
        grad_query_low = grad_queries.reshape(-1, head_count * FDIM).astype(jnp.bfloat16)
        grad_key_low = (grad_keys + more_keys).reshape(-1, head_count * FDIM).astype(jnp.bfloat16)
        grad_value_low = (
            (grad_values + more_values).reshape(-1, head_count * VHEAD).astype(jnp.bfloat16)
        )
        grad_query = inner_rows(normed_one, grad_query_low)
        grad_key = inner_rows(normed_one, grad_key_low)
        grad_value = inner_rows(normed_one, grad_value_low)
        grad_normed_one = (
            by_transpose(grad_query_low, full_query)
            + by_transpose(grad_key_low, full_key)
            + by_transpose(grad_value_low, full_value)
        )
        grad_normed_one = lax.psum(grad_normed_one, "tensor")
        grad_inputs, grad_gain_one = norm_backward(
            flat_rows, scale_one, gain_one_f, grad_normed_one
        )
        outputs_grad.append((grad_resid + grad_inputs).reshape(micro_rows, span_len, model_width))
        shares = (
            grad_query,
            grad_key,
            grad_value,
            grad_gate,
            grad_up,
            grad_output,
            grad_down,
            grad_gain_one,
            grad_gain_two,
        )
        if totals is None:
            totals = shares
        else:
            totals = jax.tree.map(jnp.add, totals, shares)
    totals = (
        lax.psum_scatter(totals[0], ("dp", "seq"), scatter_dimension=0, tiled=True),
        lax.psum_scatter(totals[1], ("dp", "seq"), scatter_dimension=0, tiled=True),
        lax.psum_scatter(totals[2], ("dp", "seq"), scatter_dimension=0, tiled=True),
        lax.psum_scatter(totals[3], ("dp", "seq"), scatter_dimension=0, tiled=True),
        lax.psum_scatter(totals[4], ("dp", "seq"), scatter_dimension=0, tiled=True),
        lax.psum_scatter(totals[5], ("dp", "seq"), scatter_dimension=1, tiled=True),
        lax.psum_scatter(totals[6], ("dp", "seq"), scatter_dimension=1, tiled=True),
        lax.psum_scatter(totals[7], ("dp", "seq"), scatter_dimension=0, tiled=True),
        lax.psum_scatter(totals[8], ("dp", "seq"), scatter_dimension=0, tiled=True),
    )
    return (
        jnp.concatenate(outputs_main, axis=0),
        jnp.concatenate(outputs_grad, axis=0),
        totals[7],
        totals[8],
        totals[0],
        totals[1],
        totals[2],
        totals[5],
        totals[3],
        totals[4],
        totals[6],
    )


MESH_ID = pl.DeviceIdType.MESH
VMEM_LIMIT = 58 << 20
LANES = 128
ROW_STEP = 32


def nt_dot(a, b):
    return lax.dot_general(a, b, (((1,), (1,)), ((), ())), preferred_element_type=jnp.float32)


def tn_dot(a, b):
    return lax.dot_general(a, b, (((0,), (0,)), ((), ())), preferred_element_type=jnp.float32)


def nn_dot(a, b):
    return lax.dot_general(a, b, (((1,), (0,)), ((), ())), preferred_element_type=jnp.float32)


def plane_places():
    at, core = lax.axis_index("dp"), lax.axis_index("tensor")
    x_bit, y_bit = lax.rem(at, 2), at // 2
    return (
        at,
        y_bit * 2 + (1 - x_bit),
        (1 - y_bit) * 2 + x_bit,
        (1 - y_bit) * 2 + (1 - x_bit),
        core,
    )


def greet(places):
    barrier = pltpu.get_barrier_semaphore()
    for place in places:
        pl.semaphore_signal(barrier, inc=1, device_id=place, device_id_type=MESH_ID)
    pl.semaphore_wait(barrier, len(places))


class Sender:
    def __init__(self, sems):
        self.sems, self.used = sems, 0

    def __call__(self, src, dst, place):
        index = self.used
        self.used += 1
        return pltpu.make_async_remote_copy(
            src_ref=src,
            dst_ref=dst,
            send_sem=self.sems.at[0, index],
            recv_sem=self.sems.at[1, index],
            device_id=place,
            device_id_type=MESH_ID,
        )


def greet_plane():
    at, x_at, y_at, _, core = plane_places()
    greet([{"dp": x_at}, {"dp": y_at}, {"tensor": 1 - core}])


def add_rows(dst, *srcs, step=64):
    def body(i, carry):
        r = pl.ds(pl.multiple_of(i * step, step), step)
        total = srcs[0][r].astype(jnp.float32)
        for s in srcs[1:]:
            total = total + s[r].astype(jnp.float32)
        dst[r] = total.astype(dst.dtype)
        return carry

    lax.fori_loop(0, srcs[0].shape[0] // step, body, 0)


GATHER_COPIES = 13
SCATTER_COPIES = 10


def gather_steps(own_ref, out_ref, copy, local_sem):
    at, x_at, y_at, d_at, core = plane_places()
    half = own_ref.shape[0] // 2
    xp, yp, sp = {"dp": x_at}, {"dp": y_at}, {"tensor": 1 - core}
    lo, hi = pl.ds(0, half), pl.ds(half, half)
    mine = out_ref.at[at, core]
    x_lo = copy(own_ref.at[lo], mine.at[lo], xp)
    y_hi = copy(own_ref.at[hi], mine.at[hi], yp)
    x_hi = copy(own_ref.at[hi], mine.at[hi], xp)
    y_lo = copy(own_ref.at[lo], mine.at[lo], yp)
    pair = copy(own_ref, mine, sp)
    for c in (x_lo, y_hi, x_hi, y_lo, pair):
        c.start()
    local_copy = pltpu.make_async_copy(own_ref, mine, local_sem)
    local_copy.start()
    from_x, from_y, from_d = out_ref.at[x_at, core], out_ref.at[y_at, core], out_ref.at[d_at, core]
    on_y = copy(from_x.at[lo], from_x.at[lo], yp)
    on_x = copy(from_y.at[hi], from_y.at[hi], xp)
    handed = [
        copy(block.at[rows], block.at[rows], sp)
        for block, rows in (
            (from_x, lo),
            (from_y, hi),
            (from_x, hi),
            (from_y, lo),
            (from_d, lo),
            (from_d, hi),
        )
    ]
    yield
    local_copy.wait()
    yield
    pair.wait_recv()
    yield
    x_lo.wait_recv()
    on_y.start()
    handed[0].start()
    y_hi.wait_recv()
    on_x.start()
    handed[1].start()
    yield
    handed[0].wait_recv()
    handed[1].wait_recv()
    yield
    x_hi.wait_recv()
    handed[2].start()
    y_lo.wait_recv()
    handed[3].start()
    yield
    handed[2].wait_recv()
    handed[3].wait_recv()
    yield
    on_y.wait_recv()
    handed[4].start()
    on_x.wait_recv()
    handed[5].start()
    yield
    handed[4].wait_recv()
    handed[5].wait_recv()
    yield
    for c in [x_lo, y_hi, x_hi, y_lo, on_y, on_x, pair] + handed:
        c.wait_send()


def scatter_steps(part_ref, out_ref, pair_ref, sum_ref, got_ref, copy, held=None):
    at, x_at, y_at, d_at, core = plane_places()
    half = part_ref.shape[2] // 2
    xp, yp, sp = {"dp": x_at}, {"dp": y_at}, {"tensor": 1 - core}
    lo, hi = pl.ds(0, half), pl.ds(half, half)
    order = (d_at, x_at, y_at, at)
    pairs = [copy(part_ref.at[to, 1 - core], pair_ref.at[j], sp) for j, to in enumerate(order)]
    for c in pairs:
        c.start()
    own = [part_ref.at[to, core] for to in order]
    fetched = []
    if held is not None:
        buffer, held_sems = held
        fetched = [
            pltpu.make_async_copy(o, buffer.at[j], held_sems.at[j]) for j, o in enumerate(own)
        ]
        own = [buffer.at[j] for j in range(4)]
        for c in fetched:
            c.start()
    yield

    def ready(j):
        if fetched:
            fetched[j].wait()
        pairs[j].wait_recv()

    def total(j, rows, *more):
        add_rows(sum_ref.at[j, rows], own[j].at[rows], pair_ref.at[j, rows], *more)

    def sent(j, rows, place):
        return copy(sum_ref.at[j, rows], got_ref.at[j, rows], place)

    d_lo, d_hi = sent(0, lo, xp), sent(0, hi, yp)
    x_lo, y_hi, x_hi, y_lo = sent(1, lo, xp), sent(2, hi, yp), sent(1, hi, xp), sent(2, lo, yp)
    ready(0)
    total(0, lo)
    d_lo.start()
    total(0, hi)
    d_hi.start()
    ready(1)
    total(1, lo)
    x_lo.start()
    ready(2)
    total(2, hi)
    y_hi.start()
    yield
    d_lo.wait_recv()
    total(2, lo, got_ref.at[0, lo])
    y_lo.start()
    d_hi.wait_recv()
    total(1, hi, got_ref.at[0, hi])
    x_hi.start()
    yield
    ready(3)
    for c in (x_lo, y_hi, y_lo, x_hi):
        c.wait_recv()
    add_rows(out_ref, own[3], pair_ref.at[3], got_ref.at[1], got_ref.at[2])
    for c in pairs + [d_lo, d_hi, x_lo, y_hi, x_hi, y_lo]:
        c.wait_send()


def swap_shards(ins, outs, peers, me, take, put, copy, local_sems):
    started = [
        copy(take(i, p), put(o, me), {"dp": p}) for i, o in zip(ins, outs) for p in peers
    ]
    started += [
        pltpu.make_async_copy(take(i, me), put(o, me), local_sems.at[n])
        for n, (i, o) in enumerate(zip(ins, outs))
    ]
    for c in started:
        c.start()
    return started


def exchange_kernel(take, put, count, *refs):
    ins, outs, sems, local_sems = refs[:count], refs[count : 2 * count], refs[-2], refs[-1]
    size, me = lax.axis_size("dp"), lax.axis_index("dp")
    peers = [lax.rem(me + k, size) for k in range(1, size)]
    greet([{"dp": p} for p in peers])
    for c in swap_shards(ins, outs, peers, me, take, put, Sender(sems), local_sems):
        c.wait()


def block_of(ref, index):
    return ref.at[index]


def columns_of(ref, index):
    width = ref.shape[1] // lax.axis_size("dp")
    return ref.at[:, pl.ds(pl.multiple_of(index * width, width), width)]


def exchange(arrays, cid, shapes, take=block_of, put=block_of):
    count, peers = len(arrays), lax.axis_size("dp") - 1
    anywhere = [pl.BlockSpec(memory_space=pl.ANY)] * count
    return pl.pallas_call(
        partial(exchange_kernel, take, put, count),
        name="exchange",
        out_shape=[jax.ShapeDtypeStruct(s, x.dtype) for s, x in zip(shapes, arrays)],
        in_specs=anywhere,
        out_specs=anywhere,
        scratch_shapes=[
            pltpu.SemaphoreType.DMA((2, count * peers)),
            pltpu.SemaphoreType.DMA((count,)),
        ],
        compiler_params=pltpu.CompilerParams(collective_id=cid, has_side_effects=True),
        cost_estimate=pl.CostEstimate(
            flops=0, bytes_accessed=60 * sum(x.size for x in arrays), transcendentals=0
        ),
    )(*arrays)


def first_kernel(pack_ref, small_ref, out_ref, all_ref, sems, small_sems, local_sems):
    plane, span = lax.axis_size("dp"), lax.axis_size("seq")
    at, z = lax.axis_index("dp"), lax.axis_index("seq")
    places = [
        {"dp": lax.rem(at + i, plane), "seq": lax.rem(z + k, span)}
        for k in range(span)
        for i in range(plane)
        if i or k
    ]
    greet(places)
    copy, copy_small = Sender(sems), Sender(small_sems)
    block = all_ref.at[z * plane + at]
    copies = [copy_small(small_ref, block, p) for p in places]
    for i in range(1, plane):
        to = lax.rem(at + i, plane)
        copies.append(copy(pack_ref.at[to], columns_of(out_ref, at), {"dp": to}))
    copies.append(pltpu.make_async_copy(small_ref, block, local_sems.at[0]))
    copies.append(
        pltpu.make_async_copy(pack_ref.at[at], columns_of(out_ref, at), local_sems.at[1])
    )
    for c in copies:
        c.start()
    for c in copies:
        c.wait()


def first_exchange(pack, small, cid):
    plane, span = lax.axis_size("dp"), lax.axis_size("seq")
    _, size, chunk = pack.shape
    anywhere = pl.BlockSpec(memory_space=pl.ANY)
    whole = pl.BlockSpec(memory_space=pltpu.VMEM)
    return pl.pallas_call(
        first_kernel,
        name="first_exchange",
        out_shape=[
            jax.ShapeDtypeStruct((size, plane * chunk), pack.dtype),
            jax.ShapeDtypeStruct((span * plane,) + small.shape, small.dtype),
        ],
        in_specs=[anywhere, whole],
        out_specs=[anywhere, whole],
        scratch_shapes=[
            pltpu.SemaphoreType.DMA((2, plane - 1)),
            pltpu.SemaphoreType.DMA((2, plane * span - 1)),
            pltpu.SemaphoreType.DMA((2,)),
        ],
        compiler_params=pltpu.CompilerParams(collective_id=cid, has_side_effects=True),
        cost_estimate=pl.CostEstimate(
            flops=0, bytes_accessed=60 * pack.size, transcendentals=0
        ),
    )(pack, small)


def run(*steps):
    for g in steps:
        for _ in g:
            pass


def row_blocks(rows, step, body):
    def inner(i, carry):
        return body(pl.ds(pl.multiple_of(i * step, step), step), carry)

    return lambda init: lax.fori_loop(0, rows // step, inner, init)


def lanes(k):
    return pl.ds(k * LANES, LANES)


def seq_major_block(k):
    plane, span = lax.axis_size("dp"), lax.axis_size("seq")
    s, g = divmod(k, plane)
    return g * span + s


def mean_of(acc, width):
    return jnp.sum(acc, axis=1, keepdims=True) * (1.0 / width)


def kernel_call(body, name, cid, outs, ins, scratch, flops=0, moved=0):
    params = dict(has_side_effects=True, vmem_limit_bytes=VMEM_LIMIT)
    return pl.pallas_call(
        body,
        name=name,
        out_shape=[jax.ShapeDtypeStruct(s, d) for s, d, _ in outs],
        in_specs=[pl.BlockSpec(memory_space=m) for _, m in ins],
        out_specs=[pl.BlockSpec(memory_space=m) for _, _, m in outs],
        scratch_shapes=scratch,
        compiler_params=pltpu.CompilerParams(collective_id=cid, **params),
        cost_estimate=pl.CostEstimate(flops=flops, bytes_accessed=moved, transcendentals=0),
    )(*[a for a, _ in ins])


def copies(count):
    return pltpu.SemaphoreType.DMA((2, count))


def entry_kernel(
    tokens_ref, cot_ref, small_ref, all_ref, x_ref, cot_own_ref, normed_ref, sems, local_sem
):
    greet_plane()
    core = lax.axis_index("tensor")
    m, width = x_ref.shape
    blocks = width // LANES

    def body(r, carry):
        acc = jnp.zeros((ROW_STEP, LANES), jnp.float32)
        for k in range(blocks):
            source = lanes(seq_major_block(k))
            v = tokens_ref[core, r, source]
            x_ref[r, lanes(k)] = v
            cot_own_ref[r, lanes(k)] = cot_ref[core, r, source]
            v = v.astype(jnp.float32)
            acc += v * v
        scale = lax.rsqrt(mean_of(acc, width) + norm_epsilon)
        for k in range(blocks):
            v = x_ref[r, lanes(k)].astype(jnp.float32)
            normed_ref[r, lanes(k)] = (v * scale * small_ref[k, 0:1, :]).astype(jnp.bfloat16)
        return carry

    row_blocks(m, ROW_STEP, body)(0)
    run(gather_steps(normed_ref, all_ref, Sender(sems), local_sem))


def entry(tokens, cot, small, cid):
    cores, m, width = tokens.shape
    whole = pltpu.VMEM
    gathered, x, cot_own = kernel_call(
        entry_kernel,
        "entry",
        cid,
        [
            ((4, cores, m, width), jnp.bfloat16, pl.ANY),
            ((m, width), jnp.bfloat16, whole),
            ((m, width), jnp.bfloat16, whole),
        ],
        [(tokens, whole), (cot, whole), (small, whole)],
        [pltpu.VMEM((m, width), jnp.bfloat16), copies(GATHER_COPIES), pltpu.SemaphoreType.DMA],
        moved=tokens.size * 40,
    )
    return gathered.reshape(-1, width), x, cot_own


def head_mask(rows, head):
    lane = lax.broadcasted_iota(jnp.int32, (rows, LANES), 1)
    return (lane >= head * FDIM) & (lane < (head + 1) * FDIM)


def keys_in_place(qkv_ref, keys_ref, vcols, qcols):
    for j in range(qkv_ref.shape[0]):
        tile = qkv_ref[j, :, pl.ds(vcols, LANES)].astype(jnp.float32)
        keys_ref[j] = pltpu.roll(tile, LANES - qcols, axis=1).astype(jnp.bfloat16)


def masked_weights(query, key, col_ref, row_ref, r, i, j, length):
    a = nt_dot(query, key) * 0.25
    t = lax.broadcasted_iota(jnp.int32, (length, length), 0) + i * length
    s = lax.broadcasted_iota(jnp.int32, (length, length), 1) + j * length
    keep = (s <= t) & (col_ref[r, i] == row_ref[r, j])
    return a, jnp.where(keep, 1.0 + a + 0.5 * a * a, 0.0), keep


def mix_kernel(
    heads,
    normed_ref,
    pack_ref,
    col_ref,
    row_ref,
    cot_ref,
    qkv_ref,
    mixed_ref,
    exact_ref,
    den_ref,
    cot_all_ref,
    out_qkv,
    out_mixed,
    keys_ref,
    sems,
    cot_sems,
    local_sem,
):
    span, z = lax.axis_size("seq"), lax.axis_index("seq")
    parts, _, depth = pack_ref.shape
    tokens = qkv_ref.shape[1]
    rows, length = col_ref.shape[0], col_ref.shape[2]
    vcols, qcols = heads * VHEAD, heads * FDIM
    at, x_at, y_at, _, core = plane_places()
    peers = [lax.rem(z + k, span) for k in range(1, span)]
    greet([{"dp": x_at}, {"dp": y_at}, {"tensor": 1 - core}] + [{"seq": p} for p in peers])
    gather = gather_steps(cot_ref, cot_all_ref, Sender(cot_sems), local_sem)
    next(gather)
    copy = Sender(sems)

    def project(dest, out):
        x = pl.ds(pl.multiple_of(dest * tokens, tokens), tokens)
        value = jnp.zeros((tokens, vcols), jnp.float32)
        tile = jnp.zeros((tokens, LANES), jnp.float32)
        for s in range(parts):
            piece = normed_ref[x, pl.ds(s * depth, depth)]
            value += nt_dot(piece, pack_ref[s, pl.ds(0, vcols)])
            tile += nt_dot(piece, pack_ref[s, pl.ds(vcols, LANES)])
        lane = lax.broadcasted_iota(jnp.int32, (tokens, LANES), 1)
        out[:, pl.ds(0, vcols)] = value.astype(jnp.bfloat16)
        out[:, pl.ds(vcols, LANES)] = jnp.where(lane < 2 * qcols, tile, 0.0).astype(jnp.bfloat16)

    there = []
    for k, p in enumerate(peers):
        project(p, out_qkv.at[k])
        there.append(copy(out_qkv.at[k], qkv_ref.at[z], {"seq": p}))
        there[-1].start()
    project(z, qkv_ref.at[z])
    run(gather)
    for c in there:
        c.wait()
    keys_in_place(qkv_ref, keys_ref, vcols, qcols)

    def mixer(i, out):
        def one_row(r, carry):
            t = pl.ds(pl.multiple_of(r * length, length), length)
            tile = qkv_ref[i, t, pl.ds(vcols, LANES)]
            queries = [
                jnp.where(head_mask(length, h), tile, jnp.zeros_like(tile)) for h in range(heads)
            ]

            def block(j, carry):
                new = []
                for h in range(heads):
                    num, den = carry[h]
                    _, w, _ = masked_weights(
                        queries[h], keys_ref[j, t], col_ref, row_ref, r, i, j, length
                    )
                    value = qkv_ref[j, t, pl.ds(h * VHEAD, VHEAD)]
                    new.append(
                        (
                            num + nn_dot(w.astype(jnp.bfloat16), value),
                            den + jnp.sum(w, axis=1, keepdims=True),
                        )
                    )
                return tuple(new)

            zero = (
                jnp.zeros((length, VHEAD), jnp.float32),
                jnp.zeros((length, 1), jnp.float32),
            )
            done = lax.fori_loop(0, i + 1, block, (zero,) * heads)
            lane = lax.broadcasted_iota(jnp.int32, (length, LANES), 1)
            dens = jnp.zeros((length, LANES), jnp.float32)
            for h, (num, den) in enumerate(done):
                v = num / den
                exact_ref[i, t, pl.ds(h * VHEAD, VHEAD)] = v
                out[t, pl.ds(h * VHEAD, VHEAD)] = v.astype(jnp.bfloat16)
                dens = jnp.where(lane == h, den, dens)
            den_ref[i, t] = dens
            return carry

        lax.fori_loop(0, rows, one_row, 0)

    back = []
    for k, p in enumerate(peers):
        mixer(p, out_mixed.at[k])
        back.append(copy(out_mixed.at[k], mixed_ref.at[z], {"seq": p}))
        back[-1].start()
    mixer(z, mixed_ref.at[z])
    for c in back:
        c.wait()


def mix(normed, pack, seg_col, seg_row, cot_own, heads, cid):
    span = lax.axis_size("seq")
    tokens = normed.shape[0] // span
    vcols = heads * VHEAD
    m, width = cot_own.shape
    whole = pltpu.VMEM
    qkv, mixed, exact, den, cot = kernel_call(
        partial(mix_kernel, heads),
        "mix",
        cid,
        [
            ((span, tokens, vcols + LANES), jnp.bfloat16, whole),
            ((span, tokens, vcols), jnp.bfloat16, whole),
            ((span, tokens, vcols), jnp.float32, whole),
            ((span, tokens, LANES), jnp.float32, whole),
            ((4, 2, m, width), jnp.bfloat16, pl.ANY),
        ],
        [(normed, whole), (pack, whole), (seg_col, whole), (seg_row, whole), (cot_own, whole)],
        [
            pltpu.VMEM((span - 1, tokens, vcols + LANES), jnp.bfloat16),
            pltpu.VMEM((span - 1, tokens, vcols), jnp.bfloat16),
            pltpu.VMEM((span, tokens, LANES), jnp.bfloat16),
            copies(2 * (span - 1)),
            copies(GATHER_COPIES),
            pltpu.SemaphoreType.DMA,
        ],
        moved=normed.size * 40,
    )
    return qkv, mixed.reshape(-1, vcols), exact, den, cot.reshape(-1, width)


def branch_kernel(
    mixed_ref,
    pack_ref,
    x_ref,
    small_ref,
    residual_ref,
    normed_ref,
    part_ref,
    pair_ref,
    sum_ref,
    got_ref,
    sems,
):
    greet_plane()
    parts, _, depth = pack_ref.shape
    m, width = x_ref.shape
    vcols = mixed_ref.shape[1]
    first = pack_ref.shape[1] - vcols

    def project(b, carry):
        left = mixed_ref[pl.ds(pl.multiple_of(b * m, m), m)]
        for s in range(parts):
            part_ref[b // 2, lax.rem(b, 2), :, pl.ds(s * depth, depth)] = nn_dot(
                left, pack_ref[s, pl.ds(first, vcols)]
            ).astype(jnp.bfloat16)
        return carry

    lax.fori_loop(0, 8, project, 0)
    run(scatter_steps(part_ref, residual_ref, pair_ref, sum_ref, got_ref, Sender(sems)))

    def body(r, carry):
        acc = jnp.zeros((ROW_STEP, LANES), jnp.float32)
        for k in range(width // LANES):
            v = residual_ref[r, lanes(k)] + x_ref[r, lanes(k)].astype(jnp.float32)
            residual_ref[r, lanes(k)] = v
            acc += v * v
        scale = lax.rsqrt(mean_of(acc, width) + norm_epsilon)
        for k in range(width // LANES):
            normed_ref[r, lanes(k)] = (
                residual_ref[r, lanes(k)] * scale * small_ref[k, 1:2, :]
            ).astype(jnp.bfloat16)
        return carry

    row_blocks(m, ROW_STEP, body)(0)


def scatter_scratch(m, width):
    return [
        pltpu.VMEM((4, m, width), jnp.bfloat16),
        pltpu.VMEM((3, m, width), jnp.bfloat16),
        pltpu.VMEM((3, m, width), jnp.bfloat16),
    ]


def branch(mixed, pack, x, small, cid):
    m, width = x.shape
    whole = pltpu.VMEM
    return kernel_call(
        branch_kernel,
        "branch",
        cid,
        [((m, width), jnp.float32, whole), ((m, width), jnp.bfloat16, whole)],
        [(mixed, whole), (pack, whole), (x, whole), (small, whole)],
        [pltpu.VMEM((4, 2, m, width), jnp.bfloat16)]
        + scatter_scratch(m, width)
        + [copies(SCATTER_COPIES)],
        moved=x.size * 80,
    )


def parity(i):
    return i % 2 if isinstance(i, int) else lax.rem(i, 2)


def choose(test, a, b):
    if isinstance(test, bool):
        return a if test else b
    return jnp.where(test, a, b)


def ffn_block(x_at, cot_at, w_ref, out_ref, dnormed_ref, dgate_ref, dup_ref, hidden_ref):
    parts, units, depth = w_ref.shape
    units //= 3

    def rows(k):
        return pl.ds(k * units, units)

    def cols(s):
        return pl.ds(s * depth, depth)

    def project(at, k):
        total = nt_dot(at(cols(0)), w_ref[0, rows(k)])
        for s in range(1, parts):
            total += nt_dot(at(cols(s)), w_ref[s, rows(k)])
        return total

    gate, up, dhidden = project(x_at, 0), project(x_at, 1), project(cot_at, 2)
    sig = jax.nn.sigmoid(gate)
    silu = gate * sig
    hidden = (silu * up).astype(jnp.bfloat16)
    dgate = (dhidden * up * sig * (1.0 + gate * (1.0 - sig))).astype(jnp.bfloat16)
    dup = (dhidden * silu).astype(jnp.bfloat16)
    for s in range(parts):
        dnormed_ref[:, cols(s)] = (
            nn_dot(dgate, w_ref[s, rows(0)]) + nn_dot(dup, w_ref[s, rows(1)])
        ).astype(jnp.bfloat16)
        out_ref[:, cols(s)] = nn_dot(hidden, w_ref[s, rows(2)]).astype(jnp.bfloat16)
    hidden_ref[...], dgate_ref[...], dup_ref[...] = hidden.T, dgate.T, dup.T


def expand_kernel(
    own_ref,
    cot_hbm,
    w_hbm,
    normed_hbm,
    out_hbm,
    dnormed_hbm,
    dgate_hbm,
    dup_hbm,
    hidden_hbm,
    normed_ref,
    w_ref,
    cot_ref,
    out_ref,
    dnormed_ref,
    dgate_ref,
    dup_ref,
    hidden_ref,
    sems,
    local_sem,
    w_sem,
    cot_sems,
    store_sems,
    keep_sems,
):
    greet_plane()
    at, x_at, y_at, d_at, core = plane_places()
    m = own_ref.shape[0]
    half = m // 2
    gather = gather_steps(own_ref, normed_ref, Sender(sems), local_sem)
    next(gather)
    weights = pltpu.make_async_copy(w_hbm, w_ref, w_sem)
    weights.start()

    def halves(i):
        k = choose(parity(i) == 0, core, 1 - core)
        one = choose(i < 2, at, choose(i < 6, x_at, d_at))
        two = choose(i < 2, at, choose(i < 6, y_at, d_at))
        late = (i >= 4) & (i < 6)
        late = int(late) if isinstance(late, bool) else late.astype(jnp.int32)
        first, second = late * half, (1 - late) * half
        if not isinstance(i, int):
            first, second = pl.multiple_of(first, half), pl.multiple_of(second, half)
        return (one, k, first), (two, k, second)

    def cot_copies(i):
        slot = parity(i)
        return [
            pltpu.make_async_copy(
                cot_hbm.at[c, k, pl.ds(r, half)],
                cot_ref.at[slot, pl.ds(n * half, half)],
                cot_sems.at[slot, n],
            )
            for n, (c, k, r) in enumerate(halves(i))
        ]

    def store_copies(i):
        slot = parity(i)
        found = []
        for n, (c, k, r) in enumerate(halves(i)):
            rows = pl.ds(n * half, half)
            column = pl.ds(pl.multiple_of((c * 2 + k) * m + r, half), half)
            pairs = [
                (out_ref.at[slot, rows], out_hbm.at[c, k, pl.ds(r, half)]),
                (dnormed_ref.at[slot, rows], dnormed_hbm.at[c, k, pl.ds(r, half)]),
                (dgate_ref.at[slot, :, rows], dgate_hbm.at[:, column]),
                (dup_ref.at[slot, :, rows], dup_hbm.at[:, column]),
                (hidden_ref.at[slot, :, rows], hidden_hbm.at[:, column]),
            ]
            found += [
                pltpu.make_async_copy(a, b, store_sems.at[slot, n * len(pairs) + q])
                for q, (a, b) in enumerate(pairs)
            ]
        return found

    for c in cot_copies(0):
        c.start()
    next(gather)
    weights.wait()

    def body(i, carry):
        for step in range(1, 8):

            @pl.when(i == step)
            def _():
                next(gather)

        @pl.when(i < 7)
        def _():
            for c in cot_copies(i + 1):
                c.start()

        for c in cot_copies(i):
            c.wait()

        @pl.when(i >= 2)
        def _():
            for c in store_copies(i - 2):
                c.wait()

        slot = lax.rem(i, 2)
        pieces = halves(i)

        def x_cols(cols):
            return jnp.concatenate([normed_ref[c, k, pl.ds(r, half), cols] for c, k, r in pieces])

        def cot_cols(cols):
            return cot_ref[slot, :, cols]

        ffn_block(
            x_cols,
            cot_cols,
            w_ref,
            out_ref.at[slot],
            dnormed_ref.at[slot],
            dgate_ref.at[slot],
            dup_ref.at[slot],
            hidden_ref.at[slot],
        )
        for c in store_copies(i):
            c.start()
        return carry

    lax.fori_loop(0, 8, body, 0)
    keep = pltpu.make_async_copy(normed_ref, normed_hbm, keep_sems.at[0])
    keep.start()
    for i in (6, 7):
        for c in store_copies(i):
            c.wait()
    keep.wait()
    run(gather)


def expand(own, cot, weights, cid):
    m, width = own.shape
    units = weights.shape[1] // 3
    tokens = 8 * m
    whole, low = pltpu.VMEM, jnp.bfloat16
    blocks = ((4, 2, m, width), low, pl.ANY)
    thin = ((units, tokens), low, pl.ANY)
    normed, out, dnormed, dgate, dup, hidden = kernel_call(
        expand_kernel,
        "expand",
        cid,
        [blocks, blocks, blocks, thin, thin, thin],
        [(own, whole), (cot.reshape(4, 2, m, width), pl.ANY), (weights, pl.ANY)],
        [
            pltpu.VMEM((4, 2, m, width), low),
            pltpu.VMEM(weights.shape, low),
            pltpu.VMEM((2, m, width), low),
            pltpu.VMEM((2, m, width), low),
            pltpu.VMEM((2, m, width), low),
            pltpu.VMEM((2, units, m), low),
            pltpu.VMEM((2, units, m), low),
            pltpu.VMEM((2, units, m), low),
            copies(GATHER_COPIES),
            pltpu.SemaphoreType.DMA,
            pltpu.SemaphoreType.DMA,
            pltpu.SemaphoreType.DMA((2, 2)),
            pltpu.SemaphoreType.DMA((2, 10)),
            pltpu.SemaphoreType.DMA((1,)),
        ],
        flops=12 * tokens * width * units,
        moved=1 << 28,
    )
    return normed.reshape(tokens, width), out, dnormed, dgate, dup, hidden


def norm_gradient(r, value_at, grad_ref, gain_at, gain_grad, finish, width):
    squares = jnp.zeros((ROW_STEP, LANES), jnp.float32)
    cross = jnp.zeros((ROW_STEP, LANES), jnp.float32)
    for k in range(width // LANES):
        v = value_at(r, k)
        squares += v * v
        cross += v * grad_ref[r, lanes(k)] * gain_at(k)
    scale = lax.rsqrt(mean_of(squares, width) + norm_epsilon)
    pull = mean_of(cross, width) * scale * scale * scale
    for k in range(width // LANES):
        v, g = value_at(r, k), grad_ref[r, lanes(k)]
        gain_grad[:, lanes(k)] += jnp.sum(
            (g * v * scale).reshape(ROW_STEP // 8, 8, LANES), axis=0
        )
        finish(r, k, scale * g * gain_at(k) - v * pull)


def middle_kernel(
    part_hbm,
    normed_hbm,
    dgate_hbm,
    dup_hbm,
    total_ref,
    gate_hbm,
    up_hbm,
    held_ref,
    pair_ref,
    sum_ref,
    got_ref,
    normed_ref,
    left_ref,
    grad_ref,
    sems,
    held_sems,
    load_sems,
    store_sems,
):
    greet_plane()
    scatter = scatter_steps(
        part_hbm, total_ref, pair_ref, sum_ref, got_ref, Sender(sems), (held_ref, held_sems)
    )
    next(scatter)
    loads = [
        pltpu.make_async_copy(a, b, load_sems.at[n])
        for n, (a, b) in enumerate(
            (
                (dgate_hbm, left_ref.at[0]),
                (normed_hbm, normed_ref),
                (dup_hbm, left_ref.at[1]),
            )
        )
    ]
    for c in loads:
        c.start()
    next(scatter)
    width = grad_ref.shape[2]
    blocks = normed_ref.shape[1] // width

    def gradients(which, out_hbm):
        def stored(i):
            column = pl.ds(pl.multiple_of(i * width, width), width)
            slot = parity(i)
            return pltpu.make_async_copy(
                grad_ref.at[slot], out_hbm.at[:, column], store_sems.at[slot]
            )

        def body(i, carry):
            column = pl.ds(pl.multiple_of(i * width, width), width)

            @pl.when(i >= 2)
            def _():
                stored(i - 2).wait()

            grad_ref[lax.rem(i, 2)] = nn_dot(left_ref[which], normed_ref[:, column]).astype(
                jnp.bfloat16
            )
            stored(i).start()
            return carry

        lax.fori_loop(0, blocks, body, 0)
        for i in (blocks - 2, blocks - 1):
            stored(i).wait()

    loads[0].wait()
    loads[1].wait()
    gradients(0, gate_hbm)
    next(scatter)
    loads[2].wait()
    gradients(1, up_hbm)
    run(scatter)


def middle(part, normed, dgate, dup, cid):
    _, _, m, width = part.shape
    units, tokens = dgate.shape
    low = jnp.bfloat16
    return kernel_call(
        middle_kernel,
        "middle",
        cid,
        [
            ((m, width), jnp.float32, pltpu.VMEM),
            ((units, width), low, pl.ANY),
            ((units, width), low, pl.ANY),
        ],
        [(a, pl.ANY) for a in (part, normed, dgate, dup)],
        [pltpu.VMEM((4, m, width), low)]
        + scatter_scratch(m, width)
        + [
            pltpu.VMEM((tokens, width), low),
            pltpu.VMEM((2, units, tokens), low),
            pltpu.VMEM((2, units, 256), low),
            copies(SCATTER_COPIES),
            pltpu.SemaphoreType.DMA((4,)),
            pltpu.SemaphoreType.DMA((3,)),
            pltpu.SemaphoreType.DMA((2,)),
        ],
        flops=4 * units * tokens * width,
        moved=m * width * 80,
    )


def turn_kernel(
    total_ref,
    residual_ref,
    cot_ref,
    small_ref,
    dresid_ref,
    gain_ref,
    all_ref,
    low_ref,
    gather_sems,
    local_sem,
):
    greet_plane()
    m, width = residual_ref.shape
    gain_ref[...] = jnp.zeros_like(gain_ref)

    def finish(r, k, v):
        v += cot_ref[r, lanes(k)].astype(jnp.float32)
        dresid_ref[r, lanes(k)] = v
        low_ref[r, lanes(k)] = v.astype(jnp.bfloat16)

    def body(r, carry):
        norm_gradient(
            r,
            lambda r, k: residual_ref[r, lanes(k)],
            total_ref,
            lambda k: small_ref[k, 1:2, :],
            gain_ref,
            finish,
            width,
        )
        return carry

    row_blocks(m, ROW_STEP, body)(0)
    run(gather_steps(low_ref, all_ref, Sender(gather_sems), local_sem))


def turn(total, residual, cot_own, small, cid):
    m, width = residual.shape
    whole = pltpu.VMEM
    dresid, gain, gathered = kernel_call(
        turn_kernel,
        "turn",
        cid,
        [
            ((m, width), jnp.float32, whole),
            ((8, width), jnp.float32, whole),
            ((4, 2, m, width), jnp.bfloat16, pl.ANY),
        ],
        [(a, whole) for a in (total, residual, cot_own, small)],
        [
            pltpu.VMEM((m, width), jnp.bfloat16),
            copies(GATHER_COPIES),
            pltpu.SemaphoreType.DMA,
        ],
        moved=residual.size * 80,
    )
    return dresid, gain, gathered.reshape(-1, width)


def back_kernel(
    dresid_ref,
    pack_ref,
    part_ref,
    residual_ref,
    dmixed_ref,
    block_ref,
    out_dmixed,
    total_ref,
    held_ref,
    pair_ref,
    sum_ref,
    got_ref,
    sems,
    scatter_sems,
    held_sems,
):
    span, z = lax.axis_size("seq"), lax.axis_index("seq")
    parts, _, depth = pack_ref.shape
    tokens, vcols = dmixed_ref.shape[1:]
    first = pack_ref.shape[1] - vcols
    at, x_at, y_at, _, core = plane_places()
    peers = [lax.rem(z + k, span) for k in range(1, span)]
    greet([{"dp": x_at}, {"dp": y_at}, {"tensor": 1 - core}] + [{"seq": p} for p in peers])
    scatter = scatter_steps(
        part_ref,
        total_ref,
        pair_ref,
        sum_ref,
        got_ref,
        Sender(scatter_sems),
        (held_ref, held_sems),
    )
    next(scatter)
    copy = Sender(sems)

    def project(dest, out):
        x = pl.ds(pl.multiple_of(dest * tokens, tokens), tokens)
        total = jnp.zeros((tokens, vcols), jnp.float32)
        for s in range(parts):
            total += nt_dot(
                dresid_ref[x, pl.ds(s * depth, depth)], pack_ref[s, pl.ds(first, vcols)]
            )
        out[...] = total.astype(jnp.bfloat16)

    there = []
    for k, p in enumerate(peers):
        project(p, out_dmixed.at[k])
        there.append(copy(out_dmixed.at[k], dmixed_ref.at[z], {"seq": p}))
        there[-1].start()
    project(z, dmixed_ref.at[z])
    run(scatter)

    def finish(r, carry):
        block_ref[r] = (residual_ref[r] + total_ref[r]).astype(jnp.bfloat16)
        return carry

    row_blocks(block_ref.shape[0], ROW_STEP, finish)(0)
    for c in there:
        c.wait()


def back(dresid_low, pack, part, residual, vcols, cid):
    span = lax.axis_size("seq")
    tokens = dresid_low.shape[0] // span
    m, width = residual.shape
    whole = pltpu.VMEM
    return kernel_call(
        back_kernel,
        "back",
        cid,
        [((span, tokens, vcols), jnp.bfloat16, whole), ((m, width), jnp.bfloat16, whole)],
        [(dresid_low, whole), (pack, whole), (part, pl.ANY), (residual, whole)],
        [
            pltpu.VMEM((span - 1, tokens, vcols), jnp.bfloat16),
            pltpu.VMEM((m, width), jnp.float32),
            pltpu.VMEM((4, m, width), jnp.bfloat16),
        ]
        + scatter_scratch(m, width)
        + [copies(span - 1), copies(SCATTER_COPIES), pltpu.SemaphoreType.DMA((4,))],
        moved=residual.size * 120,
    )


def unmix_kernel(
    heads,
    count,
    col_ref,
    row_ref,
    qkv_ref,
    exact_ref,
    den_ref,
    dmixed_ref,
    *refs,
):
    ins, dqkv_ref, outs = refs[:count], refs[count], refs[count + 1 : 2 * count + 1]
    out_dqkv, keys_ref, dtile_ref, dkey_ref, dvalue_ref, sems, shard_sems, local_sems = refs[
        2 * count + 1 :
    ]
    span, z = lax.axis_size("seq"), lax.axis_index("seq")
    rows, length = col_ref.shape[0], col_ref.shape[2]
    vcols, qcols = heads * VHEAD, heads * FDIM
    plane, at = lax.axis_size("dp"), lax.axis_index("dp")
    peers = [lax.rem(z + k, span) for k in range(1, span)]
    chips = [lax.rem(at + k, plane) for k in range(1, plane)]
    greet([{"dp": p} for p in chips] + [{"seq": p} for p in peers])
    copy = Sender(sems)
    shards = swap_shards(ins, outs, chips, at, columns_of, block_of, Sender(shard_sems), local_sems)
    keys_in_place(qkv_ref, keys_ref, vcols, qcols)
    dkey_ref[...] = jnp.zeros_like(dkey_ref)
    dvalue_ref[...] = jnp.zeros_like(dvalue_ref)

    def one_block(step, carry):
        r, i = step // span, lax.rem(step, span)
        t = pl.ds(pl.multiple_of(r * length, length), length)
        tile = qkv_ref[i, t, pl.ds(vcols, LANES)]
        dtile = jnp.zeros((length, LANES), jnp.float32)
        for h in range(heads):
            inside = head_mask(length, h)
            v = pl.ds(h * VHEAD, VHEAD)
            query = jnp.where(inside, tile, jnp.zeros_like(tile))
            dn = dmixed_ref[i, t, v].astype(jnp.float32) / den_ref[i, t, pl.ds(h, 1)]
            dd = -jnp.sum(dn * exact_ref[i, t, v], axis=1, keepdims=True)
            dn_low = dn.astype(jnp.bfloat16)

            def block(j, dquery, query=query, v=v, dn_low=dn_low, dd=dd, inside=inside):
                key = keys_ref[j, t]
                a, w, keep = masked_weights(query, key, col_ref, row_ref, r, i, j, length)
                dw = jnp.where(keep, nt_dot(dn_low, qkv_ref[j, t, v]) + dd, 0.0)
                da = (dw * (1.0 + a) * 0.25).astype(jnp.bfloat16)
                dvalue_ref[j, t, v] += tn_dot(w.astype(jnp.bfloat16), dn_low)
                dkey_ref[j, t] += jnp.where(inside, tn_dot(da, query), 0.0)
                return dquery + nn_dot(da, key)

            dquery = lax.fori_loop(0, i + 1, block, jnp.zeros((length, LANES), jnp.float32))
            dtile += jnp.where(inside, dquery, 0.0)
        dtile_ref[i, t] = dtile
        return carry

    lax.fori_loop(0, rows * span, one_block, 0)

    def pack(i, out):
        out[:, pl.ds(0, vcols)] = dvalue_ref[i].astype(jnp.bfloat16)
        out[:, pl.ds(vcols, LANES)] = (
            dtile_ref[i] + pltpu.roll(dkey_ref[i], qcols, axis=1)
        ).astype(jnp.bfloat16)

    home = []
    for k, p in enumerate(peers):
        pack(p, out_dqkv.at[k])
        home.append(copy(out_dqkv.at[k], dqkv_ref.at[z], {"seq": p}))
        home[-1].start()
    pack(z, dqkv_ref.at[z])
    for c in home + shards:
        c.wait()


def unmix(seg_col, seg_row, qkv, exact, den, dmixed, shards, heads, cid):
    span, tokens, wide = qkv.shape
    plane = lax.axis_size("dp")
    vcols = heads * VHEAD
    count = len(shards)
    whole = pltpu.VMEM
    dqkv, *swapped = kernel_call(
        partial(unmix_kernel, heads, count),
        "unmix",
        cid,
        [((span, tokens, wide), jnp.bfloat16, whole)]
        + [((plane, p.shape[0], p.shape[1] // plane), p.dtype, pl.ANY) for p in shards],
        [(a, whole) for a in (seg_col, seg_row, qkv, exact, den, dmixed)]
        + [(p, pl.ANY) for p in shards],
        [
            pltpu.VMEM((span - 1, tokens, wide), jnp.bfloat16),
            pltpu.VMEM((span, tokens, LANES), jnp.bfloat16),
            pltpu.VMEM((span, tokens, LANES), jnp.float32),
            pltpu.VMEM((span, tokens, LANES), jnp.float32),
            pltpu.VMEM((span, tokens, vcols), jnp.float32),
            copies(span - 1),
            copies(count * (plane - 1)),
            pltpu.SemaphoreType.DMA((count,)),
        ],
        moved=qkv.size * 120,
    )
    return dqkv.reshape(-1, wide), swapped


def last_kernel(count, *refs):
    ins, gain_ref, outs, sum_ref = (
        refs[:count],
        refs[count],
        refs[count + 1 : 2 * count + 1],
        refs[2 * count + 1],
    )
    got_gain, sems, gain_sems, local_sems = refs[2 * count + 2 :]
    plane, at = lax.axis_size("dp"), lax.axis_index("dp")
    others, me = everyone()
    greet(others)
    copy_gain = Sender(gain_sems)
    gains = [
        copy_gain(gain_ref.at[p["seq"] * plane + p["dp"]], got_gain.at[me], p) for p in others
    ]
    for c in gains:
        c.start()
    chips = [lax.rem(at + k, plane) for k in range(1, plane)]
    shards = swap_shards(ins, outs, chips, at, columns_of, block_of, Sender(sems), local_sems)
    got_gain[me] = gain_ref[lax.axis_index("seq") * plane + at]
    for c in gains:
        c.wait()
    total = got_gain[0]
    for k in range(1, len(others) + 1):
        total += got_gain[k]
    sum_ref[...] = total
    for c in shards:
        c.wait()


def last(shards, gains, cid):
    plane = lax.axis_size("dp")
    count = len(shards)
    devices = lax.axis_size(("dp", "seq", "tensor"))
    *swapped, total = kernel_call(
        partial(last_kernel, count),
        "last",
        cid,
        [((plane, p.shape[0], p.shape[1] // plane), p.dtype, pl.ANY) for p in shards]
        + [(gains.shape[1:], jnp.float32, pltpu.VMEM)],
        [(p, pl.ANY) for p in shards] + [(gains, pltpu.VMEM)],
        [
            pltpu.VMEM((devices,) + gains.shape[1:], jnp.float32),
            copies(count * (plane - 1)),
            copies(devices - 1),
            pltpu.SemaphoreType.DMA((count,)),
        ],
        moved=1 << 26,
    )
    return swapped, total


def everyone():
    plane, span, cores = (lax.axis_size(a) for a in ("dp", "seq", "tensor"))
    at, z, core = (lax.axis_index(a) for a in ("dp", "seq", "tensor"))
    others = [
        {
            "dp": lax.rem(at + i, plane),
            "seq": lax.rem(z + k, span),
            "tensor": lax.rem(core + c, cores),
        }
        for k in range(span)
        for i in range(plane)
        for c in range(cores)
        if i or k or c
    ]
    return others, (at * span + z) * cores + core


def exit_kernel(
    dqkv_ref,
    pack_ref,
    x_ref,
    dresid_ref,
    block_ref,
    small_ref,
    gain_two_ref,
    grad_ref,
    out_ref,
    gains_ref,
    gain_ref,
    part_ref,
    total_ref,
    ordered_ref,
    low_ref,
    pair_ref,
    sum_ref,
    got_ref,
    sems,
    pair_sems,
    local_sems,
):
    greet_plane()
    core = lax.axis_index("tensor")
    parts, _, depth = pack_ref.shape
    m, width = x_ref.shape
    wide = dqkv_ref.shape[1] - LANES + 2 * FDIM * ((dqkv_ref.shape[1] - LANES) // VHEAD)
    blocks = width // LANES
    copy = Sender(pair_sems)

    def project(b, carry):
        left = dqkv_ref[pl.ds(pl.multiple_of(b * m, m), m), pl.ds(0, wide)]
        for s in range(parts):
            part_ref[b // 2, lax.rem(b, 2), :, pl.ds(s * depth, depth)] = nn_dot(
                left, pack_ref[s, pl.ds(0, wide)]
            ).astype(jnp.bfloat16)
        return carry

    lax.fori_loop(0, 8, project, 0)
    scatter = scatter_steps(part_ref, total_ref, pair_ref, sum_ref, got_ref, Sender(sems))
    next(scatter)

    def order(r, carry):
        for k in range(blocks):
            low_ref[r, lanes(seq_major_block(k))] = block_ref[r, lanes(k)]
        return carry

    row_blocks(m, ROW_STEP, order)(0)
    to_pair = [copy(low_ref, out_ref.at[core], {"tensor": 1 - core})]
    local = [pltpu.make_async_copy(low_ref, out_ref.at[core], local_sems.at[0])]
    to_pair[0].start()
    local[0].start()
    run(scatter)
    gain_ref[...] = jnp.zeros_like(gain_ref)

    def finish(r, k, v):
        ordered_ref[r, lanes(seq_major_block(k))] = v + dresid_ref[r, lanes(k)]

    def body(r, carry):
        norm_gradient(
            r,
            lambda r, k: x_ref[r, lanes(k)].astype(jnp.float32),
            total_ref,
            lambda k: small_ref[k, 0:1, :],
            gain_ref,
            finish,
            width,
        )
        return carry

    row_blocks(m, ROW_STEP, body)(0)
    to_pair.append(copy(ordered_ref, grad_ref.at[core], {"tensor": 1 - core}))
    local.append(pltpu.make_async_copy(ordered_ref, grad_ref.at[core], local_sems.at[1]))
    to_pair[1].start()
    local[1].start()
    gains_ref[...] = jnp.zeros_like(gains_ref)
    for k in range(blocks):
        for row, ref in enumerate((gain_ref, gain_two_ref)):
            gains_ref[k, row : row + 1] = jnp.sum(ref[:, lanes(k)], axis=0, keepdims=True)
    for c in to_pair + local:
        c.wait()


def leave(dqkv, pack, x, dresid, block, small, gain_two, cid):
    m, width = x.shape
    whole = pltpu.VMEM
    return kernel_call(
        exit_kernel,
        "leave",
        cid,
        [
            ((2, m, width), jnp.float32, pl.ANY),
            ((2, m, width), jnp.bfloat16, pl.ANY),
            ((width // LANES, 8, LANES), jnp.float32, whole),
        ],
        [(a, whole) for a in (dqkv, pack, x, dresid, block, small, gain_two)],
        [
            pltpu.VMEM((8, width), jnp.float32),
            pltpu.VMEM((4, 2, m, width), jnp.bfloat16),
            pltpu.VMEM((m, width), jnp.float32),
            pltpu.VMEM((m, width), jnp.float32),
            pltpu.VMEM((m, width), jnp.bfloat16),
        ]
        + scatter_scratch(m, width)
        + [
            copies(SCATTER_COPIES),
            copies(2),
            pltpu.SemaphoreType.DMA((2,)),
        ],
        moved=x.size * 120,
    )


def plane_local(
    tokens,
    doc_starts,
    attn_gain,
    mlp_gain,
    query_weight,
    key_weight,
    value_weight,
    output_weight,
    gate_weight,
    up_weight,
    down_weight,
    cotangent,
):
    plane, span, cores = (lax.axis_size("dp"), lax.axis_size("seq"), lax.axis_size("tensor"))
    rows, length, width = tokens.shape
    chunk = width // (plane * span)
    own = rows * length // cores
    heads = query_weight.shape[1] // FDIM // plane
    hidden_part = gate_weight.shape[1] // plane
    vcols, qcols = heads * VHEAD, heads * FDIM
    all_rows = rows * plane // span

    def over_seq(pack):
        return lax.all_gather(pack, "seq", axis=0, tiled=False)

    def summed(grads):
        return lax.psum_scatter(
            grads.astype(jnp.bfloat16), "seq", scatter_dimension=1, tiled=True
        )

    def split(w):
        return w.reshape(plane, -1, chunk)

    small = jnp.concatenate(
        [
            attn_gain.astype(jnp.float32)[None],
            mlp_gain.astype(jnp.float32)[None],
            doc_starts.astype(jnp.float32).reshape(-1, chunk),
            jnp.zeros((2, chunk), jnp.float32),
        ]
    )
    attn_pack = jnp.concatenate(
        [split(value_weight.T), split(query_weight.T), split(key_weight.T), split(output_weight)],
        axis=1,
    )
    attn_pack, small = first_exchange(attn_pack, small, 1)
    ffn_pack = jnp.concatenate([split(gate_weight.T), split(up_weight.T), split(down_weight)], axis=1)
    ffn_pack, _ = lax.optimization_barrier((ffn_pack, attn_pack))
    [ffn_pack] = exchange(
        [ffn_pack], 2, [(ffn_pack.shape[1], plane * chunk)], put=columns_of
    )
    attn_pack, ffn_pack = over_seq(attn_pack), over_seq(ffn_pack)
    starts = small[:, 2:-2].reshape(span, plane * rows, length)
    starts = lax.dynamic_slice_in_dim(starts, lax.axis_index("seq") * all_rows, all_rows, 1)
    segments = jnp.cumsum(starts.transpose(1, 0, 2).reshape(all_rows, span * length), axis=1)

    qkv_rows = vcols + 2 * qcols
    seg_col = segments.reshape(all_rows, span, length, 1)
    seg_row = segments.reshape(all_rows, span, 1, length)
    normed_one, x, cot_own = entry(
        tokens.reshape(cores, own, width), cotangent.reshape(cores, own, width), small, 3
    )
    qkv, mixed, exact, den, cot = mix(normed_one, attn_pack, seg_col, seg_row, cot_own, heads, 4)
    residual, normed_own = branch(mixed, attn_pack, x, small, 5)
    normed_two, out_part, dnormed_part, dgate, dup, hidden = expand(
        normed_own, cot, ffn_pack, 11
    )
    down_grad = nn_dot(hidden, cot).astype(jnp.bfloat16)
    dnormed_part, down_grad = lax.optimization_barrier((dnormed_part, down_grad))
    down_grad = summed(down_grad)
    dnormed_two, gate_grad, up_grad = middle(dnormed_part, normed_two, dgate, dup, 6)
    gate_grad, up_grad = summed(gate_grad), summed(up_grad)
    dresid, gain_two_grad, dresid_low = turn(dnormed_two, residual, cot_own, small, 12)
    dresid_low, down_grad = lax.optimization_barrier((dresid_low, down_grad))
    dmixed, block_own = back(dresid_low, attn_pack, out_part, residual, vcols, 7)
    out_grad = tn_dot(mixed, dresid_low).astype(jnp.bfloat16)
    dmixed, gate_grad, out_grad = lax.optimization_barrier((dmixed, gate_grad, out_grad))
    dqkv, (down_grad, gate_grad) = unmix(
        seg_col, seg_row, qkv, exact, den, dmixed, [down_grad, gate_grad], heads, 8
    )
    qkv_grad = tn_dot(dqkv, normed_one).astype(jnp.bfloat16)[:qkv_rows]
    out_grad = summed(out_grad)
    dqkv, qkv_grad, up_grad = lax.optimization_barrier((dqkv, qkv_grad, up_grad))
    qkv_grad = summed(qkv_grad)
    dtokens, block_out, gains = leave(
        dqkv, attn_pack, x, dresid, block_own, small, gain_two_grad, 9
    )
    (up_grad, out_grad, qkv_grad), gain_grads = last([up_grad, out_grad, qkv_grad], gains, 10)

    def stacked(a, start, size):
        return a[:, start : start + size].reshape(plane * size, chunk).astype(jnp.float32)

    h = hidden_part
    return (
        block_out.reshape(rows, length, width),
        dtokens.reshape(rows, length, width),
        gain_grads[0],
        gain_grads[1],
        stacked(qkv_grad, vcols, qcols).T,
        stacked(qkv_grad, vcols + qcols, qcols).T,
        stacked(qkv_grad, 0, vcols).T,
        stacked(out_grad, 0, vcols),
        stacked(gate_grad, 0, h).T,
        stacked(up_grad, 0, h).T,
        stacked(down_grad, 0, h),
    )


def fits_plane(mesh, tokens, query_weight, gate_weight):
    plane, span, cores = (mesh.shape[a] for a in ("dp", "seq", "tensor"))
    heads = query_weight.shape[1] // FDIM // cores
    return (
        plane == 4
        and cores == 2
        and heads % plane == 0
        and (gate_weight.shape[1] // cores) % (16 * plane) == 0
        and tokens.shape[0] % span == 0
    )


def solution(mesh):
    def step(*args):
        use = fits_plane(mesh, args[0], args[4], args[8])
        return sharded(mesh, plane_local if use else local)(*args)

    return step


def sharded(mesh, body):
    return jax.shard_map(
        body,
        mesh=mesh,
        in_specs=(
            P("dp", "seq", None),
            P("dp", "seq"),
            P(("dp", "seq")),
            P(("dp", "seq")),
            P(("dp", "seq"), "tensor"),
            P(("dp", "seq"), "tensor"),
            P(("dp", "seq"), "tensor"),
            P("tensor", ("dp", "seq")),
            P(("dp", "seq"), "tensor"),
            P(("dp", "seq"), "tensor"),
            P("tensor", ("dp", "seq")),
            P("dp", "seq", None),
        ),
        out_specs=(
            P("dp", "seq", None),
            P("dp", "seq", None),
            P(("dp", "seq")),
            P(("dp", "seq")),
            P(("dp", "seq"), "tensor"),
            P(("dp", "seq"), "tensor"),
            P(("dp", "seq"), "tensor"),
            P("tensor", ("dp", "seq")),
            P(("dp", "seq"), "tensor"),
            P(("dp", "seq"), "tensor"),
            P("tensor", ("dp", "seq")),
        ),
        check_vma=False,
    )
```

```python
from functools import partial

import jax
import jax.numpy as jnp
import numpy as np
from jax import lax
from jax.experimental import pallas as pl
from jax.experimental.pallas import tpu as pltpu
from jax.sharding import PartitionSpec as P

FDIM = 16
VHEAD = 128
MICRO = 2


norm_epsilon = 1e-05
highest = lax.Precision.HIGHEST
outer_scale = 0.17677669529663687


def prefix(x, axis, combine, identity, reverse):
    size, index = (lax.axis_size(axis), lax.axis_index(axis))
    everything = jax.tree.map(lambda part: lax.all_gather(part, axis), x)
    start = jax.tree.map(
        lambda part, zero: jnp.broadcast_to(jnp.asarray(zero, part.dtype), part.shape), x, identity
    )

    def turn(k, before):
        at = size - 1 - k if reverse else k
        reached = at > index if reverse else at < index
        new = combine(before, jax.tree.map(lambda part: part[at], everything))
        return jax.tree.map(lambda a, b: jnp.where(reached, a, b), new, before)

    return lax.fori_loop(0, size, turn, start)


def features(vectors):
    ones_col = jnp.ones(vectors.shape[:-1] + (1,), jnp.float32)
    outer_terms = vectors[..., :, None] * vectors[..., None, :] * outer_scale
    outer_terms = outer_terms.reshape(vectors.shape[:-1] + (vectors.shape[-1] * vectors.shape[-1],))
    return jnp.concatenate([ones_col, 0.5 * vectors, outer_terms], axis=-1)


def mix_span(queries, key_rows, values, state_in, norm_in, segments):
    length = queries.shape[1]
    scores = jnp.einsum("rthf,rshf->rhts", queries, key_rows, precision=highest) / 4.0
    kernel = 1.0 + scores + 0.5 * scores * scores
    position = jnp.arange(length)
    causal = position[None, :] <= position[:, None]
    allowed = causal[None] & (segments[:, :, None] == segments[:, None, :])
    kernel = jnp.where(allowed[:, None], kernel, 0.0)
    numerator = jnp.einsum("rhts,rshe->rthe", kernel, values, precision=highest)
    denominator = jnp.transpose(jnp.sum(kernel, axis=-1), (0, 2, 1))
    head_part = (segments == 0).astype(jnp.float32)[:, :, None]
    lifted = features(queries)
    numerator = numerator + head_part[..., None] * jnp.einsum(
        "rthf,rhfe->rthe", lifted, state_in, precision=highest
    )
    denominator = denominator + head_part * jnp.einsum(
        "rthf,rhf->rth", lifted, norm_in, precision=highest
    )
    return numerator / denominator[..., None]


def tail_span(key_rows, values, segments):
    tail_mask = (segments == segments[:, -1:]).astype(jnp.float32)
    lifted = features(key_rows) * tail_mask[:, :, None, None]
    tail_state = jnp.einsum("rshf,rshe->rhfe", lifted, values, precision=highest)
    return (tail_state, jnp.sum(lifted, axis=1))


def combine_carry(earlier_part, later_part):
    keep_rate = 1.0 - later_part[2]
    return (
        later_part[0] + keep_rate[:, None, None, None] * earlier_part[0],
        later_part[1] + keep_rate[:, None, None] * earlier_part[1],
        jnp.maximum(earlier_part[2], later_part[2]),
    )


def inverse_rms(inputs):
    return lax.rsqrt(jnp.mean(inputs * inputs, axis=-1, keepdims=True) + norm_epsilon)


def norm_backward(inputs, scale_row, gain_vec, grad_normed):
    scaled_grad = grad_normed * gain_vec
    grad_gain = jnp.sum(grad_normed * inputs * scale_row, axis=0)
    grad_inputs = scale_row * scaled_grad - inputs * scale_row * scale_row * scale_row * jnp.mean(
        scaled_grad * inputs, axis=-1, keepdims=True
    )
    return (grad_inputs, grad_gain)


def inner_rows(left_mat, right_mat):
    return lax.dot_general(
        left_mat, right_mat, (((0,), (0,)), ((), ())), preferred_element_type=jnp.float32
    )


def by_transpose(left_mat, right_mat):
    return lax.dot_general(
        left_mat, right_mat, (((1,), (1,)), ((), ())), preferred_element_type=jnp.float32
    )


def local(
    tokens,
    doc_starts,
    attn_gain,
    mlp_gain,
    query_weight,
    key_weight,
    value_weight,
    output_weight,
    gate_weight,
    up_weight,
    down_weight,
    cotangent,
):
    micro_rows = tokens.shape[0] // MICRO
    span_len = tokens.shape[1]
    model_width = tokens.shape[2]
    head_count = query_weight.shape[1] // FDIM
    outputs_main = []
    outputs_grad = []
    totals = None
    for micro_index in range(MICRO):
        row_start = micro_index * micro_rows
        rows_in = tokens[row_start : row_start + micro_rows]
        starts_in = doc_starts[row_start : row_start + micro_rows]
        cot_in = cotangent[row_start : row_start + micro_rows].reshape(-1, model_width)
        (
            full_query,
            full_key,
            full_value,
            full_gate,
            full_up,
            full_output,
            full_down,
            gain_one,
            gain_two,
        ) = (
            lax.all_gather(query_weight, ("dp", "seq"), axis=0, tiled=True),
            lax.all_gather(key_weight, ("dp", "seq"), axis=0, tiled=True),
            lax.all_gather(value_weight, ("dp", "seq"), axis=0, tiled=True),
            lax.all_gather(gate_weight, ("dp", "seq"), axis=0, tiled=True),
            lax.all_gather(up_weight, ("dp", "seq"), axis=0, tiled=True),
            lax.all_gather(output_weight, ("dp", "seq"), axis=1, tiled=True),
            lax.all_gather(down_weight, ("dp", "seq"), axis=1, tiled=True),
            lax.all_gather(attn_gain, ("dp", "seq"), axis=0, tiled=True),
            lax.all_gather(mlp_gain, ("dp", "seq"), axis=0, tiled=True),
        )
        gain_one_f = gain_one.astype(jnp.float32)
        gain_two_f = gain_two.astype(jnp.float32)
        flat_rows = rows_in.reshape(-1, model_width).astype(jnp.float32)
        scale_one = inverse_rms(flat_rows)
        normed_one = (flat_rows * scale_one * gain_one_f).astype(jnp.bfloat16)
        query_low = jnp.dot(normed_one, full_query, preferred_element_type=jnp.float32).astype(
            jnp.bfloat16
        )
        key_low = jnp.dot(normed_one, full_key, preferred_element_type=jnp.float32).astype(
            jnp.bfloat16
        )
        value_low = jnp.dot(normed_one, full_value, preferred_element_type=jnp.float32).astype(
            jnp.bfloat16
        )
        queries = query_low.astype(jnp.float32).reshape(micro_rows, span_len, head_count, FDIM)
        key_rows = key_low.astype(jnp.float32).reshape(micro_rows, span_len, head_count, FDIM)
        values = value_low.astype(jnp.float32).reshape(micro_rows, span_len, head_count, VHEAD)
        segments = jnp.cumsum(starts_in, axis=1)
        reset_flag = (segments[:, -1] > 0).astype(jnp.float32)
        (tail_state, tail_norm), tail_pull = jax.vjp(
            partial(tail_span, segments=segments), key_rows, values
        )
        state_in, norm_in, reset_in = prefix(
            (tail_state, tail_norm, reset_flag),
            "seq",
            combine_carry,
            (jnp.zeros_like(tail_state), jnp.zeros_like(tail_norm), jnp.zeros_like(reset_flag)),
            False,
        )
        mixed_heads, mix_pull = jax.vjp(
            partial(mix_span, segments=segments), queries, key_rows, values, state_in, norm_in
        )
        mixed_low = mixed_heads.reshape(-1, head_count * VHEAD).astype(jnp.bfloat16)
        branch_one = jnp.dot(mixed_low, full_output, preferred_element_type=jnp.float32)
        residual = flat_rows + lax.psum(branch_one, "tensor")
        scale_two = inverse_rms(residual)
        normed_two = (residual * scale_two * gain_two_f).astype(jnp.bfloat16)
        gate_proj = jnp.dot(normed_two, full_gate, preferred_element_type=jnp.float32)
        up_proj = jnp.dot(normed_two, full_up, preferred_element_type=jnp.float32)
        sigmoid_gate = jax.nn.sigmoid(gate_proj)
        hidden = (gate_proj * sigmoid_gate * up_proj).astype(jnp.bfloat16)
        branch_two = jnp.dot(hidden, full_down, preferred_element_type=jnp.float32)
        block_low = (
            residual + lax.psum(branch_two.astype(jnp.bfloat16), "tensor").astype(jnp.float32)
        ).astype(jnp.bfloat16)
        outputs_main.append(block_low.reshape(micro_rows, span_len, model_width))
        grad_down = inner_rows(hidden, cot_in)
        grad_hidden = by_transpose(cot_in, full_down)
        grad_gate_low = (
            grad_hidden * up_proj * sigmoid_gate * (1.0 + gate_proj * (1.0 - sigmoid_gate))
        ).astype(jnp.bfloat16)
        grad_up_low = (grad_hidden * gate_proj * sigmoid_gate).astype(jnp.bfloat16)
        grad_gate = inner_rows(normed_two, grad_gate_low)
        grad_up = inner_rows(normed_two, grad_up_low)
        grad_normed_two = by_transpose(grad_gate_low, full_gate) + by_transpose(
            grad_up_low, full_up
        )
        grad_normed_two = lax.psum(grad_normed_two, "tensor")
        grad_resid, grad_gain_two = norm_backward(residual, scale_two, gain_two_f, grad_normed_two)
        grad_resid = grad_resid + cot_in.astype(jnp.float32)
        grad_resid_low = grad_resid.astype(jnp.bfloat16)
        grad_output = inner_rows(mixed_low, grad_resid_low)
        grad_mixed = by_transpose(grad_resid_low, full_output).astype(jnp.bfloat16)
        grad_mixed = (
            lax.optimization_barrier(grad_mixed)
            .astype(jnp.float32)
            .reshape(micro_rows, span_len, head_count, VHEAD)
        )
        grad_queries, grad_keys, grad_values, grad_state, grad_norm = mix_pull(grad_mixed)
        carried_state, carried_norm, reset_out = prefix(
            (grad_state, grad_norm, reset_flag),
            "seq",
            combine_carry,
            (jnp.zeros_like(grad_state), jnp.zeros_like(grad_norm), jnp.zeros_like(reset_flag)),
            True,
        )
        more_keys, more_values = tail_pull((carried_state, carried_norm))
        grad_query_low = grad_queries.reshape(-1, head_count * FDIM).astype(jnp.bfloat16)
        grad_key_low = (grad_keys + more_keys).reshape(-1, head_count * FDIM).astype(jnp.bfloat16)
        grad_value_low = (
            (grad_values + more_values).reshape(-1, head_count * VHEAD).astype(jnp.bfloat16)
        )
        grad_query = inner_rows(normed_one, grad_query_low)
        grad_key = inner_rows(normed_one, grad_key_low)
        grad_value = inner_rows(normed_one, grad_value_low)
        grad_normed_one = (
            by_transpose(grad_query_low, full_query)
            + by_transpose(grad_key_low, full_key)
            + by_transpose(grad_value_low, full_value)
        )
        grad_normed_one = lax.psum(grad_normed_one, "tensor")
        grad_inputs, grad_gain_one = norm_backward(
            flat_rows, scale_one, gain_one_f, grad_normed_one
        )
        outputs_grad.append((grad_resid + grad_inputs).reshape(micro_rows, span_len, model_width))
        shares = (
            grad_query,
            grad_key,
            grad_value,
            grad_gate,
            grad_up,
            grad_output,
            grad_down,
            grad_gain_one,
            grad_gain_two,
        )
        if totals is None:
            totals = shares
        else:
            totals = jax.tree.map(jnp.add, totals, shares)
    totals = (
        lax.psum_scatter(totals[0], ("dp", "seq"), scatter_dimension=0, tiled=True),
        lax.psum_scatter(totals[1], ("dp", "seq"), scatter_dimension=0, tiled=True),
        lax.psum_scatter(totals[2], ("dp", "seq"), scatter_dimension=0, tiled=True),
        lax.psum_scatter(totals[3], ("dp", "seq"), scatter_dimension=0, tiled=True),
        lax.psum_scatter(totals[4], ("dp", "seq"), scatter_dimension=0, tiled=True),
        lax.psum_scatter(totals[5], ("dp", "seq"), scatter_dimension=1, tiled=True),
        lax.psum_scatter(totals[6], ("dp", "seq"), scatter_dimension=1, tiled=True),
        lax.psum_scatter(totals[7], ("dp", "seq"), scatter_dimension=0, tiled=True),
        lax.psum_scatter(totals[8], ("dp", "seq"), scatter_dimension=0, tiled=True),
    )
    return (
        jnp.concatenate(outputs_main, axis=0),
        jnp.concatenate(outputs_grad, axis=0),
        totals[7],
        totals[8],
        totals[0],
        totals[1],
        totals[2],
        totals[5],
        totals[3],
        totals[4],
        totals[6],
    )


MESH_ID = pl.DeviceIdType.MESH
VMEM_LIMIT = 58 << 20
LANES = 128
ROW_STEP = 32


def nt_dot(a, b):
    return lax.dot_general(a, b, (((1,), (1,)), ((), ())), preferred_element_type=jnp.float32)


def tn_dot(a, b):
    return lax.dot_general(a, b, (((0,), (0,)), ((), ())), preferred_element_type=jnp.float32)


def nn_dot(a, b):
    return lax.dot_general(a, b, (((1,), (0,)), ((), ())), preferred_element_type=jnp.float32)


def plane_places():
    at, core = lax.axis_index("dp"), lax.axis_index("tensor")
    x_bit, y_bit = lax.rem(at, 2), at // 2
    return (
        at,
        y_bit * 2 + (1 - x_bit),
        (1 - y_bit) * 2 + x_bit,
        (1 - y_bit) * 2 + (1 - x_bit),
        core,
    )


def greet(places):
    barrier = pltpu.get_barrier_semaphore()
    for place in places:
        pl.semaphore_signal(barrier, inc=1, device_id=place, device_id_type=MESH_ID)
    pl.semaphore_wait(barrier, len(places))


class Sender:
    def __init__(self, sems):
        self.sems, self.used = sems, 0

    def __call__(self, src, dst, place):
        index = self.used
        self.used += 1
        return pltpu.make_async_remote_copy(
            src_ref=src,
            dst_ref=dst,
            send_sem=self.sems.at[0, index],
            recv_sem=self.sems.at[1, index],
            device_id=place,
            device_id_type=MESH_ID,
        )


def greet_plane():
    at, x_at, y_at, _, core = plane_places()
    greet([{"dp": x_at}, {"dp": y_at}, {"tensor": 1 - core}])


def add_rows(dst, *srcs, step=64):
    def body(i, carry):
        r = pl.ds(pl.multiple_of(i * step, step), step)
        total = srcs[0][r].astype(jnp.float32)
        for s in srcs[1:]:
            total = total + s[r].astype(jnp.float32)
        dst[r] = total.astype(dst.dtype)
        return carry

    lax.fori_loop(0, srcs[0].shape[0] // step, body, 0)


GATHER_COPIES = 13
SCATTER_COPIES = 10


def gather_steps(own_ref, out_ref, copy, local_sem):
    at, x_at, y_at, d_at, core = plane_places()
    half = own_ref.shape[0] // 2
    xp, yp, sp = {"dp": x_at}, {"dp": y_at}, {"tensor": 1 - core}
    lo, hi = pl.ds(0, half), pl.ds(half, half)
    mine = out_ref.at[at, core]
    x_lo = copy(own_ref.at[lo], mine.at[lo], xp)
    y_hi = copy(own_ref.at[hi], mine.at[hi], yp)
    x_hi = copy(own_ref.at[hi], mine.at[hi], xp)
    y_lo = copy(own_ref.at[lo], mine.at[lo], yp)
    pair = copy(own_ref, mine, sp)
    for c in (x_lo, y_hi, x_hi, y_lo, pair):
        c.start()
    local_copy = pltpu.make_async_copy(own_ref, mine, local_sem)
    local_copy.start()
    from_x, from_y, from_d = out_ref.at[x_at, core], out_ref.at[y_at, core], out_ref.at[d_at, core]
    on_y = copy(from_x.at[lo], from_x.at[lo], yp)
    on_x = copy(from_y.at[hi], from_y.at[hi], xp)
    handed = [
        copy(block.at[rows], block.at[rows], sp)
        for block, rows in (
            (from_x, lo),
            (from_y, hi),
            (from_x, hi),
            (from_y, lo),
            (from_d, lo),
            (from_d, hi),
        )
    ]
    yield
    local_copy.wait()
    yield
    pair.wait_recv()
    yield
    x_lo.wait_recv()
    on_y.start()
    handed[0].start()
    y_hi.wait_recv()
    on_x.start()
    handed[1].start()
    yield
    handed[0].wait_recv()
    handed[1].wait_recv()
    yield
    x_hi.wait_recv()
    handed[2].start()
    y_lo.wait_recv()
    handed[3].start()
    yield
    handed[2].wait_recv()
    handed[3].wait_recv()
    yield
    on_y.wait_recv()
    handed[4].start()
    on_x.wait_recv()
    handed[5].start()
    yield
    handed[4].wait_recv()
    handed[5].wait_recv()
    yield
    for c in [x_lo, y_hi, x_hi, y_lo, on_y, on_x, pair] + handed:
        c.wait_send()


def scatter_steps(part_ref, out_ref, pair_ref, sum_ref, got_ref, copy, held=None):
    at, x_at, y_at, d_at, core = plane_places()
    half = part_ref.shape[2] // 2
    xp, yp, sp = {"dp": x_at}, {"dp": y_at}, {"tensor": 1 - core}
    lo, hi = pl.ds(0, half), pl.ds(half, half)
    order = (d_at, x_at, y_at, at)
    pairs = [copy(part_ref.at[to, 1 - core], pair_ref.at[j], sp) for j, to in enumerate(order)]
    for c in pairs:
        c.start()
    own = [part_ref.at[to, core] for to in order]
    fetched = []
    if held is not None:
        buffer, held_sems = held
        fetched = [
            pltpu.make_async_copy(o, buffer.at[j], held_sems.at[j]) for j, o in enumerate(own)
        ]
        own = [buffer.at[j] for j in range(4)]
        for c in fetched:
            c.start()
    yield

    def ready(j):
        if fetched:
            fetched[j].wait()
        pairs[j].wait_recv()

    def total(j, rows, *more):
        add_rows(sum_ref.at[j, rows], own[j].at[rows], pair_ref.at[j, rows], *more)

    def sent(j, rows, place):
        return copy(sum_ref.at[j, rows], got_ref.at[j, rows], place)

    d_lo, d_hi = sent(0, lo, xp), sent(0, hi, yp)
    x_lo, y_hi, x_hi, y_lo = sent(1, lo, xp), sent(2, hi, yp), sent(1, hi, xp), sent(2, lo, yp)
    ready(0)
    total(0, lo)
    d_lo.start()
    total(0, hi)
    d_hi.start()
    ready(1)
    total(1, lo)
    x_lo.start()
    ready(2)
    total(2, hi)
    y_hi.start()
    yield
    d_lo.wait_recv()
    total(2, lo, got_ref.at[0, lo])
    y_lo.start()
    d_hi.wait_recv()
    total(1, hi, got_ref.at[0, hi])
    x_hi.start()
    yield
    ready(3)
    for c in (x_lo, y_hi, y_lo, x_hi):
        c.wait_recv()
    add_rows(out_ref, own[3], pair_ref.at[3], got_ref.at[1], got_ref.at[2])
    for c in pairs + [d_lo, d_hi, x_lo, y_hi, x_hi, y_lo]:
        c.wait_send()


def swap_shards(ins, outs, peers, me, take, put, copy, local_sems):
    started = [
        copy(take(i, p), put(o, me), {"dp": p}) for i, o in zip(ins, outs) for p in peers
    ]
    started += [
        pltpu.make_async_copy(take(i, me), put(o, me), local_sems.at[n])
        for n, (i, o) in enumerate(zip(ins, outs))
    ]
    for c in started:
        c.start()
    return started


def exchange_kernel(take, put, count, *refs):
    ins, outs, sems, local_sems = refs[:count], refs[count : 2 * count], refs[-2], refs[-1]
    size, me = lax.axis_size("dp"), lax.axis_index("dp")
    peers = [lax.rem(me + k, size) for k in range(1, size)]
    greet([{"dp": p} for p in peers])
    for c in swap_shards(ins, outs, peers, me, take, put, Sender(sems), local_sems):
        c.wait()


def block_of(ref, index):
    return ref.at[index]


def columns_of(ref, index):
    width = ref.shape[1] // lax.axis_size("dp")
    return ref.at[:, pl.ds(pl.multiple_of(index * width, width), width)]


def exchange(arrays, cid, shapes, take=block_of, put=block_of):
    count, peers = len(arrays), lax.axis_size("dp") - 1
    anywhere = [pl.BlockSpec(memory_space=pl.ANY)] * count
    return pl.pallas_call(
        partial(exchange_kernel, take, put, count),
        name="exchange",
        out_shape=[jax.ShapeDtypeStruct(s, x.dtype) for s, x in zip(shapes, arrays)],
        in_specs=anywhere,
        out_specs=anywhere,
        scratch_shapes=[
            pltpu.SemaphoreType.DMA((2, count * peers)),
            pltpu.SemaphoreType.DMA((count,)),
        ],
        compiler_params=pltpu.CompilerParams(collective_id=cid, has_side_effects=True),
        cost_estimate=pl.CostEstimate(
            flops=0, bytes_accessed=60 * sum(x.size for x in arrays), transcendentals=0
        ),
    )(*arrays)


def first_kernel(pack_ref, small_ref, out_ref, all_ref, sems, small_sems, local_sems):
    plane, span = lax.axis_size("dp"), lax.axis_size("seq")
    at, z = lax.axis_index("dp"), lax.axis_index("seq")
    places = [
        {"dp": lax.rem(at + i, plane), "seq": lax.rem(z + k, span)}
        for k in range(span)
        for i in range(plane)
        if i or k
    ]
    greet(places)
    copy, copy_small = Sender(sems), Sender(small_sems)
    block = all_ref.at[z * plane + at]
    copies = [copy_small(small_ref, block, p) for p in places]
    for i in range(1, plane):
        to = lax.rem(at + i, plane)
        copies.append(copy(pack_ref.at[to], columns_of(out_ref, at), {"dp": to}))
    copies.append(pltpu.make_async_copy(small_ref, block, local_sems.at[0]))
    copies.append(
        pltpu.make_async_copy(pack_ref.at[at], columns_of(out_ref, at), local_sems.at[1])
    )
    for c in copies:
        c.start()
    for c in copies:
        c.wait()


def first_exchange(pack, small, cid):
    plane, span = lax.axis_size("dp"), lax.axis_size("seq")
    _, size, chunk = pack.shape
    anywhere = pl.BlockSpec(memory_space=pl.ANY)
    whole = pl.BlockSpec(memory_space=pltpu.VMEM)
    return pl.pallas_call(
        first_kernel,
        name="first_exchange",
        out_shape=[
            jax.ShapeDtypeStruct((size, plane * chunk), pack.dtype),
            jax.ShapeDtypeStruct((span * plane,) + small.shape, small.dtype),
        ],
        in_specs=[anywhere, whole],
        out_specs=[anywhere, whole],
        scratch_shapes=[
            pltpu.SemaphoreType.DMA((2, plane - 1)),
            pltpu.SemaphoreType.DMA((2, plane * span - 1)),
            pltpu.SemaphoreType.DMA((2,)),
        ],
        compiler_params=pltpu.CompilerParams(collective_id=cid, has_side_effects=True),
        cost_estimate=pl.CostEstimate(
            flops=0, bytes_accessed=60 * pack.size, transcendentals=0
        ),
    )(pack, small)


def run(*steps):
    for g in steps:
        for _ in g:
            pass


def row_blocks(rows, step, body):
    def inner(i, carry):
        return body(pl.ds(pl.multiple_of(i * step, step), step), carry)

    return lambda init: lax.fori_loop(0, rows // step, inner, init)


def lanes(k):
    return pl.ds(k * LANES, LANES)


def seq_major_block(k):
    plane, span = lax.axis_size("dp"), lax.axis_size("seq")
    s, g = divmod(k, plane)
    return g * span + s


def mean_of(acc, width):
    return jnp.sum(acc, axis=1, keepdims=True) * (1.0 / width)


def kernel_call(body, name, cid, outs, ins, scratch, flops=0, moved=0):
    params = dict(has_side_effects=True, vmem_limit_bytes=VMEM_LIMIT)
    return pl.pallas_call(
        body,
        name=name,
        out_shape=[jax.ShapeDtypeStruct(s, d) for s, d, _ in outs],
        in_specs=[pl.BlockSpec(memory_space=m) for _, m in ins],
        out_specs=[pl.BlockSpec(memory_space=m) for _, _, m in outs],
        scratch_shapes=scratch,
        compiler_params=pltpu.CompilerParams(collective_id=cid, **params),
        cost_estimate=pl.CostEstimate(flops=flops, bytes_accessed=moved, transcendentals=0),
    )(*[a for a, _ in ins])


def copies(count):
    return pltpu.SemaphoreType.DMA((2, count))


def entry_kernel(
    tokens_ref, cot_ref, small_ref, all_ref, x_ref, cot_own_ref, normed_ref, sems, local_sem
):
    greet_plane()
    core = lax.axis_index("tensor")
    m, width = x_ref.shape
    blocks = width // LANES

    def body(r, carry):
        acc = jnp.zeros((ROW_STEP, LANES), jnp.float32)
        for k in range(blocks):
            source = lanes(seq_major_block(k))
            v = tokens_ref[core, r, source]
            x_ref[r, lanes(k)] = v
            cot_own_ref[r, lanes(k)] = cot_ref[core, r, source]
            v = v.astype(jnp.float32)
            acc += v * v
        scale = lax.rsqrt(mean_of(acc, width) + norm_epsilon)
        for k in range(blocks):
            v = x_ref[r, lanes(k)].astype(jnp.float32)
            normed_ref[r, lanes(k)] = (v * scale * small_ref[k, 0:1, :]).astype(jnp.bfloat16)
        return carry

    row_blocks(m, ROW_STEP, body)(0)
    run(gather_steps(normed_ref, all_ref, Sender(sems), local_sem))


def entry(tokens, cot, small, cid):
    cores, m, width = tokens.shape
    whole = pltpu.VMEM
    gathered, x, cot_own = kernel_call(
        entry_kernel,
        "entry",
        cid,
        [
            ((4, cores, m, width), jnp.bfloat16, pl.ANY),
            ((m, width), jnp.bfloat16, whole),
            ((m, width), jnp.bfloat16, whole),
        ],
        [(tokens, whole), (cot, whole), (small, whole)],
        [pltpu.VMEM((m, width), jnp.bfloat16), copies(GATHER_COPIES), pltpu.SemaphoreType.DMA],
        moved=tokens.size * 40,
    )
    return gathered.reshape(-1, width), x, cot_own


FEATURES = 256
STATE_ROWS = 160
CHUNKS = 4


def feature_pairs():
    first = np.full(FEATURES, -4096, np.int32)
    second = np.full(FEATURES, -4096, np.int32)
    pairs = [(i, j) for i in range(FDIM + 1) for j in range(i, FDIM + 1)]
    for f, (i, j) in enumerate(pairs):
        first[f], second[f] = i, j
    return jnp.asarray(np.stack([first, second] + [first] * 6))


def feature_scale(pairs_ref):
    i, j = pairs_ref[0:1, :], pairs_ref[1:2, :]
    square = jnp.where(i == j, 1.0 / 32.0, 1.0 / 16.0)
    return jnp.where(j == FDIM, jnp.where(i == FDIM, 1.0, 0.25), square)


def fill_selectors(pairs_ref, pick_ref, qcols):
    kinds, heads = pick_ref.shape[:2]
    lane = lax.broadcasted_iota(jnp.int32, (LANES, FEATURES), 0)
    for kind in range(kinds):
        for h in range(heads):
            for side in range(2):
                index = pairs_ref[side : side + 1, :]
                source = jnp.where(
                    index == FDIM, 2 * qcols, index + (kind * qcols + h * FDIM)
                )
                pick_ref[kind, h, side] = jnp.where(lane == source, 1.0, 0.0).astype(jnp.bfloat16)


def factors(tile, pick_ref, kind, h):
    return nn_dot(tile, pick_ref[kind, h, 0]), nn_dot(tile, pick_ref[kind, h, 1])


def keys_in_place(tile, qcols):
    return pltpu.roll(tile.astype(jnp.float32), LANES - qcols, axis=1).astype(jnp.bfloat16)


def head_mask(rows, head):
    lane = lax.broadcasted_iota(jnp.int32, (rows, LANES), 1)
    return (lane >= head * FDIM) & (lane < (head + 1) * FDIM)


def masked_weights(query, key, column, row):
    length = query.shape[0]
    a = nt_dot(query, key) * 0.25
    t = lax.broadcasted_iota(jnp.int32, (length, length), 0)
    s = lax.broadcasted_iota(jnp.int32, (length, length), 1)
    keep = (s <= t) & (column == row)
    return a, jnp.where(keep, 1.0 + a + 0.5 * a * a, 0.0), keep


class Segments:
    def __init__(self, col_ref, row_ref, b):
        self.column, self.row = col_ref[b], row_ref[b]
        last = self.row[:, -1:]
        self.head = self.column == 0.0
        self.tail = self.column == last
        self.keep = jnp.where(last == 0.0, 1.0, 0.0)


def pass_states(state_ref, sums_ref, own_ref, own_sums_ref, out_ref, out_sums_ref, col_row, chunk):
    col_ref, row_ref = col_row
    rows, heads = state_ref.shape[0] // CHUNKS, state_ref.shape[1]
    for n in range(rows):
        b = chunk * rows + n
        keep = Segments(col_ref, row_ref, b).keep
        for h in range(heads):
            out_ref[b, h] = (own_ref[b, h] + keep * state_ref[b, h].astype(jnp.float32)).astype(
                jnp.bfloat16
            )
        out_sums_ref[b] = own_sums_ref[b] + keep * sums_ref[b]


class Chain:
    def __init__(self, forward, state_ref, sums_ref, out_ref, out_sums_ref, copy):
        span, z = lax.axis_size("seq"), lax.axis_index("seq")
        to = lax.rem(z + (1 if forward else span - 1), span)
        self.gets = z > 0 if forward else z < span - 1
        self.gives = z < span - 1 if forward else z > 0
        rows = state_ref.shape[0] // CHUNKS
        self.moves = []
        for g in range(CHUNKS):
            part = pl.ds(g * rows, rows)
            used = pl.ds(0, STATE_ROWS)
            self.moves.append(
                (
                    copy(
                        out_ref.at[part, :, used], state_ref.at[part, :, used], {"seq": to}
                    ),
                    copy(out_sums_ref.at[part], sums_ref.at[part], {"seq": to}),
                )
            )

    def get(self, g):
        @pl.when(self.gets)
        def _():
            for c in self.moves[g]:
                c.wait_recv()

    def give(self, g):
        @pl.when(self.gives)
        def _():
            for c in self.moves[g]:
                c.start()

    def close(self):
        @pl.when(self.gives)
        def _():
            for move in self.moves:
                for c in move:
                    c.wait_send()


def mix_kernel(
    heads,
    normed_ref,
    pack_ref,
    col_ref,
    row_ref,
    pairs_ref,
    cot_ref,
    up_ref,
    down_ref,
    qkv_ref,
    mixed_ref,
    exact_ref,
    den_ref,
    state_ref,
    sums_ref,
    cot_all_ref,
    up_all_ref,
    down_all_ref,
    pick_ref,
    own_ref,
    own_sums_ref,
    out_ref,
    out_sums_ref,
    sems,
    cot_sems,
    local_sem,
    shard_sems,
    shard_local_sems,
):
    parts, _, depth = pack_ref.shape
    rows, length = col_ref.shape[0], col_ref.shape[1]
    vcols, qcols = heads * VHEAD, heads * FDIM
    at, x_at, y_at, _, core = plane_places()
    plane, span, z = lax.axis_size("dp"), lax.axis_size("seq"), lax.axis_index("seq")
    chips = [lax.rem(at + k, plane) for k in range(1, plane)]
    state_ref[...] = jnp.zeros_like(state_ref)
    sums_ref[...] = jnp.zeros_like(sums_ref)
    greet(
        [{"dp": p} for p in chips]
        + [{"tensor": 1 - core}]
        + [{"seq": lax.rem(z + k, span)} for k in (1, span - 1)]
    )
    gather = gather_steps(cot_ref, cot_all_ref, Sender(cot_sems), local_sem)
    next(gather)
    shards = swap_shards(
        (up_ref, down_ref),
        (up_all_ref, down_all_ref),
        chips,
        at,
        block_of,
        columns_of,
        Sender(shard_sems),
        shard_local_sems,
    )
    chain = Chain(True, state_ref, sums_ref, out_ref, out_sums_ref, Sender(sems))
    fill_selectors(pairs_ref, pick_ref, qcols)
    scale = feature_scale(pairs_ref)

    def tokens_of(b):
        return pl.ds(pl.multiple_of(b * length, length), length)

    def first(b, carry):
        t = tokens_of(b)
        value = jnp.zeros((length, vcols), jnp.float32)
        tile = jnp.zeros((length, LANES), jnp.float32)
        for s in range(parts):
            piece = normed_ref[t, pl.ds(s * depth, depth)]
            value += nt_dot(piece, pack_ref[s, pl.ds(0, vcols)])
            tile += nt_dot(piece, pack_ref[s, pl.ds(vcols, LANES)])
        lane = lax.broadcasted_iota(jnp.int32, (length, LANES), 1)
        tile = jnp.where(lane < 2 * qcols, tile, jnp.where(lane == 2 * qcols, 1.0, 0.0))
        value, tile = value.astype(jnp.bfloat16), tile.astype(jnp.bfloat16)
        qkv_ref[t, pl.ds(0, vcols)] = value
        qkv_ref[t, pl.ds(vcols, LANES)] = tile
        tail = Segments(col_ref, row_ref, b).tail
        for h in range(heads):
            one, two = factors(tile, pick_ref, 1, h)
            lifted = jnp.where(tail, one * two * scale, 0.0)
            own_ref[b, h] = tn_dot(
                lifted.astype(jnp.bfloat16), value[:, h * VHEAD : (h + 1) * VHEAD]
            )
            own_sums_ref[b, h : h + 1] = jnp.sum(lifted, axis=0, keepdims=True)
        return carry

    own_sums_ref[...] = jnp.zeros_like(own_sums_ref)
    lax.fori_loop(0, rows, first, 0)

    def mixer(b, carry):
        t = tokens_of(b)
        seg = Segments(col_ref, row_ref, b)
        tile = qkv_ref[t, pl.ds(vcols, LANES)]
        key = keys_in_place(tile, qcols)
        lane = lax.broadcasted_iota(jnp.int32, (length, LANES), 1)
        dens = jnp.zeros((length, LANES), jnp.float32)
        for h in range(heads):
            v = pl.ds(h * VHEAD, VHEAD)
            query = jnp.where(head_mask(length, h), tile, jnp.zeros_like(tile))
            _, w, _ = masked_weights(query, key, seg.column, seg.row)
            one, two = factors(tile, pick_ref, 0, h)
            lifted = jnp.where(seg.head, one * two, 0.0)
            num = nn_dot(w.astype(jnp.bfloat16), qkv_ref[t, v])
            num += nn_dot(lifted.astype(jnp.bfloat16), state_ref[b, h])
            den = jnp.sum(w, axis=1, keepdims=True)
            den += jnp.sum(lifted * sums_ref[b, h : h + 1], axis=1, keepdims=True)
            value = num / den
            exact_ref[t, v] = value
            mixed_ref[t, v] = value.astype(jnp.bfloat16)
            dens = jnp.where(lane == h, den, dens)
        den_ref[t] = dens
        return carry

    each = rows // CHUNKS
    for g in range(CHUNKS):
        chain.get(g)
        pass_states(
            state_ref, sums_ref, own_ref, own_sums_ref, out_ref, out_sums_ref, (col_ref, row_ref), g
        )
        chain.give(g)
        if g == 0:
            next(gather)
            next(gather)
            next(gather)
        lax.fori_loop(g * each, (g + 1) * each, mixer, 0)
    run(gather)
    for c in shards:
        c.wait()
    chain.close()


def state_scratch(rows, heads):
    return [
        pltpu.VMEM((2, heads, 2, LANES, FEATURES), jnp.bfloat16),
        pltpu.VMEM((rows, heads, FEATURES, VHEAD), jnp.float32),
        pltpu.VMEM((rows, 8, FEATURES), jnp.float32),
        pltpu.VMEM((rows, heads, FEATURES, VHEAD), jnp.bfloat16),
        pltpu.VMEM((rows, 8, FEATURES), jnp.float32),
    ]


def mix(normed, pack, seg_col, seg_row, pairs, cot_own, up, down, heads, cid):
    tokens = normed.shape[0]
    rows = seg_col.shape[0]
    vcols = heads * VHEAD
    m, width = cot_own.shape
    plane, size, chunk = up.shape
    whole = pltpu.VMEM
    out = kernel_call(
        partial(mix_kernel, heads),
        "mix",
        cid,
        [
            ((tokens, vcols + LANES), jnp.bfloat16, whole),
            ((tokens, vcols), jnp.bfloat16, whole),
            ((tokens, vcols), jnp.float32, whole),
            ((tokens, LANES), jnp.float32, whole),
            ((rows, heads, FEATURES, VHEAD), jnp.bfloat16, whole),
            ((rows, 8, FEATURES), jnp.float32, whole),
            ((4, 2, m, width), jnp.bfloat16, pl.ANY),
            ((size, plane * chunk), jnp.bfloat16, pl.ANY),
            ((size, plane * chunk), jnp.bfloat16, pl.ANY),
        ],
        [(a, whole) for a in (normed, pack, seg_col, seg_row, pairs, cot_own)]
        + [(up, pl.ANY), (down, pl.ANY)],
        state_scratch(rows, heads)
        + [
            copies(2 * CHUNKS),
            copies(GATHER_COPIES),
            pltpu.SemaphoreType.DMA,
            copies(2 * (plane - 1)),
            pltpu.SemaphoreType.DMA((2,)),
        ],
        moved=normed.size * 30,
    )
    qkv, mixed, exact, den, state, sums, cot, up, down = out
    return (qkv, mixed, exact, den, state, sums), cot.reshape(-1, width), up, down


def branch_kernel(
    mixed_ref,
    pack_ref,
    x_ref,
    small_ref,
    residual_ref,
    normed_ref,
    part_ref,
    pair_ref,
    sum_ref,
    got_ref,
    sems,
):
    greet_plane()
    parts, _, depth = pack_ref.shape
    m, width = x_ref.shape
    vcols = mixed_ref.shape[1]
    first = pack_ref.shape[1] - vcols

    def project(b, carry):
        left = mixed_ref[pl.ds(pl.multiple_of(b * m, m), m)]
        for s in range(parts):
            part_ref[b // 2, lax.rem(b, 2), :, pl.ds(s * depth, depth)] = nn_dot(
                left, pack_ref[s, pl.ds(first, vcols)]
            ).astype(jnp.bfloat16)
        return carry

    lax.fori_loop(0, 8, project, 0)
    run(scatter_steps(part_ref, residual_ref, pair_ref, sum_ref, got_ref, Sender(sems)))

    def body(r, carry):
        acc = jnp.zeros((ROW_STEP, LANES), jnp.float32)
        for k in range(width // LANES):
            v = residual_ref[r, lanes(k)] + x_ref[r, lanes(k)].astype(jnp.float32)
            residual_ref[r, lanes(k)] = v
            acc += v * v
        scale = lax.rsqrt(mean_of(acc, width) + norm_epsilon)
        for k in range(width // LANES):
            normed_ref[r, lanes(k)] = (
                residual_ref[r, lanes(k)] * scale * small_ref[k, 1:2, :]
            ).astype(jnp.bfloat16)
        return carry

    row_blocks(m, ROW_STEP, body)(0)


def scatter_scratch(m, width):
    return [
        pltpu.VMEM((4, m, width), jnp.bfloat16),
        pltpu.VMEM((3, m, width), jnp.bfloat16),
        pltpu.VMEM((3, m, width), jnp.bfloat16),
    ]


def branch(mixed, pack, x, small, cid):
    m, width = x.shape
    whole = pltpu.VMEM
    return kernel_call(
        branch_kernel,
        "branch",
        cid,
        [((m, width), jnp.float32, whole), ((m, width), jnp.bfloat16, whole)],
        [(mixed, whole), (pack, whole), (x, whole), (small, whole)],
        [pltpu.VMEM((4, 2, m, width), jnp.bfloat16)]
        + scatter_scratch(m, width)
        + [copies(SCATTER_COPIES)],
        moved=x.size * 80,
    )


def parity(i):
    return i % 2 if isinstance(i, int) else lax.rem(i, 2)


def choose(test, a, b):
    if isinstance(test, bool):
        return a if test else b
    return jnp.where(test, a, b)


def project(at, w_ref):
    parts, _, depth = w_ref.shape
    total = nt_dot(at(pl.ds(0, depth)), w_ref[0])
    for s in range(1, parts):
        total += nt_dot(at(pl.ds(s * depth, depth)), w_ref[s])
    return total


def expand_kernel(
    own_ref,
    gate_w_hbm,
    up_w_hbm,
    normed_hbm,
    gate_hbm,
    up_hbm,
    normed_ref,
    gate_w_ref,
    up_w_ref,
    gate_ref,
    up_ref,
    sems,
    local_sem,
    w_sems,
    store_sems,
    keep_sem,
):
    greet_plane()
    at, x_at, y_at, d_at, core = plane_places()
    half = own_ref.shape[0] // 2
    gather = gather_steps(own_ref, normed_ref, Sender(sems), local_sem)
    next(gather)
    weights = [
        pltpu.make_async_copy(gate_w_hbm, gate_w_ref, w_sems.at[0]),
        pltpu.make_async_copy(up_w_hbm, up_w_ref, w_sems.at[1]),
    ]
    for c in weights:
        c.start()

    def halves(i):
        k = choose(parity(i) == 0, core, 1 - core)
        one = choose(i < 2, at, choose(i < 6, x_at, d_at))
        two = choose(i < 2, at, choose(i < 6, y_at, d_at))
        late = (i >= 4) & (i < 6)
        late = int(late) if isinstance(late, bool) else late.astype(jnp.int32)
        first, second = late * half, (1 - late) * half
        if not isinstance(i, int):
            first, second = pl.multiple_of(first, half), pl.multiple_of(second, half)
        return (one, k, first), (two, k, second)

    def store_copies(i):
        slot = parity(i)
        found = []
        for n, (c, k, r) in enumerate(halves(i)):
            rows = pl.ds(n * half, half)
            for q, (a, b) in enumerate(((gate_ref, gate_hbm), (up_ref, up_hbm))):
                found.append(
                    pltpu.make_async_copy(
                        a.at[slot, rows], b.at[c, k, pl.ds(r, half)], store_sems.at[slot, 2 * n + q]
                    )
                )
        return found

    next(gather)
    for c in weights:
        c.wait()

    def body(i, carry):
        for step in range(1, 8):

            @pl.when(i == step)
            def _():
                next(gather)

        @pl.when(i >= 2)
        def _():
            for c in store_copies(i - 2):
                c.wait()

        slot = parity(i)
        pieces = halves(i)

        def columns(cols):
            return jnp.concatenate([normed_ref[c, k, pl.ds(r, half), cols] for c, k, r in pieces])

        gate_ref[slot] = project(columns, gate_w_ref)
        up_ref[slot] = project(columns, up_w_ref)
        for c in store_copies(i):
            c.start()
        return carry

    lax.fori_loop(0, 8, body, 0)
    keep = pltpu.make_async_copy(normed_ref, normed_hbm, keep_sem)
    keep.start()
    for i in (6, 7):
        for c in store_copies(i):
            c.wait()
    keep.wait()
    run(gather)


def expand(own, gate_w, up_w, cid):
    m, width = own.shape
    units = gate_w.shape[1]
    low = jnp.bfloat16
    thin = ((4, 2, m, units), jnp.float32, pl.ANY)
    normed, gate, up = kernel_call(
        expand_kernel,
        "expand",
        cid,
        [((4, 2, m, width), low, pl.ANY), thin, thin],
        [(own, pltpu.VMEM), (gate_w, pl.ANY), (up_w, pl.ANY)],
        [
            pltpu.VMEM((4, 2, m, width), low),
            pltpu.VMEM(gate_w.shape, low),
            pltpu.VMEM(up_w.shape, low),
            pltpu.VMEM((2, m, units), jnp.float32),
            pltpu.VMEM((2, m, units), jnp.float32),
            copies(GATHER_COPIES),
            pltpu.SemaphoreType.DMA,
            pltpu.SemaphoreType.DMA((2,)),
            pltpu.SemaphoreType.DMA((2, 4)),
            pltpu.SemaphoreType.DMA,
        ],
        flops=32 * m * width * units,
        moved=1 << 27,
    )
    return normed.reshape(8 * m, width), gate.reshape(8 * m, units), up.reshape(8 * m, units)


def hidden_kernel(
    gate_ref,
    up_ref,
    cot_ref,
    gate_w_ref,
    up_w_ref,
    down_w_ref,
    out_ref,
    dnormed_ref,
    dgate_ref,
    dup_ref,
    hidden_ref,
):
    parts, _, depth = down_w_ref.shape
    gate, up = gate_ref[...], up_ref[...]
    dhidden = project(lambda cols: cot_ref[:, cols], down_w_ref)
    sig = jax.nn.sigmoid(gate)
    silu = gate * sig
    hidden = (silu * up).astype(jnp.bfloat16)
    dgate = (dhidden * up * sig * (1.0 + gate * (1.0 - sig))).astype(jnp.bfloat16)
    dup = (dhidden * silu).astype(jnp.bfloat16)
    for s in range(parts):
        cols = pl.ds(s * depth, depth)
        dnormed_ref[:, cols] = (nn_dot(dgate, gate_w_ref[s]) + nn_dot(dup, up_w_ref[s])).astype(
            jnp.bfloat16
        )
        out_ref[:, cols] = nn_dot(hidden, down_w_ref[s]).astype(jnp.bfloat16)
    hidden_ref[...], dgate_ref[...], dup_ref[...] = hidden.T, dgate.T, dup.T


def hidden_units(gate, up, cot, gate_w, up_w, down_w, block=256):
    tokens, units = gate.shape
    width = cot.shape[1]
    low = jnp.bfloat16
    wide = pl.BlockSpec((block, width), lambda i: (i, 0))
    thin = pl.BlockSpec((block, units), lambda i: (i, 0))
    turned = pl.BlockSpec((units, block), lambda i: (0, i))
    weights = pl.BlockSpec(gate_w.shape, lambda i: (0, 0, 0), pipeline_mode=pl.Buffered(1))
    return pl.pallas_call(
        hidden_kernel,
        name="hidden_units",
        grid=(tokens // block,),
        out_shape=[jax.ShapeDtypeStruct((tokens, width), low)] * 2
        + [jax.ShapeDtypeStruct((units, tokens), low)] * 3,
        in_specs=[thin, thin, wide, weights, weights, weights],
        out_specs=[wide, wide, turned, turned, turned],
        compiler_params=pltpu.CompilerParams(vmem_limit_bytes=VMEM_LIMIT),
        cost_estimate=pl.CostEstimate(
            flops=8 * tokens * width * units,
            bytes_accessed=1 << 27,
            transcendentals=tokens * units,
        ),
    )(gate, up, cot, gate_w, up_w, down_w)


def norm_gradient(r, value_at, grad_ref, gain_at, gain_grad, finish, width):
    squares = jnp.zeros((ROW_STEP, LANES), jnp.float32)
    cross = jnp.zeros((ROW_STEP, LANES), jnp.float32)
    for k in range(width // LANES):
        v = value_at(r, k)
        squares += v * v
        cross += v * grad_ref[r, lanes(k)] * gain_at(k)
    scale = lax.rsqrt(mean_of(squares, width) + norm_epsilon)
    pull = mean_of(cross, width) * scale * scale * scale
    for k in range(width // LANES):
        v, g = value_at(r, k), grad_ref[r, lanes(k)]
        gain_grad[:, lanes(k)] += jnp.sum(
            (g * v * scale).reshape(ROW_STEP // 8, 8, LANES), axis=0
        )
        finish(r, k, scale * g * gain_at(k) - v * pull)


def middle_kernel(
    part_hbm,
    normed_hbm,
    dgate_hbm,
    dup_hbm,
    total_ref,
    gate_hbm,
    up_hbm,
    held_ref,
    pair_ref,
    sum_ref,
    got_ref,
    normed_ref,
    left_ref,
    grad_ref,
    sems,
    held_sems,
    load_sems,
    store_sems,
):
    greet_plane()
    scatter = scatter_steps(
        part_hbm, total_ref, pair_ref, sum_ref, got_ref, Sender(sems), (held_ref, held_sems)
    )
    next(scatter)
    loads = [
        pltpu.make_async_copy(a, b, load_sems.at[n])
        for n, (a, b) in enumerate(
            (
                (dgate_hbm, left_ref.at[0]),
                (normed_hbm, normed_ref),
                (dup_hbm, left_ref.at[1]),
            )
        )
    ]
    for c in loads:
        c.start()
    next(scatter)
    width = grad_ref.shape[2]
    blocks = normed_ref.shape[1] // width

    def gradients(which, out_hbm):
        def stored(i):
            column = pl.ds(pl.multiple_of(i * width, width), width)
            slot = parity(i)
            return pltpu.make_async_copy(
                grad_ref.at[slot], out_hbm.at[:, column], store_sems.at[slot]
            )

        def body(i, carry):
            column = pl.ds(pl.multiple_of(i * width, width), width)

            @pl.when(i >= 2)
            def _():
                stored(i - 2).wait()

            grad_ref[lax.rem(i, 2)] = nn_dot(left_ref[which], normed_ref[:, column]).astype(
                jnp.bfloat16
            )
            stored(i).start()
            return carry

        lax.fori_loop(0, blocks, body, 0)
        for i in (blocks - 2, blocks - 1):
            stored(i).wait()

    loads[0].wait()
    loads[1].wait()
    gradients(0, gate_hbm)
    next(scatter)
    loads[2].wait()
    gradients(1, up_hbm)
    run(scatter)


def middle(part, normed, dgate, dup, cid):
    m, width = part.shape[0] // 8, part.shape[1]
    part = part.reshape(4, 2, m, width)
    units, tokens = dgate.shape
    low = jnp.bfloat16
    return kernel_call(
        middle_kernel,
        "middle",
        cid,
        [
            ((m, width), jnp.float32, pltpu.VMEM),
            ((units, width), low, pl.ANY),
            ((units, width), low, pl.ANY),
        ],
        [(a, pl.ANY) for a in (part, normed, dgate, dup)],
        [pltpu.VMEM((4, m, width), low)]
        + scatter_scratch(m, width)
        + [
            pltpu.VMEM((tokens, width), low),
            pltpu.VMEM((2, units, tokens), low),
            pltpu.VMEM((2, units, 256), low),
            copies(SCATTER_COPIES),
            pltpu.SemaphoreType.DMA((4,)),
            pltpu.SemaphoreType.DMA((3,)),
            pltpu.SemaphoreType.DMA((2,)),
        ],
        flops=4 * units * tokens * width,
        moved=m * width * 80,
    )


def turn_kernel(
    total_ref,
    residual_ref,
    cot_ref,
    small_ref,
    dresid_ref,
    gain_ref,
    all_ref,
    low_ref,
    gather_sems,
    local_sem,
):
    greet_plane()
    m, width = residual_ref.shape
    gain_ref[...] = jnp.zeros_like(gain_ref)

    def finish(r, k, v):
        v += cot_ref[r, lanes(k)].astype(jnp.float32)
        dresid_ref[r, lanes(k)] = v
        low_ref[r, lanes(k)] = v.astype(jnp.bfloat16)

    def body(r, carry):
        norm_gradient(
            r,
            lambda r, k: residual_ref[r, lanes(k)],
            total_ref,
            lambda k: small_ref[k, 1:2, :],
            gain_ref,
            finish,
            width,
        )
        return carry

    row_blocks(m, ROW_STEP, body)(0)
    run(gather_steps(low_ref, all_ref, Sender(gather_sems), local_sem))


def turn(total, residual, cot_own, small, cid):
    m, width = residual.shape
    whole = pltpu.VMEM
    dresid, gain, gathered = kernel_call(
        turn_kernel,
        "turn",
        cid,
        [
            ((m, width), jnp.float32, whole),
            ((8, width), jnp.float32, whole),
            ((4, 2, m, width), jnp.bfloat16, pl.ANY),
        ],
        [(a, whole) for a in (total, residual, cot_own, small)],
        [
            pltpu.VMEM((m, width), jnp.bfloat16),
            copies(GATHER_COPIES),
            pltpu.SemaphoreType.DMA,
        ],
        moved=residual.size * 80,
    )
    return dresid, gain, gathered.reshape(-1, width)


def unmix_kernel(
    heads,
    count,
    dresid_ref,
    pack_ref,
    part_ref,
    residual_ref,
    col_ref,
    row_ref,
    pairs_ref,
    qkv_ref,
    exact_ref,
    den_ref,
    state_ref,
    sums_ref,
    *refs,
):
    ins, dqkv_ref, block_ref = refs[:count], refs[count], refs[count + 1]
    outs = refs[count + 2 : 2 * count + 2]
    (
        dmixed_ref,
        back_ref,
        back_sums_ref,
        pick_ref,
        own_ref,
        own_sums_ref,
        out_ref,
        out_sums_ref,
        total_ref,
        held_ref,
        pair_ref,
        sum_ref,
        got_ref,
        sems,
        shard_sems,
        local_sems,
        scatter_sems,
        held_sems,
    ) = refs[2 * count + 2 :]
    parts, _, depth = pack_ref.shape
    rows, length = col_ref.shape[0], col_ref.shape[1]
    vcols, qcols = heads * VHEAD, heads * FDIM
    first_row = pack_ref.shape[1] - vcols
    at, x_at, y_at, _, core = plane_places()
    plane, span, z = lax.axis_size("dp"), lax.axis_size("seq"), lax.axis_index("seq")
    chips = [lax.rem(at + k, plane) for k in range(1, plane)]
    back_ref[...] = jnp.zeros_like(back_ref)
    back_sums_ref[...] = jnp.zeros_like(back_sums_ref)
    greet(
        [{"dp": p} for p in chips]
        + [{"tensor": 1 - core}]
        + [{"seq": lax.rem(z + k, span)} for k in (1, span - 1)]
    )
    scatter = scatter_steps(
        part_ref,
        total_ref,
        pair_ref,
        sum_ref,
        got_ref,
        Sender(scatter_sems),
        (held_ref, held_sems),
    )
    next(scatter)
    chain = Chain(False, back_ref, back_sums_ref, out_ref, out_sums_ref, Sender(sems))
    fill_selectors(pairs_ref, pick_ref, qcols)
    scale = feature_scale(pairs_ref)

    def tokens_of(b):
        return pl.ds(pl.multiple_of(b * length, length), length)

    def cotangents(t, h):
        v = pl.ds(h * VHEAD, VHEAD)
        dn = dmixed_ref[t, v].astype(jnp.float32) / den_ref[t, pl.ds(h, 1)]
        dd = -jnp.sum(dn * exact_ref[t, v], axis=1, keepdims=True)
        return dn.astype(jnp.bfloat16), dd

    def first(b, carry):
        t = tokens_of(b)
        total = jnp.zeros((length, vcols), jnp.float32)
        for s in range(parts):
            total += nt_dot(
                dresid_ref[t, pl.ds(s * depth, depth)], pack_ref[s, pl.ds(first_row, vcols)]
            )
        dmixed_ref[t] = total.astype(jnp.bfloat16)
        head = Segments(col_ref, row_ref, b).head
        tile = qkv_ref[t, pl.ds(vcols, LANES)]
        for h in range(heads):
            dn, dd = cotangents(t, h)
            one, two = factors(tile, pick_ref, 0, h)
            lifted = jnp.where(head, one * two, 0.0)
            own_ref[b, h] = tn_dot(lifted.astype(jnp.bfloat16), dn)
            own_sums_ref[b, h : h + 1] = jnp.sum(lifted * dd, axis=0, keepdims=True)
        return carry

    own_sums_ref[...] = jnp.zeros_like(own_sums_ref)
    lax.fori_loop(0, rows, first, 0)
    next(scatter)
    shards = swap_shards(ins, outs, chips, at, columns_of, block_of, Sender(shard_sems), local_sems)

    def lowered(dlifted, kind, h, one, two):
        return nt_dot((dlifted * two).astype(jnp.bfloat16), pick_ref[kind, h, 0]) + nt_dot(
            (dlifted * one).astype(jnp.bfloat16), pick_ref[kind, h, 1]
        )

    def mixer(b, carry):
        t = tokens_of(b)
        seg = Segments(col_ref, row_ref, b)
        tile = qkv_ref[t, pl.ds(vcols, LANES)]
        key = keys_in_place(tile, qcols)
        dtile = jnp.zeros((length, LANES), jnp.float32)
        dkey = jnp.zeros((length, LANES), jnp.float32)
        for h in range(heads):
            inside = head_mask(length, h)
            v = pl.ds(h * VHEAD, VHEAD)
            value = qkv_ref[t, v]
            query = jnp.where(inside, tile, jnp.zeros_like(tile))
            dn, dd = cotangents(t, h)
            a, w, keep = masked_weights(query, key, seg.column, seg.row)
            dw = jnp.where(keep, nt_dot(dn, value) + dd, 0.0)
            da = (dw * (1.0 + a) * 0.25).astype(jnp.bfloat16)
            dvalue = tn_dot(w.astype(jnp.bfloat16), dn)
            dtile += jnp.where(inside, nn_dot(da, key), 0.0)
            dkey += jnp.where(inside, tn_dot(da, query), 0.0)
            one, two = factors(tile, pick_ref, 0, h)
            dlifted = nt_dot(dn, state_ref[b, h]) + dd * sums_ref[b, h : h + 1]
            dtile += lowered(jnp.where(seg.head, dlifted, 0.0), 0, h, one, two)
            one, two = factors(tile, pick_ref, 1, h)
            lifted = jnp.where(seg.tail, one * two * scale, 0.0)
            dlifted = (nt_dot(value, back_ref[b, h]) + back_sums_ref[b, h : h + 1]) * scale
            dtile += lowered(jnp.where(seg.tail, dlifted, 0.0), 1, h, one, two)
            dvalue += nn_dot(lifted.astype(jnp.bfloat16), back_ref[b, h])
            dqkv_ref[t, v] = dvalue.astype(jnp.bfloat16)
        dtile += pltpu.roll(dkey, qcols, axis=1)
        lane = lax.broadcasted_iota(jnp.int32, (length, LANES), 1)
        dqkv_ref[t, pl.ds(vcols, LANES)] = jnp.where(lane < 2 * qcols, dtile, 0.0).astype(
            jnp.bfloat16
        )
        return carry

    each = rows // CHUNKS
    for g in range(CHUNKS):
        chain.get(g)
        pass_states(
            back_ref,
            back_sums_ref,
            own_ref,
            own_sums_ref,
            out_ref,
            out_sums_ref,
            (col_ref, row_ref),
            g,
        )
        chain.give(g)
        if g == 1:
            next(scatter)
        lax.fori_loop(g * each, (g + 1) * each, mixer, 0)
    run(scatter)

    def finish(r, carry):
        block_ref[r] = (residual_ref[r] + total_ref[r]).astype(jnp.bfloat16)
        return carry

    row_blocks(block_ref.shape[0], ROW_STEP, finish)(0)
    for c in shards:
        c.wait()
    chain.close()


def unmix(dresid_low, pack, part, residual, seg_col, seg_row, pairs, kept, shards, heads, cid):
    tokens = dresid_low.shape[0]
    plane, rows = lax.axis_size("dp"), seg_col.shape[0]
    vcols = heads * VHEAD
    m, width = residual.shape
    count = len(shards)
    whole, low = pltpu.VMEM, jnp.bfloat16
    dqkv, block, *swapped = kernel_call(
        partial(unmix_kernel, heads, count),
        "unmix",
        cid,
        [((tokens, vcols + LANES), low, whole), ((m, width), low, whole)]
        + [((plane, p.shape[0], p.shape[1] // plane), p.dtype, pl.ANY) for p in shards],
        [
            (dresid_low, whole),
            (pack, whole),
            (part.reshape(4, 2, m, width), pl.ANY),
            (residual, whole),
            (seg_col, whole),
            (seg_row, whole),
            (pairs, whole),
        ]
        + [(kept[n], whole) for n in (0, 2, 3, 4, 5)]
        + [(p, pl.ANY) for p in shards],
        [
            pltpu.VMEM((tokens, vcols), low),
            pltpu.VMEM((rows, heads, FEATURES, VHEAD), low),
            pltpu.VMEM((rows, 8, FEATURES), jnp.float32),
        ]
        + state_scratch(rows, heads)
        + [pltpu.VMEM((m, width), jnp.float32), pltpu.VMEM((4, m, width), low)]
        + scatter_scratch(m, width)
        + [
            copies(2 * CHUNKS),
            copies(count * (plane - 1)),
            pltpu.SemaphoreType.DMA((count,)),
            copies(SCATTER_COPIES),
            pltpu.SemaphoreType.DMA((4,)),
        ],
        moved=residual.size * 120,
    )
    return dqkv, block, swapped


def last_kernel(count, *refs):
    ins, gain_ref, outs, sum_ref = (
        refs[:count],
        refs[count],
        refs[count + 1 : 2 * count + 1],
        refs[2 * count + 1],
    )
    got_gain, sems, gain_sems, local_sems = refs[2 * count + 2 :]
    plane, at = lax.axis_size("dp"), lax.axis_index("dp")
    others, me = everyone()
    greet(others)
    copy_gain = Sender(gain_sems)
    gains = [
        copy_gain(gain_ref.at[p["seq"] * plane + p["dp"]], got_gain.at[me], p) for p in others
    ]
    for c in gains:
        c.start()
    chips = [lax.rem(at + k, plane) for k in range(1, plane)]
    shards = swap_shards(ins, outs, chips, at, columns_of, block_of, Sender(sems), local_sems)
    got_gain[me] = gain_ref[lax.axis_index("seq") * plane + at]
    for c in gains:
        c.wait()
    total = got_gain[0]
    for k in range(1, len(others) + 1):
        total += got_gain[k]
    sum_ref[...] = total
    for c in shards:
        c.wait()


def last(shards, gains, cid):
    plane = lax.axis_size("dp")
    count = len(shards)
    devices = lax.axis_size(("dp", "seq", "tensor"))
    *swapped, total = kernel_call(
        partial(last_kernel, count),
        "last",
        cid,
        [((plane, p.shape[0], p.shape[1] // plane), p.dtype, pl.ANY) for p in shards]
        + [(gains.shape[1:], jnp.float32, pltpu.VMEM)],
        [(p, pl.ANY) for p in shards] + [(gains, pltpu.VMEM)],
        [
            pltpu.VMEM((devices,) + gains.shape[1:], jnp.float32),
            copies(count * (plane - 1)),
            copies(devices - 1),
            pltpu.SemaphoreType.DMA((count,)),
        ],
        moved=1 << 26,
    )
    return swapped, total


def everyone():
    plane, span, cores = (lax.axis_size(a) for a in ("dp", "seq", "tensor"))
    at, z, core = (lax.axis_index(a) for a in ("dp", "seq", "tensor"))
    others = [
        {
            "dp": lax.rem(at + i, plane),
            "seq": lax.rem(z + k, span),
            "tensor": lax.rem(core + c, cores),
        }
        for k in range(span)
        for i in range(plane)
        for c in range(cores)
        if i or k or c
    ]
    return others, (at * span + z) * cores + core


def exit_kernel(
    dqkv_ref,
    pack_ref,
    x_ref,
    dresid_ref,
    block_ref,
    small_ref,
    gain_two_ref,
    grad_ref,
    out_ref,
    gains_ref,
    gain_ref,
    part_ref,
    total_ref,
    ordered_ref,
    low_ref,
    pair_ref,
    sum_ref,
    got_ref,
    sems,
    pair_sems,
    local_sems,
):
    greet_plane()
    core = lax.axis_index("tensor")
    parts, _, depth = pack_ref.shape
    m, width = x_ref.shape
    wide = dqkv_ref.shape[1] - LANES + 2 * FDIM * ((dqkv_ref.shape[1] - LANES) // VHEAD)
    blocks = width // LANES
    copy = Sender(pair_sems)

    def project(b, carry):
        left = dqkv_ref[pl.ds(pl.multiple_of(b * m, m), m), pl.ds(0, wide)]
        for s in range(parts):
            part_ref[b // 2, lax.rem(b, 2), :, pl.ds(s * depth, depth)] = nn_dot(
                left, pack_ref[s, pl.ds(0, wide)]
            ).astype(jnp.bfloat16)
        return carry

    lax.fori_loop(0, 8, project, 0)
    scatter = scatter_steps(part_ref, total_ref, pair_ref, sum_ref, got_ref, Sender(sems))
    next(scatter)

    def order(r, carry):
        for k in range(blocks):
            low_ref[r, lanes(seq_major_block(k))] = block_ref[r, lanes(k)]
        return carry

    row_blocks(m, ROW_STEP, order)(0)
    to_pair = [copy(low_ref, out_ref.at[core], {"tensor": 1 - core})]
    local = [pltpu.make_async_copy(low_ref, out_ref.at[core], local_sems.at[0])]
    to_pair[0].start()
    local[0].start()
    run(scatter)
    gain_ref[...] = jnp.zeros_like(gain_ref)

    def finish(r, k, v):
        ordered_ref[r, lanes(seq_major_block(k))] = v + dresid_ref[r, lanes(k)]

    def body(r, carry):
        norm_gradient(
            r,
            lambda r, k: x_ref[r, lanes(k)].astype(jnp.float32),
            total_ref,
            lambda k: small_ref[k, 0:1, :],
            gain_ref,
            finish,
            width,
        )
        return carry

    row_blocks(m, ROW_STEP, body)(0)
    to_pair.append(copy(ordered_ref, grad_ref.at[core], {"tensor": 1 - core}))
    local.append(pltpu.make_async_copy(ordered_ref, grad_ref.at[core], local_sems.at[1]))
    to_pair[1].start()
    local[1].start()
    gains_ref[...] = jnp.zeros_like(gains_ref)
    for k in range(blocks):
        for row, ref in enumerate((gain_ref, gain_two_ref)):
            gains_ref[k, row : row + 1] = jnp.sum(ref[:, lanes(k)], axis=0, keepdims=True)
    for c in to_pair + local:
        c.wait()


def leave(dqkv, pack, x, dresid, block, small, gain_two, cid):
    m, width = x.shape
    whole = pltpu.VMEM
    return kernel_call(
        exit_kernel,
        "leave",
        cid,
        [
            ((2, m, width), jnp.float32, pl.ANY),
            ((2, m, width), jnp.bfloat16, pl.ANY),
            ((width // LANES, 8, LANES), jnp.float32, whole),
        ],
        [(a, whole) for a in (dqkv, pack, x, dresid, block, small, gain_two)],
        [
            pltpu.VMEM((8, width), jnp.float32),
            pltpu.VMEM((4, 2, m, width), jnp.bfloat16),
            pltpu.VMEM((m, width), jnp.float32),
            pltpu.VMEM((m, width), jnp.float32),
            pltpu.VMEM((m, width), jnp.bfloat16),
        ]
        + scatter_scratch(m, width)
        + [
            copies(SCATTER_COPIES),
            copies(2),
            pltpu.SemaphoreType.DMA((2,)),
        ],
        moved=x.size * 120,
    )


def plane_local(
    tokens,
    doc_starts,
    attn_gain,
    mlp_gain,
    query_weight,
    key_weight,
    value_weight,
    output_weight,
    gate_weight,
    up_weight,
    down_weight,
    cotangent,
):
    plane, span, cores = (lax.axis_size("dp"), lax.axis_size("seq"), lax.axis_size("tensor"))
    rows, length, width = tokens.shape
    chunk = width // (plane * span)
    own = rows * length // cores
    heads = query_weight.shape[1] // FDIM // plane
    hidden_part = gate_weight.shape[1] // plane
    vcols, qcols = heads * VHEAD, heads * FDIM

    def over_seq(pack):
        return lax.all_gather(pack, "seq", axis=0, tiled=False)

    def summed(grads):
        return lax.psum_scatter(
            grads.astype(jnp.bfloat16), "seq", scatter_dimension=1, tiled=True
        )

    def split(w):
        return w.reshape(plane, -1, chunk)

    small = jnp.concatenate(
        [
            attn_gain.astype(jnp.float32)[None],
            mlp_gain.astype(jnp.float32)[None],
            doc_starts.astype(jnp.float32).reshape(-1, chunk),
            jnp.zeros((2, chunk), jnp.float32),
        ]
    )
    attn_pack = jnp.concatenate(
        [split(value_weight.T), split(query_weight.T), split(key_weight.T), split(output_weight)],
        axis=1,
    )
    [attn_pack] = exchange(
        [attn_pack], 1, [(attn_pack.shape[1], plane * chunk)], put=columns_of
    )
    gate_w, small = lax.optimization_barrier((split(gate_weight.T), small, attn_pack))[:2]
    gate_w, small = first_exchange(gate_w, small, 2)
    attn_pack, gate_w = over_seq(attn_pack), over_seq(gate_w)
    starts = small[:, 2:-2].reshape(span, plane * rows, length)
    segments = jnp.cumsum(
        lax.dynamic_index_in_dim(starts, lax.axis_index("seq"), 0, keepdims=False), axis=1
    )

    qkv_rows = vcols + 2 * qcols
    seg_col = segments[:, :, None]
    seg_row = segments[:, None, :]
    pairs = feature_pairs()
    normed_one, x, cot_own = entry(
        tokens.reshape(cores, own, width), cotangent.reshape(cores, own, width), small, 3
    )
    kept, cot, up_w, down_w = mix(
        normed_one,
        attn_pack,
        seg_col,
        seg_row,
        pairs,
        cot_own,
        split(up_weight.T),
        split(down_weight),
        heads,
        4,
    )
    mixed = kept[1]
    up_w, down_w = over_seq(up_w), over_seq(down_w)
    residual, normed_own = branch(mixed, attn_pack, x, small, 5)
    normed_two, gate, up = expand(normed_own, gate_w, up_w, 11)
    out_part, dnormed_part, dgate, dup, hidden = hidden_units(
        gate, up, cot, gate_w, up_w, down_w
    )
    down_grad = nn_dot(hidden, cot).astype(jnp.bfloat16)
    dnormed_part, down_grad = lax.optimization_barrier((dnormed_part, down_grad))
    down_grad = summed(down_grad)
    dnormed_two, gate_grad, up_grad = middle(dnormed_part, normed_two, dgate, dup, 6)
    gate_grad, up_grad = summed(gate_grad), summed(up_grad)
    dresid, gain_two_grad, dresid_low = turn(dnormed_two, residual, cot_own, small, 12)
    out_grad = tn_dot(mixed, dresid_low).astype(jnp.bfloat16)
    dresid_low, down_grad, out_grad = lax.optimization_barrier((dresid_low, down_grad, out_grad))
    dqkv, block_own, (down_grad,) = unmix(
        dresid_low,
        attn_pack,
        out_part,
        residual,
        seg_col,
        seg_row,
        pairs,
        kept,
        [down_grad],
        heads,
        8,
    )
    qkv_grad = tn_dot(dqkv, normed_one).astype(jnp.bfloat16)[:qkv_rows]
    out_grad = summed(out_grad)
    dqkv, qkv_grad, gate_grad = lax.optimization_barrier((dqkv, qkv_grad, gate_grad))
    qkv_grad = summed(qkv_grad)
    dtokens, block_out, gains = leave(
        dqkv, attn_pack, x, dresid, block_own, small, gain_two_grad, 9
    )
    (gate_grad, up_grad, out_grad, qkv_grad), gain_grads = last(
        [gate_grad, up_grad, out_grad, qkv_grad], gains, 10
    )

    def stacked(a, start, size):
        return a[:, start : start + size].reshape(plane * size, chunk).astype(jnp.float32)

    h = hidden_part
    return (
        block_out.reshape(rows, length, width),
        dtokens.reshape(rows, length, width),
        gain_grads[0],
        gain_grads[1],
        stacked(qkv_grad, vcols, qcols).T,
        stacked(qkv_grad, vcols + qcols, qcols).T,
        stacked(qkv_grad, 0, vcols).T,
        stacked(out_grad, 0, vcols),
        stacked(gate_grad, 0, h).T,
        stacked(up_grad, 0, h).T,
        stacked(down_grad, 0, h),
    )


def fits_plane(mesh, tokens, query_weight, gate_weight):
    plane, span, cores = (mesh.shape[a] for a in ("dp", "seq", "tensor"))
    heads = query_weight.shape[1] // FDIM // cores
    return (
        plane == 4
        and cores == 2
        and heads % plane == 0
        and (gate_weight.shape[1] // cores) % (16 * plane) == 0
        and tokens.shape[0] % CHUNKS == 0
    )


def solution(mesh):
    def step(*args):
        use = fits_plane(mesh, args[0], args[4], args[8])
        return sharded(mesh, plane_local if use else local)(*args)

    return step


def sharded(mesh, body):
    return jax.shard_map(
        body,
        mesh=mesh,
        in_specs=(
            P("dp", "seq", None),
            P("dp", "seq"),
            P(("dp", "seq")),
            P(("dp", "seq")),
            P(("dp", "seq"), "tensor"),
            P(("dp", "seq"), "tensor"),
            P(("dp", "seq"), "tensor"),
            P("tensor", ("dp", "seq")),
            P(("dp", "seq"), "tensor"),
            P(("dp", "seq"), "tensor"),
            P("tensor", ("dp", "seq")),
            P("dp", "seq", None),
        ),
        out_specs=(
            P("dp", "seq", None),
            P("dp", "seq", None),
            P(("dp", "seq")),
            P(("dp", "seq")),
            P(("dp", "seq"), "tensor"),
            P(("dp", "seq"), "tensor"),
            P(("dp", "seq"), "tensor"),
            P("tensor", ("dp", "seq")),
            P(("dp", "seq"), "tensor"),
            P(("dp", "seq"), "tensor"),
            P("tensor", ("dp", "seq")),
        ),
        check_vma=False,
    )
```

```python
from functools import partial

import jax
import jax.numpy as jnp
import numpy as np
from jax import lax
from jax.experimental import pallas as pl
from jax.experimental.pallas import tpu as pltpu
from jax.sharding import PartitionSpec as P

FDIM = 16
VHEAD = 128
MICRO = 2


norm_epsilon = 1e-05
highest = lax.Precision.HIGHEST
outer_scale = 0.17677669529663687


def prefix(x, axis, combine, identity, reverse):
    size, index = (lax.axis_size(axis), lax.axis_index(axis))
    everything = jax.tree.map(lambda part: lax.all_gather(part, axis), x)
    start = jax.tree.map(
        lambda part, zero: jnp.broadcast_to(jnp.asarray(zero, part.dtype), part.shape), x, identity
    )

    def turn(k, before):
        at = size - 1 - k if reverse else k
        reached = at > index if reverse else at < index
        new = combine(before, jax.tree.map(lambda part: part[at], everything))
        return jax.tree.map(lambda a, b: jnp.where(reached, a, b), new, before)

    return lax.fori_loop(0, size, turn, start)


def features(vectors):
    ones_col = jnp.ones(vectors.shape[:-1] + (1,), jnp.float32)
    outer_terms = vectors[..., :, None] * vectors[..., None, :] * outer_scale
    outer_terms = outer_terms.reshape(vectors.shape[:-1] + (vectors.shape[-1] * vectors.shape[-1],))
    return jnp.concatenate([ones_col, 0.5 * vectors, outer_terms], axis=-1)


def mix_span(queries, key_rows, values, state_in, norm_in, segments):
    length = queries.shape[1]
    scores = jnp.einsum("rthf,rshf->rhts", queries, key_rows, precision=highest) / 4.0
    kernel = 1.0 + scores + 0.5 * scores * scores
    position = jnp.arange(length)
    causal = position[None, :] <= position[:, None]
    allowed = causal[None] & (segments[:, :, None] == segments[:, None, :])
    kernel = jnp.where(allowed[:, None], kernel, 0.0)
    numerator = jnp.einsum("rhts,rshe->rthe", kernel, values, precision=highest)
    denominator = jnp.transpose(jnp.sum(kernel, axis=-1), (0, 2, 1))
    head_part = (segments == 0).astype(jnp.float32)[:, :, None]
    lifted = features(queries)
    numerator = numerator + head_part[..., None] * jnp.einsum(
        "rthf,rhfe->rthe", lifted, state_in, precision=highest
    )
    denominator = denominator + head_part * jnp.einsum(
        "rthf,rhf->rth", lifted, norm_in, precision=highest
    )
    return numerator / denominator[..., None]


def tail_span(key_rows, values, segments):
    tail_mask = (segments == segments[:, -1:]).astype(jnp.float32)
    lifted = features(key_rows) * tail_mask[:, :, None, None]
    tail_state = jnp.einsum("rshf,rshe->rhfe", lifted, values, precision=highest)
    return (tail_state, jnp.sum(lifted, axis=1))


def combine_carry(earlier_part, later_part):
    keep_rate = 1.0 - later_part[2]
    return (
        later_part[0] + keep_rate[:, None, None, None] * earlier_part[0],
        later_part[1] + keep_rate[:, None, None] * earlier_part[1],
        jnp.maximum(earlier_part[2], later_part[2]),
    )


def inverse_rms(inputs):
    return lax.rsqrt(jnp.mean(inputs * inputs, axis=-1, keepdims=True) + norm_epsilon)


def norm_backward(inputs, scale_row, gain_vec, grad_normed):
    scaled_grad = grad_normed * gain_vec
    grad_gain = jnp.sum(grad_normed * inputs * scale_row, axis=0)
    grad_inputs = scale_row * scaled_grad - inputs * scale_row * scale_row * scale_row * jnp.mean(
        scaled_grad * inputs, axis=-1, keepdims=True
    )
    return (grad_inputs, grad_gain)


def inner_rows(left_mat, right_mat):
    return lax.dot_general(
        left_mat, right_mat, (((0,), (0,)), ((), ())), preferred_element_type=jnp.float32
    )


def by_transpose(left_mat, right_mat):
    return lax.dot_general(
        left_mat, right_mat, (((1,), (1,)), ((), ())), preferred_element_type=jnp.float32
    )


def local(
    tokens,
    doc_starts,
    attn_gain,
    mlp_gain,
    query_weight,
    key_weight,
    value_weight,
    output_weight,
    gate_weight,
    up_weight,
    down_weight,
    cotangent,
):
    micro_rows = tokens.shape[0] // MICRO
    span_len = tokens.shape[1]
    model_width = tokens.shape[2]
    head_count = query_weight.shape[1] // FDIM
    outputs_main = []
    outputs_grad = []
    totals = None
    for micro_index in range(MICRO):
        row_start = micro_index * micro_rows
        rows_in = tokens[row_start : row_start + micro_rows]
        starts_in = doc_starts[row_start : row_start + micro_rows]
        cot_in = cotangent[row_start : row_start + micro_rows].reshape(-1, model_width)
        (
            full_query,
            full_key,
            full_value,
            full_gate,
            full_up,
            full_output,
            full_down,
            gain_one,
            gain_two,
        ) = (
            lax.all_gather(query_weight, ("dp", "seq"), axis=0, tiled=True),
            lax.all_gather(key_weight, ("dp", "seq"), axis=0, tiled=True),
            lax.all_gather(value_weight, ("dp", "seq"), axis=0, tiled=True),
            lax.all_gather(gate_weight, ("dp", "seq"), axis=0, tiled=True),
            lax.all_gather(up_weight, ("dp", "seq"), axis=0, tiled=True),
            lax.all_gather(output_weight, ("dp", "seq"), axis=1, tiled=True),
            lax.all_gather(down_weight, ("dp", "seq"), axis=1, tiled=True),
            lax.all_gather(attn_gain, ("dp", "seq"), axis=0, tiled=True),
            lax.all_gather(mlp_gain, ("dp", "seq"), axis=0, tiled=True),
        )
        gain_one_f = gain_one.astype(jnp.float32)
        gain_two_f = gain_two.astype(jnp.float32)
        flat_rows = rows_in.reshape(-1, model_width).astype(jnp.float32)
        scale_one = inverse_rms(flat_rows)
        normed_one = (flat_rows * scale_one * gain_one_f).astype(jnp.bfloat16)
        query_low = jnp.dot(normed_one, full_query, preferred_element_type=jnp.float32).astype(
            jnp.bfloat16
        )
        key_low = jnp.dot(normed_one, full_key, preferred_element_type=jnp.float32).astype(
            jnp.bfloat16
        )
        value_low = jnp.dot(normed_one, full_value, preferred_element_type=jnp.float32).astype(
            jnp.bfloat16
        )
        queries = query_low.astype(jnp.float32).reshape(micro_rows, span_len, head_count, FDIM)
        key_rows = key_low.astype(jnp.float32).reshape(micro_rows, span_len, head_count, FDIM)
        values = value_low.astype(jnp.float32).reshape(micro_rows, span_len, head_count, VHEAD)
        segments = jnp.cumsum(starts_in, axis=1)
        reset_flag = (segments[:, -1] > 0).astype(jnp.float32)
        (tail_state, tail_norm), tail_pull = jax.vjp(
            partial(tail_span, segments=segments), key_rows, values
        )
        state_in, norm_in, reset_in = prefix(
            (tail_state, tail_norm, reset_flag),
            "seq",
            combine_carry,
            (jnp.zeros_like(tail_state), jnp.zeros_like(tail_norm), jnp.zeros_like(reset_flag)),
            False,
        )
        mixed_heads, mix_pull = jax.vjp(
            partial(mix_span, segments=segments), queries, key_rows, values, state_in, norm_in
        )
        mixed_low = mixed_heads.reshape(-1, head_count * VHEAD).astype(jnp.bfloat16)
        branch_one = jnp.dot(mixed_low, full_output, preferred_element_type=jnp.float32)
        residual = flat_rows + lax.psum(branch_one, "tensor")
        scale_two = inverse_rms(residual)
        normed_two = (residual * scale_two * gain_two_f).astype(jnp.bfloat16)
        gate_proj = jnp.dot(normed_two, full_gate, preferred_element_type=jnp.float32)
        up_proj = jnp.dot(normed_two, full_up, preferred_element_type=jnp.float32)
        sigmoid_gate = jax.nn.sigmoid(gate_proj)
        hidden = (gate_proj * sigmoid_gate * up_proj).astype(jnp.bfloat16)
        branch_two = jnp.dot(hidden, full_down, preferred_element_type=jnp.float32)
        block_low = (
            residual + lax.psum(branch_two.astype(jnp.bfloat16), "tensor").astype(jnp.float32)
        ).astype(jnp.bfloat16)
        outputs_main.append(block_low.reshape(micro_rows, span_len, model_width))
        grad_down = inner_rows(hidden, cot_in)
        grad_hidden = by_transpose(cot_in, full_down)
        grad_gate_low = (
            grad_hidden * up_proj * sigmoid_gate * (1.0 + gate_proj * (1.0 - sigmoid_gate))
        ).astype(jnp.bfloat16)
        grad_up_low = (grad_hidden * gate_proj * sigmoid_gate).astype(jnp.bfloat16)
        grad_gate = inner_rows(normed_two, grad_gate_low)
        grad_up = inner_rows(normed_two, grad_up_low)
        grad_normed_two = by_transpose(grad_gate_low, full_gate) + by_transpose(
            grad_up_low, full_up
        )
        grad_normed_two = lax.psum(grad_normed_two, "tensor")
        grad_resid, grad_gain_two = norm_backward(residual, scale_two, gain_two_f, grad_normed_two)
        grad_resid = grad_resid + cot_in.astype(jnp.float32)
        grad_resid_low = grad_resid.astype(jnp.bfloat16)
        grad_output = inner_rows(mixed_low, grad_resid_low)
        grad_mixed = by_transpose(grad_resid_low, full_output).astype(jnp.bfloat16)
        grad_mixed = (
            lax.optimization_barrier(grad_mixed)
            .astype(jnp.float32)
            .reshape(micro_rows, span_len, head_count, VHEAD)
        )
        grad_queries, grad_keys, grad_values, grad_state, grad_norm = mix_pull(grad_mixed)
        carried_state, carried_norm, reset_out = prefix(
            (grad_state, grad_norm, reset_flag),
            "seq",
            combine_carry,
            (jnp.zeros_like(grad_state), jnp.zeros_like(grad_norm), jnp.zeros_like(reset_flag)),
            True,
        )
        more_keys, more_values = tail_pull((carried_state, carried_norm))
        grad_query_low = grad_queries.reshape(-1, head_count * FDIM).astype(jnp.bfloat16)
        grad_key_low = (grad_keys + more_keys).reshape(-1, head_count * FDIM).astype(jnp.bfloat16)
        grad_value_low = (
            (grad_values + more_values).reshape(-1, head_count * VHEAD).astype(jnp.bfloat16)
        )
        grad_query = inner_rows(normed_one, grad_query_low)
        grad_key = inner_rows(normed_one, grad_key_low)
        grad_value = inner_rows(normed_one, grad_value_low)
        grad_normed_one = (
            by_transpose(grad_query_low, full_query)
            + by_transpose(grad_key_low, full_key)
            + by_transpose(grad_value_low, full_value)
        )
        grad_normed_one = lax.psum(grad_normed_one, "tensor")
        grad_inputs, grad_gain_one = norm_backward(
            flat_rows, scale_one, gain_one_f, grad_normed_one
        )
        outputs_grad.append((grad_resid + grad_inputs).reshape(micro_rows, span_len, model_width))
        shares = (
            grad_query,
            grad_key,
            grad_value,
            grad_gate,
            grad_up,
            grad_output,
            grad_down,
            grad_gain_one,
            grad_gain_two,
        )
        if totals is None:
            totals = shares
        else:
            totals = jax.tree.map(jnp.add, totals, shares)
    totals = (
        lax.psum_scatter(totals[0], ("dp", "seq"), scatter_dimension=0, tiled=True),
        lax.psum_scatter(totals[1], ("dp", "seq"), scatter_dimension=0, tiled=True),
        lax.psum_scatter(totals[2], ("dp", "seq"), scatter_dimension=0, tiled=True),
        lax.psum_scatter(totals[3], ("dp", "seq"), scatter_dimension=0, tiled=True),
        lax.psum_scatter(totals[4], ("dp", "seq"), scatter_dimension=0, tiled=True),
        lax.psum_scatter(totals[5], ("dp", "seq"), scatter_dimension=1, tiled=True),
        lax.psum_scatter(totals[6], ("dp", "seq"), scatter_dimension=1, tiled=True),
        lax.psum_scatter(totals[7], ("dp", "seq"), scatter_dimension=0, tiled=True),
        lax.psum_scatter(totals[8], ("dp", "seq"), scatter_dimension=0, tiled=True),
    )
    return (
        jnp.concatenate(outputs_main, axis=0),
        jnp.concatenate(outputs_grad, axis=0),
        totals[7],
        totals[8],
        totals[0],
        totals[1],
        totals[2],
        totals[5],
        totals[3],
        totals[4],
        totals[6],
    )


MESH_ID = pl.DeviceIdType.MESH
VMEM_LIMIT = 58 << 20
LANES = 128
ROW_STEP = 32


def nt_dot(a, b):
    return lax.dot_general(a, b, (((1,), (1,)), ((), ())), preferred_element_type=jnp.float32)


def tn_dot(a, b):
    return lax.dot_general(a, b, (((0,), (0,)), ((), ())), preferred_element_type=jnp.float32)


def nn_dot(a, b):
    return lax.dot_general(a, b, (((1,), (0,)), ((), ())), preferred_element_type=jnp.float32)


def plane_places():
    at, core = lax.axis_index("dp"), lax.axis_index("tensor")
    x_bit, y_bit = lax.rem(at, 2), at // 2
    return (
        at,
        y_bit * 2 + (1 - x_bit),
        (1 - y_bit) * 2 + x_bit,
        (1 - y_bit) * 2 + (1 - x_bit),
        core,
    )


def greet(places):
    barrier = pltpu.get_barrier_semaphore()
    for place in places:
        pl.semaphore_signal(barrier, inc=1, device_id=place, device_id_type=MESH_ID)
    pl.semaphore_wait(barrier, len(places))


class Sender:
    def __init__(self, sems):
        self.sems, self.used = sems, 0

    def __call__(self, src, dst, place):
        index = self.used
        self.used += 1
        return pltpu.make_async_remote_copy(
            src_ref=src,
            dst_ref=dst,
            send_sem=self.sems.at[0, index],
            recv_sem=self.sems.at[1, index],
            device_id=place,
            device_id_type=MESH_ID,
        )


def greet_plane():
    at, x_at, y_at, _, core = plane_places()
    greet([{"dp": x_at}, {"dp": y_at}, {"tensor": 1 - core}])


def add_rows(dst, *srcs, step=64):
    def body(i, carry):
        r = pl.ds(pl.multiple_of(i * step, step), step)
        total = srcs[0][r].astype(jnp.float32)
        for s in srcs[1:]:
            total = total + s[r].astype(jnp.float32)
        dst[r] = total.astype(dst.dtype)
        return carry

    lax.fori_loop(0, srcs[0].shape[0] // step, body, 0)


GATHER_COPIES = 13
SCATTER_COPIES = 10


def gather_steps(own_ref, out_ref, copy, local_sem):
    at, x_at, y_at, d_at, core = plane_places()
    half = own_ref.shape[0] // 2
    xp, yp, sp = {"dp": x_at}, {"dp": y_at}, {"tensor": 1 - core}
    lo, hi = pl.ds(0, half), pl.ds(half, half)
    mine = out_ref.at[at, core]
    x_lo = copy(own_ref.at[lo], mine.at[lo], xp)
    y_hi = copy(own_ref.at[hi], mine.at[hi], yp)
    x_hi = copy(own_ref.at[hi], mine.at[hi], xp)
    y_lo = copy(own_ref.at[lo], mine.at[lo], yp)
    pair = copy(own_ref, mine, sp)
    for c in (x_lo, y_hi, x_hi, y_lo, pair):
        c.start()
    local_copy = pltpu.make_async_copy(own_ref, mine, local_sem)
    local_copy.start()
    from_x, from_y, from_d = out_ref.at[x_at, core], out_ref.at[y_at, core], out_ref.at[d_at, core]
    on_y = copy(from_x.at[lo], from_x.at[lo], yp)
    on_x = copy(from_y.at[hi], from_y.at[hi], xp)
    handed = [
        copy(block.at[rows], block.at[rows], sp)
        for block, rows in (
            (from_x, lo),
            (from_y, hi),
            (from_x, hi),
            (from_y, lo),
            (from_d, lo),
            (from_d, hi),
        )
    ]
    yield
    local_copy.wait()
    yield
    pair.wait_recv()
    yield
    x_lo.wait_recv()
    on_y.start()
    handed[0].start()
    y_hi.wait_recv()
    on_x.start()
    handed[1].start()
    yield
    handed[0].wait_recv()
    handed[1].wait_recv()
    yield
    x_hi.wait_recv()
    handed[2].start()
    y_lo.wait_recv()
    handed[3].start()
    yield
    handed[2].wait_recv()
    handed[3].wait_recv()
    yield
    on_y.wait_recv()
    handed[4].start()
    on_x.wait_recv()
    handed[5].start()
    yield
    handed[4].wait_recv()
    handed[5].wait_recv()
    yield
    for c in [x_lo, y_hi, x_hi, y_lo, on_y, on_x, pair] + handed:
        c.wait_send()


def scatter_steps(part_ref, out_ref, pair_ref, sum_ref, got_ref, copy, held=None):
    at, x_at, y_at, d_at, core = plane_places()
    half = part_ref.shape[2] // 2
    xp, yp, sp = {"dp": x_at}, {"dp": y_at}, {"tensor": 1 - core}
    lo, hi = pl.ds(0, half), pl.ds(half, half)
    order = (d_at, x_at, y_at, at)
    pairs = [copy(part_ref.at[to, 1 - core], pair_ref.at[j], sp) for j, to in enumerate(order)]
    own = [part_ref.at[to, core] for to in order]
    fetched = []
    if held is not None:
        buffer, held_sems = held
        fetched = [
            pltpu.make_async_copy(o, buffer.at[j], held_sems.at[j]) for j, o in enumerate(own)
        ]
        own = [buffer.at[j] for j in range(4)]

    def sent(j, rows, place):
        return copy(sum_ref.at[j, rows], got_ref.at[j, rows], place)

    d_lo, d_hi = sent(0, lo, xp), sent(0, hi, yp)
    x_lo, y_hi, x_hi, y_lo = sent(1, lo, xp), sent(2, hi, yp), sent(1, hi, xp), sent(2, lo, yp)
    for c in pairs + fetched:
        c.start()
    yield

    def ready(j):
        if fetched:
            fetched[j].wait()
        pairs[j].wait_recv()

    def total(j, rows, *more):
        add_rows(sum_ref.at[j, rows], own[j].at[rows], pair_ref.at[j, rows], *more)

    ready(0)
    total(0, lo)
    d_lo.start()
    total(0, hi)
    d_hi.start()
    ready(1)
    total(1, lo)
    x_lo.start()
    ready(2)
    total(2, hi)
    y_hi.start()
    yield
    d_lo.wait_recv()
    total(2, lo, got_ref.at[0, lo])
    y_lo.start()
    d_hi.wait_recv()
    total(1, hi, got_ref.at[0, hi])
    x_hi.start()
    yield
    ready(3)
    for c in (x_lo, y_hi, y_lo, x_hi):
        c.wait_recv()
    add_rows(out_ref, own[3], pair_ref.at[3], got_ref.at[1], got_ref.at[2])
    for c in pairs + [d_lo, d_hi, x_lo, y_hi, x_hi, y_lo]:
        c.wait_send()


def swap_shards(ins, outs, peers, me, take, put, copy, local_sems):
    started = [
        copy(take(i, p), put(o, me), {"dp": p}) for i, o in zip(ins, outs) for p in peers
    ]
    started += [
        pltpu.make_async_copy(take(i, me), put(o, me), local_sems.at[n])
        for n, (i, o) in enumerate(zip(ins, outs))
    ]
    for c in started:
        c.start()
    return started


def exchange_kernel(take, put, count, *refs):
    ins, outs, sems, local_sems = refs[:count], refs[count : 2 * count], refs[-2], refs[-1]
    size, me = lax.axis_size("dp"), lax.axis_index("dp")
    peers = [lax.rem(me + k, size) for k in range(1, size)]
    greet([{"dp": p} for p in peers])
    for c in swap_shards(ins, outs, peers, me, take, put, Sender(sems), local_sems):
        c.wait()


def block_of(ref, index):
    return ref.at[index]


def columns_of(ref, index, rows=slice(None)):
    width = ref.shape[1] // lax.axis_size("dp")
    return ref.at[rows, pl.ds(pl.multiple_of(index * width, width), width)]


def exchange(arrays, cid, shapes, take=block_of, put=block_of):
    count, peers = len(arrays), lax.axis_size("dp") - 1
    anywhere = [pl.BlockSpec(memory_space=pl.ANY)] * count
    return pl.pallas_call(
        partial(exchange_kernel, take, put, count),
        name="exchange",
        out_shape=[jax.ShapeDtypeStruct(s, x.dtype) for s, x in zip(shapes, arrays)],
        in_specs=anywhere,
        out_specs=anywhere,
        scratch_shapes=[
            pltpu.SemaphoreType.DMA((2, count * peers)),
            pltpu.SemaphoreType.DMA((count,)),
        ],
        compiler_params=pltpu.CompilerParams(collective_id=cid, has_side_effects=True),
        cost_estimate=pl.CostEstimate(
            flops=0, bytes_accessed=60 * sum(x.size for x in arrays), transcendentals=0
        ),
    )(*arrays)


def first_kernel(count, *refs):
    ins, small_ref, outs, all_ref = (
        refs[:count],
        refs[count],
        refs[count + 1 : 2 * count + 1],
        refs[2 * count + 1],
    )
    sems, small_sems, local_sems, small_local_sem = refs[2 * count + 2 :]
    plane, span = lax.axis_size("dp"), lax.axis_size("seq")
    at, z = lax.axis_index("dp"), lax.axis_index("seq")
    places = [
        {"dp": lax.rem(at + i, plane), "seq": lax.rem(z + k, span)}
        for k in range(span)
        for i in range(plane)
        if i or k
    ]
    greet(places)
    copy_small = Sender(small_sems)
    block = all_ref.at[z * plane + at]
    started = [copy_small(small_ref, block, p) for p in places]
    started.append(pltpu.make_async_copy(small_ref, block, small_local_sem))
    for c in started:
        c.start()
    chips = [lax.rem(at + k, plane) for k in range(1, plane)]
    started += swap_shards(ins, outs, chips, at, block_of, columns_of, Sender(sems), local_sems)
    for c in started:
        c.wait()


def first_exchange(packs, small, cid):
    plane, span = lax.axis_size("dp"), lax.axis_size("seq")
    count = len(packs)
    return kernel_call(
        partial(first_kernel, count),
        "first_exchange",
        cid,
        [((p.shape[1], plane * p.shape[2]), p.dtype, pl.ANY) for p in packs]
        + [((span * plane,) + small.shape, small.dtype, pltpu.VMEM)],
        [(p, pl.ANY) for p in packs] + [(small, pltpu.VMEM)],
        [
            copies(count * (plane - 1)),
            copies(plane * span - 1),
            pltpu.SemaphoreType.DMA((count,)),
            pltpu.SemaphoreType.DMA,
        ],
        moved=1 << 26,
    )


def run(*steps):
    for g in steps:
        for _ in g:
            pass


def row_blocks(rows, step, body):
    def inner(i, carry):
        return body(pl.ds(pl.multiple_of(i * step, step), step), carry)

    return lambda init: lax.fori_loop(0, rows // step, inner, init)


def lanes(k):
    return pl.ds(k * LANES, LANES)


def seq_major_block(k):
    plane, span = lax.axis_size("dp"), lax.axis_size("seq")
    s, g = divmod(k, plane)
    return g * span + s


def mean_of(acc, width):
    return jnp.sum(acc, axis=1, keepdims=True) * (1.0 / width)


def kernel_call(body, name, cid, outs, ins, scratch, flops=0, moved=0):
    params = dict(has_side_effects=True, vmem_limit_bytes=VMEM_LIMIT)
    return pl.pallas_call(
        body,
        name=name,
        out_shape=[jax.ShapeDtypeStruct(s, d) for s, d, _ in outs],
        in_specs=[pl.BlockSpec(memory_space=m) for _, m in ins],
        out_specs=[pl.BlockSpec(memory_space=m) for _, _, m in outs],
        scratch_shapes=scratch,
        compiler_params=pltpu.CompilerParams(collective_id=cid, **params),
        cost_estimate=pl.CostEstimate(flops=flops, bytes_accessed=moved, transcendentals=0),
    )(*[a for a, _ in ins])


def copies(count):
    return pltpu.SemaphoreType.DMA((2, count))


def entry_kernel(
    tokens_ref, cot_ref, small_ref, all_ref, x_ref, cot_own_ref, normed_ref, sems, local_sem
):
    greet_plane()
    core = lax.axis_index("tensor")
    m, width = x_ref.shape
    blocks = width // LANES

    def body(r, carry):
        acc = jnp.zeros((ROW_STEP, LANES), jnp.float32)
        for k in range(blocks):
            source = lanes(seq_major_block(k))
            v = tokens_ref[core, r, source]
            x_ref[r, lanes(k)] = v
            cot_own_ref[r, lanes(k)] = cot_ref[core, r, source]
            v = v.astype(jnp.float32)
            acc += v * v
        scale = lax.rsqrt(mean_of(acc, width) + norm_epsilon)
        for k in range(blocks):
            v = x_ref[r, lanes(k)].astype(jnp.float32)
            normed_ref[r, lanes(k)] = (v * scale * small_ref[k, 0:1, :]).astype(jnp.bfloat16)
        return carry

    row_blocks(m, ROW_STEP, body)(0)
    run(gather_steps(normed_ref, all_ref, Sender(sems), local_sem))


def entry(tokens, cot, small, cid):
    cores, m, width = tokens.shape
    whole = pltpu.VMEM
    gathered, x, cot_own = kernel_call(
        entry_kernel,
        "entry",
        cid,
        [
            ((4, cores, m, width), jnp.bfloat16, pl.ANY),
            ((m, width), jnp.bfloat16, whole),
            ((m, width), jnp.bfloat16, whole),
        ],
        [(tokens, whole), (cot, whole), (small, whole)],
        [pltpu.VMEM((m, width), jnp.bfloat16), copies(GATHER_COPIES), pltpu.SemaphoreType.DMA],
        moved=tokens.size * 40,
    )
    return gathered.reshape(-1, width), x, cot_own


FEATURES = 256
STATE_ROWS = 160
CHUNKS = 4
EARLY = 320


def feature_pairs():
    first = np.full(FEATURES, -4096, np.int32)
    second = np.full(FEATURES, -4096, np.int32)
    pairs = [(i, j) for i in range(FDIM + 1) for j in range(i, FDIM + 1)]
    for f, (i, j) in enumerate(pairs):
        first[f], second[f] = i, j
    return jnp.asarray(np.stack([first, second] + [first] * 6))


def feature_scale(pairs_ref):
    i, j = pairs_ref[0:1, :], pairs_ref[1:2, :]
    square = jnp.where(i == j, 1.0 / 32.0, 1.0 / 16.0)
    return jnp.where(j == FDIM, jnp.where(i == FDIM, 1.0, 0.25), square)


def fill_selectors(pairs_ref, pick_ref, qcols):
    kinds, heads = pick_ref.shape[:2]
    lane = lax.broadcasted_iota(jnp.int32, (LANES, FEATURES), 0)
    for kind in range(kinds):
        for h in range(heads):
            for side in range(2):
                index = pairs_ref[side : side + 1, :]
                source = jnp.where(
                    index == FDIM, 2 * qcols, index + (kind * qcols + h * FDIM)
                )
                pick_ref[kind, h, side] = jnp.where(lane == source, 1.0, 0.0).astype(jnp.bfloat16)


def factors(tile, pick_ref, kind, h):
    return nn_dot(tile, pick_ref[kind, h, 0]), nn_dot(tile, pick_ref[kind, h, 1])


def keys_in_place(tile, qcols):
    return pltpu.roll(tile.astype(jnp.float32), LANES - qcols, axis=1).astype(jnp.bfloat16)


def head_mask(rows, head):
    lane = lax.broadcasted_iota(jnp.int32, (rows, LANES), 1)
    return (lane >= head * FDIM) & (lane < (head + 1) * FDIM)


def masked_weights(query, key, column, row):
    length = query.shape[0]
    a = nt_dot(query, key) * 0.25
    t = lax.broadcasted_iota(jnp.int32, (length, length), 0)
    s = lax.broadcasted_iota(jnp.int32, (length, length), 1)
    keep = (s <= t) & (column == row)
    return a, jnp.where(keep, 1.0 + a + 0.5 * a * a, 0.0), keep


class Segments:
    def __init__(self, col_ref, row_ref, b):
        self.column, self.row = col_ref[b], row_ref[b]
        last = self.row[:, -1:]
        self.head = self.column == 0.0
        self.tail = self.column == last
        self.keep = jnp.where(last == 0.0, 1.0, 0.0)


class Chain:
    def __init__(self, forward, col_ref, row_ref, state_ref, sums_ref, scratch, copy_sems):
        span, z = lax.axis_size("seq"), lax.axis_index("seq")
        self.span = span
        self.to = {"seq": lax.rem(z + (1 if forward else span - 1), span)}
        self.distance = z if forward else span - 1 - z
        self.gets, self.gives = self.distance > 0, self.distance < span - 1
        self.segments = (col_ref, row_ref)
        self.state_ref, self.sums_ref = state_ref, sums_ref
        self.own_ref, self.own_sums_ref, self.out_ref, self.out_sums_ref = scratch
        self.sems = copy_sems
        self.rows = state_ref.shape[0] // CHUNKS

    def moves(self, g):
        part = pl.ds(g * self.rows, self.rows)
        used = pl.ds(0, STATE_ROWS)
        pairs = (
            (self.out_ref.at[part, :, used], self.state_ref.at[part, :, used]),
            (self.out_sums_ref.at[part], self.sums_ref.at[part]),
        )
        return [
            pltpu.make_async_remote_copy(
                src_ref=a,
                dst_ref=b,
                send_sem=self.sems.at[0, 2 * g + n],
                recv_sem=self.sems.at[1, 2 * g + n],
                device_id=self.to,
                device_id_type=MESH_ID,
            )
            for n, (a, b) in enumerate(pairs)
        ]

    def step(self, n):
        g = n - self.distance

        @pl.when((g >= 0) & (g < CHUNKS))
        def _():
            @pl.when(self.gets)
            def _():
                for c in self.moves(g):
                    c.wait_recv()

            for i in range(self.rows):
                b = g * self.rows + i
                keep = Segments(*self.segments, b).keep
                for h in range(self.state_ref.shape[1]):
                    before = self.state_ref[b, h].astype(jnp.float32)
                    self.out_ref[b, h] = (self.own_ref[b, h] + keep * before).astype(jnp.bfloat16)
                self.out_sums_ref[b] = self.own_sums_ref[b] + keep * self.sums_ref[b]

            @pl.when(self.gives)
            def _():
                for c in self.moves(g):
                    c.start()

    def run(self, work, between=()):
        def body(n, carry):
            for at, piece in enumerate(between):

                @pl.when(n == at)
                def _():
                    piece()

            work(n, self.step)
            return carry

        lax.fori_loop(0, CHUNKS + self.span - 1, body, 0)

    def close(self):
        @pl.when(self.gives)
        def _():
            for g in range(CHUNKS):
                for c in self.moves(g):
                    c.wait_send()


def states_kernel(
    heads,
    normed_ref,
    pack_ref,
    col_ref,
    row_ref,
    pairs_ref,
    down_ref,
    qkv_ref,
    state_ref,
    sums_ref,
    down_all_ref,
    pick_ref,
    own_ref,
    own_sums_ref,
    out_ref,
    out_sums_ref,
    sems,
    shard_sems,
    shard_local_sems,
):
    parts, _, depth = pack_ref.shape
    rows, length = col_ref.shape[0], col_ref.shape[1]
    vcols, qcols = heads * VHEAD, heads * FDIM
    plane, span = lax.axis_size("dp"), lax.axis_size("seq")
    at, z = lax.axis_index("dp"), lax.axis_index("seq")
    chips = [lax.rem(at + k, plane) for k in range(1, plane)]
    state_ref[...] = jnp.zeros_like(state_ref)
    sums_ref[...] = jnp.zeros_like(sums_ref)
    greet(
        [{"dp": p} for p in chips] + [{"seq": lax.rem(z + k, span)} for k in (1, span - 1)]
    )
    shards = swap_shards(
        (down_ref,),
        (down_all_ref,),
        chips,
        at,
        block_of,
        columns_of,
        Sender(shard_sems),
        shard_local_sems,
    )
    chain = Chain(
        True,
        col_ref,
        row_ref,
        state_ref,
        sums_ref,
        (own_ref, own_sums_ref, out_ref, out_sums_ref),
        sems,
    )
    fill_selectors(pairs_ref, pick_ref, qcols)
    scale = feature_scale(pairs_ref)

    def tokens_of(b):
        return pl.ds(pl.multiple_of(b * length, length), length)

    def first(b, carry):
        t = tokens_of(b)
        value = jnp.zeros((length, vcols), jnp.float32)
        tile = jnp.zeros((length, LANES), jnp.float32)
        for s in range(parts):
            piece = normed_ref[t, pl.ds(s * depth, depth)]
            value += nt_dot(piece, pack_ref[s, pl.ds(0, vcols)])
            tile += nt_dot(piece, pack_ref[s, pl.ds(vcols, LANES)])
        lane = lax.broadcasted_iota(jnp.int32, (length, LANES), 1)
        tile = jnp.where(lane < 2 * qcols, tile, jnp.where(lane == 2 * qcols, 1.0, 0.0))
        value, tile = value.astype(jnp.bfloat16), tile.astype(jnp.bfloat16)
        qkv_ref[t, pl.ds(0, vcols)] = value
        qkv_ref[t, pl.ds(vcols, LANES)] = tile
        tail = Segments(col_ref, row_ref, b).tail
        for h in range(heads):
            one, two = factors(tile, pick_ref, 1, h)
            lifted = jnp.where(tail, one * two * scale, 0.0)
            own_ref[b, h] = tn_dot(
                lifted.astype(jnp.bfloat16), value[:, h * VHEAD : (h + 1) * VHEAD]
            )
            own_sums_ref[b, h : h + 1] = jnp.sum(lifted, axis=0, keepdims=True)
        return carry

    own_sums_ref[...] = jnp.zeros_like(own_sums_ref)
    each = rows // CHUNKS

    def work(n, step):
        @pl.when(n < CHUNKS)
        def _():
            lax.fori_loop(n * each, (n + 1) * each, first, 0)

        step(n)

    chain.run(work)
    for c in shards:
        c.wait()
    chain.close()


def mix_kernel(
    heads,
    qkv_ref,
    col_ref,
    row_ref,
    pairs_ref,
    state_ref,
    sums_ref,
    cot_ref,
    mixed_ref,
    exact_ref,
    den_ref,
    cot_all_ref,
    pick_ref,
    cot_sems,
    local_sem,
):
    rows, length = col_ref.shape[0], col_ref.shape[1]
    vcols, qcols = heads * VHEAD, heads * FDIM
    greet_plane()
    gather = gather_steps(cot_ref, cot_all_ref, Sender(cot_sems), local_sem)
    next(gather)
    fill_selectors(pairs_ref, pick_ref, qcols)

    def tokens_of(b):
        return pl.ds(pl.multiple_of(b * length, length), length)

    lane = lax.broadcasted_iota(jnp.int32, (length, LANES), 1)

    def here(b, carry):
        t = tokens_of(b)
        seg = Segments(col_ref, row_ref, b)
        tile = qkv_ref[t, pl.ds(vcols, LANES)]
        key = keys_in_place(tile, qcols)
        dens = jnp.zeros((length, LANES), jnp.float32)
        for h in range(heads):
            v = pl.ds(h * VHEAD, VHEAD)
            query = jnp.where(head_mask(length, h), tile, jnp.zeros_like(tile))
            _, w, _ = masked_weights(query, key, seg.column, seg.row)
            exact_ref[t, v] = nn_dot(w.astype(jnp.bfloat16), qkv_ref[t, v])
            dens = jnp.where(lane == h, jnp.sum(w, axis=1, keepdims=True), dens)
        den_ref[t] = dens
        return carry

    def before(b, carry):
        t = tokens_of(b)
        head = Segments(col_ref, row_ref, b).head
        tile = qkv_ref[t, pl.ds(vcols, LANES)]
        dens = den_ref[t]
        for h in range(heads):
            v = pl.ds(h * VHEAD, VHEAD)
            one, two = factors(tile, pick_ref, 0, h)
            lifted = jnp.where(head, one * two, 0.0)
            num = exact_ref[t, v] + nn_dot(lifted.astype(jnp.bfloat16), state_ref[b, h])
            den = dens[:, h : h + 1]
            den += jnp.sum(lifted * sums_ref[b, h : h + 1], axis=1, keepdims=True)
            value = num / den
            exact_ref[t, v] = value
            mixed_ref[t, v] = value.astype(jnp.bfloat16)
            dens = jnp.where(lane == h, den, dens)
        den_ref[t] = dens
        return carry

    def row(b, carry):
        for at in range(1, 6):

            @pl.when(b == at)
            def _():
                next(gather)

        here(b, 0)
        before(b, 0)
        return carry

    lax.fori_loop(0, rows, row, 0)
    run(gather)


def state_scratch(rows, heads):
    return [
        pltpu.VMEM((2, heads, 2, LANES, FEATURES), jnp.bfloat16),
        pltpu.VMEM((rows, heads, FEATURES, VHEAD), jnp.float32),
        pltpu.VMEM((rows, 8, FEATURES), jnp.float32),
        pltpu.VMEM((rows, heads, FEATURES, VHEAD), jnp.bfloat16),
        pltpu.VMEM((rows, 8, FEATURES), jnp.float32),
    ]


def states(normed, pack, seg_col, seg_row, pairs, down, heads, cid):
    tokens = normed.shape[0]
    rows = seg_col.shape[0]
    vcols = heads * VHEAD
    plane, size, chunk = down.shape
    whole = pltpu.VMEM
    return kernel_call(
        partial(states_kernel, heads),
        "states",
        cid,
        [
            ((tokens, vcols + LANES), jnp.bfloat16, whole),
            ((rows, heads, FEATURES, VHEAD), jnp.bfloat16, whole),
            ((rows, 8, FEATURES), jnp.float32, whole),
            ((size, plane * chunk), jnp.bfloat16, pl.ANY),
        ],
        [(a, whole) for a in (normed, pack, seg_col, seg_row, pairs)] + [(down, pl.ANY)],
        state_scratch(rows, heads)
        + [copies(2 * CHUNKS), copies(plane - 1), pltpu.SemaphoreType.DMA((1,))],
        moved=normed.size * 20,
    )


def mix(qkv, seg_col, seg_row, pairs, state, sums, cot_own, heads, cid):
    tokens = qkv.shape[0]
    vcols = heads * VHEAD
    m, width = cot_own.shape
    whole = pltpu.VMEM
    mixed, exact, den, cot = kernel_call(
        partial(mix_kernel, heads),
        "mix",
        cid,
        [
            ((tokens, vcols), jnp.bfloat16, whole),
            ((tokens, vcols), jnp.float32, whole),
            ((tokens, LANES), jnp.float32, whole),
            ((4, 2, m, width), jnp.bfloat16, pl.ANY),
        ],
        [(a, whole) for a in (qkv, seg_col, seg_row, pairs, state, sums, cot_own)],
        [
            pltpu.VMEM((2, heads, 2, LANES, FEATURES), jnp.bfloat16),
            copies(GATHER_COPIES),
            pltpu.SemaphoreType.DMA,
        ],
        moved=cot_own.size * 80,
    )
    return mixed, exact, den, cot.reshape(-1, width)


def branch_kernel(
    mixed_ref,
    pack_ref,
    x_ref,
    small_ref,
    residual_ref,
    normed_ref,
    part_ref,
    pair_ref,
    sum_ref,
    got_ref,
    sems,
):
    greet_plane()
    parts, _, depth = pack_ref.shape
    m, width = x_ref.shape
    vcols = mixed_ref.shape[1]
    first = pack_ref.shape[1] - vcols

    def project(b, carry):
        left = mixed_ref[pl.ds(pl.multiple_of(b * m, m), m)]
        for s in range(parts):
            part_ref[b // 2, lax.rem(b, 2), :, pl.ds(s * depth, depth)] = nn_dot(
                left, pack_ref[s, pl.ds(first, vcols)]
            ).astype(jnp.bfloat16)
        return carry

    lax.fori_loop(0, 8, project, 0)
    run(scatter_steps(part_ref, residual_ref, pair_ref, sum_ref, got_ref, Sender(sems)))

    def body(r, carry):
        acc = jnp.zeros((ROW_STEP, LANES), jnp.float32)
        for k in range(width // LANES):
            v = residual_ref[r, lanes(k)] + x_ref[r, lanes(k)].astype(jnp.float32)
            residual_ref[r, lanes(k)] = v
            acc += v * v
        scale = lax.rsqrt(mean_of(acc, width) + norm_epsilon)
        for k in range(width // LANES):
            normed_ref[r, lanes(k)] = (
                residual_ref[r, lanes(k)] * scale * small_ref[k, 1:2, :]
            ).astype(jnp.bfloat16)
        return carry

    row_blocks(m, ROW_STEP, body)(0)


def scatter_scratch(m, width):
    return [
        pltpu.VMEM((4, m, width), jnp.bfloat16),
        pltpu.VMEM((3, m, width), jnp.bfloat16),
        pltpu.VMEM((3, m, width), jnp.bfloat16),
    ]


def branch(mixed, pack, x, small, cid):
    m, width = x.shape
    whole = pltpu.VMEM
    return kernel_call(
        branch_kernel,
        "branch",
        cid,
        [((m, width), jnp.float32, whole), ((m, width), jnp.bfloat16, whole)],
        [(mixed, whole), (pack, whole), (x, whole), (small, whole)],
        [pltpu.VMEM((4, 2, m, width), jnp.bfloat16)]
        + scatter_scratch(m, width)
        + [copies(SCATTER_COPIES)],
        moved=x.size * 80,
    )


def parity(i):
    return i % 2 if isinstance(i, int) else lax.rem(i, 2)


def choose(test, a, b):
    if isinstance(test, bool):
        return a if test else b
    return jnp.where(test, a, b)


def project(at, w_ref, rows):
    parts, _, depth = w_ref.shape
    total = nt_dot(at(pl.ds(0, depth)), w_ref[0, rows])
    for s in range(1, parts):
        total += nt_dot(at(pl.ds(s * depth, depth)), w_ref[s, rows])
    return total


def arrivals(i, half):
    at, x_at, y_at, d_at, core = plane_places()
    k = choose(parity(i) == 0, core, 1 - core)
    one = choose(i < 2, at, choose(i < 6, x_at, d_at))
    two = choose(i < 2, at, choose(i < 6, y_at, d_at))
    late = (i >= 4) & (i < 6)
    late = int(late) if isinstance(late, bool) else late.astype(jnp.int32)
    first, second = late * half, (1 - late) * half
    if not isinstance(i, int):
        first, second = pl.multiple_of(first, half), pl.multiple_of(second, half)
    return (one, k, first), (two, k, second)


def stacked_copies(early, late, out, sems):
    rows = early.shape[1]
    return [
        pltpu.make_async_copy(early, out.at[:, pl.ds(0, rows)], sems.at[0]),
        pltpu.make_async_copy(late, out.at[:, pl.ds(rows, late.shape[1])], sems.at[1]),
    ]


def expand_kernel(
    own_ref,
    early_hbm,
    late_hbm,
    normed_hbm,
    gate_hbm,
    up_hbm,
    hidden_hbm,
    normed_ref,
    w_ref,
    gate_ref,
    up_ref,
    hidden_ref,
    sems,
    local_sem,
    w_sems,
    store_sems,
    keep_sem,
):
    greet_plane()
    half = own_ref.shape[0] // 2
    units = gate_ref.shape[2]
    gather = gather_steps(own_ref, normed_ref, Sender(sems), local_sem)
    next(gather)
    weights = stacked_copies(early_hbm, late_hbm, w_ref, w_sems)
    for c in weights:
        c.start()

    def store_copies(i):
        slot = parity(i)
        found = []
        for n, (c, k, r) in enumerate(arrivals(i, half)):
            rows = pl.ds(n * half, half)
            column = (c * 2 + k) * (2 * half) + r
            pairs = (
                (gate_ref.at[slot, rows], gate_hbm.at[c, k, pl.ds(r, half)]),
                (up_ref.at[slot, rows], up_hbm.at[c, k, pl.ds(r, half)]),
                (
                    hidden_ref.at[slot, :, rows],
                    hidden_hbm.at[:, pl.ds(pl.multiple_of(column, half), half)],
                ),
            )
            for q, (a, b) in enumerate(pairs):
                found.append(pltpu.make_async_copy(a, b, store_sems.at[slot, 3 * n + q]))
        return found

    next(gather)
    for c in weights:
        c.wait()

    def body(i, carry):
        for step in range(1, 8):

            @pl.when(i == step)
            def _():
                next(gather)

        @pl.when(i >= 2)
        def _():
            for c in store_copies(i - 2):
                c.wait()

        slot = parity(i)
        pieces = arrivals(i, half)

        def columns(cols):
            return jnp.concatenate([normed_ref[c, k, pl.ds(r, half), cols] for c, k, r in pieces])

        gate = project(columns, w_ref, pl.ds(0, units))
        up = project(columns, w_ref, pl.ds(units, units))
        gate_ref[slot], up_ref[slot] = gate, up
        hidden_ref[slot] = (gate * jax.nn.sigmoid(gate) * up).astype(jnp.bfloat16).T
        for c in store_copies(i):
            c.start()
        return carry

    lax.fori_loop(0, 8, body, 0)
    keep = pltpu.make_async_copy(normed_ref, normed_hbm, keep_sem)
    keep.start()
    for i in (6, 7):
        for c in store_copies(i):
            c.wait()
    keep.wait()
    run(gather)


def expand(own, early, late, cid):
    m, width = own.shape
    weights = (early.shape[0], early.shape[1] + late.shape[1], early.shape[2])
    units = weights[1] // 2
    low = jnp.bfloat16
    thin = ((4, 2, m, units), jnp.float32, pl.ANY)
    normed, gate, up, hidden = kernel_call(
        expand_kernel,
        "expand",
        cid,
        [((4, 2, m, width), low, pl.ANY), thin, thin, ((units, 8 * m), low, pl.ANY)],
        [(own, pltpu.VMEM), (early, pl.ANY), (late, pl.ANY)],
        [
            pltpu.VMEM((4, 2, m, width), low),
            pltpu.VMEM(weights, low),
            pltpu.VMEM((2, m, units), jnp.float32),
            pltpu.VMEM((2, m, units), jnp.float32),
            pltpu.VMEM((2, units, m), low),
            copies(GATHER_COPIES),
            pltpu.SemaphoreType.DMA,
            pltpu.SemaphoreType.DMA((2,)),
            pltpu.SemaphoreType.DMA((2, 6)),
            pltpu.SemaphoreType.DMA,
        ],
        flops=32 * m * width * units,
        moved=1 << 27,
    )
    flat = (8 * m, units)
    return normed.reshape(8 * m, width), gate.reshape(flat), up.reshape(flat), hidden


def hidden_kernel(
    gate_ref,
    up_ref,
    cot_ref,
    early_hbm,
    late_hbm,
    down_hbm,
    out_ref,
    dnormed_ref,
    dgate_ref,
    dup_ref,
    w_ref,
    down_w_ref,
    w_sems,
):
    parts, units, depth = down_w_ref.shape

    @pl.when(pl.program_id(0) == 0)
    def _():
        weights = stacked_copies(early_hbm, late_hbm, w_ref, w_sems)
        weights.append(pltpu.make_async_copy(down_hbm, down_w_ref, w_sems.at[2]))
        for c in weights:
            c.start()
        for c in weights:
            c.wait()

    gate, up = gate_ref[...], up_ref[...]
    dhidden = project(lambda cols: cot_ref[:, cols], down_w_ref, pl.ds(0, units))
    sig = jax.nn.sigmoid(gate)
    silu = gate * sig
    hidden = (silu * up).astype(jnp.bfloat16)
    dgate = (dhidden * up * sig * (1.0 + gate * (1.0 - sig))).astype(jnp.bfloat16)
    dup = (dhidden * silu).astype(jnp.bfloat16)
    for s in range(parts):
        cols = pl.ds(s * depth, depth)
        dnormed_ref[:, cols] = (
            nn_dot(dgate, w_ref[s, pl.ds(0, units)]) + nn_dot(dup, w_ref[s, pl.ds(units, units)])
        ).astype(jnp.bfloat16)
        out_ref[:, cols] = nn_dot(hidden, down_w_ref[s]).astype(jnp.bfloat16)
    dgate_ref[...], dup_ref[...] = dgate.T, dup.T


def hidden_units(gate, up, cot, early, late, down_w, block=256):
    tokens, units = gate.shape
    width = cot.shape[1]
    low = jnp.bfloat16
    wide = pl.BlockSpec((block, width), lambda i: (i, 0))
    thin = pl.BlockSpec((block, units), lambda i: (i, 0))
    turned = pl.BlockSpec((units, block), lambda i: (0, i))
    anywhere = pl.BlockSpec(memory_space=pl.ANY)
    stacked = (early.shape[0], early.shape[1] + late.shape[1], early.shape[2])
    return pl.pallas_call(
        hidden_kernel,
        name="hidden_units",
        grid=(tokens // block,),
        out_shape=[jax.ShapeDtypeStruct((tokens, width), low)] * 2
        + [jax.ShapeDtypeStruct((units, tokens), low)] * 2,
        in_specs=[thin, thin, wide, anywhere, anywhere, anywhere],
        out_specs=[wide, wide, turned, turned],
        scratch_shapes=[
            pltpu.VMEM(stacked, low),
            pltpu.VMEM(down_w.shape, low),
            pltpu.SemaphoreType.DMA((3,)),
        ],
        compiler_params=pltpu.CompilerParams(vmem_limit_bytes=VMEM_LIMIT),
        cost_estimate=pl.CostEstimate(
            flops=8 * tokens * width * units,
            bytes_accessed=1 << 27,
            transcendentals=tokens * units,
        ),
    )(gate, up, cot, early, late, down_w)


def norm_gradient(r, value_at, grad_ref, gain_at, gain_grad, finish, width):
    squares = jnp.zeros((ROW_STEP, LANES), jnp.float32)
    cross = jnp.zeros((ROW_STEP, LANES), jnp.float32)
    for k in range(width // LANES):
        v = value_at(r, k)
        squares += v * v
        cross += v * grad_ref[r, lanes(k)] * gain_at(k)
    scale = lax.rsqrt(mean_of(squares, width) + norm_epsilon)
    pull = mean_of(cross, width) * scale * scale * scale
    for k in range(width // LANES):
        v, g = value_at(r, k), grad_ref[r, lanes(k)]
        gain_grad[:, lanes(k)] += jnp.sum(
            (g * v * scale).reshape(ROW_STEP // 8, 8, LANES), axis=0
        )
        finish(r, k, scale * g * gain_at(k) - v * pull)


def middle_kernel(
    part_hbm,
    normed_hbm,
    dgate_hbm,
    dup_hbm,
    total_ref,
    grads_hbm,
    held_ref,
    pair_ref,
    sum_ref,
    got_ref,
    normed_ref,
    left_ref,
    grad_ref,
    sems,
    held_sems,
    load_sems,
    store_sems,
):
    greet_plane()
    scatter = scatter_steps(
        part_hbm, total_ref, pair_ref, sum_ref, got_ref, Sender(sems), (held_ref, held_sems)
    )
    next(scatter)
    loads = [
        pltpu.make_async_copy(a, b, load_sems.at[n])
        for n, (a, b) in enumerate(
            (
                (dgate_hbm, left_ref.at[0]),
                (normed_hbm, normed_ref),
                (dup_hbm, left_ref.at[1]),
            )
        )
    ]
    for c in loads:
        c.start()
    next(scatter)
    width = grad_ref.shape[2]
    blocks = normed_ref.shape[1] // width

    def gradients(which):
        rows = pl.ds(which * grad_ref.shape[1], grad_ref.shape[1])

        def stored(i):
            column = pl.ds(pl.multiple_of(i * width, width), width)
            slot = parity(i)
            return pltpu.make_async_copy(
                grad_ref.at[slot], grads_hbm.at[rows, column], store_sems.at[slot]
            )

        def body(i, carry):
            column = pl.ds(pl.multiple_of(i * width, width), width)

            @pl.when(i >= 2)
            def _():
                stored(i - 2).wait()

            grad_ref[lax.rem(i, 2)] = nn_dot(left_ref[which], normed_ref[:, column]).astype(
                jnp.bfloat16
            )
            stored(i).start()
            return carry

        lax.fori_loop(0, blocks, body, 0)
        for i in (blocks - 2, blocks - 1):
            stored(i).wait()

    loads[0].wait()
    loads[1].wait()
    gradients(0)
    next(scatter)
    loads[2].wait()
    gradients(1)
    run(scatter)


def middle(part, normed, dgate, dup, cid):
    m, width = part.shape[0] // 8, part.shape[1]
    part = part.reshape(4, 2, m, width)
    units, tokens = dgate.shape
    low = jnp.bfloat16
    return kernel_call(
        middle_kernel,
        "middle",
        cid,
        [
            ((m, width), jnp.float32, pltpu.VMEM),
            ((2 * units, width), low, pl.ANY),
        ],
        [(a, pl.ANY) for a in (part, normed, dgate, dup)],
        [pltpu.VMEM((4, m, width), low)]
        + scatter_scratch(m, width)
        + [
            pltpu.VMEM((tokens, width), low),
            pltpu.VMEM((2, units, tokens), low),
            pltpu.VMEM((2, units, 256), low),
            copies(SCATTER_COPIES),
            pltpu.SemaphoreType.DMA((4,)),
            pltpu.SemaphoreType.DMA((3,)),
            pltpu.SemaphoreType.DMA((2,)),
        ],
        flops=4 * units * tokens * width,
        moved=m * width * 80,
    )


def turn_kernel(
    total_ref,
    residual_ref,
    cot_ref,
    small_ref,
    pack_ref,
    mixed_ref,
    dresid_ref,
    gain_ref,
    dmixed_ref,
    grad_ref,
    all_ref,
    low_ref,
    sum_ref,
    gather_sems,
    local_sem,
):
    greet_plane()
    m, width = residual_ref.shape
    half = m // 2
    parts, _, depth = pack_ref.shape
    vcols = mixed_ref.shape[3]
    first_row = pack_ref.shape[1] - vcols
    gain_ref[...] = jnp.zeros_like(gain_ref)

    def finish(r, k, v):
        v += cot_ref[r, lanes(k)].astype(jnp.float32)
        dresid_ref[r, lanes(k)] = v
        low_ref[r, lanes(k)] = v.astype(jnp.bfloat16)

    def body(r, carry):
        norm_gradient(
            r,
            lambda r, k: residual_ref[r, lanes(k)],
            total_ref,
            lambda k: small_ref[k, 1:2, :],
            gain_ref,
            finish,
            width,
        )
        return carry

    row_blocks(m, ROW_STEP, body)(0)
    gather = gather_steps(low_ref, all_ref, Sender(gather_sems), local_sem)
    next(gather)
    sum_ref[...] = jnp.zeros_like(sum_ref)
    next(gather)

    def block(i, carry):
        for step in range(1, 8):

            @pl.when(i == step)
            def _():
                next(gather)

        pieces = arrivals(i, half)

        def columns(cols):
            return jnp.concatenate([all_ref[c, k, pl.ds(r, half), cols] for c, k, r in pieces])

        left = jnp.concatenate([mixed_ref[c, k, pl.ds(r, half)] for c, k, r in pieces])
        dmixed = project(columns, pack_ref, pl.ds(first_row, vcols)).astype(jnp.bfloat16)
        for n, (c, k, r) in enumerate(pieces):
            dmixed_ref[c, k, pl.ds(r, half)] = dmixed[n * half : (n + 1) * half]
        for s in range(parts):
            cols = pl.ds(s * depth, depth)
            sum_ref[:, cols] += tn_dot(left, columns(cols))
        return carry

    lax.fori_loop(0, 8, block, 0)
    grad_ref[...] = sum_ref[...].astype(jnp.bfloat16)
    run(gather)


def turn(total, residual, cot_own, small, pack, mixed, cid):
    m, width = residual.shape
    vcols = mixed.shape[1]
    whole, low = pltpu.VMEM, jnp.bfloat16
    dresid, gain, dmixed, grad = kernel_call(
        turn_kernel,
        "turn",
        cid,
        [
            ((m, width), jnp.float32, whole),
            ((8, width), jnp.float32, whole),
            ((4, 2, m, vcols), low, whole),
            ((vcols, width), low, whole),
        ],
        [(a, whole) for a in (total, residual, cot_own, small, pack)]
        + [(mixed.reshape(4, 2, m, vcols), whole)],
        [
            pltpu.VMEM((4, 2, m, width), low),
            pltpu.VMEM((m, width), low),
            pltpu.VMEM((vcols, width), jnp.float32),
            copies(GATHER_COPIES),
            pltpu.SemaphoreType.DMA,
        ],
        moved=residual.size * 80,
    )
    return dresid, gain, dmixed.reshape(8 * m, vcols), grad


def unmix_kernel(
    heads,
    count,
    dmixed_ref,
    normed_hbm,
    output_grad_ref,
    part_ref,
    residual_ref,
    col_ref,
    row_ref,
    pairs_ref,
    qkv_ref,
    exact_ref,
    den_ref,
    state_ref,
    sums_ref,
    *refs,
):
    ins, dqkv_ref, block_ref, grad_ref = refs[:count], *refs[count : count + 3]
    outs = refs[count + 3 : 2 * count + 3]
    (
        normed_ref,
        turned_ref,
        dvalue_ref,
        dtile_ref,
        back_ref,
        back_sums_ref,
        pick_ref,
        own_ref,
        own_sums_ref,
        out_ref,
        out_sums_ref,
        total_ref,
        held_ref,
        pair_ref,
        sum_ref,
        got_ref,
        sems,
        shard_sems,
        local_sems,
        scatter_sems,
        held_sems,
        normed_sem,
    ) = refs[2 * count + 3 :]
    rows, length = col_ref.shape[0], col_ref.shape[1]
    vcols, qcols = heads * VHEAD, heads * FDIM
    at, x_at, y_at, _, core = plane_places()
    plane, span, z = lax.axis_size("dp"), lax.axis_size("seq"), lax.axis_index("seq")
    chips = [lax.rem(at + k, plane) for k in range(1, plane)]
    normed_copy = pltpu.make_async_copy(normed_hbm, normed_ref, normed_sem)
    normed_copy.start()
    back_ref[...] = jnp.zeros_like(back_ref)
    back_sums_ref[...] = jnp.zeros_like(back_sums_ref)
    greet(
        [{"dp": p} for p in chips]
        + [{"tensor": 1 - core}]
        + [{"seq": lax.rem(z + k, span)} for k in (1, span - 1)]
    )
    scatter = scatter_steps(
        part_ref,
        total_ref,
        pair_ref,
        sum_ref,
        got_ref,
        Sender(scatter_sems),
        (held_ref, held_sems),
    )
    next(scatter)
    chain = Chain(
        False,
        col_ref,
        row_ref,
        back_ref,
        back_sums_ref,
        (own_ref, own_sums_ref, out_ref, out_sums_ref),
        sems,
    )
    fill_selectors(pairs_ref, pick_ref, qcols)
    scale = feature_scale(pairs_ref)

    def tokens_of(b):
        return pl.ds(pl.multiple_of(b * length, length), length)

    def cotangents(t, h):
        v = pl.ds(h * VHEAD, VHEAD)
        dn = dmixed_ref[t, v].astype(jnp.float32) / den_ref[t, pl.ds(h, 1)]
        dd = -jnp.sum(dn * exact_ref[t, v], axis=1, keepdims=True)
        return dn.astype(jnp.bfloat16), dd

    def first(b, carry):
        t = tokens_of(b)
        head = Segments(col_ref, row_ref, b).head
        tile = qkv_ref[t, pl.ds(vcols, LANES)]
        for h in range(heads):
            dn, dd = cotangents(t, h)
            one, two = factors(tile, pick_ref, 0, h)
            lifted = jnp.where(head, one * two, 0.0)
            own_ref[b, h] = tn_dot(lifted.astype(jnp.bfloat16), dn)
            own_sums_ref[b, h : h + 1] = jnp.sum(lifted * dd, axis=0, keepdims=True)
        return carry

    own_sums_ref[...] = jnp.zeros_like(own_sums_ref)
    shards = swap_shards(ins, outs, chips, at, columns_of, block_of, Sender(shard_sems), local_sems)

    def lowered(dlifted, kind, h, one, two):
        return nt_dot((dlifted * two).astype(jnp.bfloat16), pick_ref[kind, h, 0]) + nt_dot(
            (dlifted * one).astype(jnp.bfloat16), pick_ref[kind, h, 1]
        )

    def here(b, carry):
        t = tokens_of(b)
        seg = Segments(col_ref, row_ref, b)
        tile = qkv_ref[t, pl.ds(vcols, LANES)]
        key = keys_in_place(tile, qcols)
        dtile = jnp.zeros((length, LANES), jnp.float32)
        dkey = jnp.zeros((length, LANES), jnp.float32)
        for h in range(heads):
            inside = head_mask(length, h)
            v = pl.ds(h * VHEAD, VHEAD)
            query = jnp.where(inside, tile, jnp.zeros_like(tile))
            dn, dd = cotangents(t, h)
            a, w, keep = masked_weights(query, key, seg.column, seg.row)
            dw = jnp.where(keep, nt_dot(dn, qkv_ref[t, v]) + dd, 0.0)
            da = (dw * (1.0 + a) * 0.25).astype(jnp.bfloat16)
            dvalue_ref[t, v] = tn_dot(w.astype(jnp.bfloat16), dn)
            dtile += jnp.where(inside, nn_dot(da, key), 0.0)
            dkey += jnp.where(inside, tn_dot(da, query), 0.0)
            one, two = factors(tile, pick_ref, 0, h)
            dlifted = nt_dot(dn, state_ref[b, h]) + dd * sums_ref[b, h : h + 1]
            dtile += lowered(jnp.where(seg.head, dlifted, 0.0), 0, h, one, two)
        dtile_ref[t] = dtile + pltpu.roll(dkey, qcols, axis=1)
        return carry

    def after(b, carry):
        t = tokens_of(b)
        tail = Segments(col_ref, row_ref, b).tail
        tile = qkv_ref[t, pl.ds(vcols, LANES)]
        dtile = dtile_ref[t]
        for h in range(heads):
            v = pl.ds(h * VHEAD, VHEAD)
            one, two = factors(tile, pick_ref, 1, h)
            lifted = jnp.where(tail, one * two * scale, 0.0)
            dlifted = nt_dot(qkv_ref[t, v], back_ref[b, h]) + back_sums_ref[b, h : h + 1]
            dtile += lowered(jnp.where(tail, dlifted * scale, 0.0), 1, h, one, two)
            dvalue = dvalue_ref[t, v] + nn_dot(lifted.astype(jnp.bfloat16), back_ref[b, h])
            dqkv_ref[t, v] = dvalue.astype(jnp.bfloat16)
        lane = lax.broadcasted_iota(jnp.int32, (length, LANES), 1)
        dqkv_ref[t, pl.ds(vcols, LANES)] = jnp.where(lane < 2 * qcols, dtile, 0.0).astype(
            jnp.bfloat16
        )
        turned_ref[:, t] = dqkv_ref[t].T
        return carry

    each = rows // CHUNKS

    def work(n, step):
        @pl.when(n < CHUNKS)
        def _():
            lax.fori_loop(n * each, (n + 1) * each, first, 0)

        step(n)

        @pl.when(n < CHUNKS)
        def _():
            lax.fori_loop(n * each, (n + 1) * each, here, 0)

    def advance():
        next(scatter)

    chain.run(work, [lambda: None, advance, lambda: None, lambda: None, advance])
    lax.fori_loop(0, rows, after, 0)
    run(scatter)

    def finish(r, carry):
        block_ref[r] = (residual_ref[r] + total_ref[r]).astype(jnp.bfloat16)
        return carry

    row_blocks(block_ref.shape[0], ROW_STEP, finish)(0)
    normed_copy.wait()
    wide = 4 * LANES
    qkv_rows = grad_ref.shape[0] - vcols
    grad_ref[pl.ds(qkv_rows, vcols)] = output_grad_ref[...]

    def gradient(i, carry):
        cols = pl.ds(pl.multiple_of(i * wide, wide), wide)
        grad_ref[pl.ds(0, qkv_rows), cols] = nn_dot(
            turned_ref[pl.ds(0, qkv_rows)], normed_ref[:, cols]
        ).astype(jnp.bfloat16)
        return carry

    lax.fori_loop(0, normed_ref.shape[1] // wide, gradient, 0)
    for c in shards:
        c.wait()
    chain.close()


def unmix(dmixed, normed, output_grad, part, residual, segments, pairs, kept, shards, heads, cid):
    seg_col, seg_row = segments
    tokens, vcols = dmixed.shape
    plane, rows = lax.axis_size("dp"), seg_col.shape[0]
    grad_rows = 2 * vcols + 2 * heads * FDIM
    m, width = residual.shape
    count = len(shards)
    whole, low = pltpu.VMEM, jnp.bfloat16
    dqkv, block, grad, *swapped = kernel_call(
        partial(unmix_kernel, heads, count),
        "unmix",
        cid,
        [
            ((tokens, vcols + LANES), low, whole),
            ((m, width), low, whole),
            ((grad_rows, width), low, whole),
        ]
        + [((plane, p.shape[0], p.shape[1] // plane), p.dtype, pl.ANY) for p in shards],
        [
            (dmixed, whole),
            (normed, pl.ANY),
            (output_grad, whole),
            (part.reshape(4, 2, m, width), pl.ANY),
            (residual, whole),
            (seg_col, whole),
            (seg_row, whole),
            (pairs, whole),
        ]
        + [(a, whole) for a in kept]
        + [(p, pl.ANY) for p in shards],
        [
            pltpu.VMEM((tokens, width), low),
            pltpu.VMEM((vcols + LANES, tokens), low),
            pltpu.VMEM((tokens, vcols), jnp.float32),
            pltpu.VMEM((tokens, LANES), jnp.float32),
            pltpu.VMEM((rows, heads, FEATURES, VHEAD), low),
            pltpu.VMEM((rows, 8, FEATURES), jnp.float32),
        ]
        + state_scratch(rows, heads)
        + [pltpu.VMEM((m, width), jnp.float32), pltpu.VMEM((4, m, width), low)]
        + scatter_scratch(m, width)
        + [
            copies(2 * CHUNKS),
            copies(count * (plane - 1)),
            pltpu.SemaphoreType.DMA((count,)),
            copies(SCATTER_COPIES),
            pltpu.SemaphoreType.DMA((4,)),
            pltpu.SemaphoreType.DMA,
        ],
        moved=residual.size * 120,
    )
    return dqkv, block, grad, swapped


def last_kernel(count, *refs):
    ins, gain_ref, outs, sum_ref = (
        refs[:count],
        refs[count],
        refs[count + 1 : 2 * count + 1],
        refs[2 * count + 1],
    )
    got_gain, sems, gain_sems, local_sems = refs[2 * count + 2 :]
    plane, at = lax.axis_size("dp"), lax.axis_index("dp")
    others, me = everyone()
    greet(others)
    copy_gain = Sender(gain_sems)
    gains = [
        copy_gain(gain_ref.at[p["seq"] * plane + p["dp"]], got_gain.at[me], p) for p in others
    ]
    for c in gains:
        c.start()
    chips = [lax.rem(at + k, plane) for k in range(1, plane)]
    shards = swap_shards(ins, outs, chips, at, columns_of, block_of, Sender(sems), local_sems)
    got_gain[me] = gain_ref[lax.axis_index("seq") * plane + at]
    for c in gains:
        c.wait()
    total = got_gain[0]
    for k in range(1, len(others) + 1):
        total += got_gain[k]
    sum_ref[...] = total
    for c in shards:
        c.wait()


def last(shards, gains, cid):
    plane = lax.axis_size("dp")
    count = len(shards)
    devices = lax.axis_size(("dp", "seq", "tensor"))
    *swapped, total = kernel_call(
        partial(last_kernel, count),
        "last",
        cid,
        [((plane, p.shape[0], p.shape[1] // plane), p.dtype, pl.ANY) for p in shards]
        + [(gains.shape[1:], jnp.float32, pltpu.VMEM)],
        [(p, pl.ANY) for p in shards] + [(gains, pltpu.VMEM)],
        [
            pltpu.VMEM((devices,) + gains.shape[1:], jnp.float32),
            copies(count * (plane - 1)),
            copies(devices - 1),
            pltpu.SemaphoreType.DMA((count,)),
        ],
        moved=1 << 26,
    )
    return swapped, total


def everyone():
    plane, span, cores = (lax.axis_size(a) for a in ("dp", "seq", "tensor"))
    at, z, core = (lax.axis_index(a) for a in ("dp", "seq", "tensor"))
    others = [
        {
            "dp": lax.rem(at + i, plane),
            "seq": lax.rem(z + k, span),
            "tensor": lax.rem(core + c, cores),
        }
        for k in range(span)
        for i in range(plane)
        for c in range(cores)
        if i or k or c
    ]
    return others, (at * span + z) * cores + core


def exit_kernel(
    dqkv_ref,
    pack_ref,
    x_ref,
    dresid_ref,
    block_ref,
    small_ref,
    gain_two_ref,
    shards_ref,
    grad_ref,
    out_ref,
    gains_ref,
    shards_all_ref,
    gain_ref,
    part_ref,
    total_ref,
    ordered_ref,
    low_ref,
    pair_ref,
    sum_ref,
    got_ref,
    sems,
    pair_sems,
    local_sems,
    shard_sems,
    shard_local_sems,
):
    plane, at = lax.axis_size("dp"), lax.axis_index("dp")
    core = lax.axis_index("tensor")
    chips = [lax.rem(at + k, plane) for k in range(1, plane)]
    greet([{"dp": p} for p in chips] + [{"tensor": 1 - core}])
    shard_copy = Sender(shard_sems)

    half = shards_ref.shape[0] // 2

    def swap(n):
        rows = pl.ds(n * half, half)
        return swap_shards(
            (shards_ref,),
            (shards_all_ref,),
            chips,
            at,
            lambda ref, p: columns_of(ref, p, rows),
            lambda ref, p: ref.at[p, rows],
            shard_copy,
            shard_local_sems.at[pl.ds(n, 1)],
        )

    shards = swap(0)
    parts, _, depth = pack_ref.shape
    m, width = x_ref.shape
    wide = dqkv_ref.shape[1] - LANES + 2 * FDIM * ((dqkv_ref.shape[1] - LANES) // VHEAD)
    blocks = width // LANES
    copy = Sender(pair_sems)

    def project(b, carry):
        left = dqkv_ref[pl.ds(pl.multiple_of(b * m, m), m), pl.ds(0, wide)]
        for s in range(parts):
            part_ref[b // 2, lax.rem(b, 2), :, pl.ds(s * depth, depth)] = nn_dot(
                left, pack_ref[s, pl.ds(0, wide)]
            ).astype(jnp.bfloat16)
        return carry

    lax.fori_loop(0, 8, project, 0)
    scatter = scatter_steps(part_ref, total_ref, pair_ref, sum_ref, got_ref, Sender(sems))
    next(scatter)

    def order(r, carry):
        for k in range(blocks):
            low_ref[r, lanes(seq_major_block(k))] = block_ref[r, lanes(k)]
        return carry

    row_blocks(m, ROW_STEP, order)(0)
    to_pair = [copy(low_ref, out_ref.at[core], {"tensor": 1 - core})]
    local = [pltpu.make_async_copy(low_ref, out_ref.at[core], local_sems.at[0])]
    to_pair[0].start()
    local[0].start()
    next(scatter)
    next(scatter)
    shards += swap(1)
    run(scatter)
    gain_ref[...] = jnp.zeros_like(gain_ref)

    def finish(r, k, v):
        ordered_ref[r, lanes(seq_major_block(k))] = v + dresid_ref[r, lanes(k)]

    def body(r, carry):
        norm_gradient(
            r,
            lambda r, k: x_ref[r, lanes(k)].astype(jnp.float32),
            total_ref,
            lambda k: small_ref[k, 0:1, :],
            gain_ref,
            finish,
            width,
        )
        return carry

    row_blocks(m, ROW_STEP, body)(0)
    to_pair.append(copy(ordered_ref, grad_ref.at[core], {"tensor": 1 - core}))
    local.append(pltpu.make_async_copy(ordered_ref, grad_ref.at[core], local_sems.at[1]))
    to_pair[1].start()
    local[1].start()
    gains_ref[...] = jnp.zeros_like(gains_ref)
    for k in range(blocks):
        for row, ref in enumerate((gain_ref, gain_two_ref)):
            gains_ref[k, row : row + 1] = jnp.sum(ref[:, lanes(k)], axis=0, keepdims=True)
    for c in to_pair + local + shards:
        c.wait()


def leave(dqkv, pack, x, dresid, block, small, gain_two, shards, cid):
    m, width = x.shape
    plane = lax.axis_size("dp")
    whole = pltpu.VMEM
    return kernel_call(
        exit_kernel,
        "leave",
        cid,
        [
            ((2, m, width), jnp.float32, pl.ANY),
            ((2, m, width), jnp.bfloat16, pl.ANY),
            ((width // LANES, 8, LANES), jnp.float32, whole),
        ]
        + [((plane, p.shape[0], p.shape[1] // plane), p.dtype, pl.ANY) for p in shards],
        [(a, whole) for a in (dqkv, pack, x, dresid, block, small, gain_two)]
        + [(p, pl.ANY) for p in shards],
        [
            pltpu.VMEM((8, width), jnp.float32),
            pltpu.VMEM((4, 2, m, width), jnp.bfloat16),
            pltpu.VMEM((m, width), jnp.float32),
            pltpu.VMEM((m, width), jnp.float32),
            pltpu.VMEM((m, width), jnp.bfloat16),
        ]
        + scatter_scratch(m, width)
        + [
            copies(SCATTER_COPIES),
            copies(2),
            pltpu.SemaphoreType.DMA((2,)),
            copies(2 * (plane - 1)),
            pltpu.SemaphoreType.DMA((2,)),
        ],
        moved=x.size * 120,
    )


def plane_local(
    tokens,
    doc_starts,
    attn_gain,
    mlp_gain,
    query_weight,
    key_weight,
    value_weight,
    output_weight,
    gate_weight,
    up_weight,
    down_weight,
    cotangent,
):
    plane, span, cores = (lax.axis_size("dp"), lax.axis_size("seq"), lax.axis_size("tensor"))
    rows, length, width = tokens.shape
    chunk = width // (plane * span)
    own = rows * length // cores
    heads = query_weight.shape[1] // FDIM // plane
    hidden_part = gate_weight.shape[1] // plane
    vcols, qcols = heads * VHEAD, heads * FDIM

    def over_seq(pack):
        return lax.all_gather(pack, "seq", axis=0, tiled=False)

    def summed(grads):
        return lax.psum_scatter(
            grads.astype(jnp.bfloat16), "seq", scatter_dimension=1, tiled=True
        )

    def split(w):
        return w.reshape(plane, -1, chunk)

    small = jnp.concatenate(
        [
            attn_gain.astype(jnp.float32)[None],
            mlp_gain.astype(jnp.float32)[None],
            doc_starts.astype(jnp.float32).reshape(-1, chunk),
            jnp.zeros((2, chunk), jnp.float32),
        ]
    )
    attn_pack = jnp.concatenate(
        [split(value_weight.T), split(query_weight.T), split(key_weight.T), split(output_weight)],
        axis=1,
    )
    [attn_pack] = exchange(
        [attn_pack], 1, [(attn_pack.shape[1], plane * chunk)], put=columns_of
    )
    gate_w = split(gate_weight.T)
    early_w = gate_w[:, :EARLY]
    late_w = jnp.concatenate([gate_w[:, EARLY:], split(up_weight.T)], axis=1)
    early_w, late_w, small = lax.optimization_barrier((early_w, late_w, small, attn_pack))[:3]
    early_w, late_w, small = first_exchange([early_w, late_w], small, 2)
    attn_pack, early_w = over_seq(attn_pack), over_seq(early_w)
    starts = small[:, 2:-2].reshape(span, plane * rows, length)
    segments = jnp.cumsum(
        lax.dynamic_index_in_dim(starts, lax.axis_index("seq"), 0, keepdims=False), axis=1
    )

    qkv_rows = vcols + 2 * qcols
    seg_col = segments[:, :, None]
    seg_row = segments[:, None, :]
    pairs = feature_pairs()
    normed_one, x, cot_own = entry(
        tokens.reshape(cores, own, width), cotangent.reshape(cores, own, width), small, 3
    )
    qkv, state, sums, down_w = states(
        normed_one, attn_pack, seg_col, seg_row, pairs, split(down_weight), heads, 4
    )
    late_w, down_w = lax.optimization_barrier((late_w, down_w))
    late_w, down_w = over_seq(late_w), over_seq(down_w)
    mixed, exact, den, cot = mix(
        qkv, seg_col, seg_row, pairs, state, sums, cot_own, heads, 13
    )
    residual, normed_own = branch(mixed, attn_pack, x, small, 5)
    normed_two, gate, up, hidden = expand(normed_own, early_w, late_w, 11)
    down_grad = nn_dot(hidden, cot).astype(jnp.bfloat16)
    gate, down_grad = lax.optimization_barrier((gate, down_grad))
    down_grad = summed(down_grad)
    out_part, dnormed_part, dgate, dup = hidden_units(
        gate, up, cot, early_w, late_w, down_w
    )
    dnormed_two, gate_up_grad = middle(dnormed_part, normed_two, dgate, dup, 6)
    gate_up_grad = summed(gate_up_grad)
    dresid, gain_two_grad, dmixed, out_grad = turn(
        dnormed_two, residual, cot_own, small, attn_pack, mixed, 12
    )
    dmixed, down_grad = lax.optimization_barrier((dmixed, down_grad))
    dqkv, block_own, attn_grad, (down_grad,) = unmix(
        dmixed,
        normed_one,
        out_grad,
        out_part,
        residual,
        (seg_col, seg_row),
        pairs,
        (qkv, exact, den, state, sums),
        [down_grad],
        heads,
        8,
    )
    attn_grad = summed(attn_grad)
    dtokens, block_out, gains, gate_up_grad = leave(
        dqkv, attn_pack, x, dresid, block_own, small, gain_two_grad, [gate_up_grad], 9
    )
    (attn_grad,), gain_grads = last([attn_grad], gains, 10)

    def stacked(a, start, size):
        return a[:, start : start + size].reshape(plane * size, chunk).astype(jnp.float32)

    h = hidden_part
    return (
        block_out.reshape(rows, length, width),
        dtokens.reshape(rows, length, width),
        gain_grads[0],
        gain_grads[1],
        stacked(attn_grad, vcols, qcols).T,
        stacked(attn_grad, vcols + qcols, qcols).T,
        stacked(attn_grad, 0, vcols).T,
        stacked(attn_grad, qkv_rows, vcols),
        stacked(gate_up_grad, 0, h).T,
        stacked(gate_up_grad, h, h).T,
        stacked(down_grad, 0, h),
    )


def fits_plane(mesh, tokens, query_weight, gate_weight):
    plane, span, cores = (mesh.shape[a] for a in ("dp", "seq", "tensor"))
    heads = query_weight.shape[1] // FDIM // cores
    return (
        plane == 4
        and cores == 2
        and heads % plane == 0
        and (gate_weight.shape[1] // cores) % (16 * plane) == 0
        and gate_weight.shape[1] // cores // plane > EARLY
        and tokens.shape[0] % CHUNKS == 0
    )


def solution(mesh):
    def step(*args):
        use = fits_plane(mesh, args[0], args[4], args[8])
        return sharded(mesh, plane_local if use else local)(*args)

    return step


def sharded(mesh, body):
    return jax.shard_map(
        body,
        mesh=mesh,
        in_specs=(
            P("dp", "seq", None),
            P("dp", "seq"),
            P(("dp", "seq")),
            P(("dp", "seq")),
            P(("dp", "seq"), "tensor"),
            P(("dp", "seq"), "tensor"),
            P(("dp", "seq"), "tensor"),
            P("tensor", ("dp", "seq")),
            P(("dp", "seq"), "tensor"),
            P(("dp", "seq"), "tensor"),
            P("tensor", ("dp", "seq")),
            P("dp", "seq", None),
        ),
        out_specs=(
            P("dp", "seq", None),
            P("dp", "seq", None),
            P(("dp", "seq")),
            P(("dp", "seq")),
            P(("dp", "seq"), "tensor"),
            P(("dp", "seq"), "tensor"),
            P(("dp", "seq"), "tensor"),
            P("tensor", ("dp", "seq")),
            P(("dp", "seq"), "tensor"),
            P(("dp", "seq"), "tensor"),
            P("tensor", ("dp", "seq")),
        ),
        check_vma=False,
    )
```

```python
from functools import partial

import jax
import jax.numpy as jnp
import numpy as np
from jax import lax
from jax.experimental import pallas as pl
from jax.experimental.pallas import tpu as pltpu
from jax.sharding import PartitionSpec as P

FDIM = 16
VHEAD = 128
MICRO = 2


norm_epsilon = 1e-05
highest = lax.Precision.HIGHEST
outer_scale = 0.17677669529663687


def prefix(x, axis, combine, identity, reverse):
    size, index = (lax.axis_size(axis), lax.axis_index(axis))
    everything = jax.tree.map(lambda part: lax.all_gather(part, axis), x)
    start = jax.tree.map(
        lambda part, zero: jnp.broadcast_to(jnp.asarray(zero, part.dtype), part.shape), x, identity
    )

    def turn(k, before):
        at = size - 1 - k if reverse else k
        reached = at > index if reverse else at < index
        new = combine(before, jax.tree.map(lambda part: part[at], everything))
        return jax.tree.map(lambda a, b: jnp.where(reached, a, b), new, before)

    return lax.fori_loop(0, size, turn, start)


def features(vectors):
    ones_col = jnp.ones(vectors.shape[:-1] + (1,), jnp.float32)
    outer_terms = vectors[..., :, None] * vectors[..., None, :] * outer_scale
    outer_terms = outer_terms.reshape(vectors.shape[:-1] + (vectors.shape[-1] * vectors.shape[-1],))
    return jnp.concatenate([ones_col, 0.5 * vectors, outer_terms], axis=-1)


def mix_span(queries, key_rows, values, state_in, norm_in, segments):
    length = queries.shape[1]
    scores = jnp.einsum("rthf,rshf->rhts", queries, key_rows, precision=highest) / 4.0
    kernel = 1.0 + scores + 0.5 * scores * scores
    position = jnp.arange(length)
    causal = position[None, :] <= position[:, None]
    allowed = causal[None] & (segments[:, :, None] == segments[:, None, :])
    kernel = jnp.where(allowed[:, None], kernel, 0.0)
    numerator = jnp.einsum("rhts,rshe->rthe", kernel, values, precision=highest)
    denominator = jnp.transpose(jnp.sum(kernel, axis=-1), (0, 2, 1))
    head_part = (segments == 0).astype(jnp.float32)[:, :, None]
    lifted = features(queries)
    numerator = numerator + head_part[..., None] * jnp.einsum(
        "rthf,rhfe->rthe", lifted, state_in, precision=highest
    )
    denominator = denominator + head_part * jnp.einsum(
        "rthf,rhf->rth", lifted, norm_in, precision=highest
    )
    return numerator / denominator[..., None]


def tail_span(key_rows, values, segments):
    tail_mask = (segments == segments[:, -1:]).astype(jnp.float32)
    lifted = features(key_rows) * tail_mask[:, :, None, None]
    tail_state = jnp.einsum("rshf,rshe->rhfe", lifted, values, precision=highest)
    return (tail_state, jnp.sum(lifted, axis=1))


def combine_carry(earlier_part, later_part):
    keep_rate = 1.0 - later_part[2]
    return (
        later_part[0] + keep_rate[:, None, None, None] * earlier_part[0],
        later_part[1] + keep_rate[:, None, None] * earlier_part[1],
        jnp.maximum(earlier_part[2], later_part[2]),
    )


def inverse_rms(inputs):
    return lax.rsqrt(jnp.mean(inputs * inputs, axis=-1, keepdims=True) + norm_epsilon)


def norm_backward(inputs, scale_row, gain_vec, grad_normed):
    scaled_grad = grad_normed * gain_vec
    grad_gain = jnp.sum(grad_normed * inputs * scale_row, axis=0)
    grad_inputs = scale_row * scaled_grad - inputs * scale_row * scale_row * scale_row * jnp.mean(
        scaled_grad * inputs, axis=-1, keepdims=True
    )
    return (grad_inputs, grad_gain)


def inner_rows(left_mat, right_mat):
    return lax.dot_general(
        left_mat, right_mat, (((0,), (0,)), ((), ())), preferred_element_type=jnp.float32
    )


def by_transpose(left_mat, right_mat):
    return lax.dot_general(
        left_mat, right_mat, (((1,), (1,)), ((), ())), preferred_element_type=jnp.float32
    )


def local(
    tokens,
    doc_starts,
    attn_gain,
    mlp_gain,
    query_weight,
    key_weight,
    value_weight,
    output_weight,
    gate_weight,
    up_weight,
    down_weight,
    cotangent,
):
    micro_rows = tokens.shape[0] // MICRO
    span_len = tokens.shape[1]
    model_width = tokens.shape[2]
    head_count = query_weight.shape[1] // FDIM
    outputs_main = []
    outputs_grad = []
    totals = None
    for micro_index in range(MICRO):
        row_start = micro_index * micro_rows
        rows_in = tokens[row_start : row_start + micro_rows]
        starts_in = doc_starts[row_start : row_start + micro_rows]
        cot_in = cotangent[row_start : row_start + micro_rows].reshape(-1, model_width)
        (
            full_query,
            full_key,
            full_value,
            full_gate,
            full_up,
            full_output,
            full_down,
            gain_one,
            gain_two,
        ) = (
            lax.all_gather(query_weight, ("dp", "seq"), axis=0, tiled=True),
            lax.all_gather(key_weight, ("dp", "seq"), axis=0, tiled=True),
            lax.all_gather(value_weight, ("dp", "seq"), axis=0, tiled=True),
            lax.all_gather(gate_weight, ("dp", "seq"), axis=0, tiled=True),
            lax.all_gather(up_weight, ("dp", "seq"), axis=0, tiled=True),
            lax.all_gather(output_weight, ("dp", "seq"), axis=1, tiled=True),
            lax.all_gather(down_weight, ("dp", "seq"), axis=1, tiled=True),
            lax.all_gather(attn_gain, ("dp", "seq"), axis=0, tiled=True),
            lax.all_gather(mlp_gain, ("dp", "seq"), axis=0, tiled=True),
        )
        gain_one_f = gain_one.astype(jnp.float32)
        gain_two_f = gain_two.astype(jnp.float32)
        flat_rows = rows_in.reshape(-1, model_width).astype(jnp.float32)
        scale_one = inverse_rms(flat_rows)
        normed_one = (flat_rows * scale_one * gain_one_f).astype(jnp.bfloat16)
        query_low = jnp.dot(normed_one, full_query, preferred_element_type=jnp.float32).astype(
            jnp.bfloat16
        )
        key_low = jnp.dot(normed_one, full_key, preferred_element_type=jnp.float32).astype(
            jnp.bfloat16
        )
        value_low = jnp.dot(normed_one, full_value, preferred_element_type=jnp.float32).astype(
            jnp.bfloat16
        )
        queries = query_low.astype(jnp.float32).reshape(micro_rows, span_len, head_count, FDIM)
        key_rows = key_low.astype(jnp.float32).reshape(micro_rows, span_len, head_count, FDIM)
        values = value_low.astype(jnp.float32).reshape(micro_rows, span_len, head_count, VHEAD)
        segments = jnp.cumsum(starts_in, axis=1)
        reset_flag = (segments[:, -1] > 0).astype(jnp.float32)
        (tail_state, tail_norm), tail_pull = jax.vjp(
            partial(tail_span, segments=segments), key_rows, values
        )
        state_in, norm_in, reset_in = prefix(
            (tail_state, tail_norm, reset_flag),
            "seq",
            combine_carry,
            (jnp.zeros_like(tail_state), jnp.zeros_like(tail_norm), jnp.zeros_like(reset_flag)),
            False,
        )
        mixed_heads, mix_pull = jax.vjp(
            partial(mix_span, segments=segments), queries, key_rows, values, state_in, norm_in
        )
        mixed_low = mixed_heads.reshape(-1, head_count * VHEAD).astype(jnp.bfloat16)
        branch_one = jnp.dot(mixed_low, full_output, preferred_element_type=jnp.float32)
        residual = flat_rows + lax.psum(branch_one, "tensor")
        scale_two = inverse_rms(residual)
        normed_two = (residual * scale_two * gain_two_f).astype(jnp.bfloat16)
        gate_proj = jnp.dot(normed_two, full_gate, preferred_element_type=jnp.float32)
        up_proj = jnp.dot(normed_two, full_up, preferred_element_type=jnp.float32)
        sigmoid_gate = jax.nn.sigmoid(gate_proj)
        hidden = (gate_proj * sigmoid_gate * up_proj).astype(jnp.bfloat16)
        branch_two = jnp.dot(hidden, full_down, preferred_element_type=jnp.float32)
        block_low = (
            residual + lax.psum(branch_two.astype(jnp.bfloat16), "tensor").astype(jnp.float32)
        ).astype(jnp.bfloat16)
        outputs_main.append(block_low.reshape(micro_rows, span_len, model_width))
        grad_down = inner_rows(hidden, cot_in)
        grad_hidden = by_transpose(cot_in, full_down)
        grad_gate_low = (
            grad_hidden * up_proj * sigmoid_gate * (1.0 + gate_proj * (1.0 - sigmoid_gate))
        ).astype(jnp.bfloat16)
        grad_up_low = (grad_hidden * gate_proj * sigmoid_gate).astype(jnp.bfloat16)
        grad_gate = inner_rows(normed_two, grad_gate_low)
        grad_up = inner_rows(normed_two, grad_up_low)
        grad_normed_two = by_transpose(grad_gate_low, full_gate) + by_transpose(
            grad_up_low, full_up
        )
        grad_normed_two = lax.psum(grad_normed_two, "tensor")
        grad_resid, grad_gain_two = norm_backward(residual, scale_two, gain_two_f, grad_normed_two)
        grad_resid = grad_resid + cot_in.astype(jnp.float32)
        grad_resid_low = grad_resid.astype(jnp.bfloat16)
        grad_output = inner_rows(mixed_low, grad_resid_low)
        grad_mixed = by_transpose(grad_resid_low, full_output).astype(jnp.bfloat16)
        grad_mixed = (
            lax.optimization_barrier(grad_mixed)
            .astype(jnp.float32)
            .reshape(micro_rows, span_len, head_count, VHEAD)
        )
        grad_queries, grad_keys, grad_values, grad_state, grad_norm = mix_pull(grad_mixed)
        carried_state, carried_norm, reset_out = prefix(
            (grad_state, grad_norm, reset_flag),
            "seq",
            combine_carry,
            (jnp.zeros_like(grad_state), jnp.zeros_like(grad_norm), jnp.zeros_like(reset_flag)),
            True,
        )
        more_keys, more_values = tail_pull((carried_state, carried_norm))
        grad_query_low = grad_queries.reshape(-1, head_count * FDIM).astype(jnp.bfloat16)
        grad_key_low = (grad_keys + more_keys).reshape(-1, head_count * FDIM).astype(jnp.bfloat16)
        grad_value_low = (
            (grad_values + more_values).reshape(-1, head_count * VHEAD).astype(jnp.bfloat16)
        )
        grad_query = inner_rows(normed_one, grad_query_low)
        grad_key = inner_rows(normed_one, grad_key_low)
        grad_value = inner_rows(normed_one, grad_value_low)
        grad_normed_one = (
            by_transpose(grad_query_low, full_query)
            + by_transpose(grad_key_low, full_key)
            + by_transpose(grad_value_low, full_value)
        )
        grad_normed_one = lax.psum(grad_normed_one, "tensor")
        grad_inputs, grad_gain_one = norm_backward(
            flat_rows, scale_one, gain_one_f, grad_normed_one
        )
        outputs_grad.append((grad_resid + grad_inputs).reshape(micro_rows, span_len, model_width))
        shares = (
            grad_query,
            grad_key,
            grad_value,
            grad_gate,
            grad_up,
            grad_output,
            grad_down,
            grad_gain_one,
            grad_gain_two,
        )
        if totals is None:
            totals = shares
        else:
            totals = jax.tree.map(jnp.add, totals, shares)
    totals = (
        lax.psum_scatter(totals[0], ("dp", "seq"), scatter_dimension=0, tiled=True),
        lax.psum_scatter(totals[1], ("dp", "seq"), scatter_dimension=0, tiled=True),
        lax.psum_scatter(totals[2], ("dp", "seq"), scatter_dimension=0, tiled=True),
        lax.psum_scatter(totals[3], ("dp", "seq"), scatter_dimension=0, tiled=True),
        lax.psum_scatter(totals[4], ("dp", "seq"), scatter_dimension=0, tiled=True),
        lax.psum_scatter(totals[5], ("dp", "seq"), scatter_dimension=1, tiled=True),
        lax.psum_scatter(totals[6], ("dp", "seq"), scatter_dimension=1, tiled=True),
        lax.psum_scatter(totals[7], ("dp", "seq"), scatter_dimension=0, tiled=True),
        lax.psum_scatter(totals[8], ("dp", "seq"), scatter_dimension=0, tiled=True),
    )
    return (
        jnp.concatenate(outputs_main, axis=0),
        jnp.concatenate(outputs_grad, axis=0),
        totals[7],
        totals[8],
        totals[0],
        totals[1],
        totals[2],
        totals[5],
        totals[3],
        totals[4],
        totals[6],
    )


MESH_ID = pl.DeviceIdType.MESH
VMEM_LIMIT = 58 << 20
LANES = 128
ROW_STEP = 32


def nt_dot(a, b):
    return lax.dot_general(a, b, (((1,), (1,)), ((), ())), preferred_element_type=jnp.float32)


def tn_dot(a, b):
    return lax.dot_general(a, b, (((0,), (0,)), ((), ())), preferred_element_type=jnp.float32)


def nn_dot(a, b):
    return lax.dot_general(a, b, (((1,), (0,)), ((), ())), preferred_element_type=jnp.float32)


def plane_places():
    at, core = lax.axis_index("dp"), lax.axis_index("tensor")
    x_bit, y_bit = lax.rem(at, 2), at // 2
    return (
        at,
        y_bit * 2 + (1 - x_bit),
        (1 - y_bit) * 2 + x_bit,
        (1 - y_bit) * 2 + (1 - x_bit),
        core,
    )


def greet(places):
    barrier = pltpu.get_barrier_semaphore()
    for place in places:
        pl.semaphore_signal(barrier, inc=1, device_id=place, device_id_type=MESH_ID)
    pl.semaphore_wait(barrier, len(places))


class Sender:
    def __init__(self, sems):
        self.sems, self.used = sems, 0

    def __call__(self, src, dst, place):
        index = self.used
        self.used += 1
        return pltpu.make_async_remote_copy(
            src_ref=src,
            dst_ref=dst,
            send_sem=self.sems.at[0, index],
            recv_sem=self.sems.at[1, index],
            device_id=place,
            device_id_type=MESH_ID,
        )


def greet_plane():
    at, x_at, y_at, _, core = plane_places()
    greet([{"dp": x_at}, {"dp": y_at}, {"tensor": 1 - core}])


def add_rows(dst, *srcs, step=64):
    def body(i, carry):
        r = pl.ds(pl.multiple_of(i * step, step), step)
        total = srcs[0][r].astype(jnp.float32)
        for s in srcs[1:]:
            total = total + s[r].astype(jnp.float32)
        dst[r] = total.astype(dst.dtype)
        return carry

    lax.fori_loop(0, srcs[0].shape[0] // step, body, 0)


GATHER_COPIES = 13
SCATTER_COPIES = 10


def gather_steps(own_ref, out_ref, copy, local_sem):
    at, x_at, y_at, d_at, core = plane_places()
    half = own_ref.shape[0] // 2
    xp, yp, sp = {"dp": x_at}, {"dp": y_at}, {"tensor": 1 - core}
    lo, hi = pl.ds(0, half), pl.ds(half, half)
    mine = out_ref.at[at, core]
    x_lo = copy(own_ref.at[lo], mine.at[lo], xp)
    y_hi = copy(own_ref.at[hi], mine.at[hi], yp)
    x_hi = copy(own_ref.at[hi], mine.at[hi], xp)
    y_lo = copy(own_ref.at[lo], mine.at[lo], yp)
    pair = copy(own_ref, mine, sp)
    for c in (x_lo, y_hi, x_hi, y_lo, pair):
        c.start()
    local_copy = pltpu.make_async_copy(own_ref, mine, local_sem)
    local_copy.start()
    from_x, from_y, from_d = out_ref.at[x_at, core], out_ref.at[y_at, core], out_ref.at[d_at, core]
    on_y = copy(from_x.at[lo], from_x.at[lo], yp)
    on_x = copy(from_y.at[hi], from_y.at[hi], xp)
    handed = [
        copy(block.at[rows], block.at[rows], sp)
        for block, rows in (
            (from_x, lo),
            (from_y, hi),
            (from_x, hi),
            (from_y, lo),
            (from_d, lo),
            (from_d, hi),
        )
    ]
    yield
    local_copy.wait()
    yield
    pair.wait_recv()
    yield
    x_lo.wait_recv()
    on_y.start()
    handed[0].start()
    y_hi.wait_recv()
    on_x.start()
    handed[1].start()
    yield
    handed[0].wait_recv()
    handed[1].wait_recv()
    yield
    x_hi.wait_recv()
    handed[2].start()
    y_lo.wait_recv()
    handed[3].start()
    yield
    handed[2].wait_recv()
    handed[3].wait_recv()
    yield
    on_y.wait_recv()
    handed[4].start()
    on_x.wait_recv()
    handed[5].start()
    yield
    handed[4].wait_recv()
    handed[5].wait_recv()
    yield
    for c in [x_lo, y_hi, x_hi, y_lo, on_y, on_x, pair] + handed:
        c.wait_send()


def scatter_steps(part_ref, out_ref, pair_ref, sum_ref, got_ref, copy, held=None, start=True):
    at, x_at, y_at, d_at, core = plane_places()
    half = part_ref.shape[2] // 2
    xp, yp, sp = {"dp": x_at}, {"dp": y_at}, {"tensor": 1 - core}
    lo, hi = pl.ds(0, half), pl.ds(half, half)
    order = (d_at, x_at, y_at, at)
    pairs = [copy(part_ref.at[to, 1 - core], pair_ref.at[j], sp) for j, to in enumerate(order)]
    own = [part_ref.at[to, core] for to in order]
    fetched = []
    if held is not None:
        buffer, held_sems = held
        fetched = [
            pltpu.make_async_copy(o, buffer.at[j], held_sems.at[j]) for j, o in enumerate(own)
        ]
        own = [buffer.at[j] for j in range(4)]

    def sent(j, rows, place):
        return copy(sum_ref.at[j, rows], got_ref.at[j, rows], place)

    d_lo, d_hi = sent(0, lo, xp), sent(0, hi, yp)
    x_lo, y_hi, x_hi, y_lo = sent(1, lo, xp), sent(2, hi, yp), sent(1, hi, xp), sent(2, lo, yp)
    for c in (pairs if start else []) + fetched:
        c.start()
    yield pairs

    def ready(j):
        if fetched:
            fetched[j].wait()
        pairs[j].wait_recv()

    def total(j, rows, *more):
        add_rows(sum_ref.at[j, rows], own[j].at[rows], pair_ref.at[j, rows], *more)

    ready(0)
    total(0, lo)
    d_lo.start()
    total(0, hi)
    d_hi.start()
    yield
    ready(1)
    total(1, lo)
    x_lo.start()
    yield
    ready(2)
    total(2, hi)
    y_hi.start()
    yield
    d_lo.wait_recv()
    total(2, lo, got_ref.at[0, lo])
    y_lo.start()
    d_hi.wait_recv()
    total(1, hi, got_ref.at[0, hi])
    x_hi.start()
    yield
    ready(3)
    for c in (x_lo, y_hi, y_lo, x_hi):
        c.wait_recv()
    add_rows(out_ref, own[3], pair_ref.at[3], got_ref.at[1], got_ref.at[2])
    for c in pairs + [d_lo, d_hi, x_lo, y_hi, x_hi, y_lo]:
        c.wait_send()


def swap_shards(ins, outs, peers, me, take, put, copy, local_sems):
    started = [
        copy(take(i, p), put(o, me), {"dp": p}) for i, o in zip(ins, outs) for p in peers
    ]
    started += [
        pltpu.make_async_copy(take(i, me), put(o, me), local_sems.at[n])
        for n, (i, o) in enumerate(zip(ins, outs))
    ]
    for c in started:
        c.start()
    return started


def exchange_kernel(take, put, count, *refs):
    ins, outs, sems, local_sems = refs[:count], refs[count : 2 * count], refs[-2], refs[-1]
    size, me = lax.axis_size("dp"), lax.axis_index("dp")
    peers = [lax.rem(me + k, size) for k in range(1, size)]
    greet([{"dp": p} for p in peers])
    for c in swap_shards(ins, outs, peers, me, take, put, Sender(sems), local_sems):
        c.wait()


def block_of(ref, index):
    return ref.at[index]


def columns_of(ref, index, rows=slice(None)):
    width = ref.shape[1] // lax.axis_size("dp")
    return ref.at[rows, pl.ds(pl.multiple_of(index * width, width), width)]


def exchange(arrays, cid, shapes, take=block_of, put=block_of):
    count, peers = len(arrays), lax.axis_size("dp") - 1
    anywhere = [pl.BlockSpec(memory_space=pl.ANY)] * count
    return pl.pallas_call(
        partial(exchange_kernel, take, put, count),
        name="exchange",
        out_shape=[jax.ShapeDtypeStruct(s, x.dtype) for s, x in zip(shapes, arrays)],
        in_specs=anywhere,
        out_specs=anywhere,
        scratch_shapes=[
            pltpu.SemaphoreType.DMA((2, count * peers)),
            pltpu.SemaphoreType.DMA((count,)),
        ],
        compiler_params=pltpu.CompilerParams(collective_id=cid, has_side_effects=True),
        cost_estimate=pl.CostEstimate(
            flops=0, bytes_accessed=60 * sum(x.size for x in arrays), transcendentals=0
        ),
    )(*arrays)


def first_kernel(count, *refs):
    ins, small_ref, outs, all_ref = (
        refs[:count],
        refs[count],
        refs[count + 1 : 2 * count + 1],
        refs[2 * count + 1],
    )
    sems, small_sems, local_sems, small_local_sem = refs[2 * count + 2 :]
    plane, span = lax.axis_size("dp"), lax.axis_size("seq")
    at, z = lax.axis_index("dp"), lax.axis_index("seq")
    places = [
        {"dp": lax.rem(at + i, plane), "seq": lax.rem(z + k, span)}
        for k in range(span)
        for i in range(plane)
        if i or k
    ]
    greet(places)
    copy_small = Sender(small_sems)
    block = all_ref.at[z * plane + at]
    started = [copy_small(small_ref, block, p) for p in places]
    started.append(pltpu.make_async_copy(small_ref, block, small_local_sem))
    for c in started:
        c.start()
    chips = [lax.rem(at + k, plane) for k in range(1, plane)]
    started += swap_shards(ins, outs, chips, at, block_of, columns_of, Sender(sems), local_sems)
    for c in started:
        c.wait()


def first_exchange(packs, small, cid):
    plane, span = lax.axis_size("dp"), lax.axis_size("seq")
    count = len(packs)
    return kernel_call(
        partial(first_kernel, count),
        "first_exchange",
        cid,
        [((p.shape[1], plane * p.shape[2]), p.dtype, pl.ANY) for p in packs]
        + [((span * plane,) + small.shape, small.dtype, pltpu.VMEM)],
        [(p, pl.ANY) for p in packs] + [(small, pltpu.VMEM)],
        [
            copies(count * (plane - 1)),
            copies(plane * span - 1),
            pltpu.SemaphoreType.DMA((count,)),
            pltpu.SemaphoreType.DMA,
        ],
        moved=1 << 26,
    )


def advance(steps, count=1):
    for _ in range(count):
        next(steps)


def run(*steps):
    for g in steps:
        for _ in g:
            pass


def row_blocks(rows, step, body):
    def inner(i, carry):
        return body(pl.ds(pl.multiple_of(i * step, step), step), carry)

    return lambda init: lax.fori_loop(0, rows // step, inner, init)


def lanes(k):
    return pl.ds(k * LANES, LANES)


def seq_major_block(k):
    plane, span = lax.axis_size("dp"), lax.axis_size("seq")
    s, g = divmod(k, plane)
    return g * span + s


def mean_of(acc, width):
    return jnp.sum(acc, axis=1, keepdims=True) * (1.0 / width)


def kernel_call(body, name, cid, outs, ins, scratch, flops=0, moved=0):
    params = dict(has_side_effects=True, vmem_limit_bytes=VMEM_LIMIT)
    return pl.pallas_call(
        body,
        name=name,
        out_shape=[jax.ShapeDtypeStruct(s, d) for s, d, _ in outs],
        in_specs=[pl.BlockSpec(memory_space=m) for _, m in ins],
        out_specs=[pl.BlockSpec(memory_space=m) for _, _, m in outs],
        scratch_shapes=scratch,
        compiler_params=pltpu.CompilerParams(collective_id=cid, **params),
        cost_estimate=pl.CostEstimate(flops=flops, bytes_accessed=moved, transcendentals=0),
    )(*[a for a, _ in ins])


def copies(count):
    return pltpu.SemaphoreType.DMA((2, count))


def entry_kernel(
    tokens_ref, cot_ref, small_ref, all_ref, x_ref, cot_own_ref, normed_ref, sems, local_sem
):
    greet_plane()
    core = lax.axis_index("tensor")
    m, width = x_ref.shape
    blocks = width // LANES

    def body(r, carry):
        acc = jnp.zeros((ROW_STEP, LANES), jnp.float32)
        for k in range(blocks):
            source = lanes(seq_major_block(k))
            v = tokens_ref[core, r, source]
            x_ref[r, lanes(k)] = v
            cot_own_ref[r, lanes(k)] = cot_ref[core, r, source]
            v = v.astype(jnp.float32)
            acc += v * v
        scale = lax.rsqrt(mean_of(acc, width) + norm_epsilon)
        for k in range(blocks):
            v = x_ref[r, lanes(k)].astype(jnp.float32)
            normed_ref[r, lanes(k)] = (v * scale * small_ref[k, 0:1, :]).astype(jnp.bfloat16)
        return carry

    row_blocks(m, ROW_STEP, body)(0)
    run(gather_steps(normed_ref, all_ref, Sender(sems), local_sem))


def entry(tokens, cot, small, cid):
    cores, m, width = tokens.shape
    whole = pltpu.VMEM
    gathered, x, cot_own = kernel_call(
        entry_kernel,
        "entry",
        cid,
        [
            ((4, cores, m, width), jnp.bfloat16, pl.ANY),
            ((m, width), jnp.bfloat16, whole),
            ((m, width), jnp.bfloat16, whole),
        ],
        [(tokens, whole), (cot, whole), (small, whole)],
        [pltpu.VMEM((m, width), jnp.bfloat16), copies(GATHER_COPIES), pltpu.SemaphoreType.DMA],
        moved=tokens.size * 40,
    )
    return gathered.reshape(-1, width), x, cot_own


FEATURES = 256
STATE_ROWS = 160
CHUNKS = 8
EARLY = 272


def feature_pairs():
    first = np.full(FEATURES, -4096, np.int32)
    second = np.full(FEATURES, -4096, np.int32)
    pairs = [(i, j) for i in range(FDIM + 1) for j in range(i, FDIM + 1)]
    for f, (i, j) in enumerate(pairs):
        first[f], second[f] = i, j
    return jnp.asarray(np.stack([first, second] + [first] * 6))


def feature_scale(pairs_ref):
    i, j = pairs_ref[0:1, :], pairs_ref[1:2, :]
    square = jnp.where(i == j, 1.0 / 32.0, 1.0 / 16.0)
    return jnp.where(j == FDIM, jnp.where(i == FDIM, 1.0, 0.25), square)


def fill_selectors(pairs_ref, pick_ref, qcols):
    kinds, heads = pick_ref.shape[:2]
    lane = lax.broadcasted_iota(jnp.int32, (LANES, FEATURES), 0)
    for kind in range(kinds):
        for h in range(heads):
            for side in range(2):
                index = pairs_ref[side : side + 1, :]
                source = jnp.where(
                    index == FDIM, 2 * qcols, index + (kind * qcols + h * FDIM)
                )
                pick_ref[kind, h, side] = jnp.where(lane == source, 1.0, 0.0).astype(jnp.bfloat16)


def factors(tile, pick_ref, kind, h):
    return nn_dot(tile, pick_ref[kind, h, 0]), nn_dot(tile, pick_ref[kind, h, 1])


def keys_in_place(tile, qcols):
    return pltpu.roll(tile.astype(jnp.float32), LANES - qcols, axis=1).astype(jnp.bfloat16)


def head_mask(rows, head):
    lane = lax.broadcasted_iota(jnp.int32, (rows, LANES), 1)
    return (lane >= head * FDIM) & (lane < (head + 1) * FDIM)


def masked_weights(query, key, column, row):
    length = query.shape[0]
    a = nt_dot(query, key) * 0.25
    t = lax.broadcasted_iota(jnp.int32, (length, length), 0)
    s = lax.broadcasted_iota(jnp.int32, (length, length), 1)
    keep = (s <= t) & (column == row)
    return a, jnp.where(keep, 1.0 + a + 0.5 * a * a, 0.0), keep


class Segments:
    def __init__(self, col_ref, row_ref, b):
        self.column, self.row = col_ref[b], row_ref[b]
        last = self.row[:, -1:]
        self.head = self.column == 0.0
        self.tail = self.column == last
        self.keep = jnp.where(last == 0.0, 1.0, 0.0)


class Chain:
    def __init__(self, forward, col_ref, row_ref, state_ref, sums_ref, scratch, copy_sems):
        span, z = lax.axis_size("seq"), lax.axis_index("seq")
        self.span = span
        self.to = {"seq": lax.rem(z + (1 if forward else span - 1), span)}
        self.distance = z if forward else span - 1 - z
        self.gets, self.gives = self.distance > 0, self.distance < span - 1
        self.segments = (col_ref, row_ref)
        self.state_ref, self.sums_ref = state_ref, sums_ref
        self.own_ref, self.own_sums_ref, self.out_ref, self.out_sums_ref = scratch
        self.sems = copy_sems
        self.rows = state_ref.shape[0] // CHUNKS

    def moves(self, g):
        part = pl.ds(g * self.rows, self.rows)
        used = pl.ds(0, STATE_ROWS)
        pairs = (
            (self.out_ref.at[part, :, used], self.state_ref.at[part, :, used]),
            (self.out_sums_ref.at[part], self.sums_ref.at[part]),
        )
        return [
            pltpu.make_async_remote_copy(
                src_ref=a,
                dst_ref=b,
                send_sem=self.sems.at[0, 2 * g + n],
                recv_sem=self.sems.at[1, 2 * g + n],
                device_id=self.to,
                device_id_type=MESH_ID,
            )
            for n, (a, b) in enumerate(pairs)
        ]

    def step(self, n):
        g = n - self.distance

        @pl.when((g >= 0) & (g < CHUNKS))
        def _():
            @pl.when(self.gets)
            def _():
                for c in self.moves(g):
                    c.wait_recv()

            for i in range(self.rows):
                b = g * self.rows + i
                keep = Segments(*self.segments, b).keep
                for h in range(self.state_ref.shape[1]):
                    before = self.state_ref[b, h].astype(jnp.float32)
                    self.out_ref[b, h] = (self.own_ref[b, h] + keep * before).astype(jnp.bfloat16)
                self.out_sums_ref[b] = self.own_sums_ref[b] + keep * self.sums_ref[b]

            @pl.when(self.gives)
            def _():
                for c in self.moves(g):
                    c.start()

    def run(self, work, between=()):
        def body(n, carry):
            for at, piece in enumerate(between):

                @pl.when(n == at)
                def _():
                    piece()

            work(n, self.step)
            return carry

        lax.fori_loop(0, CHUNKS + self.span - 1, body, 0)

    def close(self):
        @pl.when(self.gives)
        def _():
            for g in range(CHUNKS):
                for c in self.moves(g):
                    c.wait_send()


def states_kernel(
    heads,
    normed_ref,
    pack_ref,
    col_ref,
    row_ref,
    pairs_ref,
    down_ref,
    qkv_ref,
    state_ref,
    sums_ref,
    down_all_ref,
    pick_ref,
    own_ref,
    own_sums_ref,
    out_ref,
    out_sums_ref,
    sems,
    shard_sems,
    shard_local_sems,
):
    parts, _, depth = pack_ref.shape
    rows, length = col_ref.shape[0], col_ref.shape[1]
    vcols, qcols = heads * VHEAD, heads * FDIM
    plane, span = lax.axis_size("dp"), lax.axis_size("seq")
    at, z = lax.axis_index("dp"), lax.axis_index("seq")
    chips = [lax.rem(at + k, plane) for k in range(1, plane)]
    state_ref[...] = jnp.zeros_like(state_ref)
    sums_ref[...] = jnp.zeros_like(sums_ref)
    greet(
        [{"dp": p} for p in chips] + [{"seq": lax.rem(z + k, span)} for k in (1, span - 1)]
    )
    shards = swap_shards(
        (down_ref,),
        (down_all_ref,),
        chips,
        at,
        block_of,
        columns_of,
        Sender(shard_sems),
        shard_local_sems,
    )
    chain = Chain(
        True,
        col_ref,
        row_ref,
        state_ref,
        sums_ref,
        (own_ref, own_sums_ref, out_ref, out_sums_ref),
        sems,
    )
    fill_selectors(pairs_ref, pick_ref, qcols)
    scale = feature_scale(pairs_ref)

    def tokens_of(b):
        return pl.ds(pl.multiple_of(b * length, length), length)

    def first(b, carry):
        t = tokens_of(b)
        value = jnp.zeros((length, vcols), jnp.float32)
        tile = jnp.zeros((length, LANES), jnp.float32)
        for s in range(parts):
            piece = normed_ref[t, pl.ds(s * depth, depth)]
            value += nt_dot(piece, pack_ref[s, pl.ds(0, vcols)])
            tile += nt_dot(piece, pack_ref[s, pl.ds(vcols, LANES)])
        lane = lax.broadcasted_iota(jnp.int32, (length, LANES), 1)
        tile = jnp.where(lane < 2 * qcols, tile, jnp.where(lane == 2 * qcols, 1.0, 0.0))
        value, tile = value.astype(jnp.bfloat16), tile.astype(jnp.bfloat16)
        qkv_ref[t, pl.ds(0, vcols)] = value
        qkv_ref[t, pl.ds(vcols, LANES)] = tile
        tail = Segments(col_ref, row_ref, b).tail
        for h in range(heads):
            one, two = factors(tile, pick_ref, 1, h)
            lifted = jnp.where(tail, one * two * scale, 0.0)
            own_ref[b, h] = tn_dot(
                lifted.astype(jnp.bfloat16), value[:, h * VHEAD : (h + 1) * VHEAD]
            )
            own_sums_ref[b, h : h + 1] = jnp.sum(lifted, axis=0, keepdims=True)
        return carry

    own_sums_ref[...] = jnp.zeros_like(own_sums_ref)
    each = rows // CHUNKS

    def work(n, step):
        @pl.when(n < CHUNKS)
        def _():
            lax.fori_loop(n * each, (n + 1) * each, first, 0)

        step(n)

    chain.run(work)
    for c in shards:
        c.wait()
    chain.close()


def mix_kernel(
    heads,
    qkv_ref,
    col_ref,
    row_ref,
    pairs_ref,
    state_ref,
    sums_ref,
    cot_ref,
    mixed_ref,
    exact_ref,
    den_ref,
    cot_all_ref,
    pick_ref,
    cot_sems,
    local_sem,
):
    rows, length = col_ref.shape[0], col_ref.shape[1]
    vcols, qcols = heads * VHEAD, heads * FDIM
    greet_plane()
    gather = gather_steps(cot_ref, cot_all_ref, Sender(cot_sems), local_sem)
    next(gather)
    fill_selectors(pairs_ref, pick_ref, qcols)

    def tokens_of(b):
        return pl.ds(pl.multiple_of(b * length, length), length)

    lane = lax.broadcasted_iota(jnp.int32, (length, LANES), 1)

    def here(b, carry):
        t = tokens_of(b)
        seg = Segments(col_ref, row_ref, b)
        tile = qkv_ref[t, pl.ds(vcols, LANES)]
        key = keys_in_place(tile, qcols)
        dens = jnp.zeros((length, LANES), jnp.float32)
        for h in range(heads):
            v = pl.ds(h * VHEAD, VHEAD)
            query = jnp.where(head_mask(length, h), tile, jnp.zeros_like(tile))
            _, w, _ = masked_weights(query, key, seg.column, seg.row)
            exact_ref[t, v] = nn_dot(w.astype(jnp.bfloat16), qkv_ref[t, v])
            dens = jnp.where(lane == h, jnp.sum(w, axis=1, keepdims=True), dens)
        den_ref[t] = dens
        return carry

    def before(b, carry):
        t = tokens_of(b)
        head = Segments(col_ref, row_ref, b).head
        tile = qkv_ref[t, pl.ds(vcols, LANES)]
        dens = den_ref[t]
        for h in range(heads):
            v = pl.ds(h * VHEAD, VHEAD)
            one, two = factors(tile, pick_ref, 0, h)
            lifted = jnp.where(head, one * two, 0.0)
            num = exact_ref[t, v] + nn_dot(lifted.astype(jnp.bfloat16), state_ref[b, h])
            den = dens[:, h : h + 1]
            den += jnp.sum(lifted * sums_ref[b, h : h + 1], axis=1, keepdims=True)
            value = num / den
            exact_ref[t, v] = value
            mixed_ref[t, v] = value.astype(jnp.bfloat16)
            dens = jnp.where(lane == h, den, dens)
        den_ref[t] = dens
        return carry

    def row(b, carry):
        for at in range(1, 6):

            @pl.when(b == at)
            def _():
                next(gather)

        here(b, 0)
        before(b, 0)
        return carry

    lax.fori_loop(0, rows, row, 0)
    run(gather)


def state_scratch(rows, heads):
    return [
        pltpu.VMEM((2, heads, 2, LANES, FEATURES), jnp.bfloat16),
        pltpu.VMEM((rows, heads, FEATURES, VHEAD), jnp.float32),
        pltpu.VMEM((rows, 8, FEATURES), jnp.float32),
        pltpu.VMEM((rows, heads, FEATURES, VHEAD), jnp.bfloat16),
        pltpu.VMEM((rows, 8, FEATURES), jnp.float32),
    ]


def states(normed, pack, seg_col, seg_row, pairs, down, heads, cid):
    tokens = normed.shape[0]
    rows = seg_col.shape[0]
    vcols = heads * VHEAD
    plane, size, chunk = down.shape
    whole = pltpu.VMEM
    return kernel_call(
        partial(states_kernel, heads),
        "states",
        cid,
        [
            ((tokens, vcols + LANES), jnp.bfloat16, whole),
            ((rows, heads, FEATURES, VHEAD), jnp.bfloat16, whole),
            ((rows, 8, FEATURES), jnp.float32, whole),
            ((size, plane * chunk), jnp.bfloat16, pl.ANY),
        ],
        [(a, whole) for a in (normed, pack, seg_col, seg_row, pairs)] + [(down, pl.ANY)],
        state_scratch(rows, heads)
        + [copies(2 * CHUNKS), copies(plane - 1), pltpu.SemaphoreType.DMA((1,))],
        moved=normed.size * 20,
    )


def mix(qkv, seg_col, seg_row, pairs, state, sums, cot_own, heads, cid):
    tokens = qkv.shape[0]
    vcols = heads * VHEAD
    m, width = cot_own.shape
    whole = pltpu.VMEM
    mixed, exact, den, cot = kernel_call(
        partial(mix_kernel, heads),
        "mix",
        cid,
        [
            ((tokens, vcols), jnp.bfloat16, whole),
            ((tokens, vcols), jnp.float32, whole),
            ((tokens, LANES), jnp.float32, whole),
            ((4, 2, m, width), jnp.bfloat16, pl.ANY),
        ],
        [(a, whole) for a in (qkv, seg_col, seg_row, pairs, state, sums, cot_own)],
        [
            pltpu.VMEM((2, heads, 2, LANES, FEATURES), jnp.bfloat16),
            copies(GATHER_COPIES),
            pltpu.SemaphoreType.DMA,
        ],
        moved=cot_own.size * 80,
    )
    return mixed, exact, den, cot.reshape(-1, width)


def branch_kernel(
    mixed_ref,
    pack_ref,
    x_ref,
    small_ref,
    residual_ref,
    normed_ref,
    part_ref,
    pair_ref,
    sum_ref,
    got_ref,
    sems,
):
    greet_plane()
    parts, _, depth = pack_ref.shape
    m, width = x_ref.shape
    vcols = mixed_ref.shape[1]
    first = pack_ref.shape[1] - vcols

    def project(b, carry):
        left = mixed_ref[pl.ds(pl.multiple_of(b * m, m), m)]
        for s in range(parts):
            part_ref[b // 2, lax.rem(b, 2), :, pl.ds(s * depth, depth)] = nn_dot(
                left, pack_ref[s, pl.ds(first, vcols)]
            ).astype(jnp.bfloat16)
        return carry

    lax.fori_loop(0, 8, project, 0)
    run(scatter_steps(part_ref, residual_ref, pair_ref, sum_ref, got_ref, Sender(sems)))

    def body(r, carry):
        acc = jnp.zeros((ROW_STEP, LANES), jnp.float32)
        for k in range(width // LANES):
            v = residual_ref[r, lanes(k)] + x_ref[r, lanes(k)].astype(jnp.float32)
            residual_ref[r, lanes(k)] = v
            acc += v * v
        scale = lax.rsqrt(mean_of(acc, width) + norm_epsilon)
        for k in range(width // LANES):
            normed_ref[r, lanes(k)] = (
                residual_ref[r, lanes(k)] * scale * small_ref[k, 1:2, :]
            ).astype(jnp.bfloat16)
        return carry

    row_blocks(m, ROW_STEP, body)(0)


def scatter_scratch(m, width):
    return [
        pltpu.VMEM((4, m, width), jnp.bfloat16),
        pltpu.VMEM((3, m, width), jnp.bfloat16),
        pltpu.VMEM((3, m, width), jnp.bfloat16),
    ]


def branch(mixed, pack, x, small, cid):
    m, width = x.shape
    whole = pltpu.VMEM
    return kernel_call(
        branch_kernel,
        "branch",
        cid,
        [((m, width), jnp.float32, whole), ((m, width), jnp.bfloat16, whole)],
        [(mixed, whole), (pack, whole), (x, whole), (small, whole)],
        [pltpu.VMEM((4, 2, m, width), jnp.bfloat16)]
        + scatter_scratch(m, width)
        + [copies(SCATTER_COPIES)],
        moved=x.size * 80,
    )


def parity(i):
    return i % 2 if isinstance(i, int) else lax.rem(i, 2)


def choose(test, a, b):
    if isinstance(test, bool):
        return a if test else b
    return jnp.where(test, a, b)


def project(at, w_ref, rows):
    parts, _, depth = w_ref.shape
    total = nt_dot(at(pl.ds(0, depth)), w_ref[0, rows])
    for s in range(1, parts):
        total += nt_dot(at(pl.ds(s * depth, depth)), w_ref[s, rows])
    return total


def arrivals(i, half):
    at, x_at, y_at, d_at, core = plane_places()
    k = choose(parity(i) == 0, core, 1 - core)
    one = choose(i < 2, at, choose(i < 6, x_at, d_at))
    two = choose(i < 2, at, choose(i < 6, y_at, d_at))
    late = (i >= 4) & (i < 6)
    late = int(late) if isinstance(late, bool) else late.astype(jnp.int32)
    first, second = late * half, (1 - late) * half
    if not isinstance(i, int):
        first, second = pl.multiple_of(first, half), pl.multiple_of(second, half)
    return (one, k, first), (two, k, second)


def stacked_copies(early, late, out, sems):
    rows = early.shape[1]
    return [
        pltpu.make_async_copy(early, out.at[:, pl.ds(0, rows)], sems.at[0]),
        pltpu.make_async_copy(late, out.at[:, pl.ds(rows, late.shape[1])], sems.at[1]),
    ]


def expand_kernel(
    own_ref,
    early_hbm,
    late_hbm,
    normed_hbm,
    gate_hbm,
    up_hbm,
    hidden_hbm,
    normed_ref,
    w_ref,
    gate_ref,
    up_ref,
    hidden_ref,
    sems,
    local_sem,
    w_sems,
    store_sems,
    keep_sem,
):
    greet_plane()
    half = own_ref.shape[0] // 2
    units = gate_ref.shape[2]
    gather = gather_steps(own_ref, normed_ref, Sender(sems), local_sem)
    next(gather)
    weights = stacked_copies(early_hbm, late_hbm, w_ref, w_sems)
    for c in weights:
        c.start()

    def store_copies(i):
        slot = parity(i)
        found = []
        for n, (c, k, r) in enumerate(arrivals(i, half)):
            rows = pl.ds(n * half, half)
            column = (c * 2 + k) * (2 * half) + r
            pairs = (
                (gate_ref.at[slot, rows], gate_hbm.at[c, k, pl.ds(r, half)]),
                (up_ref.at[slot, rows], up_hbm.at[c, k, pl.ds(r, half)]),
                (
                    hidden_ref.at[slot, :, rows],
                    hidden_hbm.at[:, pl.ds(pl.multiple_of(column, half), half)],
                ),
            )
            for q, (a, b) in enumerate(pairs):
                found.append(pltpu.make_async_copy(a, b, store_sems.at[slot, 3 * n + q]))
        return found

    next(gather)
    for c in weights:
        c.wait()

    def body(i, carry):
        for step in range(1, 8):

            @pl.when(i == step)
            def _():
                next(gather)

        @pl.when(i >= 2)
        def _():
            for c in store_copies(i - 2):
                c.wait()

        slot = parity(i)
        pieces = arrivals(i, half)

        def columns(cols):
            return jnp.concatenate([normed_ref[c, k, pl.ds(r, half), cols] for c, k, r in pieces])

        gate = project(columns, w_ref, pl.ds(0, units))
        up = project(columns, w_ref, pl.ds(units, units))
        gate_ref[slot], up_ref[slot] = gate, up
        hidden_ref[slot] = (gate * jax.nn.sigmoid(gate) * up).astype(jnp.bfloat16).T
        for c in store_copies(i):
            c.start()
        return carry

    lax.fori_loop(0, 8, body, 0)
    keep = pltpu.make_async_copy(normed_ref, normed_hbm, keep_sem)
    keep.start()
    for i in (6, 7):
        for c in store_copies(i):
            c.wait()
    keep.wait()
    run(gather)


def expand(own, early, late, cid):
    m, width = own.shape
    weights = (early.shape[0], early.shape[1] + late.shape[1], early.shape[2])
    units = weights[1] // 2
    low = jnp.bfloat16
    thin = ((4, 2, m, units), jnp.float32, pl.ANY)
    normed, gate, up, hidden = kernel_call(
        expand_kernel,
        "expand",
        cid,
        [((4, 2, m, width), low, pl.ANY), thin, thin, ((units, 8 * m), low, pl.ANY)],
        [(own, pltpu.VMEM), (early, pl.ANY), (late, pl.ANY)],
        [
            pltpu.VMEM((4, 2, m, width), low),
            pltpu.VMEM(weights, low),
            pltpu.VMEM((2, m, units), jnp.float32),
            pltpu.VMEM((2, m, units), jnp.float32),
            pltpu.VMEM((2, units, m), low),
            copies(GATHER_COPIES),
            pltpu.SemaphoreType.DMA,
            pltpu.SemaphoreType.DMA((2,)),
            pltpu.SemaphoreType.DMA((2, 6)),
            pltpu.SemaphoreType.DMA,
        ],
        flops=32 * m * width * units,
        moved=1 << 27,
    )
    return normed.reshape(8 * m, width), gate, up, hidden


def hidden_kernel(
    gate_hbm,
    up_hbm,
    cot_hbm,
    early_hbm,
    late_hbm,
    down_hbm,
    normed_hbm,
    out_hbm,
    total_ref,
    grads_hbm,
    gate_ref,
    up_ref,
    cot_ref,
    out_ref,
    w_ref,
    down_w_ref,
    part_ref,
    pair_ref,
    sum_ref,
    got_ref,
    turned_ref,
    normed_ref,
    grad_ref,
    sems,
    w_sems,
    load_sems,
    store_sems,
    normed_sem,
    grad_sems,
):
    greet_plane()
    at, x_at, y_at, d_at, core = plane_places()
    parts, units, depth = down_w_ref.shape
    m = cot_ref.shape[1]
    scatter = scatter_steps(
        part_ref, total_ref, pair_ref, sum_ref, got_ref, Sender(sems), start=False
    )
    pairs = next(scatter)
    weights = stacked_copies(early_hbm, late_hbm, w_ref, w_sems)
    weights.append(pltpu.make_async_copy(down_hbm, down_w_ref, w_sems.at[2]))
    normed_copy = pltpu.make_async_copy(normed_hbm, normed_ref, normed_sem)

    def place(i):
        chip = choose(i < 2, d_at, choose(i < 4, x_at, choose(i < 6, y_at, at)))
        return chip, choose(parity(i) == 0, 1 - core, core)

    def loads(i):
        slot, (c, k) = parity(i), place(i)
        return [
            pltpu.make_async_copy(a.at[c, k], b.at[slot], load_sems.at[slot, n])
            for n, (a, b) in enumerate(
                ((gate_hbm, gate_ref), (up_hbm, up_ref), (cot_hbm, cot_ref))
            )
        ]

    def store(i):
        slot, (c, k) = parity(i), place(i)
        return pltpu.make_async_copy(out_ref.at[slot], out_hbm.at[c, k], store_sems.at[slot])

    for c in weights + loads(0):
        c.start()
    normed_copy.start()
    for c in weights:
        c.wait()

    def body(i, carry):
        for step in (2, 4, 6):

            @pl.when(i == step)
            def _():
                next(scatter)

        @pl.when(i < 7)
        def _():
            for c in loads(i + 1):
                c.start()

        for c in loads(i):
            c.wait()

        @pl.when(i >= 2)
        def _():
            store(i - 2).wait()

        slot, (chip, k) = parity(i), place(i)
        gate, up = gate_ref[slot], up_ref[slot]
        dhidden = project(lambda cols: cot_ref[slot, :, cols], down_w_ref, pl.ds(0, units))
        sig = jax.nn.sigmoid(gate)
        silu = gate * sig
        hidden = (silu * up).astype(jnp.bfloat16)
        dgate = (dhidden * up * sig * (1.0 + gate * (1.0 - sig))).astype(jnp.bfloat16)
        dup = (dhidden * silu).astype(jnp.bfloat16)
        for s in range(parts):
            cols = pl.ds(s * depth, depth)
            part_ref[chip, k, :, cols] = (
                nn_dot(dgate, w_ref[s, pl.ds(0, units)])
                + nn_dot(dup, w_ref[s, pl.ds(units, units)])
            ).astype(jnp.bfloat16)
            out_ref[slot, :, cols] = nn_dot(hidden, down_w_ref[s]).astype(jnp.bfloat16)
        store(i).start()
        for j in range(4):

            @pl.when(i == 2 * j)
            def _():
                pairs[j].start()

        column = pl.ds(pl.multiple_of((chip * 2 + k) * m, m), m)
        turned_ref[0, :, column], turned_ref[1, :, column] = dgate.T, dup.T
        return carry

    lax.fori_loop(0, 8, body, 0)
    next(scatter)
    store(6).wait()
    store(7).wait()
    normed_copy.wait()
    width = grad_ref.shape[2]
    blocks = normed_ref.shape[1] // width

    def gradients(which):
        rows = pl.ds(which * units, units)

        def stored(i):
            column = pl.ds(pl.multiple_of(i * width, width), width)
            slot = parity(i)
            return pltpu.make_async_copy(
                grad_ref.at[slot], grads_hbm.at[rows, column], grad_sems.at[slot]
            )

        def body(i, carry):
            column = pl.ds(pl.multiple_of(i * width, width), width)

            @pl.when(i >= 2)
            def _():
                stored(i - 2).wait()

            grad_ref[parity(i)] = nn_dot(turned_ref[which], normed_ref[:, column]).astype(
                jnp.bfloat16
            )
            stored(i).start()
            return carry

        lax.fori_loop(0, blocks, body, 0)
        for i in (blocks - 2, blocks - 1):
            stored(i).wait()

    gradients(0)
    gradients(1)
    run(scatter)


def hidden_units(gate, up, cot, early, late, down_w, normed, cid):
    _, _, m, units = gate.shape
    tokens, width = normed.shape
    low = jnp.bfloat16
    stacked = (early.shape[0], early.shape[1] + late.shape[1], early.shape[2])
    ins = (gate, up, cot.reshape(4, 2, m, width), early, late, down_w, normed)
    return kernel_call(
        hidden_kernel,
        "hidden_units",
        cid,
        [
            ((4, 2, m, width), low, pl.ANY),
            ((m, width), jnp.float32, pltpu.VMEM),
            ((2 * units, width), low, pl.ANY),
        ],
        [(a, pl.ANY) for a in ins],
        [
            pltpu.VMEM((2, m, units), jnp.float32),
            pltpu.VMEM((2, m, units), jnp.float32),
            pltpu.VMEM((2, m, width), low),
            pltpu.VMEM((2, m, width), low),
            pltpu.VMEM(stacked, low),
            pltpu.VMEM(down_w.shape, low),
            pltpu.VMEM((4, 2, m, width), low),
        ]
        + scatter_scratch(m, width)
        + [
            pltpu.VMEM((2, units, tokens), low),
            pltpu.VMEM((tokens, width), low),
            pltpu.VMEM((2, units, 2 * LANES), low),
            copies(SCATTER_COPIES),
            pltpu.SemaphoreType.DMA((3,)),
            pltpu.SemaphoreType.DMA((2, 3)),
            pltpu.SemaphoreType.DMA((2,)),
            pltpu.SemaphoreType.DMA,
            pltpu.SemaphoreType.DMA((2,)),
        ],
        flops=12 * tokens * width * units,
        moved=1 << 27,
    )


def norm_gradient(r, value_at, grad_ref, gain_at, gain_grad, finish, width):
    squares = jnp.zeros((ROW_STEP, LANES), jnp.float32)
    cross = jnp.zeros((ROW_STEP, LANES), jnp.float32)
    for k in range(width // LANES):
        v = value_at(r, k)
        squares += v * v
        cross += v * grad_ref[r, lanes(k)] * gain_at(k)
    scale = lax.rsqrt(mean_of(squares, width) + norm_epsilon)
    pull = mean_of(cross, width) * scale * scale * scale
    for k in range(width // LANES):
        v, g = value_at(r, k), grad_ref[r, lanes(k)]
        gain_grad[:, lanes(k)] += jnp.sum(
            (g * v * scale).reshape(ROW_STEP // 8, 8, LANES), axis=0
        )
        finish(r, k, scale * g * gain_at(k) - v * pull)


def turn_kernel(
    total_ref,
    residual_ref,
    cot_ref,
    small_ref,
    pack_ref,
    mixed_ref,
    dresid_ref,
    gain_ref,
    dmixed_ref,
    grad_ref,
    all_ref,
    low_ref,
    sum_ref,
    gather_sems,
    local_sem,
):
    greet_plane()
    m, width = residual_ref.shape
    half = m // 2
    parts, _, depth = pack_ref.shape
    vcols = mixed_ref.shape[3]
    first_row = pack_ref.shape[1] - vcols
    gain_ref[...] = jnp.zeros_like(gain_ref)

    def finish(r, k, v):
        v += cot_ref[r, lanes(k)].astype(jnp.float32)
        dresid_ref[r, lanes(k)] = v
        low_ref[r, lanes(k)] = v.astype(jnp.bfloat16)

    def body(r, carry):
        norm_gradient(
            r,
            lambda r, k: residual_ref[r, lanes(k)],
            total_ref,
            lambda k: small_ref[k, 1:2, :],
            gain_ref,
            finish,
            width,
        )
        return carry

    row_blocks(m, ROW_STEP, body)(0)
    gather = gather_steps(low_ref, all_ref, Sender(gather_sems), local_sem)
    next(gather)
    sum_ref[...] = jnp.zeros_like(sum_ref)
    next(gather)

    def block(i, carry):
        for step in range(1, 8):

            @pl.when(i == step)
            def _():
                next(gather)

        pieces = arrivals(i, half)

        def columns(cols):
            return jnp.concatenate([all_ref[c, k, pl.ds(r, half), cols] for c, k, r in pieces])

        left = jnp.concatenate([mixed_ref[c, k, pl.ds(r, half)] for c, k, r in pieces])
        dmixed = project(columns, pack_ref, pl.ds(first_row, vcols)).astype(jnp.bfloat16)
        for n, (c, k, r) in enumerate(pieces):
            dmixed_ref[c, k, pl.ds(r, half)] = dmixed[n * half : (n + 1) * half]
        for s in range(parts):
            cols = pl.ds(s * depth, depth)
            sum_ref[:, cols] += tn_dot(left, columns(cols))
        return carry

    lax.fori_loop(0, 8, block, 0)
    grad_ref[...] = sum_ref[...].astype(jnp.bfloat16)
    run(gather)


def turn(total, residual, cot_own, small, pack, mixed, cid):
    m, width = residual.shape
    vcols = mixed.shape[1]
    whole, low = pltpu.VMEM, jnp.bfloat16
    dresid, gain, dmixed, grad = kernel_call(
        turn_kernel,
        "turn",
        cid,
        [
            ((m, width), jnp.float32, whole),
            ((8, width), jnp.float32, whole),
            ((4, 2, m, vcols), low, whole),
            ((vcols, width), low, whole),
        ],
        [(a, whole) for a in (total, residual, cot_own, small, pack)]
        + [(mixed.reshape(4, 2, m, vcols), whole)],
        [
            pltpu.VMEM((4, 2, m, width), low),
            pltpu.VMEM((m, width), low),
            pltpu.VMEM((vcols, width), jnp.float32),
            copies(GATHER_COPIES),
            pltpu.SemaphoreType.DMA,
        ],
        moved=residual.size * 80,
    )
    return dresid, gain, dmixed.reshape(8 * m, vcols), grad


def unmix_kernel(
    heads,
    count,
    dmixed_ref,
    normed_hbm,
    output_grad_ref,
    part_ref,
    residual_ref,
    col_ref,
    row_ref,
    pairs_ref,
    qkv_ref,
    exact_ref,
    den_ref,
    state_ref,
    sums_ref,
    *refs,
):
    ins, dqkv_ref, block_ref, grad_ref = refs[:count], *refs[count : count + 3]
    outs = refs[count + 3 : 2 * count + 3]
    (
        normed_ref,
        turned_ref,
        dvalue_ref,
        dtile_ref,
        back_ref,
        back_sums_ref,
        pick_ref,
        own_ref,
        own_sums_ref,
        out_ref,
        out_sums_ref,
        total_ref,
        held_ref,
        pair_ref,
        sum_ref,
        got_ref,
        sems,
        shard_sems,
        local_sems,
        scatter_sems,
        held_sems,
        normed_sem,
    ) = refs[2 * count + 3 :]
    rows, length = col_ref.shape[0], col_ref.shape[1]
    vcols, qcols = heads * VHEAD, heads * FDIM
    at, x_at, y_at, _, core = plane_places()
    plane, span, z = lax.axis_size("dp"), lax.axis_size("seq"), lax.axis_index("seq")
    chips = [lax.rem(at + k, plane) for k in range(1, plane)]
    normed_copy = pltpu.make_async_copy(normed_hbm, normed_ref, normed_sem)
    normed_copy.start()
    back_ref[...] = jnp.zeros_like(back_ref)
    back_sums_ref[...] = jnp.zeros_like(back_sums_ref)
    greet(
        [{"dp": p} for p in chips]
        + [{"tensor": 1 - core}]
        + [{"seq": lax.rem(z + k, span)} for k in (1, span - 1)]
    )
    scatter = scatter_steps(
        part_ref,
        total_ref,
        pair_ref,
        sum_ref,
        got_ref,
        Sender(scatter_sems),
        (held_ref, held_sems),
    )
    next(scatter)
    chain = Chain(
        False,
        col_ref,
        row_ref,
        back_ref,
        back_sums_ref,
        (own_ref, own_sums_ref, out_ref, out_sums_ref),
        sems,
    )
    fill_selectors(pairs_ref, pick_ref, qcols)
    scale = feature_scale(pairs_ref)

    def tokens_of(b):
        return pl.ds(pl.multiple_of(b * length, length), length)

    def cotangents(t, h):
        v = pl.ds(h * VHEAD, VHEAD)
        dn = dmixed_ref[t, v].astype(jnp.float32) / den_ref[t, pl.ds(h, 1)]
        dd = -jnp.sum(dn * exact_ref[t, v], axis=1, keepdims=True)
        return dn.astype(jnp.bfloat16), dd

    def first(b, carry):
        t = tokens_of(b)
        head = Segments(col_ref, row_ref, b).head
        tile = qkv_ref[t, pl.ds(vcols, LANES)]
        for h in range(heads):
            dn, dd = cotangents(t, h)
            one, two = factors(tile, pick_ref, 0, h)
            lifted = jnp.where(head, one * two, 0.0)
            own_ref[b, h] = tn_dot(lifted.astype(jnp.bfloat16), dn)
            own_sums_ref[b, h : h + 1] = jnp.sum(lifted * dd, axis=0, keepdims=True)
        return carry

    own_sums_ref[...] = jnp.zeros_like(own_sums_ref)
    shards = swap_shards(ins, outs, chips, at, columns_of, block_of, Sender(shard_sems), local_sems)

    def lowered(dlifted, kind, h, one, two):
        return nt_dot((dlifted * two).astype(jnp.bfloat16), pick_ref[kind, h, 0]) + nt_dot(
            (dlifted * one).astype(jnp.bfloat16), pick_ref[kind, h, 1]
        )

    def here(b, carry):
        t = tokens_of(b)
        seg = Segments(col_ref, row_ref, b)
        tile = qkv_ref[t, pl.ds(vcols, LANES)]
        key = keys_in_place(tile, qcols)
        dtile = jnp.zeros((length, LANES), jnp.float32)
        dkey = jnp.zeros((length, LANES), jnp.float32)
        for h in range(heads):
            inside = head_mask(length, h)
            v = pl.ds(h * VHEAD, VHEAD)
            query = jnp.where(inside, tile, jnp.zeros_like(tile))
            dn, dd = cotangents(t, h)
            a, w, keep = masked_weights(query, key, seg.column, seg.row)
            dw = jnp.where(keep, nt_dot(dn, qkv_ref[t, v]) + dd, 0.0)
            da = (dw * (1.0 + a) * 0.25).astype(jnp.bfloat16)
            dvalue_ref[t, v] = tn_dot(w.astype(jnp.bfloat16), dn)
            dtile += jnp.where(inside, nn_dot(da, key), 0.0)
            dkey += jnp.where(inside, tn_dot(da, query), 0.0)
            one, two = factors(tile, pick_ref, 0, h)
            dlifted = nt_dot(dn, state_ref[b, h]) + dd * sums_ref[b, h : h + 1]
            dtile += lowered(jnp.where(seg.head, dlifted, 0.0), 0, h, one, two)
        dtile_ref[t] = dtile + pltpu.roll(dkey, qcols, axis=1)
        return carry

    def after(b, carry):
        t = tokens_of(b)
        tail = Segments(col_ref, row_ref, b).tail
        tile = qkv_ref[t, pl.ds(vcols, LANES)]
        dtile = dtile_ref[t]
        for h in range(heads):
            v = pl.ds(h * VHEAD, VHEAD)
            one, two = factors(tile, pick_ref, 1, h)
            lifted = jnp.where(tail, one * two * scale, 0.0)
            dlifted = nt_dot(qkv_ref[t, v], back_ref[b, h]) + back_sums_ref[b, h : h + 1]
            dtile += lowered(jnp.where(tail, dlifted * scale, 0.0), 1, h, one, two)
            dvalue = dvalue_ref[t, v] + nn_dot(lifted.astype(jnp.bfloat16), back_ref[b, h])
            dqkv_ref[t, v] = dvalue.astype(jnp.bfloat16)
        lane = lax.broadcasted_iota(jnp.int32, (length, LANES), 1)
        dqkv_ref[t, pl.ds(vcols, LANES)] = jnp.where(lane < 2 * qcols, dtile, 0.0).astype(
            jnp.bfloat16
        )
        turned_ref[:, t] = dqkv_ref[t].T
        return carry

    each = rows // CHUNKS

    def work(n, step):
        @pl.when(n < CHUNKS)
        def _():
            lax.fori_loop(n * each, (n + 1) * each, first, 0)

        step(n)

        @pl.when(n < CHUNKS)
        def _():
            lax.fori_loop(n * each, (n + 1) * each, here, 0)

        done = n - chain.distance

        @pl.when((done >= 0) & (done < CHUNKS))
        def _():
            lax.fori_loop(done * each, (done + 1) * each, after, 0)

    nothing = lambda: None
    chain.run(
        work,
        [nothing] * 2 + [lambda: advance(scatter, 3)] + [nothing] * 3 + [lambda: advance(scatter)],
    )
    run(scatter)

    def finish(r, carry):
        block_ref[r] = (residual_ref[r] + total_ref[r]).astype(jnp.bfloat16)
        return carry

    row_blocks(block_ref.shape[0], ROW_STEP, finish)(0)
    normed_copy.wait()
    wide = 4 * LANES
    qkv_rows = grad_ref.shape[0] - vcols
    grad_ref[pl.ds(qkv_rows, vcols)] = output_grad_ref[...]

    def gradient(i, carry):
        cols = pl.ds(pl.multiple_of(i * wide, wide), wide)
        grad_ref[pl.ds(0, qkv_rows), cols] = nn_dot(
            turned_ref[pl.ds(0, qkv_rows)], normed_ref[:, cols]
        ).astype(jnp.bfloat16)
        return carry

    lax.fori_loop(0, normed_ref.shape[1] // wide, gradient, 0)
    for c in shards:
        c.wait()
    chain.close()


def unmix(dmixed, normed, output_grad, part, residual, segments, pairs, kept, shards, heads, cid):
    seg_col, seg_row = segments
    tokens, vcols = dmixed.shape
    plane, rows = lax.axis_size("dp"), seg_col.shape[0]
    grad_rows = 2 * vcols + 2 * heads * FDIM
    m, width = residual.shape
    count = len(shards)
    whole, low = pltpu.VMEM, jnp.bfloat16
    dqkv, block, grad, *swapped = kernel_call(
        partial(unmix_kernel, heads, count),
        "unmix",
        cid,
        [
            ((tokens, vcols + LANES), low, whole),
            ((m, width), low, whole),
            ((grad_rows, width), low, whole),
        ]
        + [((plane, p.shape[0], p.shape[1] // plane), p.dtype, pl.ANY) for p in shards],
        [
            (dmixed, whole),
            (normed, pl.ANY),
            (output_grad, whole),
            (part, pl.ANY),
            (residual, whole),
            (seg_col, whole),
            (seg_row, whole),
            (pairs, whole),
        ]
        + [(a, whole) for a in kept]
        + [(p, pl.ANY) for p in shards],
        [
            pltpu.VMEM((tokens, width), low),
            pltpu.VMEM((vcols + LANES, tokens), low),
            pltpu.VMEM((tokens, vcols), jnp.float32),
            pltpu.VMEM((tokens, LANES), jnp.float32),
            pltpu.VMEM((rows, heads, FEATURES, VHEAD), low),
            pltpu.VMEM((rows, 8, FEATURES), jnp.float32),
        ]
        + state_scratch(rows, heads)
        + [pltpu.VMEM((m, width), jnp.float32), pltpu.VMEM((4, m, width), low)]
        + scatter_scratch(m, width)
        + [
            copies(2 * CHUNKS),
            copies(count * (plane - 1)),
            pltpu.SemaphoreType.DMA((count,)),
            copies(SCATTER_COPIES),
            pltpu.SemaphoreType.DMA((4,)),
            pltpu.SemaphoreType.DMA,
        ],
        moved=residual.size * 120,
    )
    return dqkv, block, grad, swapped


def last_kernel(count, *refs):
    ins, gain_ref, outs, sum_ref = (
        refs[:count],
        refs[count],
        refs[count + 1 : 2 * count + 1],
        refs[2 * count + 1],
    )
    got_gain, sems, gain_sems, local_sems = refs[2 * count + 2 :]
    plane, at = lax.axis_size("dp"), lax.axis_index("dp")
    others, me = everyone()
    greet(others)
    copy_gain = Sender(gain_sems)
    gains = [
        copy_gain(gain_ref.at[p["seq"] * plane + p["dp"]], got_gain.at[me], p) for p in others
    ]
    for c in gains:
        c.start()
    chips = [lax.rem(at + k, plane) for k in range(1, plane)]
    shards = swap_shards(ins, outs, chips, at, columns_of, block_of, Sender(sems), local_sems)
    got_gain[me] = gain_ref[lax.axis_index("seq") * plane + at]
    for c in gains:
        c.wait()
    total = got_gain[0]
    for k in range(1, len(others) + 1):
        total += got_gain[k]
    sum_ref[...] = total
    for c in shards:
        c.wait()


def last(shards, gains, cid):
    plane = lax.axis_size("dp")
    count = len(shards)
    devices = lax.axis_size(("dp", "seq", "tensor"))
    *swapped, total = kernel_call(
        partial(last_kernel, count),
        "last",
        cid,
        [((plane, p.shape[0], p.shape[1] // plane), p.dtype, pl.ANY) for p in shards]
        + [(gains.shape[1:], jnp.float32, pltpu.VMEM)],
        [(p, pl.ANY) for p in shards] + [(gains, pltpu.VMEM)],
        [
            pltpu.VMEM((devices,) + gains.shape[1:], jnp.float32),
            copies(count * (plane - 1)),
            copies(devices - 1),
            pltpu.SemaphoreType.DMA((count,)),
        ],
        moved=1 << 26,
    )
    return swapped, total


def everyone():
    plane, span, cores = (lax.axis_size(a) for a in ("dp", "seq", "tensor"))
    at, z, core = (lax.axis_index(a) for a in ("dp", "seq", "tensor"))
    others = [
        {
            "dp": lax.rem(at + i, plane),
            "seq": lax.rem(z + k, span),
            "tensor": lax.rem(core + c, cores),
        }
        for k in range(span)
        for i in range(plane)
        for c in range(cores)
        if i or k or c
    ]
    return others, (at * span + z) * cores + core


def exit_kernel(
    dqkv_ref,
    pack_ref,
    x_ref,
    dresid_ref,
    block_ref,
    small_ref,
    gain_two_ref,
    shards_ref,
    grad_ref,
    out_ref,
    gains_ref,
    shards_all_ref,
    gain_ref,
    part_ref,
    total_ref,
    ordered_ref,
    low_ref,
    pair_ref,
    sum_ref,
    got_ref,
    sems,
    pair_sems,
    local_sems,
    shard_sems,
    shard_local_sems,
):
    plane, at = lax.axis_size("dp"), lax.axis_index("dp")
    core = lax.axis_index("tensor")
    chips = [lax.rem(at + k, plane) for k in range(1, plane)]
    greet([{"dp": p} for p in chips] + [{"tensor": 1 - core}])
    shard_copy = Sender(shard_sems)

    half = shards_ref.shape[0] // 2

    def swap(n):
        rows = pl.ds(n * half, half)
        return swap_shards(
            (shards_ref,),
            (shards_all_ref,),
            chips,
            at,
            lambda ref, p: columns_of(ref, p, rows),
            lambda ref, p: ref.at[p, rows],
            shard_copy,
            shard_local_sems.at[pl.ds(n, 1)],
        )

    shards = swap(0)
    parts, _, depth = pack_ref.shape
    m, width = x_ref.shape
    wide = dqkv_ref.shape[1] - LANES + 2 * FDIM * ((dqkv_ref.shape[1] - LANES) // VHEAD)
    blocks = width // LANES
    copy = Sender(pair_sems)

    def project(b, carry):
        left = dqkv_ref[pl.ds(pl.multiple_of(b * m, m), m), pl.ds(0, wide)]
        for s in range(parts):
            part_ref[b // 2, lax.rem(b, 2), :, pl.ds(s * depth, depth)] = nn_dot(
                left, pack_ref[s, pl.ds(0, wide)]
            ).astype(jnp.bfloat16)
        return carry

    lax.fori_loop(0, 8, project, 0)
    scatter = scatter_steps(part_ref, total_ref, pair_ref, sum_ref, got_ref, Sender(sems))
    next(scatter)

    def order(r, carry):
        for k in range(blocks):
            low_ref[r, lanes(seq_major_block(k))] = block_ref[r, lanes(k)]
        return carry

    row_blocks(m, ROW_STEP, order)(0)
    to_pair = [copy(low_ref, out_ref.at[core], {"tensor": 1 - core})]
    local = [pltpu.make_async_copy(low_ref, out_ref.at[core], local_sems.at[0])]
    to_pair[0].start()
    local[0].start()
    advance(scatter, 4)
    shards += swap(1)
    run(scatter)
    gain_ref[...] = jnp.zeros_like(gain_ref)

    def finish(r, k, v):
        ordered_ref[r, lanes(seq_major_block(k))] = v + dresid_ref[r, lanes(k)]

    def body(r, carry):
        norm_gradient(
            r,
            lambda r, k: x_ref[r, lanes(k)].astype(jnp.float32),
            total_ref,
            lambda k: small_ref[k, 0:1, :],
            gain_ref,
            finish,
            width,
        )
        return carry

    row_blocks(m, ROW_STEP, body)(0)
    to_pair.append(copy(ordered_ref, grad_ref.at[core], {"tensor": 1 - core}))
    local.append(pltpu.make_async_copy(ordered_ref, grad_ref.at[core], local_sems.at[1]))
    to_pair[1].start()
    local[1].start()
    gains_ref[...] = jnp.zeros_like(gains_ref)
    for k in range(blocks):
        for row, ref in enumerate((gain_ref, gain_two_ref)):
            gains_ref[k, row : row + 1] = jnp.sum(ref[:, lanes(k)], axis=0, keepdims=True)
    for c in to_pair + local + shards:
        c.wait()


def leave(dqkv, pack, x, dresid, block, small, gain_two, shards, cid):
    m, width = x.shape
    plane = lax.axis_size("dp")
    whole = pltpu.VMEM
    return kernel_call(
        exit_kernel,
        "leave",
        cid,
        [
            ((2, m, width), jnp.float32, pl.ANY),
            ((2, m, width), jnp.bfloat16, pl.ANY),
            ((width // LANES, 8, LANES), jnp.float32, whole),
        ]
        + [((plane, p.shape[0], p.shape[1] // plane), p.dtype, pl.ANY) for p in shards],
        [(a, whole) for a in (dqkv, pack, x, dresid, block, small, gain_two)]
        + [(p, pl.ANY) for p in shards],
        [
            pltpu.VMEM((8, width), jnp.float32),
            pltpu.VMEM((4, 2, m, width), jnp.bfloat16),
            pltpu.VMEM((m, width), jnp.float32),
            pltpu.VMEM((m, width), jnp.float32),
            pltpu.VMEM((m, width), jnp.bfloat16),
        ]
        + scatter_scratch(m, width)
        + [
            copies(SCATTER_COPIES),
            copies(2),
            pltpu.SemaphoreType.DMA((2,)),
            copies(2 * (plane - 1)),
            pltpu.SemaphoreType.DMA((2,)),
        ],
        moved=x.size * 120,
    )


def plane_local(
    tokens,
    doc_starts,
    attn_gain,
    mlp_gain,
    query_weight,
    key_weight,
    value_weight,
    output_weight,
    gate_weight,
    up_weight,
    down_weight,
    cotangent,
):
    plane, span, cores = (lax.axis_size("dp"), lax.axis_size("seq"), lax.axis_size("tensor"))
    rows, length, width = tokens.shape
    chunk = width // (plane * span)
    own = rows * length // cores
    heads = query_weight.shape[1] // FDIM // plane
    hidden_part = gate_weight.shape[1] // plane
    vcols, qcols = heads * VHEAD, heads * FDIM

    def over_seq(pack):
        return lax.all_gather(pack, "seq", axis=0, tiled=False)

    def summed(grads):
        return lax.psum_scatter(
            grads.astype(jnp.bfloat16), "seq", scatter_dimension=1, tiled=True
        )

    def split(w):
        return w.reshape(plane, -1, chunk)

    small = jnp.concatenate(
        [
            attn_gain.astype(jnp.float32)[None],
            mlp_gain.astype(jnp.float32)[None],
            doc_starts.astype(jnp.float32).reshape(-1, chunk),
            jnp.zeros((2, chunk), jnp.float32),
        ]
    )
    attn_pack = jnp.concatenate(
        [split(value_weight.T), split(query_weight.T), split(key_weight.T), split(output_weight)],
        axis=1,
    )
    [attn_pack] = exchange(
        [attn_pack], 1, [(attn_pack.shape[1], plane * chunk)], put=columns_of
    )
    gate_w = split(gate_weight.T)
    early_w = gate_w[:, :EARLY]
    late_w = jnp.concatenate([gate_w[:, EARLY:], split(up_weight.T)], axis=1)
    early_w, late_w, small = lax.optimization_barrier((early_w, late_w, small, attn_pack))[:3]
    early_w, late_w, small = first_exchange([early_w, late_w], small, 2)
    attn_pack, early_w = over_seq(attn_pack), over_seq(early_w)
    starts = small[:, 2:-2].reshape(span, plane * rows, length)
    segments = jnp.cumsum(
        lax.dynamic_index_in_dim(starts, lax.axis_index("seq"), 0, keepdims=False), axis=1
    )

    qkv_rows = vcols + 2 * qcols
    seg_col = segments[:, :, None]
    seg_row = segments[:, None, :]
    pairs = feature_pairs()
    normed_one, x, cot_own = entry(
        tokens.reshape(cores, own, width), cotangent.reshape(cores, own, width), small, 3
    )
    qkv, state, sums, down_w = states(
        normed_one, attn_pack, seg_col, seg_row, pairs, split(down_weight), heads, 4
    )
    late_w, down_w = lax.optimization_barrier((late_w, down_w))
    late_w, down_w = over_seq(late_w), over_seq(down_w)
    mixed, exact, den, cot = mix(
        qkv, seg_col, seg_row, pairs, state, sums, cot_own, heads, 13
    )
    residual, normed_own = branch(mixed, attn_pack, x, small, 5)
    normed_two, gate, up, hidden = expand(normed_own, early_w, late_w, 11)
    down_grad = nn_dot(hidden, cot).astype(jnp.bfloat16)
    gate, down_grad = lax.optimization_barrier((gate, down_grad))
    down_grad = summed(down_grad)
    out_part, dnormed_two, gate_up_grad = hidden_units(
        gate, up, cot, early_w, late_w, down_w, normed_two, 6
    )
    gate_up_grad = summed(gate_up_grad)
    dresid, gain_two_grad, dmixed, out_grad = turn(
        dnormed_two, residual, cot_own, small, attn_pack, mixed, 12
    )
    dmixed, down_grad = lax.optimization_barrier((dmixed, down_grad))
    dqkv, block_own, attn_grad, (down_grad,) = unmix(
        dmixed,
        normed_one,
        out_grad,
        out_part,
        residual,
        (seg_col, seg_row),
        pairs,
        (qkv, exact, den, state, sums),
        [down_grad],
        heads,
        8,
    )
    attn_grad = summed(attn_grad)
    dtokens, block_out, gains, gate_up_grad = leave(
        dqkv, attn_pack, x, dresid, block_own, small, gain_two_grad, [gate_up_grad], 9
    )
    (attn_grad,), gain_grads = last([attn_grad], gains, 10)

    def stacked(a, start, size):
        return a[:, start : start + size].reshape(plane * size, chunk).astype(jnp.float32)

    h = hidden_part
    return (
        block_out.reshape(rows, length, width),
        dtokens.reshape(rows, length, width),
        gain_grads[0],
        gain_grads[1],
        stacked(attn_grad, vcols, qcols).T,
        stacked(attn_grad, vcols + qcols, qcols).T,
        stacked(attn_grad, 0, vcols).T,
        stacked(attn_grad, qkv_rows, vcols),
        stacked(gate_up_grad, 0, h).T,
        stacked(gate_up_grad, h, h).T,
        stacked(down_grad, 0, h),
    )


def fits_plane(mesh, tokens, query_weight, gate_weight):
    plane, span, cores = (mesh.shape[a] for a in ("dp", "seq", "tensor"))
    heads = query_weight.shape[1] // FDIM // cores
    return (
        plane == 4
        and cores == 2
        and heads % plane == 0
        and (gate_weight.shape[1] // cores) % (16 * plane) == 0
        and gate_weight.shape[1] // cores // plane > EARLY
        and tokens.shape[0] % CHUNKS == 0
    )


def solution(mesh):
    def step(*args):
        use = fits_plane(mesh, args[0], args[4], args[8])
        return sharded(mesh, plane_local if use else local)(*args)

    return step


def sharded(mesh, body):
    return jax.shard_map(
        body,
        mesh=mesh,
        in_specs=(
            P("dp", "seq", None),
            P("dp", "seq"),
            P(("dp", "seq")),
            P(("dp", "seq")),
            P(("dp", "seq"), "tensor"),
            P(("dp", "seq"), "tensor"),
            P(("dp", "seq"), "tensor"),
            P("tensor", ("dp", "seq")),
            P(("dp", "seq"), "tensor"),
            P(("dp", "seq"), "tensor"),
            P("tensor", ("dp", "seq")),
            P("dp", "seq", None),
        ),
        out_specs=(
            P("dp", "seq", None),
            P("dp", "seq", None),
            P(("dp", "seq")),
            P(("dp", "seq")),
            P(("dp", "seq"), "tensor"),
            P(("dp", "seq"), "tensor"),
            P(("dp", "seq"), "tensor"),
            P("tensor", ("dp", "seq")),
            P(("dp", "seq"), "tensor"),
            P(("dp", "seq"), "tensor"),
            P("tensor", ("dp", "seq")),
        ),
        check_vma=False,
    )
```

```python
from functools import partial

import jax
import jax.numpy as jnp
import numpy as np
from jax import lax
from jax.experimental import pallas as pl
from jax.experimental.pallas import tpu as pltpu
from jax.sharding import PartitionSpec as P

FDIM = 16
VHEAD = 128
MICRO = 2


norm_epsilon = 1e-05
highest = lax.Precision.HIGHEST
outer_scale = 0.17677669529663687


def prefix(x, axis, combine, identity, reverse):
    size, index = (lax.axis_size(axis), lax.axis_index(axis))
    everything = jax.tree.map(lambda part: lax.all_gather(part, axis), x)
    start = jax.tree.map(
        lambda part, zero: jnp.broadcast_to(jnp.asarray(zero, part.dtype), part.shape), x, identity
    )

    def turn(k, before):
        at = size - 1 - k if reverse else k
        reached = at > index if reverse else at < index
        new = combine(before, jax.tree.map(lambda part: part[at], everything))
        return jax.tree.map(lambda a, b: jnp.where(reached, a, b), new, before)

    return lax.fori_loop(0, size, turn, start)


def features(vectors):
    ones_col = jnp.ones(vectors.shape[:-1] + (1,), jnp.float32)
    outer_terms = vectors[..., :, None] * vectors[..., None, :] * outer_scale
    outer_terms = outer_terms.reshape(vectors.shape[:-1] + (vectors.shape[-1] * vectors.shape[-1],))
    return jnp.concatenate([ones_col, 0.5 * vectors, outer_terms], axis=-1)


def mix_span(queries, key_rows, values, state_in, norm_in, segments):
    length = queries.shape[1]
    scores = jnp.einsum("rthf,rshf->rhts", queries, key_rows, precision=highest) / 4.0
    kernel = 1.0 + scores + 0.5 * scores * scores
    position = jnp.arange(length)
    causal = position[None, :] <= position[:, None]
    allowed = causal[None] & (segments[:, :, None] == segments[:, None, :])
    kernel = jnp.where(allowed[:, None], kernel, 0.0)
    numerator = jnp.einsum("rhts,rshe->rthe", kernel, values, precision=highest)
    denominator = jnp.transpose(jnp.sum(kernel, axis=-1), (0, 2, 1))
    head_part = (segments == 0).astype(jnp.float32)[:, :, None]
    lifted = features(queries)
    numerator = numerator + head_part[..., None] * jnp.einsum(
        "rthf,rhfe->rthe", lifted, state_in, precision=highest
    )
    denominator = denominator + head_part * jnp.einsum(
        "rthf,rhf->rth", lifted, norm_in, precision=highest
    )
    return numerator / denominator[..., None]


def tail_span(key_rows, values, segments):
    tail_mask = (segments == segments[:, -1:]).astype(jnp.float32)
    lifted = features(key_rows) * tail_mask[:, :, None, None]
    tail_state = jnp.einsum("rshf,rshe->rhfe", lifted, values, precision=highest)
    return (tail_state, jnp.sum(lifted, axis=1))


def combine_carry(earlier_part, later_part):
    keep_rate = 1.0 - later_part[2]
    return (
        later_part[0] + keep_rate[:, None, None, None] * earlier_part[0],
        later_part[1] + keep_rate[:, None, None] * earlier_part[1],
        jnp.maximum(earlier_part[2], later_part[2]),
    )


def inverse_rms(inputs):
    return lax.rsqrt(jnp.mean(inputs * inputs, axis=-1, keepdims=True) + norm_epsilon)


def norm_backward(inputs, scale_row, gain_vec, grad_normed):
    scaled_grad = grad_normed * gain_vec
    grad_gain = jnp.sum(grad_normed * inputs * scale_row, axis=0)
    grad_inputs = scale_row * scaled_grad - inputs * scale_row * scale_row * scale_row * jnp.mean(
        scaled_grad * inputs, axis=-1, keepdims=True
    )
    return (grad_inputs, grad_gain)


def inner_rows(left_mat, right_mat):
    return lax.dot_general(
        left_mat, right_mat, (((0,), (0,)), ((), ())), preferred_element_type=jnp.float32
    )


def by_transpose(left_mat, right_mat):
    return lax.dot_general(
        left_mat, right_mat, (((1,), (1,)), ((), ())), preferred_element_type=jnp.float32
    )


def local(
    tokens,
    doc_starts,
    attn_gain,
    mlp_gain,
    query_weight,
    key_weight,
    value_weight,
    output_weight,
    gate_weight,
    up_weight,
    down_weight,
    cotangent,
):
    micro_rows = tokens.shape[0] // MICRO
    span_len = tokens.shape[1]
    model_width = tokens.shape[2]
    head_count = query_weight.shape[1] // FDIM
    outputs_main = []
    outputs_grad = []
    totals = None
    for micro_index in range(MICRO):
        row_start = micro_index * micro_rows
        rows_in = tokens[row_start : row_start + micro_rows]
        starts_in = doc_starts[row_start : row_start + micro_rows]
        cot_in = cotangent[row_start : row_start + micro_rows].reshape(-1, model_width)
        (
            full_query,
            full_key,
            full_value,
            full_gate,
            full_up,
            full_output,
            full_down,
            gain_one,
            gain_two,
        ) = (
            lax.all_gather(query_weight, ("dp", "seq"), axis=0, tiled=True),
            lax.all_gather(key_weight, ("dp", "seq"), axis=0, tiled=True),
            lax.all_gather(value_weight, ("dp", "seq"), axis=0, tiled=True),
            lax.all_gather(gate_weight, ("dp", "seq"), axis=0, tiled=True),
            lax.all_gather(up_weight, ("dp", "seq"), axis=0, tiled=True),
            lax.all_gather(output_weight, ("dp", "seq"), axis=1, tiled=True),
            lax.all_gather(down_weight, ("dp", "seq"), axis=1, tiled=True),
            lax.all_gather(attn_gain, ("dp", "seq"), axis=0, tiled=True),
            lax.all_gather(mlp_gain, ("dp", "seq"), axis=0, tiled=True),
        )
        gain_one_f = gain_one.astype(jnp.float32)
        gain_two_f = gain_two.astype(jnp.float32)
        flat_rows = rows_in.reshape(-1, model_width).astype(jnp.float32)
        scale_one = inverse_rms(flat_rows)
        normed_one = (flat_rows * scale_one * gain_one_f).astype(jnp.bfloat16)
        query_low = jnp.dot(normed_one, full_query, preferred_element_type=jnp.float32).astype(
            jnp.bfloat16
        )
        key_low = jnp.dot(normed_one, full_key, preferred_element_type=jnp.float32).astype(
            jnp.bfloat16
        )
        value_low = jnp.dot(normed_one, full_value, preferred_element_type=jnp.float32).astype(
            jnp.bfloat16
        )
        queries = query_low.astype(jnp.float32).reshape(micro_rows, span_len, head_count, FDIM)
        key_rows = key_low.astype(jnp.float32).reshape(micro_rows, span_len, head_count, FDIM)
        values = value_low.astype(jnp.float32).reshape(micro_rows, span_len, head_count, VHEAD)
        segments = jnp.cumsum(starts_in, axis=1)
        reset_flag = (segments[:, -1] > 0).astype(jnp.float32)
        (tail_state, tail_norm), tail_pull = jax.vjp(
            partial(tail_span, segments=segments), key_rows, values
        )
        state_in, norm_in, reset_in = prefix(
            (tail_state, tail_norm, reset_flag),
            "seq",
            combine_carry,
            (jnp.zeros_like(tail_state), jnp.zeros_like(tail_norm), jnp.zeros_like(reset_flag)),
            False,
        )
        mixed_heads, mix_pull = jax.vjp(
            partial(mix_span, segments=segments), queries, key_rows, values, state_in, norm_in
        )
        mixed_low = mixed_heads.reshape(-1, head_count * VHEAD).astype(jnp.bfloat16)
        branch_one = jnp.dot(mixed_low, full_output, preferred_element_type=jnp.float32)
        residual = flat_rows + lax.psum(branch_one, "tensor")
        scale_two = inverse_rms(residual)
        normed_two = (residual * scale_two * gain_two_f).astype(jnp.bfloat16)
        gate_proj = jnp.dot(normed_two, full_gate, preferred_element_type=jnp.float32)
        up_proj = jnp.dot(normed_two, full_up, preferred_element_type=jnp.float32)
        sigmoid_gate = jax.nn.sigmoid(gate_proj)
        hidden = (gate_proj * sigmoid_gate * up_proj).astype(jnp.bfloat16)
        branch_two = jnp.dot(hidden, full_down, preferred_element_type=jnp.float32)
        block_low = (
            residual + lax.psum(branch_two.astype(jnp.bfloat16), "tensor").astype(jnp.float32)
        ).astype(jnp.bfloat16)
        outputs_main.append(block_low.reshape(micro_rows, span_len, model_width))
        grad_down = inner_rows(hidden, cot_in)
        grad_hidden = by_transpose(cot_in, full_down)
        grad_gate_low = (
            grad_hidden * up_proj * sigmoid_gate * (1.0 + gate_proj * (1.0 - sigmoid_gate))
        ).astype(jnp.bfloat16)
        grad_up_low = (grad_hidden * gate_proj * sigmoid_gate).astype(jnp.bfloat16)
        grad_gate = inner_rows(normed_two, grad_gate_low)
        grad_up = inner_rows(normed_two, grad_up_low)
        grad_normed_two = by_transpose(grad_gate_low, full_gate) + by_transpose(
            grad_up_low, full_up
        )
        grad_normed_two = lax.psum(grad_normed_two, "tensor")
        grad_resid, grad_gain_two = norm_backward(residual, scale_two, gain_two_f, grad_normed_two)
        grad_resid = grad_resid + cot_in.astype(jnp.float32)
        grad_resid_low = grad_resid.astype(jnp.bfloat16)
        grad_output = inner_rows(mixed_low, grad_resid_low)
        grad_mixed = by_transpose(grad_resid_low, full_output).astype(jnp.bfloat16)
        grad_mixed = (
            lax.optimization_barrier(grad_mixed)
            .astype(jnp.float32)
            .reshape(micro_rows, span_len, head_count, VHEAD)
        )
        grad_queries, grad_keys, grad_values, grad_state, grad_norm = mix_pull(grad_mixed)
        carried_state, carried_norm, reset_out = prefix(
            (grad_state, grad_norm, reset_flag),
            "seq",
            combine_carry,
            (jnp.zeros_like(grad_state), jnp.zeros_like(grad_norm), jnp.zeros_like(reset_flag)),
            True,
        )
        more_keys, more_values = tail_pull((carried_state, carried_norm))
        grad_query_low = grad_queries.reshape(-1, head_count * FDIM).astype(jnp.bfloat16)
        grad_key_low = (grad_keys + more_keys).reshape(-1, head_count * FDIM).astype(jnp.bfloat16)
        grad_value_low = (
            (grad_values + more_values).reshape(-1, head_count * VHEAD).astype(jnp.bfloat16)
        )
        grad_query = inner_rows(normed_one, grad_query_low)
        grad_key = inner_rows(normed_one, grad_key_low)
        grad_value = inner_rows(normed_one, grad_value_low)
        grad_normed_one = (
            by_transpose(grad_query_low, full_query)
            + by_transpose(grad_key_low, full_key)
            + by_transpose(grad_value_low, full_value)
        )
        grad_normed_one = lax.psum(grad_normed_one, "tensor")
        grad_inputs, grad_gain_one = norm_backward(
            flat_rows, scale_one, gain_one_f, grad_normed_one
        )
        outputs_grad.append((grad_resid + grad_inputs).reshape(micro_rows, span_len, model_width))
        shares = (
            grad_query,
            grad_key,
            grad_value,
            grad_gate,
            grad_up,
            grad_output,
            grad_down,
            grad_gain_one,
            grad_gain_two,
        )
        if totals is None:
            totals = shares
        else:
            totals = jax.tree.map(jnp.add, totals, shares)
    totals = (
        lax.psum_scatter(totals[0], ("dp", "seq"), scatter_dimension=0, tiled=True),
        lax.psum_scatter(totals[1], ("dp", "seq"), scatter_dimension=0, tiled=True),
        lax.psum_scatter(totals[2], ("dp", "seq"), scatter_dimension=0, tiled=True),
        lax.psum_scatter(totals[3], ("dp", "seq"), scatter_dimension=0, tiled=True),
        lax.psum_scatter(totals[4], ("dp", "seq"), scatter_dimension=0, tiled=True),
        lax.psum_scatter(totals[5], ("dp", "seq"), scatter_dimension=1, tiled=True),
        lax.psum_scatter(totals[6], ("dp", "seq"), scatter_dimension=1, tiled=True),
        lax.psum_scatter(totals[7], ("dp", "seq"), scatter_dimension=0, tiled=True),
        lax.psum_scatter(totals[8], ("dp", "seq"), scatter_dimension=0, tiled=True),
    )
    return (
        jnp.concatenate(outputs_main, axis=0),
        jnp.concatenate(outputs_grad, axis=0),
        totals[7],
        totals[8],
        totals[0],
        totals[1],
        totals[2],
        totals[5],
        totals[3],
        totals[4],
        totals[6],
    )


MESH_ID = pl.DeviceIdType.MESH
VMEM_LIMIT = 58 << 20
LANES = 128
ROW_STEP = 32


def nt_dot(a, b):
    return lax.dot_general(a, b, (((1,), (1,)), ((), ())), preferred_element_type=jnp.float32)


def tn_dot(a, b):
    return lax.dot_general(a, b, (((0,), (0,)), ((), ())), preferred_element_type=jnp.float32)


def nn_dot(a, b):
    return lax.dot_general(a, b, (((1,), (0,)), ((), ())), preferred_element_type=jnp.float32)


def plane_places():
    at, core = lax.axis_index("dp"), lax.axis_index("tensor")
    x_bit, y_bit = lax.rem(at, 2), at // 2
    return (
        at,
        y_bit * 2 + (1 - x_bit),
        (1 - y_bit) * 2 + x_bit,
        (1 - y_bit) * 2 + (1 - x_bit),
        core,
    )


def greet(places):
    barrier = pltpu.get_barrier_semaphore()
    for place in places:
        pl.semaphore_signal(barrier, inc=1, device_id=place, device_id_type=MESH_ID)
    pl.semaphore_wait(barrier, len(places))


class Sender:
    def __init__(self, sems):
        self.sems, self.used = sems, 0

    def __call__(self, src, dst, place):
        index = self.used
        self.used += 1
        return pltpu.make_async_remote_copy(
            src_ref=src,
            dst_ref=dst,
            send_sem=self.sems.at[0, index],
            recv_sem=self.sems.at[1, index],
            device_id=place,
            device_id_type=MESH_ID,
        )


def greet_plane():
    at, x_at, y_at, _, core = plane_places()
    greet([{"dp": x_at}, {"dp": y_at}, {"tensor": 1 - core}])


def leaving(i):
    at, x_at, y_at, d_at, core = plane_places()
    chip = choose(i < 2, d_at, choose(i < 4, x_at, choose(i < 6, y_at, at)))
    return chip, choose(parity(i) == 0, 1 - core, core)


def produce_parts(block, pairs):
    def body(i, carry):
        block(*leaving(i))
        for j, pair in enumerate(pairs):

            @pl.when(i == 2 * j)
            def _():
                pair.start()

        return carry

    lax.fori_loop(0, 8, body, 0)


def add_rows(dst, *srcs, step=64):
    def body(i, carry):
        r = pl.ds(pl.multiple_of(i * step, step), step)
        total = srcs[0][r].astype(jnp.float32)
        for s in srcs[1:]:
            total = total + s[r].astype(jnp.float32)
        dst[r] = total.astype(dst.dtype)
        return carry

    lax.fori_loop(0, srcs[0].shape[0] // step, body, 0)


GATHER_COPIES = 13
SCATTER_COPIES = 10


def gather_steps(own_ref, out_ref, copy, local_sem):
    at, x_at, y_at, d_at, core = plane_places()
    half = own_ref.shape[0] // 2
    xp, yp, sp = {"dp": x_at}, {"dp": y_at}, {"tensor": 1 - core}
    lo, hi = pl.ds(0, half), pl.ds(half, half)
    mine = out_ref.at[at, core]
    x_lo = copy(own_ref.at[lo], mine.at[lo], xp)
    y_hi = copy(own_ref.at[hi], mine.at[hi], yp)
    x_hi = copy(own_ref.at[hi], mine.at[hi], xp)
    y_lo = copy(own_ref.at[lo], mine.at[lo], yp)
    pair = copy(own_ref, mine, sp)
    for c in (x_lo, y_hi, x_hi, y_lo, pair):
        c.start()
    local_copy = pltpu.make_async_copy(own_ref, mine, local_sem)
    local_copy.start()
    from_x, from_y, from_d = out_ref.at[x_at, core], out_ref.at[y_at, core], out_ref.at[d_at, core]
    on_y = copy(from_x.at[lo], from_x.at[lo], yp)
    on_x = copy(from_y.at[hi], from_y.at[hi], xp)
    handed = [
        copy(block.at[rows], block.at[rows], sp)
        for block, rows in (
            (from_x, lo),
            (from_y, hi),
            (from_x, hi),
            (from_y, lo),
            (from_d, lo),
            (from_d, hi),
        )
    ]
    yield
    local_copy.wait()
    yield
    pair.wait_recv()
    yield
    x_lo.wait_recv()
    on_y.start()
    handed[0].start()
    y_hi.wait_recv()
    on_x.start()
    handed[1].start()
    yield
    handed[0].wait_recv()
    handed[1].wait_recv()
    yield
    x_hi.wait_recv()
    handed[2].start()
    y_lo.wait_recv()
    handed[3].start()
    yield
    handed[2].wait_recv()
    handed[3].wait_recv()
    yield
    on_y.wait_recv()
    handed[4].start()
    on_x.wait_recv()
    handed[5].start()
    yield
    handed[4].wait_recv()
    handed[5].wait_recv()
    yield
    for c in [x_lo, y_hi, x_hi, y_lo, on_y, on_x, pair] + handed:
        c.wait_send()


def scatter_steps(part_ref, out_ref, pair_ref, sum_ref, got_ref, copy, held=None, start=True):
    at, x_at, y_at, d_at, core = plane_places()
    half = part_ref.shape[2] // 2
    xp, yp, sp = {"dp": x_at}, {"dp": y_at}, {"tensor": 1 - core}
    lo, hi = pl.ds(0, half), pl.ds(half, half)
    order = (d_at, x_at, y_at, at)
    pairs = [copy(part_ref.at[to, 1 - core], pair_ref.at[j], sp) for j, to in enumerate(order)]
    own = [part_ref.at[to, core] for to in order]
    fetched = []
    if held is not None:
        buffer, held_sems = held
        fetched = [
            pltpu.make_async_copy(o, buffer.at[j], held_sems.at[j]) for j, o in enumerate(own)
        ]
        own = [buffer.at[j] for j in range(4)]

    def sent(j, rows, place):
        return copy(sum_ref.at[j, rows], got_ref.at[j, rows], place)

    d_lo, d_hi = sent(0, lo, xp), sent(0, hi, yp)
    x_lo, y_hi, x_hi, y_lo = sent(1, lo, xp), sent(2, hi, yp), sent(1, hi, xp), sent(2, lo, yp)
    for c in (pairs if start else []) + fetched:
        c.start()
    yield pairs

    def ready(j):
        if fetched:
            fetched[j].wait()
        pairs[j].wait_recv()

    def total(j, rows, *more):
        add_rows(sum_ref.at[j, rows], own[j].at[rows], pair_ref.at[j, rows], *more)

    ready(0)
    total(0, lo)
    d_lo.start()
    total(0, hi)
    d_hi.start()
    yield
    ready(1)
    total(1, lo)
    x_lo.start()
    yield
    ready(2)
    total(2, hi)
    y_hi.start()
    yield
    d_lo.wait_recv()
    total(2, lo, got_ref.at[0, lo])
    y_lo.start()
    d_hi.wait_recv()
    total(1, hi, got_ref.at[0, hi])
    x_hi.start()
    yield
    ready(3)
    for c in (x_lo, y_hi, y_lo, x_hi):
        c.wait_recv()
    add_rows(out_ref, own[3], pair_ref.at[3], got_ref.at[1], got_ref.at[2])
    for c in pairs + [d_lo, d_hi, x_lo, y_hi, x_hi, y_lo]:
        c.wait_send()


def swap_shards(ins, outs, peers, me, take, put, copy, local_sems):
    started = [
        copy(take(i, p), put(o, me), {"dp": p}) for i, o in zip(ins, outs) for p in peers
    ]
    started += [
        pltpu.make_async_copy(take(i, me), put(o, me), local_sems.at[n])
        for n, (i, o) in enumerate(zip(ins, outs))
    ]
    for c in started:
        c.start()
    return started


def exchange_kernel(take, put, count, *refs):
    ins, outs, sems, local_sems = refs[:count], refs[count : 2 * count], refs[-2], refs[-1]
    size, me = lax.axis_size("dp"), lax.axis_index("dp")
    peers = [lax.rem(me + k, size) for k in range(1, size)]
    greet([{"dp": p} for p in peers])
    for c in swap_shards(ins, outs, peers, me, take, put, Sender(sems), local_sems):
        c.wait()


def block_of(ref, index):
    return ref.at[index]


def columns_of(ref, index, rows=slice(None)):
    width = ref.shape[1] // lax.axis_size("dp")
    return ref.at[rows, pl.ds(pl.multiple_of(index * width, width), width)]


def exchange(arrays, cid, shapes, take=block_of, put=block_of):
    count, peers = len(arrays), lax.axis_size("dp") - 1
    anywhere = [pl.BlockSpec(memory_space=pl.ANY)] * count
    return pl.pallas_call(
        partial(exchange_kernel, take, put, count),
        name="exchange",
        out_shape=[jax.ShapeDtypeStruct(s, x.dtype) for s, x in zip(shapes, arrays)],
        in_specs=anywhere,
        out_specs=anywhere,
        scratch_shapes=[
            pltpu.SemaphoreType.DMA((2, count * peers)),
            pltpu.SemaphoreType.DMA((count,)),
        ],
        compiler_params=pltpu.CompilerParams(collective_id=cid, has_side_effects=True),
        cost_estimate=pl.CostEstimate(
            flops=0, bytes_accessed=60 * sum(x.size for x in arrays), transcendentals=0
        ),
    )(*arrays)


def small_kernel(
    small_ref, pack_ref, all_ref, out_ref, small_sems, small_local_sem, sems, local_sems
):
    plane, span = lax.axis_size("dp"), lax.axis_size("seq")
    at, z = lax.axis_index("dp"), lax.axis_index("seq")
    places = [
        {"dp": lax.rem(at + i, plane), "seq": lax.rem(z + k, span)}
        for k in range(span)
        for i in range(plane)
        if i or k
    ]
    greet(places)
    copy_small = Sender(small_sems)
    block = all_ref.at[z * plane + at]
    started = [copy_small(small_ref, block, p) for p in places]
    started.append(pltpu.make_async_copy(small_ref, block, small_local_sem))
    for c in started:
        c.start()
    chips = [lax.rem(at + k, plane) for k in range(1, plane)]
    started += swap_shards(
        (pack_ref,), (out_ref,), chips, at, block_of, columns_of, Sender(sems), local_sems
    )
    for c in started:
        c.wait()


def small_exchange(small, pack, cid):
    plane, span = lax.axis_size("dp"), lax.axis_size("seq")
    _, size, chunk = pack.shape
    return kernel_call(
        small_kernel,
        "small_exchange",
        cid,
        [
            ((span * plane,) + small.shape, small.dtype, pltpu.VMEM),
            ((size, plane * chunk), pack.dtype, pl.ANY),
        ],
        [(small, pltpu.VMEM), (pack, pl.ANY)],
        [
            copies(plane * span - 1),
            pltpu.SemaphoreType.DMA,
            copies(plane - 1),
            pltpu.SemaphoreType.DMA((1,)),
        ],
        moved=1 << 24,
    )


def advance(steps, count=1):
    for _ in range(count):
        next(steps)


def run(*steps):
    for g in steps:
        for _ in g:
            pass


def row_blocks(rows, step, body):
    def inner(i, carry):
        return body(pl.ds(pl.multiple_of(i * step, step), step), carry)

    return lambda init: lax.fori_loop(0, rows // step, inner, init)


def lanes(k):
    return pl.ds(k * LANES, LANES)


def seq_major_block(k):
    plane, span = lax.axis_size("dp"), lax.axis_size("seq")
    s, g = divmod(k, plane)
    return g * span + s


def mean_of(acc, width):
    return jnp.sum(acc, axis=1, keepdims=True) * (1.0 / width)


def kernel_call(body, name, cid, outs, ins, scratch, flops=0, moved=0):
    params = dict(has_side_effects=True, vmem_limit_bytes=VMEM_LIMIT)
    return pl.pallas_call(
        body,
        name=name,
        out_shape=[jax.ShapeDtypeStruct(s, d) for s, d, _ in outs],
        in_specs=[pl.BlockSpec(memory_space=m) for _, m in ins],
        out_specs=[pl.BlockSpec(memory_space=m) for _, _, m in outs],
        scratch_shapes=scratch,
        compiler_params=pltpu.CompilerParams(collective_id=cid, **params),
        cost_estimate=pl.CostEstimate(flops=flops, bytes_accessed=moved, transcendentals=0),
    )(*[a for a, _ in ins])


def copies(count):
    return pltpu.SemaphoreType.DMA((2, count))


def entry_kernel(
    tokens_ref,
    cot_ref,
    small_ref,
    all_ref,
    x_ref,
    cot_own_ref,
    column_ref,
    row_ref,
    normed_ref,
    sems,
    local_sem,
):
    greet_plane()
    core = lax.axis_index("tensor")
    m, width = x_ref.shape
    blocks = width // LANES

    def body(r, carry):
        acc = jnp.zeros((ROW_STEP, LANES), jnp.float32)
        for k in range(blocks):
            source = lanes(seq_major_block(k))
            v = tokens_ref[core, r, source]
            x_ref[r, lanes(k)] = v
            cot_own_ref[r, lanes(k)] = cot_ref[core, r, source]
            v = v.astype(jnp.float32)
            acc += v * v
        scale = lax.rsqrt(mean_of(acc, width) + norm_epsilon)
        for k in range(blocks):
            v = x_ref[r, lanes(k)].astype(jnp.float32)
            normed_ref[r, lanes(k)] = (v * scale * small_ref[k, 0:1, :]).astype(jnp.bfloat16)
        return carry

    row_blocks(m, ROW_STEP, body)(0)
    gather = gather_steps(normed_ref, all_ref, Sender(sems), local_sem)
    next(gather)
    plane, z = lax.axis_size("dp"), lax.axis_index("seq")
    rows, _, length = row_ref.shape
    pieces = length // LANES
    starts = []
    for chip in range(plane):
        block = small_ref[z * plane + chip]
        for r in range(rows // plane):
            first = 2 + r * pieces
            starts.append(
                jnp.concatenate([block[first + p : first + p + 1] for p in range(pieces)], axis=1)
            )
    starts = jnp.concatenate(starts).astype(jnp.bfloat16)
    down = lax.broadcasted_iota(jnp.int32, (length, length), 0)
    across = lax.broadcasted_iota(jnp.int32, (length, length), 1)
    counts = nn_dot(starts, jnp.where(down <= across, 1.0, 0.0).astype(jnp.bfloat16))
    turned = nt_dot(jnp.where(across <= down, 1.0, 0.0).astype(jnp.bfloat16), starts)
    for b in range(rows):
        row_ref[b] = counts[b : b + 1]
        column_ref[b] = turned[:, b : b + 1]
    run(gather)


def entry(tokens, cot, small, length, cid):
    cores, m, width = tokens.shape
    rows = 4 * cores * m // length
    whole = pltpu.VMEM
    gathered, x, cot_own, seg_col, seg_row = kernel_call(
        entry_kernel,
        "entry",
        cid,
        [
            ((4, cores, m, width), jnp.bfloat16, pl.ANY),
            ((m, width), jnp.bfloat16, whole),
            ((m, width), jnp.bfloat16, whole),
            ((rows, length, 1), jnp.float32, whole),
            ((rows, 1, length), jnp.float32, whole),
        ],
        [(tokens, whole), (cot, whole), (small, whole)],
        [pltpu.VMEM((m, width), jnp.bfloat16), copies(GATHER_COPIES), pltpu.SemaphoreType.DMA],
        moved=tokens.size * 40,
    )
    return gathered.reshape(-1, width), x, cot_own, seg_col, seg_row


FEATURES = 256
STATE_ROWS = 160
PIECES = 1
CHUNKS = 8
EARLY = 192


def feature_pairs():
    first = np.full(FEATURES, -4096, np.int32)
    second = np.full(FEATURES, -4096, np.int32)
    pairs = [(i, j) for i in range(FDIM + 1) for j in range(i, FDIM + 1)]
    for f, (i, j) in enumerate(pairs):
        first[f], second[f] = i, j
    return jnp.asarray(np.stack([first, second] + [first] * 6))


def feature_scale(pairs_ref):
    i, j = pairs_ref[0:1, :], pairs_ref[1:2, :]
    square = jnp.where(i == j, 1.0 / 32.0, 1.0 / 16.0)
    return jnp.where(j == FDIM, jnp.where(i == FDIM, 1.0, 0.25), square)


def fill_selectors(pairs_ref, pick_ref, qcols):
    kinds, heads = pick_ref.shape[:2]
    lane = lax.broadcasted_iota(jnp.int32, (LANES, FEATURES), 0)
    for kind in range(kinds):
        for h in range(heads):
            for side in range(2):
                index = pairs_ref[side : side + 1, :]
                source = jnp.where(
                    index == FDIM, 2 * qcols, index + (kind * qcols + h * FDIM)
                )
                pick_ref[kind, h, side] = jnp.where(lane == source, 1.0, 0.0).astype(jnp.bfloat16)


def factors(tile, pick_ref, kind, h):
    return nn_dot(tile, pick_ref[kind, h, 0]), nn_dot(tile, pick_ref[kind, h, 1])


def keys_in_place(tile, qcols):
    return pltpu.roll(tile.astype(jnp.float32), LANES - qcols, axis=1).astype(jnp.bfloat16)


def head_mask(rows, head):
    lane = lax.broadcasted_iota(jnp.int32, (rows, LANES), 1)
    return (lane >= head * FDIM) & (lane < (head + 1) * FDIM)


def masked_weights(query, key, column, row):
    length = query.shape[0]
    a = nt_dot(query, key) * 0.25
    t = lax.broadcasted_iota(jnp.int32, (length, length), 0)
    s = lax.broadcasted_iota(jnp.int32, (length, length), 1)
    keep = (s <= t) & (column == row)
    return a, jnp.where(keep, 1.0 + a + 0.5 * a * a, 0.0), keep


class Segments:
    def __init__(self, col_ref, row_ref, b):
        self.column, self.row = col_ref[b], row_ref[b]
        last = self.row[:, -1:]
        self.head = self.column == 0.0
        self.tail = self.column == last
        self.keep = jnp.where(last == 0.0, 1.0, 0.0)


class Chain:
    def __init__(self, forward, col_ref, row_ref, state_ref, sums_ref, scratch, copy_sems):
        span, z = lax.axis_size("seq"), lax.axis_index("seq")
        self.span = span
        self.to = {"seq": lax.rem(z + (1 if forward else span - 1), span)}
        self.distance = z if forward else span - 1 - z
        self.gets, self.gives = self.distance > 0, self.distance < span - 1
        self.segments = (col_ref, row_ref)
        self.state_ref, self.sums_ref = state_ref, sums_ref
        self.own_ref, self.own_sums_ref, self.out_ref, self.out_sums_ref = scratch
        self.sems = copy_sems
        self.rows = state_ref.shape[0] // CHUNKS

    def pieces(self, g):
        some = STATE_ROWS // PIECES
        return [
            (g * self.rows + i, h, k * some)
            for i in range(self.rows)
            for h in range(self.state_ref.shape[1])
            for k in range(PIECES)
        ]

    def move(self, g, n, source, target):
        count = self.rows * self.state_ref.shape[1] * PIECES + 1
        return pltpu.make_async_remote_copy(
            src_ref=source,
            dst_ref=target,
            send_sem=self.sems.at[0, count * g + n],
            recv_sem=self.sems.at[1, count * g + n],
            device_id=self.to,
            device_id_type=MESH_ID,
        )

    def moves(self, g):
        part = pl.ds(g * self.rows, self.rows)
        found = [self.move(g, 0, self.out_sums_ref.at[part], self.sums_ref.at[part])]
        for n, (b, h, first) in enumerate(self.pieces(g)):
            used = pl.ds(first, STATE_ROWS // PIECES)
            found.append(
                self.move(g, n + 1, self.out_ref.at[b, h, used], self.state_ref.at[b, h, used])
            )
        return found

    def step(self, n):
        g = n - self.distance

        @pl.when((g >= 0) & (g < CHUNKS))
        def _():
            moves = self.moves(g)

            def take(move):
                @pl.when(self.gets)
                def _():
                    move.wait_recv()

            def give(move):
                @pl.when(self.gives)
                def _():
                    move.start()

            for (b, h, first), move in zip(self.pieces(g), moves[1:]):
                take(move)
                used = pl.ds(first, STATE_ROWS // PIECES)
                keep = Segments(*self.segments, b).keep
                before = self.state_ref[b, h, used].astype(jnp.float32)
                self.out_ref[b, h, used] = (self.own_ref[b, h, used] + keep * before).astype(
                    jnp.bfloat16
                )
                give(move)
            take(moves[0])
            for i in range(self.rows):
                b = g * self.rows + i
                keep = Segments(*self.segments, b).keep
                self.out_sums_ref[b] = self.own_sums_ref[b] + keep * self.sums_ref[b]
            give(moves[0])

    def run(self, work, between=()):
        def body(n, carry):
            for at, piece in enumerate(between):

                @pl.when(n == at)
                def _():
                    piece()

            work(n, self.step)
            return carry

        lax.fori_loop(0, CHUNKS + self.span - 1, body, 0)

    def close(self):
        @pl.when(self.gives)
        def _():
            for g in range(CHUNKS):
                for c in self.moves(g):
                    c.wait_send()


def states_kernel(
    heads,
    normed_ref,
    pack_ref,
    col_ref,
    row_ref,
    pairs_ref,
    late_ref,
    qkv_ref,
    state_ref,
    sums_ref,
    late_all_ref,
    pick_ref,
    own_ref,
    own_sums_ref,
    out_ref,
    out_sums_ref,
    sems,
    shard_sems,
    shard_local_sems,
):
    parts, _, depth = pack_ref.shape
    rows, length = col_ref.shape[0], col_ref.shape[1]
    vcols, qcols = heads * VHEAD, heads * FDIM
    plane, span = lax.axis_size("dp"), lax.axis_size("seq")
    at, z = lax.axis_index("dp"), lax.axis_index("seq")
    chips = [lax.rem(at + k, plane) for k in range(1, plane)]
    state_ref[...] = jnp.zeros_like(state_ref)
    sums_ref[...] = jnp.zeros_like(sums_ref)
    greet(
        [{"dp": p} for p in chips] + [{"seq": lax.rem(z + k, span)} for k in (1, span - 1)]
    )
    shards = swap_shards(
        (late_ref,),
        (late_all_ref,),
        chips,
        at,
        block_of,
        columns_of,
        Sender(shard_sems),
        shard_local_sems,
    )
    chain = Chain(
        True,
        col_ref,
        row_ref,
        state_ref,
        sums_ref,
        (own_ref, own_sums_ref, out_ref, out_sums_ref),
        sems,
    )
    fill_selectors(pairs_ref, pick_ref, qcols)
    scale = feature_scale(pairs_ref)

    def tokens_of(b):
        return pl.ds(pl.multiple_of(b * length, length), length)

    def first(b, carry):
        t = tokens_of(b)
        value = jnp.zeros((length, vcols), jnp.float32)
        tile = jnp.zeros((length, LANES), jnp.float32)
        for s in range(parts):
            piece = normed_ref[t, pl.ds(s * depth, depth)]
            value += nt_dot(piece, pack_ref[s, pl.ds(0, vcols)])
            tile += nt_dot(piece, pack_ref[s, pl.ds(vcols, LANES)])
        lane = lax.broadcasted_iota(jnp.int32, (length, LANES), 1)
        tile = jnp.where(lane < 2 * qcols, tile, jnp.where(lane == 2 * qcols, 1.0, 0.0))
        value, tile = value.astype(jnp.bfloat16), tile.astype(jnp.bfloat16)
        qkv_ref[t, pl.ds(0, vcols)] = value
        qkv_ref[t, pl.ds(vcols, LANES)] = tile
        tail = Segments(col_ref, row_ref, b).tail
        for h in range(heads):
            one, two = factors(tile, pick_ref, 1, h)
            lifted = jnp.where(tail, one * two * scale, 0.0)
            own_ref[b, h] = tn_dot(
                lifted.astype(jnp.bfloat16), value[:, h * VHEAD : (h + 1) * VHEAD]
            )
            own_sums_ref[b, h : h + 1] = jnp.sum(lifted, axis=0, keepdims=True)
        return carry

    own_sums_ref[...] = jnp.zeros_like(own_sums_ref)
    each = rows // CHUNKS

    def work(n, step):
        @pl.when(n < CHUNKS)
        def _():
            lax.fori_loop(n * each, (n + 1) * each, first, 0)

        step(n)

    chain.run(work)
    for c in shards:
        c.wait()
    chain.close()


def mix_kernel(
    heads,
    qkv_ref,
    col_ref,
    row_ref,
    pairs_ref,
    state_ref,
    sums_ref,
    cot_ref,
    mixed_ref,
    exact_ref,
    den_ref,
    cot_all_ref,
    pick_ref,
    cot_sems,
    local_sem,
):
    rows, length = col_ref.shape[0], col_ref.shape[1]
    vcols, qcols = heads * VHEAD, heads * FDIM
    greet_plane()
    gather = gather_steps(cot_ref, cot_all_ref, Sender(cot_sems), local_sem)
    next(gather)
    fill_selectors(pairs_ref, pick_ref, qcols)

    def tokens_of(b):
        return pl.ds(pl.multiple_of(b * length, length), length)

    lane = lax.broadcasted_iota(jnp.int32, (length, LANES), 1)

    def here(b, carry):
        t = tokens_of(b)
        seg = Segments(col_ref, row_ref, b)
        tile = qkv_ref[t, pl.ds(vcols, LANES)]
        key = keys_in_place(tile, qcols)
        dens = jnp.zeros((length, LANES), jnp.float32)
        for h in range(heads):
            v = pl.ds(h * VHEAD, VHEAD)
            query = jnp.where(head_mask(length, h), tile, jnp.zeros_like(tile))
            _, w, _ = masked_weights(query, key, seg.column, seg.row)
            exact_ref[t, v] = nn_dot(w.astype(jnp.bfloat16), qkv_ref[t, v])
            dens = jnp.where(lane == h, jnp.sum(w, axis=1, keepdims=True), dens)
        den_ref[t] = dens
        return carry

    def before(b, carry):
        t = tokens_of(b)
        head = Segments(col_ref, row_ref, b).head
        tile = qkv_ref[t, pl.ds(vcols, LANES)]
        dens = den_ref[t]
        for h in range(heads):
            v = pl.ds(h * VHEAD, VHEAD)
            one, two = factors(tile, pick_ref, 0, h)
            lifted = jnp.where(head, one * two, 0.0)
            num = exact_ref[t, v] + nn_dot(lifted.astype(jnp.bfloat16), state_ref[b, h])
            den = dens[:, h : h + 1]
            den += jnp.sum(lifted * sums_ref[b, h : h + 1], axis=1, keepdims=True)
            value = num / den
            exact_ref[t, v] = value
            mixed_ref[t, v] = value.astype(jnp.bfloat16)
            dens = jnp.where(lane == h, den, dens)
        den_ref[t] = dens
        return carry

    def row(b, carry):
        for at in range(1, 6):

            @pl.when(b == at)
            def _():
                next(gather)

        here(b, 0)
        before(b, 0)
        return carry

    lax.fori_loop(0, rows, row, 0)
    run(gather)


def state_scratch(rows, heads):
    return [
        pltpu.VMEM((2, heads, 2, LANES, FEATURES), jnp.bfloat16),
        pltpu.VMEM((rows, heads, FEATURES, VHEAD), jnp.float32),
        pltpu.VMEM((rows, 8, FEATURES), jnp.float32),
        pltpu.VMEM((rows, heads, FEATURES, VHEAD), jnp.bfloat16),
        pltpu.VMEM((rows, 8, FEATURES), jnp.float32),
    ]


def states(normed, pack, seg_col, seg_row, pairs, shards, heads, cid):
    tokens = normed.shape[0]
    rows = seg_col.shape[0]
    vcols = heads * VHEAD
    plane = lax.axis_size("dp")
    whole = pltpu.VMEM
    return kernel_call(
        partial(states_kernel, heads),
        "states",
        cid,
        [
            ((tokens, vcols + LANES), jnp.bfloat16, whole),
            ((rows, heads, FEATURES, VHEAD), jnp.bfloat16, whole),
            ((rows, 8, FEATURES), jnp.float32, whole),
        ]
        + [((p.shape[1], plane * p.shape[2]), p.dtype, pl.ANY) for p in shards],
        [(a, whole) for a in (normed, pack, seg_col, seg_row, pairs)]
        + [(p, pl.ANY) for p in shards],
        state_scratch(rows, heads)
        + [
            copies(rows * heads * PIECES + CHUNKS),
            copies(len(shards) * (plane - 1)),
            pltpu.SemaphoreType.DMA((len(shards),)),
        ],
        moved=normed.size * 20,
    )


def mix(qkv, seg_col, seg_row, pairs, state, sums, cot_own, heads, cid):
    tokens = qkv.shape[0]
    vcols = heads * VHEAD
    m, width = cot_own.shape
    whole = pltpu.VMEM
    mixed, exact, den, cot = kernel_call(
        partial(mix_kernel, heads),
        "mix",
        cid,
        [
            ((tokens, vcols), jnp.bfloat16, whole),
            ((tokens, vcols), jnp.float32, whole),
            ((tokens, LANES), jnp.float32, whole),
            ((4, 2, m, width), jnp.bfloat16, pl.ANY),
        ],
        [(a, whole) for a in (qkv, seg_col, seg_row, pairs, state, sums, cot_own)],
        [
            pltpu.VMEM((2, heads, 2, LANES, FEATURES), jnp.bfloat16),
            copies(GATHER_COPIES),
            pltpu.SemaphoreType.DMA,
        ],
        moved=cot_own.size * 80,
    )
    return mixed, exact, den, cot.reshape(-1, width)


def branch_kernel(
    mixed_ref,
    pack_ref,
    x_ref,
    small_ref,
    residual_ref,
    normed_ref,
    part_ref,
    pair_ref,
    sum_ref,
    got_ref,
    sems,
):
    greet_plane()
    parts, _, depth = pack_ref.shape
    m, width = x_ref.shape
    vcols = mixed_ref.shape[1]
    first = pack_ref.shape[1] - EARLY - vcols

    def block(chip, core):
        left = mixed_ref[pl.ds(pl.multiple_of((chip * 2 + core) * m, m), m)]
        for s in range(parts):
            part_ref[chip, core, :, pl.ds(s * depth, depth)] = nn_dot(
                left, pack_ref[s, pl.ds(first, vcols)]
            ).astype(jnp.bfloat16)

    scatter = scatter_steps(
        part_ref, residual_ref, pair_ref, sum_ref, got_ref, Sender(sems), start=False
    )
    produce_parts(block, next(scatter))
    run(scatter)

    def body(r, carry):
        acc = jnp.zeros((ROW_STEP, LANES), jnp.float32)
        for k in range(width // LANES):
            v = residual_ref[r, lanes(k)] + x_ref[r, lanes(k)].astype(jnp.float32)
            residual_ref[r, lanes(k)] = v
            acc += v * v
        scale = lax.rsqrt(mean_of(acc, width) + norm_epsilon)
        for k in range(width // LANES):
            normed_ref[r, lanes(k)] = (
                residual_ref[r, lanes(k)] * scale * small_ref[k, 1:2, :]
            ).astype(jnp.bfloat16)
        return carry

    row_blocks(m, ROW_STEP, body)(0)


def scatter_scratch(m, width):
    return [
        pltpu.VMEM((4, m, width), jnp.bfloat16),
        pltpu.VMEM((3, m, width), jnp.bfloat16),
        pltpu.VMEM((3, m, width), jnp.bfloat16),
    ]


def branch(mixed, pack, x, small, cid):
    m, width = x.shape
    whole = pltpu.VMEM
    return kernel_call(
        branch_kernel,
        "branch",
        cid,
        [((m, width), jnp.float32, whole), ((m, width), jnp.bfloat16, whole)],
        [(mixed, whole), (pack, whole), (x, whole), (small, whole)],
        [pltpu.VMEM((4, 2, m, width), jnp.bfloat16)]
        + scatter_scratch(m, width)
        + [copies(SCATTER_COPIES)],
        moved=x.size * 80,
    )


def parity(i):
    return i % 2 if isinstance(i, int) else lax.rem(i, 2)


def choose(test, a, b):
    if isinstance(test, bool):
        return a if test else b
    return jnp.where(test, a, b)


def project(at, w_ref, rows):
    parts, _, depth = w_ref.shape
    total = nt_dot(at(pl.ds(0, depth)), w_ref[0, rows])
    for s in range(1, parts):
        total += nt_dot(at(pl.ds(s * depth, depth)), w_ref[s, rows])
    return total


def arrivals(i, half):
    at, x_at, y_at, d_at, core = plane_places()
    k = choose(parity(i) == 0, core, 1 - core)
    one = choose(i < 2, at, choose(i < 6, x_at, d_at))
    two = choose(i < 2, at, choose(i < 6, y_at, d_at))
    late = (i >= 4) & (i < 6)
    late = int(late) if isinstance(late, bool) else late.astype(jnp.int32)
    first, second = late * half, (1 - late) * half
    if not isinstance(i, int):
        first, second = pl.multiple_of(first, half), pl.multiple_of(second, half)
    return (one, k, first), (two, k, second)


def stacked_copies(early, late, out, sems):
    rows = pl.ds(early.shape[1] - EARLY, EARLY)
    return [
        pltpu.make_async_copy(early.at[:, rows], out.at[:, pl.ds(0, EARLY)], sems.at[0]),
        pltpu.make_async_copy(late, out.at[:, pl.ds(EARLY, late.shape[1])], sems.at[1]),
    ]


def expand_kernel(
    own_ref,
    early_hbm,
    late_hbm,
    normed_hbm,
    gate_hbm,
    up_hbm,
    hidden_hbm,
    normed_ref,
    w_ref,
    gate_ref,
    up_ref,
    hidden_ref,
    sems,
    local_sem,
    w_sems,
    store_sems,
    keep_sem,
):
    greet_plane()
    half = own_ref.shape[0] // 2
    units = gate_ref.shape[2]
    gather = gather_steps(own_ref, normed_ref, Sender(sems), local_sem)
    next(gather)
    weights = stacked_copies(early_hbm, late_hbm, w_ref, w_sems)
    for c in weights:
        c.start()

    def store_copies(i):
        slot = parity(i)
        found = []
        for n, (c, k, r) in enumerate(arrivals(i, half)):
            rows = pl.ds(n * half, half)
            column = (c * 2 + k) * (2 * half) + r
            pairs = (
                (gate_ref.at[slot, rows], gate_hbm.at[c, k, pl.ds(r, half)]),
                (up_ref.at[slot, rows], up_hbm.at[c, k, pl.ds(r, half)]),
                (
                    hidden_ref.at[slot, :, rows],
                    hidden_hbm.at[:, pl.ds(pl.multiple_of(column, half), half)],
                ),
            )
            for q, (a, b) in enumerate(pairs):
                found.append(pltpu.make_async_copy(a, b, store_sems.at[slot, 3 * n + q]))
        return found

    next(gather)
    for c in weights:
        c.wait()

    def body(i, carry):
        for step in range(1, 8):

            @pl.when(i == step)
            def _():
                next(gather)

        @pl.when(i >= 2)
        def _():
            for c in store_copies(i - 2):
                c.wait()

        slot = parity(i)
        pieces = arrivals(i, half)

        def columns(cols):
            return jnp.concatenate([normed_ref[c, k, pl.ds(r, half), cols] for c, k, r in pieces])

        gate = project(columns, w_ref, pl.ds(0, units))
        up = project(columns, w_ref, pl.ds(units, units))
        gate_ref[slot], up_ref[slot] = gate, up
        hidden_ref[slot] = (gate * jax.nn.sigmoid(gate) * up).astype(jnp.bfloat16).T
        for c in store_copies(i):
            c.start()
        return carry

    lax.fori_loop(0, 8, body, 0)
    keep = pltpu.make_async_copy(normed_ref, normed_hbm, keep_sem)
    keep.start()
    for i in (6, 7):
        for c in store_copies(i):
            c.wait()
    keep.wait()
    run(gather)


def expand(own, early, late, cid):
    m, width = own.shape
    weights = (early.shape[0], EARLY + late.shape[1], early.shape[2])
    units = weights[1] // 2
    low = jnp.bfloat16
    thin = ((4, 2, m, units), jnp.float32, pl.ANY)
    normed, gate, up, hidden = kernel_call(
        expand_kernel,
        "expand",
        cid,
        [((4, 2, m, width), low, pl.ANY), thin, thin, ((units, 8 * m), low, pl.ANY)],
        [(own, pltpu.VMEM), (early, pl.ANY), (late, pl.ANY)],
        [
            pltpu.VMEM((4, 2, m, width), low),
            pltpu.VMEM(weights, low),
            pltpu.VMEM((2, m, units), jnp.float32),
            pltpu.VMEM((2, m, units), jnp.float32),
            pltpu.VMEM((2, units, m), low),
            copies(GATHER_COPIES),
            pltpu.SemaphoreType.DMA,
            pltpu.SemaphoreType.DMA((2,)),
            pltpu.SemaphoreType.DMA((2, 6)),
            pltpu.SemaphoreType.DMA,
        ],
        flops=32 * m * width * units,
        moved=1 << 27,
    )
    return normed.reshape(8 * m, width), gate, up, hidden


def hidden_kernel(
    gate_hbm,
    up_hbm,
    cot_hbm,
    early_hbm,
    late_hbm,
    down_hbm,
    normed_hbm,
    out_hbm,
    total_ref,
    grads_hbm,
    gate_ref,
    up_ref,
    cot_ref,
    out_ref,
    w_ref,
    down_w_ref,
    part_ref,
    pair_ref,
    sum_ref,
    got_ref,
    turned_ref,
    normed_ref,
    grad_ref,
    sems,
    w_sems,
    load_sems,
    store_sems,
    normed_sem,
    grad_sems,
):
    greet_plane()
    at, x_at, y_at, d_at, core = plane_places()
    parts, units, depth = down_w_ref.shape
    m = cot_ref.shape[1]
    scatter = scatter_steps(
        part_ref, total_ref, pair_ref, sum_ref, got_ref, Sender(sems), start=False
    )
    pairs = next(scatter)
    weights = stacked_copies(early_hbm, late_hbm, w_ref, w_sems)
    weights.append(pltpu.make_async_copy(down_hbm, down_w_ref, w_sems.at[2]))
    normed_copy = pltpu.make_async_copy(normed_hbm, normed_ref, normed_sem)

    def loads(i):
        slot, (c, k) = parity(i), leaving(i)
        return [
            pltpu.make_async_copy(a.at[c, k], b.at[slot], load_sems.at[slot, n])
            for n, (a, b) in enumerate(
                ((gate_hbm, gate_ref), (up_hbm, up_ref), (cot_hbm, cot_ref))
            )
        ]

    def store(i):
        slot, (c, k) = parity(i), leaving(i)
        return pltpu.make_async_copy(out_ref.at[slot], out_hbm.at[c, k], store_sems.at[slot])

    for c in weights + loads(0):
        c.start()
    normed_copy.start()
    for c in weights:
        c.wait()

    def body(i, carry):
        for step in (2, 4, 6):

            @pl.when(i == step)
            def _():
                next(scatter)

        @pl.when(i < 7)
        def _():
            for c in loads(i + 1):
                c.start()

        for c in loads(i):
            c.wait()

        @pl.when(i >= 2)
        def _():
            store(i - 2).wait()

        slot, (chip, k) = parity(i), leaving(i)
        gate, up = gate_ref[slot], up_ref[slot]
        dhidden = project(lambda cols: cot_ref[slot, :, cols], down_w_ref, pl.ds(0, units))
        sig = jax.nn.sigmoid(gate)
        silu = gate * sig
        hidden = (silu * up).astype(jnp.bfloat16)
        dgate = (dhidden * up * sig * (1.0 + gate * (1.0 - sig))).astype(jnp.bfloat16)
        dup = (dhidden * silu).astype(jnp.bfloat16)
        for s in range(parts):
            cols = pl.ds(s * depth, depth)
            part_ref[chip, k, :, cols] = (
                nn_dot(dgate, w_ref[s, pl.ds(0, units)])
                + nn_dot(dup, w_ref[s, pl.ds(units, units)])
            ).astype(jnp.bfloat16)
            out_ref[slot, :, cols] = nn_dot(hidden, down_w_ref[s]).astype(jnp.bfloat16)
        store(i).start()
        for j in range(4):

            @pl.when(i == 2 * j)
            def _():
                pairs[j].start()

        column = pl.ds(pl.multiple_of((chip * 2 + k) * m, m), m)
        turned_ref[0, :, column], turned_ref[1, :, column] = dgate.T, dup.T
        return carry

    lax.fori_loop(0, 8, body, 0)
    next(scatter)
    store(6).wait()
    store(7).wait()
    normed_copy.wait()
    width = grad_ref.shape[2]
    blocks = normed_ref.shape[1] // width

    def gradients(which):
        rows = pl.ds(which * units, units)

        def stored(i):
            column = pl.ds(pl.multiple_of(i * width, width), width)
            slot = parity(i)
            return pltpu.make_async_copy(
                grad_ref.at[slot], grads_hbm.at[rows, column], grad_sems.at[slot]
            )

        def body(i, carry):
            column = pl.ds(pl.multiple_of(i * width, width), width)

            @pl.when(i >= 2)
            def _():
                stored(i - 2).wait()

            grad_ref[parity(i)] = nn_dot(turned_ref[which], normed_ref[:, column]).astype(
                jnp.bfloat16
            )
            stored(i).start()
            return carry

        lax.fori_loop(0, blocks, body, 0)
        for i in (blocks - 2, blocks - 1):
            stored(i).wait()

    gradients(0)
    gradients(1)
    run(scatter)


def hidden_units(gate, up, cot, early, late, down_w, normed, cid):
    _, _, m, units = gate.shape
    tokens, width = normed.shape
    low = jnp.bfloat16
    stacked = (early.shape[0], EARLY + late.shape[1], early.shape[2])
    ins = (gate, up, cot.reshape(4, 2, m, width), early, late, down_w, normed)
    return kernel_call(
        hidden_kernel,
        "hidden_units",
        cid,
        [
            ((4, 2, m, width), low, pl.ANY),
            ((m, width), jnp.float32, pltpu.VMEM),
            ((2 * units, width), low, pl.ANY),
        ],
        [(a, pl.ANY) for a in ins],
        [
            pltpu.VMEM((2, m, units), jnp.float32),
            pltpu.VMEM((2, m, units), jnp.float32),
            pltpu.VMEM((2, m, width), low),
            pltpu.VMEM((2, m, width), low),
            pltpu.VMEM(stacked, low),
            pltpu.VMEM(down_w.shape, low),
            pltpu.VMEM((4, 2, m, width), low),
        ]
        + scatter_scratch(m, width)
        + [
            pltpu.VMEM((2, units, tokens), low),
            pltpu.VMEM((tokens, width), low),
            pltpu.VMEM((2, units, 2 * LANES), low),
            copies(SCATTER_COPIES),
            pltpu.SemaphoreType.DMA((3,)),
            pltpu.SemaphoreType.DMA((2, 3)),
            pltpu.SemaphoreType.DMA((2,)),
            pltpu.SemaphoreType.DMA,
            pltpu.SemaphoreType.DMA((2,)),
        ],
        flops=12 * tokens * width * units,
        moved=1 << 27,
    )


def norm_gradient(r, value_at, grad_ref, gain_at, gain_grad, finish, width):
    squares = jnp.zeros((ROW_STEP, LANES), jnp.float32)
    cross = jnp.zeros((ROW_STEP, LANES), jnp.float32)
    for k in range(width // LANES):
        v = value_at(r, k)
        squares += v * v
        cross += v * grad_ref[r, lanes(k)] * gain_at(k)
    scale = lax.rsqrt(mean_of(squares, width) + norm_epsilon)
    pull = mean_of(cross, width) * scale * scale * scale
    for k in range(width // LANES):
        v, g = value_at(r, k), grad_ref[r, lanes(k)]
        gain_grad[:, lanes(k)] += jnp.sum(
            (g * v * scale).reshape(ROW_STEP // 8, 8, LANES), axis=0
        )
        finish(r, k, scale * g * gain_at(k) - v * pull)


def turn_kernel(
    total_ref,
    residual_ref,
    cot_ref,
    small_ref,
    pack_ref,
    mixed_ref,
    dresid_ref,
    gain_ref,
    dmixed_ref,
    grad_ref,
    all_ref,
    low_ref,
    sum_ref,
    gather_sems,
    local_sem,
):
    greet_plane()
    m, width = residual_ref.shape
    half = m // 2
    parts, _, depth = pack_ref.shape
    vcols = mixed_ref.shape[3]
    first_row = pack_ref.shape[1] - EARLY - vcols
    gain_ref[...] = jnp.zeros_like(gain_ref)

    def finish(r, k, v):
        v += cot_ref[r, lanes(k)].astype(jnp.float32)
        dresid_ref[r, lanes(k)] = v
        low_ref[r, lanes(k)] = v.astype(jnp.bfloat16)

    def body(r, carry):
        norm_gradient(
            r,
            lambda r, k: residual_ref[r, lanes(k)],
            total_ref,
            lambda k: small_ref[k, 1:2, :],
            gain_ref,
            finish,
            width,
        )
        return carry

    row_blocks(m, ROW_STEP, body)(0)
    gather = gather_steps(low_ref, all_ref, Sender(gather_sems), local_sem)
    next(gather)
    sum_ref[...] = jnp.zeros_like(sum_ref)
    next(gather)

    def block(i, carry):
        for step in range(1, 8):

            @pl.when(i == step)
            def _():
                next(gather)

        pieces = arrivals(i, half)

        def columns(cols):
            return jnp.concatenate([all_ref[c, k, pl.ds(r, half), cols] for c, k, r in pieces])

        left = jnp.concatenate([mixed_ref[c, k, pl.ds(r, half)] for c, k, r in pieces])
        dmixed = project(columns, pack_ref, pl.ds(first_row, vcols)).astype(jnp.bfloat16)
        for n, (c, k, r) in enumerate(pieces):
            dmixed_ref[c, k, pl.ds(r, half)] = dmixed[n * half : (n + 1) * half]
        for s in range(parts):
            cols = pl.ds(s * depth, depth)
            sum_ref[:, cols] += tn_dot(left, columns(cols))
        return carry

    lax.fori_loop(0, 8, block, 0)
    grad_ref[...] = sum_ref[...].astype(jnp.bfloat16)
    run(gather)


def turn(total, residual, cot_own, small, pack, mixed, cid):
    m, width = residual.shape
    vcols = mixed.shape[1]
    whole, low = pltpu.VMEM, jnp.bfloat16
    dresid, gain, dmixed, grad = kernel_call(
        turn_kernel,
        "turn",
        cid,
        [
            ((m, width), jnp.float32, whole),
            ((8, width), jnp.float32, whole),
            ((4, 2, m, vcols), low, whole),
            ((vcols, width), low, whole),
        ],
        [(a, whole) for a in (total, residual, cot_own, small, pack)]
        + [(mixed.reshape(4, 2, m, vcols), whole)],
        [
            pltpu.VMEM((4, 2, m, width), low),
            pltpu.VMEM((m, width), low),
            pltpu.VMEM((vcols, width), jnp.float32),
            copies(GATHER_COPIES),
            pltpu.SemaphoreType.DMA,
        ],
        moved=residual.size * 80,
    )
    return dresid, gain, dmixed.reshape(8 * m, vcols), grad


def unmix_kernel(
    heads,
    count,
    dmixed_ref,
    normed_hbm,
    output_grad_ref,
    part_ref,
    residual_ref,
    col_ref,
    row_ref,
    pairs_ref,
    qkv_ref,
    exact_ref,
    den_ref,
    state_ref,
    sums_ref,
    *refs,
):
    ins, dqkv_ref, block_ref, grad_ref = refs[:count], *refs[count : count + 3]
    outs = refs[count + 3 : 2 * count + 3]
    (
        normed_ref,
        turned_ref,
        dvalue_ref,
        dtile_ref,
        back_ref,
        back_sums_ref,
        pick_ref,
        own_ref,
        own_sums_ref,
        out_ref,
        out_sums_ref,
        total_ref,
        held_ref,
        pair_ref,
        sum_ref,
        got_ref,
        sems,
        shard_sems,
        local_sems,
        scatter_sems,
        held_sems,
        normed_sem,
    ) = refs[2 * count + 3 :]
    rows, length = col_ref.shape[0], col_ref.shape[1]
    vcols, qcols = heads * VHEAD, heads * FDIM
    at, x_at, y_at, _, core = plane_places()
    plane, span, z = lax.axis_size("dp"), lax.axis_size("seq"), lax.axis_index("seq")
    chips = [lax.rem(at + k, plane) for k in range(1, plane)]
    normed_copy = pltpu.make_async_copy(normed_hbm, normed_ref, normed_sem)
    normed_copy.start()
    back_ref[...] = jnp.zeros_like(back_ref)
    back_sums_ref[...] = jnp.zeros_like(back_sums_ref)
    greet(
        [{"dp": p} for p in chips]
        + [{"tensor": 1 - core}]
        + [{"seq": lax.rem(z + k, span)} for k in (1, span - 1)]
    )
    scatter = scatter_steps(
        part_ref,
        total_ref,
        pair_ref,
        sum_ref,
        got_ref,
        Sender(scatter_sems),
        (held_ref, held_sems),
    )
    next(scatter)
    chain = Chain(
        False,
        col_ref,
        row_ref,
        back_ref,
        back_sums_ref,
        (own_ref, own_sums_ref, out_ref, out_sums_ref),
        sems,
    )
    fill_selectors(pairs_ref, pick_ref, qcols)
    scale = feature_scale(pairs_ref)

    def tokens_of(b):
        return pl.ds(pl.multiple_of(b * length, length), length)

    def cotangents(t, h):
        v = pl.ds(h * VHEAD, VHEAD)
        dn = dmixed_ref[t, v].astype(jnp.float32) / den_ref[t, pl.ds(h, 1)]
        dd = -jnp.sum(dn * exact_ref[t, v], axis=1, keepdims=True)
        return dn.astype(jnp.bfloat16), dd

    def first(b, carry):
        t = tokens_of(b)
        head = Segments(col_ref, row_ref, b).head
        tile = qkv_ref[t, pl.ds(vcols, LANES)]
        for h in range(heads):
            dn, dd = cotangents(t, h)
            one, two = factors(tile, pick_ref, 0, h)
            lifted = jnp.where(head, one * two, 0.0)
            own_ref[b, h] = tn_dot(lifted.astype(jnp.bfloat16), dn)
            own_sums_ref[b, h : h + 1] = jnp.sum(lifted * dd, axis=0, keepdims=True)
        return carry

    own_sums_ref[...] = jnp.zeros_like(own_sums_ref)
    shards = swap_shards(ins, outs, chips, at, columns_of, block_of, Sender(shard_sems), local_sems)

    def lowered(dlifted, kind, h, one, two):
        return nt_dot((dlifted * two).astype(jnp.bfloat16), pick_ref[kind, h, 0]) + nt_dot(
            (dlifted * one).astype(jnp.bfloat16), pick_ref[kind, h, 1]
        )

    def here(b, carry):
        t = tokens_of(b)
        seg = Segments(col_ref, row_ref, b)
        tile = qkv_ref[t, pl.ds(vcols, LANES)]
        key = keys_in_place(tile, qcols)
        dtile = jnp.zeros((length, LANES), jnp.float32)
        dkey = jnp.zeros((length, LANES), jnp.float32)
        for h in range(heads):
            inside = head_mask(length, h)
            v = pl.ds(h * VHEAD, VHEAD)
            query = jnp.where(inside, tile, jnp.zeros_like(tile))
            dn, dd = cotangents(t, h)
            a, w, keep = masked_weights(query, key, seg.column, seg.row)
            dw = jnp.where(keep, nt_dot(dn, qkv_ref[t, v]) + dd, 0.0)
            da = (dw * (1.0 + a) * 0.25).astype(jnp.bfloat16)
            dvalue_ref[t, v] = tn_dot(w.astype(jnp.bfloat16), dn)
            dtile += jnp.where(inside, nn_dot(da, key), 0.0)
            dkey += jnp.where(inside, tn_dot(da, query), 0.0)
            one, two = factors(tile, pick_ref, 0, h)
            dlifted = nt_dot(dn, state_ref[b, h]) + dd * sums_ref[b, h : h + 1]
            dtile += lowered(jnp.where(seg.head, dlifted, 0.0), 0, h, one, two)
        dtile_ref[t] = dtile + pltpu.roll(dkey, qcols, axis=1)
        return carry

    def after(b, carry):
        t = tokens_of(b)
        tail = Segments(col_ref, row_ref, b).tail
        tile = qkv_ref[t, pl.ds(vcols, LANES)]
        dtile = dtile_ref[t]
        for h in range(heads):
            v = pl.ds(h * VHEAD, VHEAD)
            one, two = factors(tile, pick_ref, 1, h)
            lifted = jnp.where(tail, one * two * scale, 0.0)
            dlifted = nt_dot(qkv_ref[t, v], back_ref[b, h]) + back_sums_ref[b, h : h + 1]
            dtile += lowered(jnp.where(tail, dlifted * scale, 0.0), 1, h, one, two)
            dvalue = dvalue_ref[t, v] + nn_dot(lifted.astype(jnp.bfloat16), back_ref[b, h])
            dqkv_ref[t, v] = dvalue.astype(jnp.bfloat16)
        lane = lax.broadcasted_iota(jnp.int32, (length, LANES), 1)
        dqkv_ref[t, pl.ds(vcols, LANES)] = jnp.where(lane < 2 * qcols, dtile, 0.0).astype(
            jnp.bfloat16
        )
        turned_ref[:, t] = dqkv_ref[t].T
        return carry

    each = rows // CHUNKS

    def work(n, step):
        @pl.when(n < CHUNKS)
        def _():
            lax.fori_loop(n * each, (n + 1) * each, first, 0)

        step(n)

        @pl.when(n < CHUNKS)
        def _():
            lax.fori_loop(n * each, (n + 1) * each, here, 0)

        done = n - chain.distance

        @pl.when((done >= 0) & (done < CHUNKS))
        def _():
            lax.fori_loop(done * each, (done + 1) * each, after, 0)

    nothing = lambda: None
    chain.run(
        work,
        [nothing] * 2 + [lambda: advance(scatter, 3)] + [nothing] * 3 + [lambda: advance(scatter)],
    )
    run(scatter)

    def finish(r, carry):
        block_ref[r] = (residual_ref[r] + total_ref[r]).astype(jnp.bfloat16)
        return carry

    row_blocks(block_ref.shape[0], ROW_STEP, finish)(0)
    normed_copy.wait()
    wide = 4 * LANES
    qkv_rows = grad_ref.shape[0] - vcols
    grad_ref[pl.ds(qkv_rows, vcols)] = output_grad_ref[...]

    def gradient(i, carry):
        cols = pl.ds(pl.multiple_of(i * wide, wide), wide)
        grad_ref[pl.ds(0, qkv_rows), cols] = nn_dot(
            turned_ref[pl.ds(0, qkv_rows)], normed_ref[:, cols]
        ).astype(jnp.bfloat16)
        return carry

    lax.fori_loop(0, normed_ref.shape[1] // wide, gradient, 0)
    for c in shards:
        c.wait()
    chain.close()


def unmix(dmixed, normed, output_grad, part, residual, segments, pairs, kept, shards, heads, cid):
    seg_col, seg_row = segments
    tokens, vcols = dmixed.shape
    plane, rows = lax.axis_size("dp"), seg_col.shape[0]
    grad_rows = 2 * vcols + 2 * heads * FDIM
    m, width = residual.shape
    count = len(shards)
    whole, low = pltpu.VMEM, jnp.bfloat16
    dqkv, block, grad, *swapped = kernel_call(
        partial(unmix_kernel, heads, count),
        "unmix",
        cid,
        [
            ((tokens, vcols + LANES), low, whole),
            ((m, width), low, whole),
            ((grad_rows, width), low, whole),
        ]
        + [((plane, p.shape[0], p.shape[1] // plane), p.dtype, pl.ANY) for p in shards],
        [
            (dmixed, whole),
            (normed, pl.ANY),
            (output_grad, whole),
            (part, pl.ANY),
            (residual, whole),
            (seg_col, whole),
            (seg_row, whole),
            (pairs, whole),
        ]
        + [(a, whole) for a in kept]
        + [(p, pl.ANY) for p in shards],
        [
            pltpu.VMEM((tokens, width), low),
            pltpu.VMEM((vcols + LANES, tokens), low),
            pltpu.VMEM((tokens, vcols), jnp.float32),
            pltpu.VMEM((tokens, LANES), jnp.float32),
            pltpu.VMEM((rows, heads, FEATURES, VHEAD), low),
            pltpu.VMEM((rows, 8, FEATURES), jnp.float32),
        ]
        + state_scratch(rows, heads)
        + [pltpu.VMEM((m, width), jnp.float32), pltpu.VMEM((4, m, width), low)]
        + scatter_scratch(m, width)
        + [
            copies(rows * heads * PIECES + CHUNKS),
            copies(count * (plane - 1)),
            pltpu.SemaphoreType.DMA((count,)),
            copies(SCATTER_COPIES),
            pltpu.SemaphoreType.DMA((4,)),
            pltpu.SemaphoreType.DMA,
        ],
        moved=residual.size * 120,
    )
    return dqkv, block, grad, swapped


def last_kernel(count, *refs):
    ins, gain_ref, outs, sum_ref = (
        refs[:count],
        refs[count],
        refs[count + 1 : 2 * count + 1],
        refs[2 * count + 1],
    )
    got_gain, sems, gain_sems, local_sems = refs[2 * count + 2 :]
    plane, at = lax.axis_size("dp"), lax.axis_index("dp")
    others, me = everyone()
    greet(others)
    copy_gain = Sender(gain_sems)
    gains = [
        copy_gain(gain_ref.at[p["seq"] * plane + p["dp"]], got_gain.at[me], p) for p in others
    ]
    for c in gains:
        c.start()
    chips = [lax.rem(at + k, plane) for k in range(1, plane)]
    shards = swap_shards(ins, outs, chips, at, columns_of, block_of, Sender(sems), local_sems)
    got_gain[me] = gain_ref[lax.axis_index("seq") * plane + at]
    for c in gains:
        c.wait()
    total = got_gain[0]
    for k in range(1, len(others) + 1):
        total += got_gain[k]
    sum_ref[...] = total
    for c in shards:
        c.wait()


def last(shards, gains, cid):
    plane = lax.axis_size("dp")
    count = len(shards)
    devices = lax.axis_size(("dp", "seq", "tensor"))
    *swapped, total = kernel_call(
        partial(last_kernel, count),
        "last",
        cid,
        [((plane, p.shape[0], p.shape[1] // plane), p.dtype, pl.ANY) for p in shards]
        + [(gains.shape[1:], jnp.float32, pltpu.VMEM)],
        [(p, pl.ANY) for p in shards] + [(gains, pltpu.VMEM)],
        [
            pltpu.VMEM((devices,) + gains.shape[1:], jnp.float32),
            copies(count * (plane - 1)),
            copies(devices - 1),
            pltpu.SemaphoreType.DMA((count,)),
        ],
        moved=1 << 26,
    )
    return swapped, total


def everyone():
    plane, span, cores = (lax.axis_size(a) for a in ("dp", "seq", "tensor"))
    at, z, core = (lax.axis_index(a) for a in ("dp", "seq", "tensor"))
    others = [
        {
            "dp": lax.rem(at + i, plane),
            "seq": lax.rem(z + k, span),
            "tensor": lax.rem(core + c, cores),
        }
        for k in range(span)
        for i in range(plane)
        for c in range(cores)
        if i or k or c
    ]
    return others, (at * span + z) * cores + core


def exit_kernel(
    dqkv_ref,
    pack_ref,
    x_ref,
    dresid_ref,
    block_ref,
    small_ref,
    gain_two_ref,
    shards_ref,
    grad_ref,
    out_ref,
    gains_ref,
    shards_all_ref,
    gain_ref,
    part_ref,
    total_ref,
    ordered_ref,
    low_ref,
    pair_ref,
    sum_ref,
    got_ref,
    sems,
    pair_sems,
    local_sems,
    shard_sems,
    shard_local_sems,
):
    plane, at = lax.axis_size("dp"), lax.axis_index("dp")
    core = lax.axis_index("tensor")
    chips = [lax.rem(at + k, plane) for k in range(1, plane)]
    greet([{"dp": p} for p in chips] + [{"tensor": 1 - core}])
    shard_copy = Sender(shard_sems)

    half = shards_ref.shape[0] // 2

    def swap(n):
        rows = pl.ds(n * half, half)
        return swap_shards(
            (shards_ref,),
            (shards_all_ref,),
            chips,
            at,
            lambda ref, p: columns_of(ref, p, rows),
            lambda ref, p: ref.at[p, rows],
            shard_copy,
            shard_local_sems.at[pl.ds(n, 1)],
        )

    shards = swap(0)
    parts, _, depth = pack_ref.shape
    m, width = x_ref.shape
    wide = dqkv_ref.shape[1] - LANES + 2 * FDIM * ((dqkv_ref.shape[1] - LANES) // VHEAD)
    blocks = width // LANES
    copy = Sender(pair_sems)

    def block(chip, core):
        left = dqkv_ref[pl.ds(pl.multiple_of((chip * 2 + core) * m, m), m), pl.ds(0, wide)]
        for s in range(parts):
            part_ref[chip, core, :, pl.ds(s * depth, depth)] = nn_dot(
                left, pack_ref[s, pl.ds(0, wide)]
            ).astype(jnp.bfloat16)

    scatter = scatter_steps(
        part_ref, total_ref, pair_ref, sum_ref, got_ref, Sender(sems), start=False
    )
    produce_parts(block, next(scatter))

    def order(r, carry):
        for k in range(blocks):
            low_ref[r, lanes(seq_major_block(k))] = block_ref[r, lanes(k)]
        return carry

    row_blocks(m, ROW_STEP, order)(0)
    to_pair = [copy(low_ref, out_ref.at[core], {"tensor": 1 - core})]
    local = [pltpu.make_async_copy(low_ref, out_ref.at[core], local_sems.at[0])]
    to_pair[0].start()
    local[0].start()
    advance(scatter, 4)
    shards += swap(1)
    run(scatter)
    gain_ref[...] = jnp.zeros_like(gain_ref)

    def finish(r, k, v):
        ordered_ref[r, lanes(seq_major_block(k))] = v + dresid_ref[r, lanes(k)]

    def body(r, carry):
        norm_gradient(
            r,
            lambda r, k: x_ref[r, lanes(k)].astype(jnp.float32),
            total_ref,
            lambda k: small_ref[k, 0:1, :],
            gain_ref,
            finish,
            width,
        )
        return carry

    row_blocks(m, ROW_STEP, body)(0)
    to_pair.append(copy(ordered_ref, grad_ref.at[core], {"tensor": 1 - core}))
    local.append(pltpu.make_async_copy(ordered_ref, grad_ref.at[core], local_sems.at[1]))
    to_pair[1].start()
    local[1].start()
    gains_ref[...] = jnp.zeros_like(gains_ref)
    for k in range(blocks):
        for row, ref in enumerate((gain_ref, gain_two_ref)):
            gains_ref[k, row : row + 1] = jnp.sum(ref[:, lanes(k)], axis=0, keepdims=True)
    for c in to_pair + local + shards:
        c.wait()


def leave(dqkv, pack, x, dresid, block, small, gain_two, shards, cid):
    m, width = x.shape
    plane = lax.axis_size("dp")
    whole = pltpu.VMEM
    return kernel_call(
        exit_kernel,
        "leave",
        cid,
        [
            ((2, m, width), jnp.float32, pl.ANY),
            ((2, m, width), jnp.bfloat16, pl.ANY),
            ((width // LANES, 8, LANES), jnp.float32, whole),
        ]
        + [((plane, p.shape[0], p.shape[1] // plane), p.dtype, pl.ANY) for p in shards],
        [(a, whole) for a in (dqkv, pack, x, dresid, block, small, gain_two)]
        + [(p, pl.ANY) for p in shards],
        [
            pltpu.VMEM((8, width), jnp.float32),
            pltpu.VMEM((4, 2, m, width), jnp.bfloat16),
            pltpu.VMEM((m, width), jnp.float32),
            pltpu.VMEM((m, width), jnp.float32),
            pltpu.VMEM((m, width), jnp.bfloat16),
        ]
        + scatter_scratch(m, width)
        + [
            copies(SCATTER_COPIES),
            copies(2),
            pltpu.SemaphoreType.DMA((2,)),
            copies(2 * (plane - 1)),
            pltpu.SemaphoreType.DMA((2,)),
        ],
        moved=x.size * 120,
    )


def plane_local(
    tokens,
    doc_starts,
    attn_gain,
    mlp_gain,
    query_weight,
    key_weight,
    value_weight,
    output_weight,
    gate_weight,
    up_weight,
    down_weight,
    cotangent,
):
    plane, span, cores = (lax.axis_size("dp"), lax.axis_size("seq"), lax.axis_size("tensor"))
    rows, length, width = tokens.shape
    chunk = width // (plane * span)
    own = rows * length // cores
    heads = query_weight.shape[1] // FDIM // plane
    hidden_part = gate_weight.shape[1] // plane
    vcols, qcols = heads * VHEAD, heads * FDIM

    def over_seq(pack):
        return lax.all_gather(pack, "seq", axis=0, tiled=False)

    def summed(grads):
        return lax.psum_scatter(
            grads.astype(jnp.bfloat16), "seq", scatter_dimension=1, tiled=True
        )

    def split(w):
        return w.reshape(plane, -1, chunk)

    small = jnp.concatenate(
        [
            attn_gain.astype(jnp.float32)[None],
            mlp_gain.astype(jnp.float32)[None],
            doc_starts.astype(jnp.float32).reshape(-1, chunk),
            jnp.zeros((2, chunk), jnp.float32),
        ]
    )
    gate_w = split(gate_weight.T)
    pack = jnp.concatenate(
        [
            split(value_weight.T),
            split(query_weight.T),
            split(key_weight.T),
            split(output_weight),
            gate_w[:, :EARLY],
        ],
        axis=1,
    )
    [pack] = exchange([pack], 1, [(pack.shape[1], plane * chunk)], put=columns_of)
    small, pack = lax.optimization_barrier((small, pack))
    small, down_w = small_exchange(small, split(down_weight), 2)
    pack = over_seq(pack)
    late_w = jnp.concatenate([gate_w[:, EARLY:], split(up_weight.T)], axis=1)
    qkv_rows = vcols + 2 * qcols
    pairs = feature_pairs()
    normed_one, x, cot_own, seg_col, seg_row = entry(
        tokens.reshape(cores, own, width), cotangent.reshape(cores, own, width), small, length, 3
    )
    qkv, state, sums, late_w = states(
        normed_one,
        pack,
        seg_col,
        seg_row,
        pairs,
        [late_w],
        heads,
        4,
    )
    late_w, down_w = lax.optimization_barrier((late_w, down_w))
    late_w, down_w = over_seq(late_w), over_seq(down_w)
    mixed, exact, den, cot = mix(
        qkv, seg_col, seg_row, pairs, state, sums, cot_own, heads, 13
    )
    residual, normed_own = branch(mixed, pack, x, small, 5)
    normed_two, gate, up, hidden = expand(normed_own, pack, late_w, 11)
    down_grad = nn_dot(hidden, cot).astype(jnp.bfloat16)
    gate, down_grad = lax.optimization_barrier((gate, down_grad))
    down_grad = summed(down_grad)
    out_part, dnormed_two, gate_up_grad = hidden_units(
        gate, up, cot, pack, late_w, down_w, normed_two, 6
    )
    gate_up_grad = summed(gate_up_grad)
    dresid, gain_two_grad, dmixed, out_grad = turn(
        dnormed_two, residual, cot_own, small, pack, mixed, 12
    )
    dmixed, down_grad = lax.optimization_barrier((dmixed, down_grad))
    dqkv, block_own, attn_grad, (down_grad,) = unmix(
        dmixed,
        normed_one,
        out_grad,
        out_part,
        residual,
        (seg_col, seg_row),
        pairs,
        (qkv, exact, den, state, sums),
        [down_grad],
        heads,
        8,
    )
    attn_grad = summed(attn_grad)
    dtokens, block_out, gains, gate_up_grad = leave(
        dqkv, pack, x, dresid, block_own, small, gain_two_grad, [gate_up_grad], 9
    )
    (attn_grad,), gain_grads = last([attn_grad], gains, 10)

    def stacked(a, start, size):
        return a[:, start : start + size].reshape(plane * size, chunk).astype(jnp.float32)

    h = hidden_part
    return (
        block_out.reshape(rows, length, width),
        dtokens.reshape(rows, length, width),
        gain_grads[0],
        gain_grads[1],
        stacked(attn_grad, vcols, qcols).T,
        stacked(attn_grad, vcols + qcols, qcols).T,
        stacked(attn_grad, 0, vcols).T,
        stacked(attn_grad, qkv_rows, vcols),
        stacked(gate_up_grad, 0, h).T,
        stacked(gate_up_grad, h, h).T,
        stacked(down_grad, 0, h),
    )


def fits_plane(mesh, tokens, query_weight, gate_weight):
    plane, span, cores = (mesh.shape[a] for a in ("dp", "seq", "tensor"))
    heads = query_weight.shape[1] // FDIM // cores
    return (
        plane == 4
        and cores == 2
        and heads % plane == 0
        and (gate_weight.shape[1] // cores) % (16 * plane) == 0
        and gate_weight.shape[1] // cores // plane > EARLY
        and tokens.shape[0] % CHUNKS == 0
    )


def solution(mesh):
    def step(*args):
        use = fits_plane(mesh, args[0], args[4], args[8])
        return sharded(mesh, plane_local if use else local)(*args)

    return step


def sharded(mesh, body):
    return jax.shard_map(
        body,
        mesh=mesh,
        in_specs=(
            P("dp", "seq", None),
            P("dp", "seq"),
            P(("dp", "seq")),
            P(("dp", "seq")),
            P(("dp", "seq"), "tensor"),
            P(("dp", "seq"), "tensor"),
            P(("dp", "seq"), "tensor"),
            P("tensor", ("dp", "seq")),
            P(("dp", "seq"), "tensor"),
            P(("dp", "seq"), "tensor"),
            P("tensor", ("dp", "seq")),
            P("dp", "seq", None),
        ),
        out_specs=(
            P("dp", "seq", None),
            P("dp", "seq", None),
            P(("dp", "seq")),
            P(("dp", "seq")),
            P(("dp", "seq"), "tensor"),
            P(("dp", "seq"), "tensor"),
            P(("dp", "seq"), "tensor"),
            P("tensor", ("dp", "seq")),
            P(("dp", "seq"), "tensor"),
            P(("dp", "seq"), "tensor"),
            P("tensor", ("dp", "seq")),
        ),
        check_vma=False,
    )
```

```python
from functools import partial

import jax
import jax.numpy as jnp
import numpy as np
from jax import lax
from jax.experimental import pallas as pl
from jax.experimental.pallas import tpu as pltpu
from jax.sharding import PartitionSpec as P

FDIM = 16
VHEAD = 128
MICRO = 2


norm_epsilon = 1e-05
highest = lax.Precision.HIGHEST
outer_scale = 0.17677669529663687


def prefix(x, axis, combine, identity, reverse):
    size, index = (lax.axis_size(axis), lax.axis_index(axis))
    everything = jax.tree.map(lambda part: lax.all_gather(part, axis), x)
    start = jax.tree.map(
        lambda part, zero: jnp.broadcast_to(jnp.asarray(zero, part.dtype), part.shape), x, identity
    )

    def turn(k, before):
        at = size - 1 - k if reverse else k
        reached = at > index if reverse else at < index
        new = combine(before, jax.tree.map(lambda part: part[at], everything))
        return jax.tree.map(lambda a, b: jnp.where(reached, a, b), new, before)

    return lax.fori_loop(0, size, turn, start)


def features(vectors):
    ones_col = jnp.ones(vectors.shape[:-1] + (1,), jnp.float32)
    outer_terms = vectors[..., :, None] * vectors[..., None, :] * outer_scale
    outer_terms = outer_terms.reshape(vectors.shape[:-1] + (vectors.shape[-1] * vectors.shape[-1],))
    return jnp.concatenate([ones_col, 0.5 * vectors, outer_terms], axis=-1)


def mix_span(queries, key_rows, values, state_in, norm_in, segments):
    length = queries.shape[1]
    scores = jnp.einsum("rthf,rshf->rhts", queries, key_rows, precision=highest) / 4.0
    kernel = 1.0 + scores + 0.5 * scores * scores
    position = jnp.arange(length)
    causal = position[None, :] <= position[:, None]
    allowed = causal[None] & (segments[:, :, None] == segments[:, None, :])
    kernel = jnp.where(allowed[:, None], kernel, 0.0)
    numerator = jnp.einsum("rhts,rshe->rthe", kernel, values, precision=highest)
    denominator = jnp.transpose(jnp.sum(kernel, axis=-1), (0, 2, 1))
    head_part = (segments == 0).astype(jnp.float32)[:, :, None]
    lifted = features(queries)
    numerator = numerator + head_part[..., None] * jnp.einsum(
        "rthf,rhfe->rthe", lifted, state_in, precision=highest
    )
    denominator = denominator + head_part * jnp.einsum(
        "rthf,rhf->rth", lifted, norm_in, precision=highest
    )
    return numerator / denominator[..., None]


def tail_span(key_rows, values, segments):
    tail_mask = (segments == segments[:, -1:]).astype(jnp.float32)
    lifted = features(key_rows) * tail_mask[:, :, None, None]
    tail_state = jnp.einsum("rshf,rshe->rhfe", lifted, values, precision=highest)
    return (tail_state, jnp.sum(lifted, axis=1))


def combine_carry(earlier_part, later_part):
    keep_rate = 1.0 - later_part[2]
    return (
        later_part[0] + keep_rate[:, None, None, None] * earlier_part[0],
        later_part[1] + keep_rate[:, None, None] * earlier_part[1],
        jnp.maximum(earlier_part[2], later_part[2]),
    )


def inverse_rms(inputs):
    return lax.rsqrt(jnp.mean(inputs * inputs, axis=-1, keepdims=True) + norm_epsilon)


def norm_backward(inputs, scale_row, gain_vec, grad_normed):
    scaled_grad = grad_normed * gain_vec
    grad_gain = jnp.sum(grad_normed * inputs * scale_row, axis=0)
    grad_inputs = scale_row * scaled_grad - inputs * scale_row * scale_row * scale_row * jnp.mean(
        scaled_grad * inputs, axis=-1, keepdims=True
    )
    return (grad_inputs, grad_gain)


def inner_rows(left_mat, right_mat):
    return lax.dot_general(
        left_mat, right_mat, (((0,), (0,)), ((), ())), preferred_element_type=jnp.float32
    )


def by_transpose(left_mat, right_mat):
    return lax.dot_general(
        left_mat, right_mat, (((1,), (1,)), ((), ())), preferred_element_type=jnp.float32
    )


def local(
    tokens,
    doc_starts,
    attn_gain,
    mlp_gain,
    query_weight,
    key_weight,
    value_weight,
    output_weight,
    gate_weight,
    up_weight,
    down_weight,
    cotangent,
):
    micro_rows = tokens.shape[0] // MICRO
    span_len = tokens.shape[1]
    model_width = tokens.shape[2]
    head_count = query_weight.shape[1] // FDIM
    outputs_main = []
    outputs_grad = []
    totals = None
    for micro_index in range(MICRO):
        row_start = micro_index * micro_rows
        rows_in = tokens[row_start : row_start + micro_rows]
        starts_in = doc_starts[row_start : row_start + micro_rows]
        cot_in = cotangent[row_start : row_start + micro_rows].reshape(-1, model_width)
        (
            full_query,
            full_key,
            full_value,
            full_gate,
            full_up,
            full_output,
            full_down,
            gain_one,
            gain_two,
        ) = (
            lax.all_gather(query_weight, ("dp", "seq"), axis=0, tiled=True),
            lax.all_gather(key_weight, ("dp", "seq"), axis=0, tiled=True),
            lax.all_gather(value_weight, ("dp", "seq"), axis=0, tiled=True),
            lax.all_gather(gate_weight, ("dp", "seq"), axis=0, tiled=True),
            lax.all_gather(up_weight, ("dp", "seq"), axis=0, tiled=True),
            lax.all_gather(output_weight, ("dp", "seq"), axis=1, tiled=True),
            lax.all_gather(down_weight, ("dp", "seq"), axis=1, tiled=True),
            lax.all_gather(attn_gain, ("dp", "seq"), axis=0, tiled=True),
            lax.all_gather(mlp_gain, ("dp", "seq"), axis=0, tiled=True),
        )
        gain_one_f = gain_one.astype(jnp.float32)
        gain_two_f = gain_two.astype(jnp.float32)
        flat_rows = rows_in.reshape(-1, model_width).astype(jnp.float32)
        scale_one = inverse_rms(flat_rows)
        normed_one = (flat_rows * scale_one * gain_one_f).astype(jnp.bfloat16)
        query_low = jnp.dot(normed_one, full_query, preferred_element_type=jnp.float32).astype(
            jnp.bfloat16
        )
        key_low = jnp.dot(normed_one, full_key, preferred_element_type=jnp.float32).astype(
            jnp.bfloat16
        )
        value_low = jnp.dot(normed_one, full_value, preferred_element_type=jnp.float32).astype(
            jnp.bfloat16
        )
        queries = query_low.astype(jnp.float32).reshape(micro_rows, span_len, head_count, FDIM)
        key_rows = key_low.astype(jnp.float32).reshape(micro_rows, span_len, head_count, FDIM)
        values = value_low.astype(jnp.float32).reshape(micro_rows, span_len, head_count, VHEAD)
        segments = jnp.cumsum(starts_in, axis=1)
        reset_flag = (segments[:, -1] > 0).astype(jnp.float32)
        (tail_state, tail_norm), tail_pull = jax.vjp(
            partial(tail_span, segments=segments), key_rows, values
        )
        state_in, norm_in, reset_in = prefix(
            (tail_state, tail_norm, reset_flag),
            "seq",
            combine_carry,
            (jnp.zeros_like(tail_state), jnp.zeros_like(tail_norm), jnp.zeros_like(reset_flag)),
            False,
        )
        mixed_heads, mix_pull = jax.vjp(
            partial(mix_span, segments=segments), queries, key_rows, values, state_in, norm_in
        )
        mixed_low = mixed_heads.reshape(-1, head_count * VHEAD).astype(jnp.bfloat16)
        branch_one = jnp.dot(mixed_low, full_output, preferred_element_type=jnp.float32)
        residual = flat_rows + lax.psum(branch_one, "tensor")
        scale_two = inverse_rms(residual)
        normed_two = (residual * scale_two * gain_two_f).astype(jnp.bfloat16)
        gate_proj = jnp.dot(normed_two, full_gate, preferred_element_type=jnp.float32)
        up_proj = jnp.dot(normed_two, full_up, preferred_element_type=jnp.float32)
        sigmoid_gate = jax.nn.sigmoid(gate_proj)
        hidden = (gate_proj * sigmoid_gate * up_proj).astype(jnp.bfloat16)
        branch_two = jnp.dot(hidden, full_down, preferred_element_type=jnp.float32)
        block_low = (
            residual + lax.psum(branch_two.astype(jnp.bfloat16), "tensor").astype(jnp.float32)
        ).astype(jnp.bfloat16)
        outputs_main.append(block_low.reshape(micro_rows, span_len, model_width))
        grad_down = inner_rows(hidden, cot_in)
        grad_hidden = by_transpose(cot_in, full_down)
        grad_gate_low = (
            grad_hidden * up_proj * sigmoid_gate * (1.0 + gate_proj * (1.0 - sigmoid_gate))
        ).astype(jnp.bfloat16)
        grad_up_low = (grad_hidden * gate_proj * sigmoid_gate).astype(jnp.bfloat16)
        grad_gate = inner_rows(normed_two, grad_gate_low)
        grad_up = inner_rows(normed_two, grad_up_low)
        grad_normed_two = by_transpose(grad_gate_low, full_gate) + by_transpose(
            grad_up_low, full_up
        )
        grad_normed_two = lax.psum(grad_normed_two, "tensor")
        grad_resid, grad_gain_two = norm_backward(residual, scale_two, gain_two_f, grad_normed_two)
        grad_resid = grad_resid + cot_in.astype(jnp.float32)
        grad_resid_low = grad_resid.astype(jnp.bfloat16)
        grad_output = inner_rows(mixed_low, grad_resid_low)
        grad_mixed = by_transpose(grad_resid_low, full_output).astype(jnp.bfloat16)
        grad_mixed = (
            lax.optimization_barrier(grad_mixed)
            .astype(jnp.float32)
            .reshape(micro_rows, span_len, head_count, VHEAD)
        )
        grad_queries, grad_keys, grad_values, grad_state, grad_norm = mix_pull(grad_mixed)
        carried_state, carried_norm, reset_out = prefix(
            (grad_state, grad_norm, reset_flag),
            "seq",
            combine_carry,
            (jnp.zeros_like(grad_state), jnp.zeros_like(grad_norm), jnp.zeros_like(reset_flag)),
            True,
        )
        more_keys, more_values = tail_pull((carried_state, carried_norm))
        grad_query_low = grad_queries.reshape(-1, head_count * FDIM).astype(jnp.bfloat16)
        grad_key_low = (grad_keys + more_keys).reshape(-1, head_count * FDIM).astype(jnp.bfloat16)
        grad_value_low = (
            (grad_values + more_values).reshape(-1, head_count * VHEAD).astype(jnp.bfloat16)
        )
        grad_query = inner_rows(normed_one, grad_query_low)
        grad_key = inner_rows(normed_one, grad_key_low)
        grad_value = inner_rows(normed_one, grad_value_low)
        grad_normed_one = (
            by_transpose(grad_query_low, full_query)
            + by_transpose(grad_key_low, full_key)
            + by_transpose(grad_value_low, full_value)
        )
        grad_normed_one = lax.psum(grad_normed_one, "tensor")
        grad_inputs, grad_gain_one = norm_backward(
            flat_rows, scale_one, gain_one_f, grad_normed_one
        )
        outputs_grad.append((grad_resid + grad_inputs).reshape(micro_rows, span_len, model_width))
        shares = (
            grad_query,
            grad_key,
            grad_value,
            grad_gate,
            grad_up,
            grad_output,
            grad_down,
            grad_gain_one,
            grad_gain_two,
        )
        if totals is None:
            totals = shares
        else:
            totals = jax.tree.map(jnp.add, totals, shares)
    totals = (
        lax.psum_scatter(totals[0], ("dp", "seq"), scatter_dimension=0, tiled=True),
        lax.psum_scatter(totals[1], ("dp", "seq"), scatter_dimension=0, tiled=True),
        lax.psum_scatter(totals[2], ("dp", "seq"), scatter_dimension=0, tiled=True),
        lax.psum_scatter(totals[3], ("dp", "seq"), scatter_dimension=0, tiled=True),
        lax.psum_scatter(totals[4], ("dp", "seq"), scatter_dimension=0, tiled=True),
        lax.psum_scatter(totals[5], ("dp", "seq"), scatter_dimension=1, tiled=True),
        lax.psum_scatter(totals[6], ("dp", "seq"), scatter_dimension=1, tiled=True),
        lax.psum_scatter(totals[7], ("dp", "seq"), scatter_dimension=0, tiled=True),
        lax.psum_scatter(totals[8], ("dp", "seq"), scatter_dimension=0, tiled=True),
    )
    return (
        jnp.concatenate(outputs_main, axis=0),
        jnp.concatenate(outputs_grad, axis=0),
        totals[7],
        totals[8],
        totals[0],
        totals[1],
        totals[2],
        totals[5],
        totals[3],
        totals[4],
        totals[6],
    )


MESH_ID = pl.DeviceIdType.MESH
VMEM_LIMIT = 58 << 20
LANES = 128
ROW_STEP = 32


def nt_dot(a, b):
    return lax.dot_general(a, b, (((1,), (1,)), ((), ())), preferred_element_type=jnp.float32)


def tn_dot(a, b):
    return lax.dot_general(a, b, (((0,), (0,)), ((), ())), preferred_element_type=jnp.float32)


def nn_dot(a, b):
    return lax.dot_general(a, b, (((1,), (0,)), ((), ())), preferred_element_type=jnp.float32)


def plane_places():
    at, core = lax.axis_index("dp"), lax.axis_index("tensor")
    x_bit, y_bit = lax.rem(at, 2), at // 2
    return (
        at,
        y_bit * 2 + (1 - x_bit),
        (1 - y_bit) * 2 + x_bit,
        (1 - y_bit) * 2 + (1 - x_bit),
        core,
    )


loading = []


def greet(places):
    barrier = pltpu.get_barrier_semaphore()
    for place in places:
        pl.semaphore_signal(barrier, inc=1, device_id=place, device_id_type=MESH_ID)
    pl.semaphore_wait(barrier, len(places))
    while loading:
        loading.pop().wait()


class Sender:
    def __init__(self, sems):
        self.sems, self.used = sems, 0

    def __call__(self, src, dst, place):
        index = self.used
        self.used += 1
        return pltpu.make_async_remote_copy(
            src_ref=src,
            dst_ref=dst,
            send_sem=self.sems.at[0, index],
            recv_sem=self.sems.at[1, index],
            device_id=place,
            device_id_type=MESH_ID,
        )


def greet_plane():
    at, x_at, y_at, _, core = plane_places()
    greet([{"dp": x_at}, {"dp": y_at}, {"tensor": 1 - core}])


def leaving(i):
    at, x_at, y_at, d_at, core = plane_places()
    chip = choose(i < 2, d_at, choose(i < 4, x_at, choose(i < 6, y_at, at)))
    return chip, choose(parity(i) == 0, 1 - core, core)


def produce_parts(block, pairs):
    def body(i, carry):
        block(*leaving(i))
        for j, pair in enumerate(pairs):

            @pl.when(i == 2 * j)
            def _():
                pair.start()

        return carry

    lax.fori_loop(0, 8, body, 0)


def add_rows(dst, *srcs, step=64):
    def body(i, carry):
        r = pl.ds(pl.multiple_of(i * step, step), step)
        total = srcs[0][r].astype(jnp.float32)
        for s in srcs[1:]:
            total = total + s[r].astype(jnp.float32)
        dst[r] = total.astype(dst.dtype)
        return carry

    lax.fori_loop(0, srcs[0].shape[0] // step, body, 0)


GATHER_COPIES = 13
SCATTER_COPIES = 10


def gather_steps(own_ref, out_ref, copy, local_sem):
    at, x_at, y_at, d_at, core = plane_places()
    half = own_ref.shape[0] // 2
    xp, yp, sp = {"dp": x_at}, {"dp": y_at}, {"tensor": 1 - core}
    lo, hi = pl.ds(0, half), pl.ds(half, half)
    mine = out_ref.at[at, core]
    x_lo = copy(own_ref.at[lo], mine.at[lo], xp)
    y_hi = copy(own_ref.at[hi], mine.at[hi], yp)
    x_hi = copy(own_ref.at[hi], mine.at[hi], xp)
    y_lo = copy(own_ref.at[lo], mine.at[lo], yp)
    pair = copy(own_ref, mine, sp)
    for c in (x_lo, y_hi, x_hi, y_lo, pair):
        c.start()
    local_copy = pltpu.make_async_copy(own_ref, mine, local_sem)
    local_copy.start()
    from_x, from_y, from_d = out_ref.at[x_at, core], out_ref.at[y_at, core], out_ref.at[d_at, core]
    on_y = copy(from_x.at[lo], from_x.at[lo], yp)
    on_x = copy(from_y.at[hi], from_y.at[hi], xp)
    handed = [
        copy(block.at[rows], block.at[rows], sp)
        for block, rows in (
            (from_x, lo),
            (from_y, hi),
            (from_x, hi),
            (from_y, lo),
            (from_d, lo),
            (from_d, hi),
        )
    ]
    yield
    local_copy.wait()
    yield
    pair.wait_recv()
    yield
    x_lo.wait_recv()
    on_y.start()
    handed[0].start()
    y_hi.wait_recv()
    on_x.start()
    handed[1].start()
    yield
    handed[0].wait_recv()
    handed[1].wait_recv()
    yield
    x_hi.wait_recv()
    handed[2].start()
    y_lo.wait_recv()
    handed[3].start()
    yield
    handed[2].wait_recv()
    handed[3].wait_recv()
    yield
    on_y.wait_recv()
    handed[4].start()
    on_x.wait_recv()
    handed[5].start()
    yield
    handed[4].wait_recv()
    handed[5].wait_recv()
    yield
    for c in [x_lo, y_hi, x_hi, y_lo, on_y, on_x, pair] + handed:
        c.wait_send()


def scatter_steps(part_ref, out_ref, pair_ref, sum_ref, got_ref, copy, held=None, start=True):
    at, x_at, y_at, d_at, core = plane_places()
    half = part_ref.shape[2] // 2
    xp, yp, sp = {"dp": x_at}, {"dp": y_at}, {"tensor": 1 - core}
    lo, hi = pl.ds(0, half), pl.ds(half, half)
    order = (d_at, x_at, y_at, at)
    pairs = [copy(part_ref.at[to, 1 - core], pair_ref.at[j], sp) for j, to in enumerate(order)]
    own = [part_ref.at[to, core] for to in order]
    fetched = []
    if held is not None:
        buffer, held_sems = held
        fetched = [
            pltpu.make_async_copy(o, buffer.at[j], held_sems.at[j]) for j, o in enumerate(own)
        ]
        own = [buffer.at[j] for j in range(4)]

    def sent(j, rows, place):
        return copy(sum_ref.at[j, rows], got_ref.at[j, rows], place)

    d_lo, d_hi = sent(0, lo, xp), sent(0, hi, yp)
    x_lo, y_hi, x_hi, y_lo = sent(1, lo, xp), sent(2, hi, yp), sent(1, hi, xp), sent(2, lo, yp)
    for c in (pairs if start else []) + fetched:
        c.start()
    yield pairs

    def ready(j):
        if fetched:
            fetched[j].wait()
        pairs[j].wait_recv()

    def total(j, rows, *more):
        add_rows(sum_ref.at[j, rows], own[j].at[rows], pair_ref.at[j, rows], *more)

    ready(0)
    total(0, lo)
    d_lo.start()
    total(0, hi)
    d_hi.start()
    yield
    ready(1)
    total(1, lo)
    x_lo.start()
    yield
    ready(2)
    total(2, hi)
    y_hi.start()
    yield
    d_lo.wait_recv()
    total(2, lo, got_ref.at[0, lo])
    y_lo.start()
    d_hi.wait_recv()
    total(1, hi, got_ref.at[0, hi])
    x_hi.start()
    yield
    ready(3)
    for c in (x_lo, y_hi, y_lo, x_hi):
        c.wait_recv()
    add_rows(out_ref, own[3], pair_ref.at[3], got_ref.at[1], got_ref.at[2])
    for c in pairs + [d_lo, d_hi, x_lo, y_hi, x_hi, y_lo]:
        c.wait_send()


def swap_shards(ins, outs, peers, me, take, put, copy, local_sems):
    started = [
        copy(take(i, p), put(o, me), {"dp": p}) for i, o in zip(ins, outs) for p in peers
    ]
    started += [
        pltpu.make_async_copy(take(i, me), put(o, me), local_sems.at[n])
        for n, (i, o) in enumerate(zip(ins, outs))
    ]
    for c in started:
        c.start()
    return started


def exchange_kernel(take, put, count, *refs):
    ins, outs, sems, local_sems = refs[:count], refs[count : 2 * count], refs[-2], refs[-1]
    size, me = lax.axis_size("dp"), lax.axis_index("dp")
    peers = [lax.rem(me + k, size) for k in range(1, size)]
    greet([{"dp": p} for p in peers])
    for c in swap_shards(ins, outs, peers, me, take, put, Sender(sems), local_sems):
        c.wait()


def block_of(ref, index):
    return ref.at[index]


def columns_of(ref, index, rows=slice(None)):
    width = ref.shape[1] // lax.axis_size("dp")
    return ref.at[rows, pl.ds(pl.multiple_of(index * width, width), width)]


def exchange(arrays, cid, shapes, take=block_of, put=block_of):
    count, peers = len(arrays), lax.axis_size("dp") - 1
    anywhere = [pl.BlockSpec(memory_space=pl.ANY)] * count
    return pl.pallas_call(
        partial(exchange_kernel, take, put, count),
        name="exchange",
        out_shape=[jax.ShapeDtypeStruct(s, x.dtype) for s, x in zip(shapes, arrays)],
        in_specs=anywhere,
        out_specs=anywhere,
        scratch_shapes=[
            pltpu.SemaphoreType.DMA((2, count * peers)),
            pltpu.SemaphoreType.DMA((count,)),
        ],
        compiler_params=pltpu.CompilerParams(collective_id=cid, has_side_effects=True),
        cost_estimate=pl.CostEstimate(
            flops=0, bytes_accessed=60 * sum(x.size for x in arrays), transcendentals=0
        ),
    )(*arrays)


def small_kernel(
    small_ref, pack_ref, all_ref, out_ref, small_sems, small_local_sem, sems, local_sems
):
    plane, span = lax.axis_size("dp"), lax.axis_size("seq")
    at, z = lax.axis_index("dp"), lax.axis_index("seq")
    places = [
        {"dp": lax.rem(at + i, plane), "seq": lax.rem(z + k, span)}
        for k in range(span)
        for i in range(plane)
        if i or k
    ]
    greet(places)
    copy_small = Sender(small_sems)
    block = all_ref.at[z * plane + at]
    started = [copy_small(small_ref, block, p) for p in places]
    started.append(pltpu.make_async_copy(small_ref, block, small_local_sem))
    for c in started:
        c.start()
    chips = [lax.rem(at + k, plane) for k in range(1, plane)]
    started += swap_shards(
        (pack_ref,), (out_ref,), chips, at, block_of, columns_of, Sender(sems), local_sems
    )
    for c in started:
        c.wait()


def small_exchange(small, pack, cid):
    plane, span = lax.axis_size("dp"), lax.axis_size("seq")
    _, size, chunk = pack.shape
    return kernel_call(
        small_kernel,
        "small_exchange",
        cid,
        [
            ((span * plane,) + small.shape, small.dtype, pltpu.VMEM),
            ((size, plane * chunk), pack.dtype, pl.ANY),
        ],
        [(small, pltpu.VMEM), (pack, pl.ANY)],
        [
            copies(plane * span - 1),
            pltpu.SemaphoreType.DMA,
            copies(plane - 1),
            pltpu.SemaphoreType.DMA((1,)),
        ],
        moved=1 << 24,
    )


def advance(steps, count=1):
    for _ in range(count):
        next(steps)


def run(*steps):
    for g in steps:
        for _ in g:
            pass


def row_blocks(rows, step, body):
    def inner(i, carry):
        return body(pl.ds(pl.multiple_of(i * step, step), step), carry)

    return lambda init: lax.fori_loop(0, rows // step, inner, init)


def lanes(k):
    return pl.ds(k * LANES, LANES)


def seq_major_block(k):
    plane, span = lax.axis_size("dp"), lax.axis_size("seq")
    s, g = divmod(k, plane)
    return g * span + s


def mean_of(acc, width):
    return jnp.sum(acc, axis=1, keepdims=True) * (1.0 / width)


class Rows:
    def __init__(self, pack, first, count):
        self.array, self.rows = pack, pl.ds(first, count)
        self.shape, self.dtype = (pack.shape[0], count, pack.shape[2]), pack.dtype
        self.size = pack.shape[0] * count * pack.shape[2]


def kernel_call(body, name, cid, outs, ins, scratch, flops=0, moved=0):
    big = [n for n, (a, m) in enumerate(ins) if m == pltpu.VMEM and a.size >= 1 << 16]
    count, params = len(ins), dict(has_side_effects=True, vmem_limit_bytes=VMEM_LIMIT)

    def loaded(*refs):
        refs, buffers, sems = list(refs[: -len(big) - 1]), refs[-len(big) - 1 : -1], refs[-1]
        for k, n in enumerate(big):
            source = refs[n]
            if isinstance(ins[n][0], Rows):
                source = source.at[:, ins[n][0].rows]
            loading.append(pltpu.make_async_copy(source, buffers[k], sems.at[k]))
            loading[-1].start()
            refs[n] = buffers[k]
        body(*refs)

    return pl.pallas_call(
        loaded if big else body,
        name=name,
        out_shape=[jax.ShapeDtypeStruct(s, d) for s, d, _ in outs],
        in_specs=[
            pl.BlockSpec(memory_space=pl.ANY if n in big else ins[n][1]) for n in range(count)
        ],
        out_specs=[pl.BlockSpec(memory_space=m) for _, _, m in outs],
        scratch_shapes=list(scratch)
        + [pltpu.VMEM(ins[n][0].shape, ins[n][0].dtype) for n in big]
        + ([pltpu.SemaphoreType.DMA((len(big),))] if big else []),
        compiler_params=pltpu.CompilerParams(collective_id=cid, **params),
        cost_estimate=pl.CostEstimate(flops=flops, bytes_accessed=moved, transcendentals=0),
    )(*[a.array if isinstance(a, Rows) else a for a, _ in ins])


def copies(count):
    return pltpu.SemaphoreType.DMA((2, count))


def entry_kernel(
    tokens_ref,
    cot_ref,
    small_ref,
    all_ref,
    x_ref,
    cot_own_ref,
    column_ref,
    row_ref,
    normed_ref,
    sems,
    local_sem,
):
    greet_plane()
    core = lax.axis_index("tensor")
    m, width = x_ref.shape
    blocks = width // LANES

    def body(r, carry):
        acc = jnp.zeros((ROW_STEP, LANES), jnp.float32)
        for k in range(blocks):
            source = lanes(seq_major_block(k))
            v = tokens_ref[core, r, source]
            x_ref[r, lanes(k)] = v
            cot_own_ref[r, lanes(k)] = cot_ref[core, r, source]
            v = v.astype(jnp.float32)
            acc += v * v
        scale = lax.rsqrt(mean_of(acc, width) + norm_epsilon)
        for k in range(blocks):
            v = x_ref[r, lanes(k)].astype(jnp.float32)
            normed_ref[r, lanes(k)] = (v * scale * small_ref[k, 0:1, :]).astype(jnp.bfloat16)
        return carry

    row_blocks(m, ROW_STEP, body)(0)
    gather = gather_steps(normed_ref, all_ref, Sender(sems), local_sem)
    next(gather)
    plane, z = lax.axis_size("dp"), lax.axis_index("seq")
    rows, _, length = row_ref.shape
    pieces = length // LANES
    starts = []
    for chip in range(plane):
        block = small_ref[z * plane + chip]
        for r in range(rows // plane):
            first = 2 + r * pieces
            starts.append(
                jnp.concatenate([block[first + p : first + p + 1] for p in range(pieces)], axis=1)
            )
    starts = jnp.concatenate(starts).astype(jnp.bfloat16)
    down = lax.broadcasted_iota(jnp.int32, (length, length), 0)
    across = lax.broadcasted_iota(jnp.int32, (length, length), 1)
    counts = nn_dot(starts, jnp.where(down <= across, 1.0, 0.0).astype(jnp.bfloat16))
    turned = nt_dot(jnp.where(across <= down, 1.0, 0.0).astype(jnp.bfloat16), starts)
    for b in range(rows):
        row_ref[b] = counts[b : b + 1]
        column_ref[b] = turned[:, b : b + 1]
    run(gather)


def entry(tokens, cot, small, length, cid):
    cores, m, width = tokens.shape
    rows = 4 * cores * m // length
    whole = pltpu.VMEM
    gathered, x, cot_own, seg_col, seg_row = kernel_call(
        entry_kernel,
        "entry",
        cid,
        [
            ((4, cores, m, width), jnp.bfloat16, pl.ANY),
            ((m, width), jnp.bfloat16, whole),
            ((m, width), jnp.bfloat16, whole),
            ((rows, length, 1), jnp.float32, whole),
            ((rows, 1, length), jnp.float32, whole),
        ],
        [(tokens, whole), (cot, whole), (small, whole)],
        [pltpu.VMEM((m, width), jnp.bfloat16), copies(GATHER_COPIES), pltpu.SemaphoreType.DMA],
        moved=tokens.size * 40,
    )
    return gathered.reshape(-1, width), x, cot_own, seg_col, seg_row


FEATURES = 256
STATE_ROWS = 160
PIECES = 1
CHUNKS = 8
EARLY = 192


def feature_pairs():
    first = np.full(FEATURES, -4096, np.int32)
    second = np.full(FEATURES, -4096, np.int32)
    pairs = [(i, j) for i in range(FDIM + 1) for j in range(i, FDIM + 1)]
    for f, (i, j) in enumerate(pairs):
        first[f], second[f] = i, j
    return jnp.asarray(np.stack([first, second] + [first] * 6))


def feature_scale(pairs_ref):
    i, j = pairs_ref[0:1, :], pairs_ref[1:2, :]
    square = jnp.where(i == j, 1.0 / 32.0, 1.0 / 16.0)
    return jnp.where(j == FDIM, jnp.where(i == FDIM, 1.0, 0.25), square)


def fill_selectors(pairs_ref, pick_ref, qcols):
    kinds, heads = pick_ref.shape[:2]
    lane = lax.broadcasted_iota(jnp.int32, (LANES, FEATURES), 0)
    for kind in range(kinds):
        for h in range(heads):
            for side in range(2):
                index = pairs_ref[side : side + 1, :]
                source = jnp.where(
                    index == FDIM, 2 * qcols, index + (kind * qcols + h * FDIM)
                )
                pick_ref[kind, h, side] = jnp.where(lane == source, 1.0, 0.0).astype(jnp.bfloat16)


def factors(tile, pick_ref, kind, h):
    return nn_dot(tile, pick_ref[kind, h, 0]), nn_dot(tile, pick_ref[kind, h, 1])


def keys_in_place(tile, qcols):
    return pltpu.roll(tile.astype(jnp.float32), LANES - qcols, axis=1).astype(jnp.bfloat16)


def head_mask(rows, head):
    lane = lax.broadcasted_iota(jnp.int32, (rows, LANES), 1)
    return (lane >= head * FDIM) & (lane < (head + 1) * FDIM)


def masked_weights(query, key, column, row):
    length = query.shape[0]
    a = nt_dot(query, key) * 0.25
    t = lax.broadcasted_iota(jnp.int32, (length, length), 0)
    s = lax.broadcasted_iota(jnp.int32, (length, length), 1)
    keep = (s <= t) & (column == row)
    return a, jnp.where(keep, 1.0 + a + 0.5 * a * a, 0.0), keep


class Segments:
    def __init__(self, col_ref, row_ref, b):
        self.column, self.row = col_ref[b], row_ref[b]
        last = self.row[:, -1:]
        self.head = self.column == 0.0
        self.tail = self.column == last
        self.keep = jnp.where(last == 0.0, 1.0, 0.0)


class Chain:
    def __init__(self, forward, col_ref, row_ref, state_ref, sums_ref, scratch, copy_sems):
        span, z = lax.axis_size("seq"), lax.axis_index("seq")
        self.span = span
        self.to = {"seq": lax.rem(z + (1 if forward else span - 1), span)}
        self.distance = z if forward else span - 1 - z
        self.gets, self.gives = self.distance > 0, self.distance < span - 1
        self.segments = (col_ref, row_ref)
        self.state_ref, self.sums_ref = state_ref, sums_ref
        self.own_ref, self.own_sums_ref, self.out_ref, self.out_sums_ref = scratch
        self.sems = copy_sems
        self.rows = state_ref.shape[0] // CHUNKS

    def pieces(self, g):
        some = STATE_ROWS // PIECES
        return [
            (g * self.rows + i, h, k * some)
            for i in range(self.rows)
            for h in range(self.state_ref.shape[1])
            for k in range(PIECES)
        ]

    def move(self, g, n, source, target):
        count = self.rows * self.state_ref.shape[1] * PIECES + 1
        return pltpu.make_async_remote_copy(
            src_ref=source,
            dst_ref=target,
            send_sem=self.sems.at[0, count * g + n],
            recv_sem=self.sems.at[1, count * g + n],
            device_id=self.to,
            device_id_type=MESH_ID,
        )

    def moves(self, g):
        part = pl.ds(g * self.rows, self.rows)
        found = [self.move(g, 0, self.out_sums_ref.at[part], self.sums_ref.at[part])]
        for n, (b, h, first) in enumerate(self.pieces(g)):
            used = pl.ds(first, STATE_ROWS // PIECES)
            found.append(
                self.move(g, n + 1, self.out_ref.at[b, h, used], self.state_ref.at[b, h, used])
            )
        return found

    def step(self, n):
        g = n - self.distance

        @pl.when((g >= 0) & (g < CHUNKS))
        def _():
            moves = self.moves(g)

            def take(move):
                @pl.when(self.gets)
                def _():
                    move.wait_recv()

            def give(move):
                @pl.when(self.gives)
                def _():
                    move.start()

            for (b, h, first), move in zip(self.pieces(g), moves[1:]):
                take(move)
                used = pl.ds(first, STATE_ROWS // PIECES)
                keep = Segments(*self.segments, b).keep
                before = self.state_ref[b, h, used].astype(jnp.float32)
                self.out_ref[b, h, used] = (self.own_ref[b, h, used] + keep * before).astype(
                    jnp.bfloat16
                )
                give(move)
            take(moves[0])
            for i in range(self.rows):
                b = g * self.rows + i
                keep = Segments(*self.segments, b).keep
                self.out_sums_ref[b] = self.own_sums_ref[b] + keep * self.sums_ref[b]
            give(moves[0])

    def run(self, work, between=()):
        def body(n, carry):
            for at, piece in enumerate(between):
                if piece is None:
                    continue

                @pl.when(n == at)
                def _():
                    piece()

            work(n, self.step)
            return carry

        lax.fori_loop(0, CHUNKS + self.span - 1, body, 0)

    def close(self):
        @pl.when(self.gives)
        def _():
            for g in range(CHUNKS):
                for c in self.moves(g):
                    c.wait_send()


def states_kernel(
    heads,
    normed_ref,
    pack_ref,
    col_ref,
    row_ref,
    pairs_ref,
    late_ref,
    qkv_ref,
    state_ref,
    sums_ref,
    late_all_ref,
    pick_ref,
    own_ref,
    own_sums_ref,
    out_ref,
    out_sums_ref,
    sems,
    shard_sems,
    shard_local_sems,
):
    parts, _, depth = pack_ref.shape
    rows, length = col_ref.shape[0], col_ref.shape[1]
    vcols, qcols = heads * VHEAD, heads * FDIM
    plane, span = lax.axis_size("dp"), lax.axis_size("seq")
    at, z = lax.axis_index("dp"), lax.axis_index("seq")
    chips = [lax.rem(at + k, plane) for k in range(1, plane)]
    state_ref[...] = jnp.zeros_like(state_ref)
    sums_ref[...] = jnp.zeros_like(sums_ref)
    greet(
        [{"dp": p} for p in chips] + [{"seq": lax.rem(z + k, span)} for k in (1, span - 1)]
    )
    shards = swap_shards(
        (late_ref,),
        (late_all_ref,),
        chips,
        at,
        block_of,
        columns_of,
        Sender(shard_sems),
        shard_local_sems,
    )
    chain = Chain(
        True,
        col_ref,
        row_ref,
        state_ref,
        sums_ref,
        (own_ref, own_sums_ref, out_ref, out_sums_ref),
        sems,
    )
    fill_selectors(pairs_ref, pick_ref, qcols)
    scale = feature_scale(pairs_ref)

    def tokens_of(b):
        return pl.ds(pl.multiple_of(b * length, length), length)

    def first(b, carry):
        t = tokens_of(b)
        value = jnp.zeros((length, vcols), jnp.float32)
        tile = jnp.zeros((length, LANES), jnp.float32)
        for s in range(parts):
            piece = normed_ref[t, pl.ds(s * depth, depth)]
            value += nt_dot(piece, pack_ref[s, pl.ds(0, vcols)])
            tile += nt_dot(piece, pack_ref[s, pl.ds(vcols, LANES)])
        lane = lax.broadcasted_iota(jnp.int32, (length, LANES), 1)
        tile = jnp.where(lane < 2 * qcols, tile, jnp.where(lane == 2 * qcols, 1.0, 0.0))
        value, tile = value.astype(jnp.bfloat16), tile.astype(jnp.bfloat16)
        qkv_ref[t, pl.ds(0, vcols)] = value
        qkv_ref[t, pl.ds(vcols, LANES)] = tile
        tail = Segments(col_ref, row_ref, b).tail
        for h in range(heads):
            one, two = factors(tile, pick_ref, 1, h)
            lifted = jnp.where(tail, one * two * scale, 0.0)
            own_ref[b, h] = tn_dot(
                lifted.astype(jnp.bfloat16), value[:, h * VHEAD : (h + 1) * VHEAD]
            )
            own_sums_ref[b, h : h + 1] = jnp.sum(lifted, axis=0, keepdims=True)
        return carry

    own_sums_ref[...] = jnp.zeros_like(own_sums_ref)
    each = rows // CHUNKS

    def work(n, step):
        @pl.when(n < CHUNKS)
        def _():
            lax.fori_loop(n * each, (n + 1) * each, first, 0)

        step(n)

    chain.run(work)
    for c in shards:
        c.wait()
    chain.close()


def mix_kernel(
    heads,
    qkv_ref,
    col_ref,
    row_ref,
    pairs_ref,
    state_ref,
    sums_ref,
    cot_ref,
    mixed_ref,
    exact_ref,
    den_ref,
    cot_all_ref,
    pick_ref,
    cot_sems,
    local_sem,
):
    rows, length = col_ref.shape[0], col_ref.shape[1]
    vcols, qcols = heads * VHEAD, heads * FDIM
    greet_plane()
    gather = gather_steps(cot_ref, cot_all_ref, Sender(cot_sems), local_sem)
    next(gather)
    fill_selectors(pairs_ref, pick_ref, qcols)

    def tokens_of(b):
        return pl.ds(pl.multiple_of(b * length, length), length)

    lane = lax.broadcasted_iota(jnp.int32, (length, LANES), 1)

    def here(b, carry):
        t = tokens_of(b)
        seg = Segments(col_ref, row_ref, b)
        tile = qkv_ref[t, pl.ds(vcols, LANES)]
        key = keys_in_place(tile, qcols)
        dens = jnp.zeros((length, LANES), jnp.float32)
        for h in range(heads):
            v = pl.ds(h * VHEAD, VHEAD)
            query = jnp.where(head_mask(length, h), tile, jnp.zeros_like(tile))
            _, w, _ = masked_weights(query, key, seg.column, seg.row)
            exact_ref[t, v] = nn_dot(w.astype(jnp.bfloat16), qkv_ref[t, v])
            dens = jnp.where(lane == h, jnp.sum(w, axis=1, keepdims=True), dens)
        den_ref[t] = dens
        return carry

    def before(b, carry):
        t = tokens_of(b)
        head = Segments(col_ref, row_ref, b).head
        tile = qkv_ref[t, pl.ds(vcols, LANES)]
        dens = den_ref[t]
        for h in range(heads):
            v = pl.ds(h * VHEAD, VHEAD)
            one, two = factors(tile, pick_ref, 0, h)
            lifted = jnp.where(head, one * two, 0.0)
            num = exact_ref[t, v] + nn_dot(lifted.astype(jnp.bfloat16), state_ref[b, h])
            den = dens[:, h : h + 1]
            den += jnp.sum(lifted * sums_ref[b, h : h + 1], axis=1, keepdims=True)
            value = num / den
            exact_ref[t, v] = value
            mixed_ref[t, v] = value.astype(jnp.bfloat16)
            dens = jnp.where(lane == h, den, dens)
        den_ref[t] = dens
        return carry

    def row(b, carry):
        for at in range(1, 6):

            @pl.when(b == at)
            def _():
                next(gather)

        here(b, 0)
        before(b, 0)
        return carry

    lax.fori_loop(0, rows, row, 0)
    run(gather)


def state_scratch(rows, heads):
    return [
        pltpu.VMEM((2, heads, 2, LANES, FEATURES), jnp.bfloat16),
        pltpu.VMEM((rows, heads, FEATURES, VHEAD), jnp.float32),
        pltpu.VMEM((rows, 8, FEATURES), jnp.float32),
        pltpu.VMEM((rows, heads, FEATURES, VHEAD), jnp.bfloat16),
        pltpu.VMEM((rows, 8, FEATURES), jnp.float32),
    ]


def states(normed, pack, seg_col, seg_row, pairs, shards, heads, cid):
    tokens = normed.shape[0]
    rows = seg_col.shape[0]
    vcols = heads * VHEAD
    plane = lax.axis_size("dp")
    whole = pltpu.VMEM
    return kernel_call(
        partial(states_kernel, heads),
        "states",
        cid,
        [
            ((tokens, vcols + LANES), jnp.bfloat16, whole),
            ((rows, heads, FEATURES, VHEAD), jnp.bfloat16, whole),
            ((rows, 8, FEATURES), jnp.float32, whole),
        ]
        + [((p.shape[1], plane * p.shape[2]), p.dtype, pl.ANY) for p in shards],
        [(a, whole) for a in (normed, pack, seg_col, seg_row, pairs)]
        + [(p, pl.ANY) for p in shards],
        state_scratch(rows, heads)
        + [
            copies(rows * heads * PIECES + CHUNKS),
            copies(len(shards) * (plane - 1)),
            pltpu.SemaphoreType.DMA((len(shards),)),
        ],
        moved=normed.size * 20,
    )


def mix(qkv, seg_col, seg_row, pairs, state, sums, cot_own, heads, cid):
    tokens = qkv.shape[0]
    vcols = heads * VHEAD
    m, width = cot_own.shape
    whole = pltpu.VMEM
    mixed, exact, den, cot = kernel_call(
        partial(mix_kernel, heads),
        "mix",
        cid,
        [
            ((tokens, vcols), jnp.bfloat16, whole),
            ((tokens, vcols), jnp.float32, whole),
            ((tokens, LANES), jnp.float32, whole),
            ((4, 2, m, width), jnp.bfloat16, pl.ANY),
        ],
        [(a, whole) for a in (qkv, seg_col, seg_row, pairs, state, sums, cot_own)],
        [
            pltpu.VMEM((2, heads, 2, LANES, FEATURES), jnp.bfloat16),
            copies(GATHER_COPIES),
            pltpu.SemaphoreType.DMA,
        ],
        moved=cot_own.size * 80,
    )
    return mixed, exact, den, cot.reshape(-1, width)


def branch_kernel(
    mixed_ref,
    pack_ref,
    x_ref,
    small_ref,
    residual_ref,
    normed_ref,
    part_ref,
    pair_ref,
    sum_ref,
    got_ref,
    sems,
):
    greet_plane()
    parts, _, depth = pack_ref.shape
    m, width = x_ref.shape
    vcols = mixed_ref.shape[1]
    first = pack_ref.shape[1] - vcols

    def block(chip, core):
        left = mixed_ref[pl.ds(pl.multiple_of((chip * 2 + core) * m, m), m)]
        for s in range(parts):
            part_ref[chip, core, :, pl.ds(s * depth, depth)] = nn_dot(
                left, pack_ref[s, pl.ds(first, vcols)]
            ).astype(jnp.bfloat16)

    scatter = scatter_steps(
        part_ref, residual_ref, pair_ref, sum_ref, got_ref, Sender(sems), start=False
    )
    produce_parts(block, next(scatter))
    run(scatter)

    def body(r, carry):
        acc = jnp.zeros((ROW_STEP, LANES), jnp.float32)
        for k in range(width // LANES):
            v = residual_ref[r, lanes(k)] + x_ref[r, lanes(k)].astype(jnp.float32)
            residual_ref[r, lanes(k)] = v
            acc += v * v
        scale = lax.rsqrt(mean_of(acc, width) + norm_epsilon)
        for k in range(width // LANES):
            normed_ref[r, lanes(k)] = (
                residual_ref[r, lanes(k)] * scale * small_ref[k, 1:2, :]
            ).astype(jnp.bfloat16)
        return carry

    row_blocks(m, ROW_STEP, body)(0)


def scatter_scratch(m, width):
    return [
        pltpu.VMEM((4, m, width), jnp.bfloat16),
        pltpu.VMEM((3, m, width), jnp.bfloat16),
        pltpu.VMEM((3, m, width), jnp.bfloat16),
    ]


def branch(mixed, pack, x, small, cid):
    m, width = x.shape
    whole = pltpu.VMEM
    return kernel_call(
        branch_kernel,
        "branch",
        cid,
        [((m, width), jnp.float32, whole), ((m, width), jnp.bfloat16, whole)],
        [(mixed, whole), (pack, whole), (x, whole), (small, whole)],
        [pltpu.VMEM((4, 2, m, width), jnp.bfloat16)]
        + scatter_scratch(m, width)
        + [copies(SCATTER_COPIES)],
        moved=x.size * 80,
    )


def parity(i):
    return i % 2 if isinstance(i, int) else lax.rem(i, 2)


def choose(test, a, b):
    if isinstance(test, bool):
        return a if test else b
    return jnp.where(test, a, b)


def project(at, w_ref, rows):
    parts, _, depth = w_ref.shape
    total = nt_dot(at(pl.ds(0, depth)), w_ref[0, rows])
    for s in range(1, parts):
        total += nt_dot(at(pl.ds(s * depth, depth)), w_ref[s, rows])
    return total


def arrivals(i, half):
    at, x_at, y_at, d_at, core = plane_places()
    k = choose(parity(i) == 0, core, 1 - core)
    one = choose(i < 2, at, choose(i < 6, x_at, d_at))
    two = choose(i < 2, at, choose(i < 6, y_at, d_at))
    late = (i >= 4) & (i < 6)
    late = int(late) if isinstance(late, bool) else late.astype(jnp.int32)
    first, second = late * half, (1 - late) * half
    if not isinstance(i, int):
        first, second = pl.multiple_of(first, half), pl.multiple_of(second, half)
    return (one, k, first), (two, k, second)


def stacked_copies(early, late, out, sems):
    rows = pl.ds(early.shape[1] - EARLY, EARLY)
    return [
        pltpu.make_async_copy(early.at[:, rows], out.at[:, pl.ds(0, EARLY)], sems.at[0]),
        pltpu.make_async_copy(late, out.at[:, pl.ds(EARLY, late.shape[1])], sems.at[1]),
    ]


def expand_kernel(
    own_ref,
    early_hbm,
    late_hbm,
    normed_hbm,
    gate_hbm,
    up_hbm,
    hidden_hbm,
    normed_ref,
    w_ref,
    gate_ref,
    up_ref,
    hidden_ref,
    sems,
    local_sem,
    w_sems,
    store_sems,
    keep_sem,
):
    greet_plane()
    half = own_ref.shape[0] // 2
    units = gate_ref.shape[2]
    gather = gather_steps(own_ref, normed_ref, Sender(sems), local_sem)
    next(gather)
    weights = stacked_copies(early_hbm, late_hbm, w_ref, w_sems)
    for c in weights:
        c.start()

    def store_copies(i):
        slot = parity(i)
        found = []
        for n, (c, k, r) in enumerate(arrivals(i, half)):
            rows = pl.ds(n * half, half)
            column = (c * 2 + k) * (2 * half) + r
            pairs = (
                (gate_ref.at[slot, rows], gate_hbm.at[c, k, pl.ds(r, half)]),
                (up_ref.at[slot, rows], up_hbm.at[c, k, pl.ds(r, half)]),
                (
                    hidden_ref.at[slot, :, rows],
                    hidden_hbm.at[:, pl.ds(pl.multiple_of(column, half), half)],
                ),
            )
            for q, (a, b) in enumerate(pairs):
                found.append(pltpu.make_async_copy(a, b, store_sems.at[slot, 3 * n + q]))
        return found

    next(gather)
    for c in weights:
        c.wait()

    def body(i, carry):
        for step in range(1, 8):

            @pl.when(i == step)
            def _():
                next(gather)

        @pl.when(i >= 2)
        def _():
            for c in store_copies(i - 2):
                c.wait()

        slot = parity(i)
        pieces = arrivals(i, half)

        def columns(cols):
            return jnp.concatenate([normed_ref[c, k, pl.ds(r, half), cols] for c, k, r in pieces])

        gate = project(columns, w_ref, pl.ds(0, units))
        up = project(columns, w_ref, pl.ds(units, units))
        gate_ref[slot], up_ref[slot] = gate, up
        hidden_ref[slot] = (gate * jax.nn.sigmoid(gate) * up).astype(jnp.bfloat16).T
        for c in store_copies(i):
            c.start()
        return carry

    lax.fori_loop(0, 8, body, 0)
    keep = pltpu.make_async_copy(normed_ref, normed_hbm, keep_sem)
    keep.start()
    for i in (6, 7):
        for c in store_copies(i):
            c.wait()
    keep.wait()
    run(gather)


def expand(own, early, late, cid):
    m, width = own.shape
    weights = (early.shape[0], EARLY + late.shape[1], early.shape[2])
    units = weights[1] // 2
    low = jnp.bfloat16
    thin = ((4, 2, m, units), jnp.float32, pl.ANY)
    normed, gate, up, hidden = kernel_call(
        expand_kernel,
        "expand",
        cid,
        [((4, 2, m, width), low, pl.ANY), thin, thin, ((units, 8 * m), low, pl.ANY)],
        [(own, pltpu.VMEM), (early, pl.ANY), (late, pl.ANY)],
        [
            pltpu.VMEM((4, 2, m, width), low),
            pltpu.VMEM(weights, low),
            pltpu.VMEM((2, m, units), jnp.float32),
            pltpu.VMEM((2, m, units), jnp.float32),
            pltpu.VMEM((2, units, m), low),
            copies(GATHER_COPIES),
            pltpu.SemaphoreType.DMA,
            pltpu.SemaphoreType.DMA((2,)),
            pltpu.SemaphoreType.DMA((2, 6)),
            pltpu.SemaphoreType.DMA,
        ],
        flops=32 * m * width * units,
        moved=1 << 27,
    )
    return normed.reshape(8 * m, width), gate, up, hidden


def hidden_kernel(
    gate_hbm,
    up_hbm,
    cot_hbm,
    early_hbm,
    late_hbm,
    down_hbm,
    normed_hbm,
    out_hbm,
    total_ref,
    grads_hbm,
    gate_ref,
    up_ref,
    cot_ref,
    out_ref,
    w_ref,
    down_w_ref,
    part_ref,
    pair_ref,
    sum_ref,
    got_ref,
    turned_ref,
    normed_ref,
    grad_ref,
    sems,
    w_sems,
    load_sems,
    store_sems,
    normed_sem,
    grad_sems,
):
    greet_plane()
    at, x_at, y_at, d_at, core = plane_places()
    parts, units, depth = down_w_ref.shape
    m = cot_ref.shape[1]
    scatter = scatter_steps(
        part_ref, total_ref, pair_ref, sum_ref, got_ref, Sender(sems), start=False
    )
    pairs = next(scatter)
    weights = stacked_copies(early_hbm, late_hbm, w_ref, w_sems)
    weights.append(pltpu.make_async_copy(down_hbm, down_w_ref, w_sems.at[2]))
    normed_copy = pltpu.make_async_copy(normed_hbm, normed_ref, normed_sem)

    def loads(i):
        slot, (c, k) = parity(i), leaving(i)
        return [
            pltpu.make_async_copy(a.at[c, k], b.at[slot], load_sems.at[slot, n])
            for n, (a, b) in enumerate(
                ((gate_hbm, gate_ref), (up_hbm, up_ref), (cot_hbm, cot_ref))
            )
        ]

    def store(i):
        slot, (c, k) = parity(i), leaving(i)
        return pltpu.make_async_copy(out_ref.at[slot], out_hbm.at[c, k], store_sems.at[slot])

    for c in weights + loads(0):
        c.start()
    normed_copy.start()
    for c in weights:
        c.wait()

    def body(i, carry):
        for step in (2, 4, 6):

            @pl.when(i == step)
            def _():
                next(scatter)

        @pl.when(i < 7)
        def _():
            for c in loads(i + 1):
                c.start()

        for c in loads(i):
            c.wait()

        @pl.when(i >= 2)
        def _():
            store(i - 2).wait()

        slot, (chip, k) = parity(i), leaving(i)
        gate, up = gate_ref[slot], up_ref[slot]
        dhidden = project(lambda cols: cot_ref[slot, :, cols], down_w_ref, pl.ds(0, units))
        sig = jax.nn.sigmoid(gate)
        silu = gate * sig
        hidden = (silu * up).astype(jnp.bfloat16)
        dgate = (dhidden * up * sig * (1.0 + gate * (1.0 - sig))).astype(jnp.bfloat16)
        dup = (dhidden * silu).astype(jnp.bfloat16)
        for s in range(parts):
            cols = pl.ds(s * depth, depth)
            part_ref[chip, k, :, cols] = (
                nn_dot(dgate, w_ref[s, pl.ds(0, units)])
                + nn_dot(dup, w_ref[s, pl.ds(units, units)])
            ).astype(jnp.bfloat16)
            out_ref[slot, :, cols] = nn_dot(hidden, down_w_ref[s]).astype(jnp.bfloat16)
        store(i).start()
        for j in range(4):

            @pl.when(i == 2 * j)
            def _():
                pairs[j].start()

        column = pl.ds(pl.multiple_of((chip * 2 + k) * m, m), m)
        turned_ref[0, :, column], turned_ref[1, :, column] = dgate.T, dup.T
        return carry

    lax.fori_loop(0, 8, body, 0)
    next(scatter)
    store(6).wait()
    store(7).wait()
    normed_copy.wait()
    width = grad_ref.shape[2]
    blocks = normed_ref.shape[1] // width

    def gradients(which):
        rows = pl.ds(which * units, units)

        def stored(i):
            column = pl.ds(pl.multiple_of(i * width, width), width)
            slot = parity(i)
            return pltpu.make_async_copy(
                grad_ref.at[slot], grads_hbm.at[rows, column], grad_sems.at[slot]
            )

        def body(i, carry):
            column = pl.ds(pl.multiple_of(i * width, width), width)

            @pl.when(i >= 2)
            def _():
                stored(i - 2).wait()

            grad_ref[parity(i)] = nn_dot(turned_ref[which], normed_ref[:, column]).astype(
                jnp.bfloat16
            )
            stored(i).start()
            return carry

        lax.fori_loop(0, blocks, body, 0)
        for i in (blocks - 2, blocks - 1):
            stored(i).wait()

    gradients(0)
    gradients(1)
    run(scatter)


def hidden_units(gate, up, cot, early, late, down_w, normed, cid):
    _, _, m, units = gate.shape
    tokens, width = normed.shape
    low = jnp.bfloat16
    stacked = (early.shape[0], EARLY + late.shape[1], early.shape[2])
    ins = (gate, up, cot.reshape(4, 2, m, width), early, late, down_w, normed)
    return kernel_call(
        hidden_kernel,
        "hidden_units",
        cid,
        [
            ((4, 2, m, width), low, pl.ANY),
            ((m, width), jnp.float32, pltpu.VMEM),
            ((2 * units, width), low, pl.ANY),
        ],
        [(a, pl.ANY) for a in ins],
        [
            pltpu.VMEM((2, m, units), jnp.float32),
            pltpu.VMEM((2, m, units), jnp.float32),
            pltpu.VMEM((2, m, width), low),
            pltpu.VMEM((2, m, width), low),
            pltpu.VMEM(stacked, low),
            pltpu.VMEM(down_w.shape, low),
            pltpu.VMEM((4, 2, m, width), low),
        ]
        + scatter_scratch(m, width)
        + [
            pltpu.VMEM((2, units, tokens), low),
            pltpu.VMEM((tokens, width), low),
            pltpu.VMEM((2, units, 2 * LANES), low),
            copies(SCATTER_COPIES),
            pltpu.SemaphoreType.DMA((3,)),
            pltpu.SemaphoreType.DMA((2, 3)),
            pltpu.SemaphoreType.DMA((2,)),
            pltpu.SemaphoreType.DMA,
            pltpu.SemaphoreType.DMA((2,)),
        ],
        flops=12 * tokens * width * units,
        moved=1 << 27,
    )


def norm_gradient(r, value_at, grad_ref, gain_at, gain_grad, finish, width):
    squares = jnp.zeros((ROW_STEP, LANES), jnp.float32)
    cross = jnp.zeros((ROW_STEP, LANES), jnp.float32)
    for k in range(width // LANES):
        v = value_at(r, k)
        squares += v * v
        cross += v * grad_ref[r, lanes(k)] * gain_at(k)
    scale = lax.rsqrt(mean_of(squares, width) + norm_epsilon)
    pull = mean_of(cross, width) * scale * scale * scale
    for k in range(width // LANES):
        v, g = value_at(r, k), grad_ref[r, lanes(k)]
        gain_grad[:, lanes(k)] += jnp.sum(
            (g * v * scale).reshape(ROW_STEP // 8, 8, LANES), axis=0
        )
        finish(r, k, scale * g * gain_at(k) - v * pull)


def turn_kernel(
    total_ref,
    residual_ref,
    cot_ref,
    small_ref,
    pack_ref,
    mixed_ref,
    dresid_ref,
    gain_ref,
    dmixed_ref,
    grad_ref,
    all_ref,
    low_ref,
    sum_ref,
    gather_sems,
    local_sem,
):
    greet_plane()
    m, width = residual_ref.shape
    half = m // 2
    parts, _, depth = pack_ref.shape
    vcols = mixed_ref.shape[3]
    first_row = pack_ref.shape[1] - vcols
    gain_ref[...] = jnp.zeros_like(gain_ref)

    def finish(r, k, v):
        v += cot_ref[r, lanes(k)].astype(jnp.float32)
        dresid_ref[r, lanes(k)] = v
        low_ref[r, lanes(k)] = v.astype(jnp.bfloat16)

    def body(r, carry):
        norm_gradient(
            r,
            lambda r, k: residual_ref[r, lanes(k)],
            total_ref,
            lambda k: small_ref[k, 1:2, :],
            gain_ref,
            finish,
            width,
        )
        return carry

    row_blocks(m, ROW_STEP, body)(0)
    gather = gather_steps(low_ref, all_ref, Sender(gather_sems), local_sem)
    next(gather)
    sum_ref[...] = jnp.zeros_like(sum_ref)
    next(gather)

    def block(i, carry):
        for step in range(1, 8):

            @pl.when(i == step)
            def _():
                next(gather)

        pieces = arrivals(i, half)

        def columns(cols):
            return jnp.concatenate([all_ref[c, k, pl.ds(r, half), cols] for c, k, r in pieces])

        left = jnp.concatenate([mixed_ref[c, k, pl.ds(r, half)] for c, k, r in pieces])
        dmixed = project(columns, pack_ref, pl.ds(first_row, vcols)).astype(jnp.bfloat16)
        for n, (c, k, r) in enumerate(pieces):
            dmixed_ref[c, k, pl.ds(r, half)] = dmixed[n * half : (n + 1) * half]
        for s in range(parts):
            cols = pl.ds(s * depth, depth)
            sum_ref[:, cols] += tn_dot(left, columns(cols))
        return carry

    lax.fori_loop(0, 8, block, 0)
    grad_ref[...] = sum_ref[...].astype(jnp.bfloat16)
    run(gather)


def turn(total, residual, cot_own, small, pack, mixed, cid):
    m, width = residual.shape
    vcols = mixed.shape[1]
    whole, low = pltpu.VMEM, jnp.bfloat16
    dresid, gain, dmixed, grad = kernel_call(
        turn_kernel,
        "turn",
        cid,
        [
            ((m, width), jnp.float32, whole),
            ((8, width), jnp.float32, whole),
            ((4, 2, m, vcols), low, whole),
            ((vcols, width), low, whole),
        ],
        [(a, whole) for a in (total, residual, cot_own, small, pack)]
        + [(mixed.reshape(4, 2, m, vcols), whole)],
        [
            pltpu.VMEM((4, 2, m, width), low),
            pltpu.VMEM((m, width), low),
            pltpu.VMEM((vcols, width), jnp.float32),
            copies(GATHER_COPIES),
            pltpu.SemaphoreType.DMA,
        ],
        moved=residual.size * 80,
    )
    return dresid, gain, dmixed.reshape(8 * m, vcols), grad


def unmix_kernel(
    heads,
    count,
    dmixed_ref,
    normed_hbm,
    output_grad_ref,
    part_ref,
    residual_ref,
    col_ref,
    row_ref,
    pairs_ref,
    qkv_ref,
    exact_ref,
    den_ref,
    state_ref,
    sums_ref,
    *refs,
):
    ins, dqkv_ref, block_ref, grad_ref = refs[:count], *refs[count : count + 3]
    outs = refs[count + 3 : 2 * count + 3]
    (
        normed_ref,
        early_ref,
        turned_ref,
        dvalue_ref,
        dtile_ref,
        back_ref,
        back_sums_ref,
        pick_ref,
        own_ref,
        own_sums_ref,
        out_ref,
        out_sums_ref,
        total_ref,
        held_ref,
        pair_ref,
        sum_ref,
        got_ref,
        sems,
        shard_sems,
        local_sems,
        scatter_sems,
        held_sems,
        normed_sem,
    ) = refs[2 * count + 3 :]
    rows, length = col_ref.shape[0], col_ref.shape[1]
    vcols, qcols = heads * VHEAD, heads * FDIM
    at, x_at, y_at, _, core = plane_places()
    plane, span, z = lax.axis_size("dp"), lax.axis_size("seq"), lax.axis_index("seq")
    chips = [lax.rem(at + k, plane) for k in range(1, plane)]
    normed_copy = pltpu.make_async_copy(normed_hbm, normed_ref, normed_sem)
    normed_copy.start()
    back_ref[...] = jnp.zeros_like(back_ref)
    back_sums_ref[...] = jnp.zeros_like(back_sums_ref)
    greet(
        [{"dp": p} for p in chips]
        + [{"tensor": 1 - core}]
        + [{"seq": lax.rem(z + k, span)} for k in (1, span - 1)]
    )
    scatter = scatter_steps(
        part_ref,
        total_ref,
        pair_ref,
        sum_ref,
        got_ref,
        Sender(scatter_sems),
        (held_ref, held_sems),
    )
    next(scatter)
    chain = Chain(
        False,
        col_ref,
        row_ref,
        back_ref,
        back_sums_ref,
        (own_ref, own_sums_ref, out_ref, out_sums_ref),
        sems,
    )
    fill_selectors(pairs_ref, pick_ref, qcols)
    scale = feature_scale(pairs_ref)

    def tokens_of(b):
        return pl.ds(pl.multiple_of(b * length, length), length)

    def cotangents(t, h):
        v = pl.ds(h * VHEAD, VHEAD)
        dn = dmixed_ref[t, v].astype(jnp.float32) / den_ref[t, pl.ds(h, 1)]
        dd = -jnp.sum(dn * exact_ref[t, v], axis=1, keepdims=True)
        return dn.astype(jnp.bfloat16), dd

    def first(b, carry):
        t = tokens_of(b)
        head = Segments(col_ref, row_ref, b).head
        tile = qkv_ref[t, pl.ds(vcols, LANES)]
        for h in range(heads):
            dn, dd = cotangents(t, h)
            one, two = factors(tile, pick_ref, 0, h)
            lifted = jnp.where(head, one * two, 0.0)
            own_ref[b, h] = tn_dot(lifted.astype(jnp.bfloat16), dn)
            own_sums_ref[b, h : h + 1] = jnp.sum(lifted * dd, axis=0, keepdims=True)
        return carry

    own_sums_ref[...] = jnp.zeros_like(own_sums_ref)
    shards = swap_shards(ins, outs, chips, at, columns_of, block_of, Sender(shard_sems), local_sems)

    def lowered(dlifted, kind, h, one, two):
        return nt_dot((dlifted * two).astype(jnp.bfloat16), pick_ref[kind, h, 0]) + nt_dot(
            (dlifted * one).astype(jnp.bfloat16), pick_ref[kind, h, 1]
        )

    def here(b, carry):
        t = tokens_of(b)
        seg = Segments(col_ref, row_ref, b)
        tile = qkv_ref[t, pl.ds(vcols, LANES)]
        key = keys_in_place(tile, qcols)
        dtile = jnp.zeros((length, LANES), jnp.float32)
        dkey = jnp.zeros((length, LANES), jnp.float32)
        for h in range(heads):
            inside = head_mask(length, h)
            v = pl.ds(h * VHEAD, VHEAD)
            query = jnp.where(inside, tile, jnp.zeros_like(tile))
            dn, dd = cotangents(t, h)
            a, w, keep = masked_weights(query, key, seg.column, seg.row)
            dw = jnp.where(keep, nt_dot(dn, qkv_ref[t, v]) + dd, 0.0)
            da = (dw * (1.0 + a) * 0.25).astype(jnp.bfloat16)
            dvalue_ref[t, v] = tn_dot(w.astype(jnp.bfloat16), dn)
            dtile += jnp.where(inside, nn_dot(da, key), 0.0)
            dkey += jnp.where(inside, tn_dot(da, query), 0.0)
            one, two = factors(tile, pick_ref, 0, h)
            dlifted = nt_dot(dn, state_ref[b, h]) + dd * sums_ref[b, h : h + 1]
            dtile += lowered(jnp.where(seg.head, dlifted, 0.0), 0, h, one, two)
        dtile_ref[t] = dtile + pltpu.roll(dkey, qcols, axis=1)
        return carry

    def after(b, carry):
        t = tokens_of(b)
        tail = Segments(col_ref, row_ref, b).tail
        tile = qkv_ref[t, pl.ds(vcols, LANES)]
        dtile = dtile_ref[t]
        for h in range(heads):
            v = pl.ds(h * VHEAD, VHEAD)
            one, two = factors(tile, pick_ref, 1, h)
            lifted = jnp.where(tail, one * two * scale, 0.0)
            dlifted = nt_dot(qkv_ref[t, v], back_ref[b, h]) + back_sums_ref[b, h : h + 1]
            dtile += lowered(jnp.where(tail, dlifted * scale, 0.0), 1, h, one, two)
            dvalue = dvalue_ref[t, v] + nn_dot(lifted.astype(jnp.bfloat16), back_ref[b, h])
            dqkv_ref[t, v] = dvalue.astype(jnp.bfloat16)
        lane = lax.broadcasted_iota(jnp.int32, (length, LANES), 1)
        dqkv_ref[t, pl.ds(vcols, LANES)] = jnp.where(lane < 2 * qcols, dtile, 0.0).astype(
            jnp.bfloat16
        )
        turned_ref[:, t] = dqkv_ref[t].T
        return carry

    each = rows // CHUNKS

    def work(n, step):
        @pl.when(n < CHUNKS)
        def _():
            lax.fori_loop(n * each, (n + 1) * each, first, 0)

        step(n)

        @pl.when(n < CHUNKS)
        def _():
            lax.fori_loop(n * each, (n + 1) * each, here, 0)

        done = n - chain.distance

        @pl.when((done >= 0) & (done < CHUNKS))
        def _():
            lax.fori_loop(done * each, (done + 1) * each, after, 0)

    def finish(r, carry):
        block_ref[r] = (residual_ref[r] + total_ref[r]).astype(jnp.bfloat16)
        return carry

    def output():
        run(scatter)
        row_blocks(block_ref.shape[0], ROW_STEP, finish)(0)

    wide = 4 * LANES
    qkv_rows = grad_ref.shape[0] - vcols
    early = (rows - each) * length

    def gradient(t, put):
        def body(i, carry):
            cols = pl.ds(pl.multiple_of(i * wide, wide), wide)
            put(cols, nn_dot(turned_ref[pl.ds(0, qkv_rows), t], normed_ref[t, cols]))
            return carry

        lax.fori_loop(0, normed_ref.shape[1] // wide, body, 0)

    def keep(cols, value):
        early_ref[:, cols] = value

    def close(cols, value):
        grad_ref[pl.ds(0, qkv_rows), cols] = (early_ref[:, cols] + value).astype(jnp.bfloat16)

    def most():
        normed_copy.wait()
        gradient(pl.ds(0, early), keep)

    steps = [None] * (CHUNKS + span - 1)
    steps[2] = lambda: advance(scatter, 3)
    steps[6] = lambda: advance(scatter)
    steps[-2], steps[-1] = output, most
    chain.run(work, steps)
    gradient(pl.ds(early, each * length), close)
    grad_ref[pl.ds(qkv_rows, vcols)] = output_grad_ref[...]
    for c in shards:
        c.wait()
    chain.close()


def unmix(dmixed, normed, output_grad, part, residual, segments, pairs, kept, shards, heads, cid):
    seg_col, seg_row = segments
    tokens, vcols = dmixed.shape
    plane, rows = lax.axis_size("dp"), seg_col.shape[0]
    grad_rows = 2 * vcols + 2 * heads * FDIM
    m, width = residual.shape
    count = len(shards)
    whole, low = pltpu.VMEM, jnp.bfloat16
    dqkv, block, grad, *swapped = kernel_call(
        partial(unmix_kernel, heads, count),
        "unmix",
        cid,
        [
            ((tokens, vcols + LANES), low, whole),
            ((m, width), low, whole),
            ((grad_rows, width), low, whole),
        ]
        + [((plane, p.shape[0], p.shape[1] // plane), p.dtype, pl.ANY) for p in shards],
        [
            (dmixed, whole),
            (normed, pl.ANY),
            (output_grad, whole),
            (part, pl.ANY),
            (residual, whole),
            (seg_col, whole),
            (seg_row, whole),
            (pairs, whole),
        ]
        + [(a, whole) for a in kept]
        + [(p, pl.ANY) for p in shards],
        [
            pltpu.VMEM((tokens, width), low),
            pltpu.VMEM((grad_rows - vcols, width), jnp.float32),
            pltpu.VMEM((vcols + LANES, tokens), low),
            pltpu.VMEM((tokens, vcols), jnp.float32),
            pltpu.VMEM((tokens, LANES), jnp.float32),
            pltpu.VMEM((rows, heads, FEATURES, VHEAD), low),
            pltpu.VMEM((rows, 8, FEATURES), jnp.float32),
        ]
        + state_scratch(rows, heads)
        + [pltpu.VMEM((m, width), jnp.float32), pltpu.VMEM((4, m, width), low)]
        + scatter_scratch(m, width)
        + [
            copies(rows * heads * PIECES + CHUNKS),
            copies(count * (plane - 1)),
            pltpu.SemaphoreType.DMA((count,)),
            copies(SCATTER_COPIES),
            pltpu.SemaphoreType.DMA((4,)),
            pltpu.SemaphoreType.DMA,
        ],
        moved=residual.size * 120,
    )
    return dqkv, block, grad, swapped


def last_kernel(count, *refs):
    ins, gain_ref, outs, sum_ref = (
        refs[:count],
        refs[count],
        refs[count + 1 : 2 * count + 1],
        refs[2 * count + 1],
    )
    got_gain, sems, gain_sems, local_sems = refs[2 * count + 2 :]
    plane, at = lax.axis_size("dp"), lax.axis_index("dp")
    others, me = everyone()
    greet(others)
    copy_gain = Sender(gain_sems)
    gains = [
        copy_gain(gain_ref.at[p["seq"] * plane + p["dp"]], got_gain.at[me], p) for p in others
    ]
    for c in gains:
        c.start()
    chips = [lax.rem(at + k, plane) for k in range(1, plane)]
    shards = swap_shards(ins, outs, chips, at, columns_of, block_of, Sender(sems), local_sems)
    got_gain[me] = gain_ref[lax.axis_index("seq") * plane + at]
    for c in gains:
        c.wait()
    total = got_gain[0]
    for k in range(1, len(others) + 1):
        total += got_gain[k]
    sum_ref[...] = total
    for c in shards:
        c.wait()


def last(shards, gains, cid):
    plane = lax.axis_size("dp")
    count = len(shards)
    devices = lax.axis_size(("dp", "seq", "tensor"))
    *swapped, total = kernel_call(
        partial(last_kernel, count),
        "last",
        cid,
        [((plane, p.shape[0], p.shape[1] // plane), p.dtype, pl.ANY) for p in shards]
        + [(gains.shape[1:], jnp.float32, pltpu.VMEM)],
        [(p, pl.ANY) for p in shards] + [(gains, pltpu.VMEM)],
        [
            pltpu.VMEM((devices,) + gains.shape[1:], jnp.float32),
            copies(count * (plane - 1)),
            copies(devices - 1),
            pltpu.SemaphoreType.DMA((count,)),
        ],
        moved=1 << 26,
    )
    return swapped, total


def everyone():
    plane, span, cores = (lax.axis_size(a) for a in ("dp", "seq", "tensor"))
    at, z, core = (lax.axis_index(a) for a in ("dp", "seq", "tensor"))
    others = [
        {
            "dp": lax.rem(at + i, plane),
            "seq": lax.rem(z + k, span),
            "tensor": lax.rem(core + c, cores),
        }
        for k in range(span)
        for i in range(plane)
        for c in range(cores)
        if i or k or c
    ]
    return others, (at * span + z) * cores + core


def exit_kernel(
    dqkv_ref,
    pack_ref,
    x_ref,
    dresid_ref,
    block_ref,
    small_ref,
    gain_two_ref,
    shards_ref,
    grad_ref,
    out_ref,
    gains_ref,
    shards_all_ref,
    gain_ref,
    part_ref,
    total_ref,
    ordered_ref,
    low_ref,
    pair_ref,
    sum_ref,
    got_ref,
    sems,
    pair_sems,
    local_sems,
    shard_sems,
    shard_local_sems,
):
    plane, at = lax.axis_size("dp"), lax.axis_index("dp")
    core = lax.axis_index("tensor")
    chips = [lax.rem(at + k, plane) for k in range(1, plane)]
    greet([{"dp": p} for p in chips] + [{"tensor": 1 - core}])
    shard_copy = Sender(shard_sems)

    half = shards_ref.shape[0] // 2

    def swap(n):
        rows = pl.ds(n * half, half)
        return swap_shards(
            (shards_ref,),
            (shards_all_ref,),
            chips,
            at,
            lambda ref, p: columns_of(ref, p, rows),
            lambda ref, p: ref.at[p, rows],
            shard_copy,
            shard_local_sems.at[pl.ds(n, 1)],
        )

    shards = swap(0)
    parts, _, depth = pack_ref.shape
    m, width = x_ref.shape
    wide = dqkv_ref.shape[1] - LANES + 2 * FDIM * ((dqkv_ref.shape[1] - LANES) // VHEAD)
    blocks = width // LANES
    copy = Sender(pair_sems)

    def block(chip, core):
        left = dqkv_ref[pl.ds(pl.multiple_of((chip * 2 + core) * m, m), m), pl.ds(0, wide)]
        for s in range(parts):
            part_ref[chip, core, :, pl.ds(s * depth, depth)] = nn_dot(
                left, pack_ref[s, pl.ds(0, wide)]
            ).astype(jnp.bfloat16)

    scatter = scatter_steps(
        part_ref, total_ref, pair_ref, sum_ref, got_ref, Sender(sems), start=False
    )
    produce_parts(block, next(scatter))

    def order(r, carry):
        for k in range(blocks):
            low_ref[r, lanes(seq_major_block(k))] = block_ref[r, lanes(k)]
        return carry

    row_blocks(m, ROW_STEP, order)(0)
    to_pair = [copy(low_ref, out_ref.at[core], {"tensor": 1 - core})]
    local = [pltpu.make_async_copy(low_ref, out_ref.at[core], local_sems.at[0])]
    to_pair[0].start()
    local[0].start()
    advance(scatter, 4)
    shards += swap(1)
    run(scatter)
    gain_ref[...] = jnp.zeros_like(gain_ref)

    def finish(r, k, v):
        ordered_ref[r, lanes(seq_major_block(k))] = v + dresid_ref[r, lanes(k)]

    def body(r, carry):
        norm_gradient(
            r,
            lambda r, k: x_ref[r, lanes(k)].astype(jnp.float32),
            total_ref,
            lambda k: small_ref[k, 0:1, :],
            gain_ref,
            finish,
            width,
        )
        return carry

    row_blocks(m, ROW_STEP, body)(0)
    to_pair.append(copy(ordered_ref, grad_ref.at[core], {"tensor": 1 - core}))
    local.append(pltpu.make_async_copy(ordered_ref, grad_ref.at[core], local_sems.at[1]))
    to_pair[1].start()
    local[1].start()
    gains_ref[...] = jnp.zeros_like(gains_ref)
    for k in range(blocks):
        for row, ref in enumerate((gain_ref, gain_two_ref)):
            gains_ref[k, row : row + 1] = jnp.sum(ref[:, lanes(k)], axis=0, keepdims=True)
    for c in to_pair + local + shards:
        c.wait()


def leave(dqkv, pack, x, dresid, block, small, gain_two, shards, cid):
    m, width = x.shape
    plane = lax.axis_size("dp")
    whole = pltpu.VMEM
    return kernel_call(
        exit_kernel,
        "leave",
        cid,
        [
            ((2, m, width), jnp.float32, pl.ANY),
            ((2, m, width), jnp.bfloat16, pl.ANY),
            ((width // LANES, 8, LANES), jnp.float32, whole),
        ]
        + [((plane, p.shape[0], p.shape[1] // plane), p.dtype, pl.ANY) for p in shards],
        [(a, whole) for a in (dqkv, pack, x, dresid, block, small, gain_two)]
        + [(p, pl.ANY) for p in shards],
        [
            pltpu.VMEM((8, width), jnp.float32),
            pltpu.VMEM((4, 2, m, width), jnp.bfloat16),
            pltpu.VMEM((m, width), jnp.float32),
            pltpu.VMEM((m, width), jnp.float32),
            pltpu.VMEM((m, width), jnp.bfloat16),
        ]
        + scatter_scratch(m, width)
        + [
            copies(SCATTER_COPIES),
            copies(2),
            pltpu.SemaphoreType.DMA((2,)),
            copies(2 * (plane - 1)),
            pltpu.SemaphoreType.DMA((2,)),
        ],
        moved=x.size * 120,
    )


def plane_local(
    tokens,
    doc_starts,
    attn_gain,
    mlp_gain,
    query_weight,
    key_weight,
    value_weight,
    output_weight,
    gate_weight,
    up_weight,
    down_weight,
    cotangent,
):
    plane, span, cores = (lax.axis_size("dp"), lax.axis_size("seq"), lax.axis_size("tensor"))
    rows, length, width = tokens.shape
    chunk = width // (plane * span)
    own = rows * length // cores
    heads = query_weight.shape[1] // FDIM // plane
    hidden_part = gate_weight.shape[1] // plane
    vcols, qcols = heads * VHEAD, heads * FDIM

    def over_seq(pack):
        return lax.all_gather(pack, "seq", axis=0, tiled=False)

    def summed(grads):
        return lax.psum_scatter(
            grads.astype(jnp.bfloat16), "seq", scatter_dimension=1, tiled=True
        )

    def split(w):
        return w.reshape(plane, -1, chunk)

    small = jnp.concatenate(
        [
            attn_gain.astype(jnp.float32)[None],
            mlp_gain.astype(jnp.float32)[None],
            doc_starts.astype(jnp.float32).reshape(-1, chunk),
            jnp.zeros((2, chunk), jnp.float32),
        ]
    )
    gate_w = split(gate_weight.T)
    pack = jnp.concatenate(
        [
            split(value_weight.T),
            split(query_weight.T),
            split(key_weight.T),
            split(output_weight),
            gate_w[:, :EARLY],
        ],
        axis=1,
    )
    [pack] = exchange([pack], 1, [(pack.shape[1], plane * chunk)], put=columns_of)
    small, pack = lax.optimization_barrier((small, pack))
    small, down_w = small_exchange(small, split(down_weight), 2)
    pack = over_seq(pack)
    late_w = jnp.concatenate([gate_w[:, EARLY:], split(up_weight.T)], axis=1)
    qkv_rows = vcols + 2 * qcols
    pairs = feature_pairs()
    normed_one, x, cot_own, seg_col, seg_row = entry(
        tokens.reshape(cores, own, width), cotangent.reshape(cores, own, width), small, length, 3
    )
    into, out_of = Rows(pack, 0, vcols + LANES), Rows(pack, qkv_rows, vcols)
    qkv, state, sums, late_w = states(
        normed_one,
        into,
        seg_col,
        seg_row,
        pairs,
        [late_w],
        heads,
        4,
    )
    late_w, down_w = lax.optimization_barrier((late_w, down_w))
    late_w, down_w = over_seq(late_w), over_seq(down_w)
    mixed, exact, den, cot = mix(
        qkv, seg_col, seg_row, pairs, state, sums, cot_own, heads, 13
    )
    residual, normed_own = branch(mixed, out_of, x, small, 5)
    normed_two, gate, up, hidden = expand(normed_own, pack, late_w, 11)
    down_grad = nn_dot(hidden, cot).astype(jnp.bfloat16)
    gate, down_grad = lax.optimization_barrier((gate, down_grad))
    down_grad = summed(down_grad)
    out_part, dnormed_two, gate_up_grad = hidden_units(
        gate, up, cot, pack, late_w, down_w, normed_two, 6
    )
    gate_up_grad = summed(gate_up_grad)
    dresid, gain_two_grad, dmixed, out_grad = turn(
        dnormed_two, residual, cot_own, small, out_of, mixed, 12
    )
    dmixed, down_grad = lax.optimization_barrier((dmixed, down_grad))
    dqkv, block_own, attn_grad, (down_grad,) = unmix(
        dmixed,
        normed_one,
        out_grad,
        out_part,
        residual,
        (seg_col, seg_row),
        pairs,
        (qkv, exact, den, state, sums),
        [down_grad],
        heads,
        8,
    )
    attn_grad = summed(attn_grad)
    dtokens, block_out, gains, gate_up_grad = leave(
        dqkv, into, x, dresid, block_own, small, gain_two_grad, [gate_up_grad], 9
    )
    (attn_grad,), gain_grads = last([attn_grad], gains, 10)

    def stacked(a, start, size):
        return a[:, start : start + size].reshape(plane * size, chunk).astype(jnp.float32)

    h = hidden_part
    return (
        block_out.reshape(rows, length, width),
        dtokens.reshape(rows, length, width),
        gain_grads[0],
        gain_grads[1],
        stacked(attn_grad, vcols, qcols).T,
        stacked(attn_grad, vcols + qcols, qcols).T,
        stacked(attn_grad, 0, vcols).T,
        stacked(attn_grad, qkv_rows, vcols),
        stacked(gate_up_grad, 0, h).T,
        stacked(gate_up_grad, h, h).T,
        stacked(down_grad, 0, h),
    )


def fits_plane(mesh, tokens, query_weight, gate_weight):
    plane, span, cores = (mesh.shape[a] for a in ("dp", "seq", "tensor"))
    heads = query_weight.shape[1] // FDIM // cores
    return (
        plane == 4
        and cores == 2
        and heads % plane == 0
        and (gate_weight.shape[1] // cores) % (16 * plane) == 0
        and gate_weight.shape[1] // cores // plane > EARLY
        and tokens.shape[0] % CHUNKS == 0
    )


def solution(mesh):
    def step(*args):
        use = fits_plane(mesh, args[0], args[4], args[8])
        return sharded(mesh, plane_local if use else local)(*args)

    return step


def sharded(mesh, body):
    return jax.shard_map(
        body,
        mesh=mesh,
        in_specs=(
            P("dp", "seq", None),
            P("dp", "seq"),
            P(("dp", "seq")),
            P(("dp", "seq")),
            P(("dp", "seq"), "tensor"),
            P(("dp", "seq"), "tensor"),
            P(("dp", "seq"), "tensor"),
            P("tensor", ("dp", "seq")),
            P(("dp", "seq"), "tensor"),
            P(("dp", "seq"), "tensor"),
            P("tensor", ("dp", "seq")),
            P("dp", "seq", None),
        ),
        out_specs=(
            P("dp", "seq", None),
            P("dp", "seq", None),
            P(("dp", "seq")),
            P(("dp", "seq")),
            P(("dp", "seq"), "tensor"),
            P(("dp", "seq"), "tensor"),
            P(("dp", "seq"), "tensor"),
            P("tensor", ("dp", "seq")),
            P(("dp", "seq"), "tensor"),
            P(("dp", "seq"), "tensor"),
            P("tensor", ("dp", "seq")),
        ),
        check_vma=False,
    )
```

```python
from functools import partial

import jax
import jax.numpy as jnp
import numpy as np
from jax import lax
from jax.experimental import pallas as pl
from jax.experimental.pallas import tpu as pltpu
from jax.sharding import PartitionSpec as P

FDIM = 16
VHEAD = 128
MICRO = 2


norm_epsilon = 1e-05
highest = lax.Precision.HIGHEST
outer_scale = 0.17677669529663687


def prefix(x, axis, combine, identity, reverse):
    size, index = (lax.axis_size(axis), lax.axis_index(axis))
    everything = jax.tree.map(lambda part: lax.all_gather(part, axis), x)
    start = jax.tree.map(
        lambda part, zero: jnp.broadcast_to(jnp.asarray(zero, part.dtype), part.shape), x, identity
    )

    def turn(k, before):
        at = size - 1 - k if reverse else k
        reached = at > index if reverse else at < index
        new = combine(before, jax.tree.map(lambda part: part[at], everything))
        return jax.tree.map(lambda a, b: jnp.where(reached, a, b), new, before)

    return lax.fori_loop(0, size, turn, start)


def features(vectors):
    ones_col = jnp.ones(vectors.shape[:-1] + (1,), jnp.float32)
    outer_terms = vectors[..., :, None] * vectors[..., None, :] * outer_scale
    outer_terms = outer_terms.reshape(vectors.shape[:-1] + (vectors.shape[-1] * vectors.shape[-1],))
    return jnp.concatenate([ones_col, 0.5 * vectors, outer_terms], axis=-1)


def mix_span(queries, key_rows, values, state_in, norm_in, segments):
    length = queries.shape[1]
    scores = jnp.einsum("rthf,rshf->rhts", queries, key_rows, precision=highest) / 4.0
    kernel = 1.0 + scores + 0.5 * scores * scores
    position = jnp.arange(length)
    causal = position[None, :] <= position[:, None]
    allowed = causal[None] & (segments[:, :, None] == segments[:, None, :])
    kernel = jnp.where(allowed[:, None], kernel, 0.0)
    numerator = jnp.einsum("rhts,rshe->rthe", kernel, values, precision=highest)
    denominator = jnp.transpose(jnp.sum(kernel, axis=-1), (0, 2, 1))
    head_part = (segments == 0).astype(jnp.float32)[:, :, None]
    lifted = features(queries)
    numerator = numerator + head_part[..., None] * jnp.einsum(
        "rthf,rhfe->rthe", lifted, state_in, precision=highest
    )
    denominator = denominator + head_part * jnp.einsum(
        "rthf,rhf->rth", lifted, norm_in, precision=highest
    )
    return numerator / denominator[..., None]


def tail_span(key_rows, values, segments):
    tail_mask = (segments == segments[:, -1:]).astype(jnp.float32)
    lifted = features(key_rows) * tail_mask[:, :, None, None]
    tail_state = jnp.einsum("rshf,rshe->rhfe", lifted, values, precision=highest)
    return (tail_state, jnp.sum(lifted, axis=1))


def combine_carry(earlier_part, later_part):
    keep_rate = 1.0 - later_part[2]
    return (
        later_part[0] + keep_rate[:, None, None, None] * earlier_part[0],
        later_part[1] + keep_rate[:, None, None] * earlier_part[1],
        jnp.maximum(earlier_part[2], later_part[2]),
    )


def inverse_rms(inputs):
    return lax.rsqrt(jnp.mean(inputs * inputs, axis=-1, keepdims=True) + norm_epsilon)


def norm_backward(inputs, scale_row, gain_vec, grad_normed):
    scaled_grad = grad_normed * gain_vec
    grad_gain = jnp.sum(grad_normed * inputs * scale_row, axis=0)
    grad_inputs = scale_row * scaled_grad - inputs * scale_row * scale_row * scale_row * jnp.mean(
        scaled_grad * inputs, axis=-1, keepdims=True
    )
    return (grad_inputs, grad_gain)


def inner_rows(left_mat, right_mat):
    return lax.dot_general(
        left_mat, right_mat, (((0,), (0,)), ((), ())), preferred_element_type=jnp.float32
    )


def by_transpose(left_mat, right_mat):
    return lax.dot_general(
        left_mat, right_mat, (((1,), (1,)), ((), ())), preferred_element_type=jnp.float32
    )


def local(
    tokens,
    doc_starts,
    attn_gain,
    mlp_gain,
    query_weight,
    key_weight,
    value_weight,
    output_weight,
    gate_weight,
    up_weight,
    down_weight,
    cotangent,
):
    micro_rows = tokens.shape[0] // MICRO
    span_len = tokens.shape[1]
    model_width = tokens.shape[2]
    head_count = query_weight.shape[1] // FDIM
    outputs_main = []
    outputs_grad = []
    totals = None
    for micro_index in range(MICRO):
        row_start = micro_index * micro_rows
        rows_in = tokens[row_start : row_start + micro_rows]
        starts_in = doc_starts[row_start : row_start + micro_rows]
        cot_in = cotangent[row_start : row_start + micro_rows].reshape(-1, model_width)
        (
            full_query,
            full_key,
            full_value,
            full_gate,
            full_up,
            full_output,
            full_down,
            gain_one,
            gain_two,
        ) = (
            lax.all_gather(query_weight, ("dp", "seq"), axis=0, tiled=True),
            lax.all_gather(key_weight, ("dp", "seq"), axis=0, tiled=True),
            lax.all_gather(value_weight, ("dp", "seq"), axis=0, tiled=True),
            lax.all_gather(gate_weight, ("dp", "seq"), axis=0, tiled=True),
            lax.all_gather(up_weight, ("dp", "seq"), axis=0, tiled=True),
            lax.all_gather(output_weight, ("dp", "seq"), axis=1, tiled=True),
            lax.all_gather(down_weight, ("dp", "seq"), axis=1, tiled=True),
            lax.all_gather(attn_gain, ("dp", "seq"), axis=0, tiled=True),
            lax.all_gather(mlp_gain, ("dp", "seq"), axis=0, tiled=True),
        )
        gain_one_f = gain_one.astype(jnp.float32)
        gain_two_f = gain_two.astype(jnp.float32)
        flat_rows = rows_in.reshape(-1, model_width).astype(jnp.float32)
        scale_one = inverse_rms(flat_rows)
        normed_one = (flat_rows * scale_one * gain_one_f).astype(jnp.bfloat16)
        query_low = jnp.dot(normed_one, full_query, preferred_element_type=jnp.float32).astype(
            jnp.bfloat16
        )
        key_low = jnp.dot(normed_one, full_key, preferred_element_type=jnp.float32).astype(
            jnp.bfloat16
        )
        value_low = jnp.dot(normed_one, full_value, preferred_element_type=jnp.float32).astype(
            jnp.bfloat16
        )
        queries = query_low.astype(jnp.float32).reshape(micro_rows, span_len, head_count, FDIM)
        key_rows = key_low.astype(jnp.float32).reshape(micro_rows, span_len, head_count, FDIM)
        values = value_low.astype(jnp.float32).reshape(micro_rows, span_len, head_count, VHEAD)
        segments = jnp.cumsum(starts_in, axis=1)
        reset_flag = (segments[:, -1] > 0).astype(jnp.float32)
        (tail_state, tail_norm), tail_pull = jax.vjp(
            partial(tail_span, segments=segments), key_rows, values
        )
        state_in, norm_in, reset_in = prefix(
            (tail_state, tail_norm, reset_flag),
            "seq",
            combine_carry,
            (jnp.zeros_like(tail_state), jnp.zeros_like(tail_norm), jnp.zeros_like(reset_flag)),
            False,
        )
        mixed_heads, mix_pull = jax.vjp(
            partial(mix_span, segments=segments), queries, key_rows, values, state_in, norm_in
        )
        mixed_low = mixed_heads.reshape(-1, head_count * VHEAD).astype(jnp.bfloat16)
        branch_one = jnp.dot(mixed_low, full_output, preferred_element_type=jnp.float32)
        residual = flat_rows + lax.psum(branch_one, "tensor")
        scale_two = inverse_rms(residual)
        normed_two = (residual * scale_two * gain_two_f).astype(jnp.bfloat16)
        gate_proj = jnp.dot(normed_two, full_gate, preferred_element_type=jnp.float32)
        up_proj = jnp.dot(normed_two, full_up, preferred_element_type=jnp.float32)
        sigmoid_gate = jax.nn.sigmoid(gate_proj)
        hidden = (gate_proj * sigmoid_gate * up_proj).astype(jnp.bfloat16)
        branch_two = jnp.dot(hidden, full_down, preferred_element_type=jnp.float32)
        block_low = (
            residual + lax.psum(branch_two.astype(jnp.bfloat16), "tensor").astype(jnp.float32)
        ).astype(jnp.bfloat16)
        outputs_main.append(block_low.reshape(micro_rows, span_len, model_width))
        grad_down = inner_rows(hidden, cot_in)
        grad_hidden = by_transpose(cot_in, full_down)
        grad_gate_low = (
            grad_hidden * up_proj * sigmoid_gate * (1.0 + gate_proj * (1.0 - sigmoid_gate))
        ).astype(jnp.bfloat16)
        grad_up_low = (grad_hidden * gate_proj * sigmoid_gate).astype(jnp.bfloat16)
        grad_gate = inner_rows(normed_two, grad_gate_low)
        grad_up = inner_rows(normed_two, grad_up_low)
        grad_normed_two = by_transpose(grad_gate_low, full_gate) + by_transpose(
            grad_up_low, full_up
        )
        grad_normed_two = lax.psum(grad_normed_two, "tensor")
        grad_resid, grad_gain_two = norm_backward(residual, scale_two, gain_two_f, grad_normed_two)
        grad_resid = grad_resid + cot_in.astype(jnp.float32)
        grad_resid_low = grad_resid.astype(jnp.bfloat16)
        grad_output = inner_rows(mixed_low, grad_resid_low)
        grad_mixed = by_transpose(grad_resid_low, full_output).astype(jnp.bfloat16)
        grad_mixed = (
            lax.optimization_barrier(grad_mixed)
            .astype(jnp.float32)
            .reshape(micro_rows, span_len, head_count, VHEAD)
        )
        grad_queries, grad_keys, grad_values, grad_state, grad_norm = mix_pull(grad_mixed)
        carried_state, carried_norm, reset_out = prefix(
            (grad_state, grad_norm, reset_flag),
            "seq",
            combine_carry,
            (jnp.zeros_like(grad_state), jnp.zeros_like(grad_norm), jnp.zeros_like(reset_flag)),
            True,
        )
        more_keys, more_values = tail_pull((carried_state, carried_norm))
        grad_query_low = grad_queries.reshape(-1, head_count * FDIM).astype(jnp.bfloat16)
        grad_key_low = (grad_keys + more_keys).reshape(-1, head_count * FDIM).astype(jnp.bfloat16)
        grad_value_low = (
            (grad_values + more_values).reshape(-1, head_count * VHEAD).astype(jnp.bfloat16)
        )
        grad_query = inner_rows(normed_one, grad_query_low)
        grad_key = inner_rows(normed_one, grad_key_low)
        grad_value = inner_rows(normed_one, grad_value_low)
        grad_normed_one = (
            by_transpose(grad_query_low, full_query)
            + by_transpose(grad_key_low, full_key)
            + by_transpose(grad_value_low, full_value)
        )
        grad_normed_one = lax.psum(grad_normed_one, "tensor")
        grad_inputs, grad_gain_one = norm_backward(
            flat_rows, scale_one, gain_one_f, grad_normed_one
        )
        outputs_grad.append((grad_resid + grad_inputs).reshape(micro_rows, span_len, model_width))
        shares = (
            grad_query,
            grad_key,
            grad_value,
            grad_gate,
            grad_up,
            grad_output,
            grad_down,
            grad_gain_one,
            grad_gain_two,
        )
        if totals is None:
            totals = shares
        else:
            totals = jax.tree.map(jnp.add, totals, shares)
    totals = (
        lax.psum_scatter(totals[0], ("dp", "seq"), scatter_dimension=0, tiled=True),
        lax.psum_scatter(totals[1], ("dp", "seq"), scatter_dimension=0, tiled=True),
        lax.psum_scatter(totals[2], ("dp", "seq"), scatter_dimension=0, tiled=True),
        lax.psum_scatter(totals[3], ("dp", "seq"), scatter_dimension=0, tiled=True),
        lax.psum_scatter(totals[4], ("dp", "seq"), scatter_dimension=0, tiled=True),
        lax.psum_scatter(totals[5], ("dp", "seq"), scatter_dimension=1, tiled=True),
        lax.psum_scatter(totals[6], ("dp", "seq"), scatter_dimension=1, tiled=True),
        lax.psum_scatter(totals[7], ("dp", "seq"), scatter_dimension=0, tiled=True),
        lax.psum_scatter(totals[8], ("dp", "seq"), scatter_dimension=0, tiled=True),
    )
    return (
        jnp.concatenate(outputs_main, axis=0),
        jnp.concatenate(outputs_grad, axis=0),
        totals[7],
        totals[8],
        totals[0],
        totals[1],
        totals[2],
        totals[5],
        totals[3],
        totals[4],
        totals[6],
    )


MESH_ID = pl.DeviceIdType.MESH
VMEM_LIMIT = 58 << 20
LANES = 128
ROW_STEP = 32


def nt_dot(a, b):
    return lax.dot_general(a, b, (((1,), (1,)), ((), ())), preferred_element_type=jnp.float32)


def tn_dot(a, b):
    return lax.dot_general(a, b, (((0,), (0,)), ((), ())), preferred_element_type=jnp.float32)


def nn_dot(a, b):
    return lax.dot_general(a, b, (((1,), (0,)), ((), ())), preferred_element_type=jnp.float32)


def plane_places():
    at, core = lax.axis_index("dp"), lax.axis_index("tensor")
    x_bit, y_bit = lax.rem(at, 2), at // 2
    return (
        at,
        y_bit * 2 + (1 - x_bit),
        (1 - y_bit) * 2 + x_bit,
        (1 - y_bit) * 2 + (1 - x_bit),
        core,
    )


loading = []


def greet(places):
    barrier = pltpu.get_barrier_semaphore()
    for place in places:
        pl.semaphore_signal(barrier, inc=1, device_id=place, device_id_type=MESH_ID)
    pl.semaphore_wait(barrier, len(places))
    while loading:
        loading.pop().wait()


class Sender:
    def __init__(self, sems):
        self.sems, self.used = sems, 0

    def __call__(self, src, dst, place):
        index = self.used
        self.used += 1
        return pltpu.make_async_remote_copy(
            src_ref=src,
            dst_ref=dst,
            send_sem=self.sems.at[0, index],
            recv_sem=self.sems.at[1, index],
            device_id=place,
            device_id_type=MESH_ID,
        )


def greet_plane():
    at, x_at, y_at, _, core = plane_places()
    greet([{"dp": x_at}, {"dp": y_at}, {"tensor": 1 - core}])


def leaving(i):
    at, x_at, y_at, d_at, core = plane_places()
    chip = choose(i < 2, d_at, choose(i < 4, x_at, choose(i < 6, y_at, at)))
    return chip, choose(parity(i) == 0, 1 - core, core)


def produce_parts(block, pairs):
    def body(i, carry):
        block(*leaving(i))
        for j, pair in enumerate(pairs):

            @pl.when(i == 2 * j)
            def _():
                pair.start()

        return carry

    lax.fori_loop(0, 8, body, 0)


def add_rows(dst, *srcs, step=64):
    def body(i, carry):
        r = pl.ds(pl.multiple_of(i * step, step), step)
        total = srcs[0][r].astype(jnp.float32)
        for s in srcs[1:]:
            total = total + s[r].astype(jnp.float32)
        dst[r] = total.astype(dst.dtype)
        return carry

    lax.fori_loop(0, srcs[0].shape[0] // step, body, 0)


GATHER_COPIES = 13
SCATTER_COPIES = 10


def gather_steps(own_ref, out_ref, copy, local_sem):
    at, x_at, y_at, d_at, core = plane_places()
    half = own_ref.shape[0] // 2
    xp, yp, sp = {"dp": x_at}, {"dp": y_at}, {"tensor": 1 - core}
    lo, hi = pl.ds(0, half), pl.ds(half, half)
    mine = out_ref.at[at, core]
    x_lo = copy(own_ref.at[lo], mine.at[lo], xp)
    y_hi = copy(own_ref.at[hi], mine.at[hi], yp)
    x_hi = copy(own_ref.at[hi], mine.at[hi], xp)
    y_lo = copy(own_ref.at[lo], mine.at[lo], yp)
    pair = copy(own_ref, mine, sp)
    for c in (x_lo, y_hi, x_hi, y_lo, pair):
        c.start()
    local_copy = pltpu.make_async_copy(own_ref, mine, local_sem)
    local_copy.start()
    from_x, from_y, from_d = out_ref.at[x_at, core], out_ref.at[y_at, core], out_ref.at[d_at, core]
    on_y = copy(from_x.at[lo], from_x.at[lo], yp)
    on_x = copy(from_y.at[hi], from_y.at[hi], xp)
    handed = [
        copy(block.at[rows], block.at[rows], sp)
        for block, rows in (
            (from_x, lo),
            (from_y, hi),
            (from_x, hi),
            (from_y, lo),
            (from_d, lo),
            (from_d, hi),
        )
    ]
    yield
    local_copy.wait()
    yield
    pair.wait_recv()
    yield
    x_lo.wait_recv()
    on_y.start()
    handed[0].start()
    y_hi.wait_recv()
    on_x.start()
    handed[1].start()
    yield
    handed[0].wait_recv()
    handed[1].wait_recv()
    yield
    x_hi.wait_recv()
    handed[2].start()
    y_lo.wait_recv()
    handed[3].start()
    yield
    handed[2].wait_recv()
    handed[3].wait_recv()
    yield
    on_y.wait_recv()
    handed[4].start()
    on_x.wait_recv()
    handed[5].start()
    yield
    handed[4].wait_recv()
    handed[5].wait_recv()
    yield
    for c in [x_lo, y_hi, x_hi, y_lo, on_y, on_x, pair] + handed:
        c.wait_send()


def scatter_steps(part_ref, out_ref, pair_ref, sum_ref, got_ref, copy, held=None, start=True):
    at, x_at, y_at, d_at, core = plane_places()
    half = part_ref.shape[2] // 2
    xp, yp, sp = {"dp": x_at}, {"dp": y_at}, {"tensor": 1 - core}
    lo, hi = pl.ds(0, half), pl.ds(half, half)
    order = (d_at, x_at, y_at, at)
    pairs = [copy(part_ref.at[to, 1 - core], pair_ref.at[j], sp) for j, to in enumerate(order)]
    own = [part_ref.at[to, core] for to in order]
    fetched = []
    if held is not None:
        buffer, held_sems = held
        fetched = [
            pltpu.make_async_copy(o, buffer.at[j], held_sems.at[j]) for j, o in enumerate(own)
        ]
        own = [buffer.at[j] for j in range(4)]

    def sent(j, rows, place):
        return copy(sum_ref.at[j, rows], got_ref.at[j, rows], place)

    d_lo, d_hi = sent(0, lo, xp), sent(0, hi, yp)
    x_lo, y_hi, x_hi, y_lo = sent(1, lo, xp), sent(2, hi, yp), sent(1, hi, xp), sent(2, lo, yp)
    for c in (pairs if start else []) + fetched:
        c.start()
    yield pairs

    def ready(j):
        if fetched:
            fetched[j].wait()
        pairs[j].wait_recv()

    def total(j, rows, *more):
        add_rows(sum_ref.at[j, rows], own[j].at[rows], pair_ref.at[j, rows], *more)

    ready(0)
    total(0, lo)
    d_lo.start()
    total(0, hi)
    d_hi.start()
    yield
    ready(1)
    total(1, lo)
    x_lo.start()
    yield
    ready(2)
    total(2, hi)
    y_hi.start()
    yield
    d_lo.wait_recv()
    total(2, lo, got_ref.at[0, lo])
    y_lo.start()
    d_hi.wait_recv()
    total(1, hi, got_ref.at[0, hi])
    x_hi.start()
    yield
    ready(3)
    for c in (x_lo, y_hi, y_lo, x_hi):
        c.wait_recv()
    add_rows(out_ref, own[3], pair_ref.at[3], got_ref.at[1], got_ref.at[2])
    for c in pairs + [d_lo, d_hi, x_lo, y_hi, x_hi, y_lo]:
        c.wait_send()


def swap_shards(ins, outs, peers, me, take, put, copy, local_sems):
    started = [
        copy(take(i, p), put(o, me), {"dp": p}) for i, o in zip(ins, outs) for p in peers
    ]
    started += [
        pltpu.make_async_copy(take(i, me), put(o, me), local_sems.at[n])
        for n, (i, o) in enumerate(zip(ins, outs))
    ]
    for c in started:
        c.start()
    return started


def block_of(ref, index):
    return ref.at[index]


def columns_of(ref, index, rows=slice(None)):
    width = ref.shape[1] // lax.axis_size("dp")
    return ref.at[rows, pl.ds(pl.multiple_of(index * width, width), width)]


def weights_kernel(
    value_ref,
    query_ref,
    key_ref,
    output_ref,
    early_ref,
    out_ref,
    pack_ref,
    sems,
    local_sems,
):
    plane, at = lax.axis_size("dp"), lax.axis_index("dp")
    chips = [lax.rem(at + k, plane) for k in range(1, plane)]
    greet([{"dp": p} for p in chips])
    vcols, qcols = value_ref.shape[1] // plane, query_ref.shape[1] // plane
    queries, keys = query_ref[...].T, key_ref[...].T
    for j in range(plane):
        first = 0
        for piece in (
            value_ref[:, j * vcols : (j + 1) * vcols].T,
            queries[j * qcols : (j + 1) * qcols],
            keys[j * qcols : (j + 1) * qcols],
            output_ref[j * vcols : (j + 1) * vcols],
            early_ref[j],
        ):
            pack_ref[j, first : first + piece.shape[0]] = piece
            first += piece.shape[0]
    for c in swap_shards(
        (pack_ref,), (out_ref,), chips, at, block_of, columns_of, Sender(sems), local_sems
    ):
        c.wait()


def weights_exchange(value, query, key, output, early, cid):
    plane, rows, chunk = early.shape
    size = rows + (value.shape[1] + query.shape[1] + key.shape[1] + output.shape[0]) // plane
    whole = pltpu.VMEM
    [pack] = kernel_call(
        weights_kernel,
        "exchange",
        cid,
        [((size, plane * chunk), value.dtype, pl.ANY)],
        [(a, whole) for a in (value, query, key, output, early)],
        [
            pltpu.VMEM((plane, size, chunk), value.dtype),
            copies(plane - 1),
            pltpu.SemaphoreType.DMA((1,)),
        ],
        moved=1 << 24,
    )
    return pack


def small_kernel(
    small_ref, pack_ref, all_ref, out_ref, small_sems, small_local_sem, sems, local_sems
):
    plane, span = lax.axis_size("dp"), lax.axis_size("seq")
    at, z = lax.axis_index("dp"), lax.axis_index("seq")
    places = [
        {"dp": lax.rem(at + i, plane), "seq": lax.rem(z + k, span)}
        for k in range(span)
        for i in range(plane)
        if i or k
    ]
    greet(places)
    copy_small = Sender(small_sems)
    block = all_ref.at[z * plane + at]
    started = [copy_small(small_ref, block, p) for p in places]
    started.append(pltpu.make_async_copy(small_ref, block, small_local_sem))
    for c in started:
        c.start()
    chips = [lax.rem(at + k, plane) for k in range(1, plane)]
    started += swap_shards(
        (pack_ref,), (out_ref,), chips, at, block_of, columns_of, Sender(sems), local_sems
    )
    for c in started:
        c.wait()


def small_exchange(small, pack, cid):
    plane, span = lax.axis_size("dp"), lax.axis_size("seq")
    _, size, chunk = pack.shape
    return kernel_call(
        small_kernel,
        "small_exchange",
        cid,
        [
            ((span * plane,) + small.shape, small.dtype, pltpu.VMEM),
            ((size, plane * chunk), pack.dtype, pl.ANY),
        ],
        [(small, pltpu.VMEM), (pack, pl.ANY)],
        [
            copies(plane * span - 1),
            pltpu.SemaphoreType.DMA,
            copies(plane - 1),
            pltpu.SemaphoreType.DMA((1,)),
        ],
        moved=1 << 24,
    )


def advance(steps, count=1):
    for _ in range(count):
        next(steps)


def run(*steps):
    for g in steps:
        for _ in g:
            pass


def row_blocks(rows, step, body):
    def inner(i, carry):
        return body(pl.ds(pl.multiple_of(i * step, step), step), carry)

    return lambda init: lax.fori_loop(0, rows // step, inner, init)


def lanes(k):
    return pl.ds(k * LANES, LANES)


def seq_major_block(k):
    plane, span = lax.axis_size("dp"), lax.axis_size("seq")
    s, g = divmod(k, plane)
    return g * span + s


def mean_of(acc, width):
    return jnp.sum(acc, axis=1, keepdims=True) * (1.0 / width)


class Rows:
    def __init__(self, pack, first, count):
        self.array, self.rows = pack, pl.ds(first, count)
        self.shape, self.dtype = (pack.shape[0], count, pack.shape[2]), pack.dtype
        self.size = pack.shape[0] * count * pack.shape[2]


def kernel_call(body, name, cid, outs, ins, scratch, flops=0, moved=0):
    big = [n for n, (a, m) in enumerate(ins) if m == pltpu.VMEM and a.size >= 1 << 16]
    count, params = len(ins), dict(has_side_effects=True, vmem_limit_bytes=VMEM_LIMIT)

    def loaded(*refs):
        refs, buffers, sems = list(refs[: -len(big) - 1]), refs[-len(big) - 1 : -1], refs[-1]
        for k, n in enumerate(big):
            source = refs[n]
            if isinstance(ins[n][0], Rows):
                source = source.at[:, ins[n][0].rows]
            loading.append(pltpu.make_async_copy(source, buffers[k], sems.at[k]))
            loading[-1].start()
            refs[n] = buffers[k]
        body(*refs)

    return pl.pallas_call(
        loaded if big else body,
        name=name,
        out_shape=[jax.ShapeDtypeStruct(s, d) for s, d, _ in outs],
        in_specs=[
            pl.BlockSpec(memory_space=pl.ANY if n in big else ins[n][1]) for n in range(count)
        ],
        out_specs=[pl.BlockSpec(memory_space=m) for _, _, m in outs],
        scratch_shapes=list(scratch)
        + [pltpu.VMEM(ins[n][0].shape, ins[n][0].dtype) for n in big]
        + ([pltpu.SemaphoreType.DMA((len(big),))] if big else []),
        compiler_params=pltpu.CompilerParams(collective_id=cid, **params),
        cost_estimate=pl.CostEstimate(flops=flops, bytes_accessed=moved, transcendentals=0),
    )(*[a.array if isinstance(a, Rows) else a for a, _ in ins])


def copies(count):
    return pltpu.SemaphoreType.DMA((2, count))


def entry_kernel(
    tokens_ref,
    cot_ref,
    small_ref,
    all_ref,
    x_ref,
    cot_own_ref,
    column_ref,
    row_ref,
    normed_ref,
    sems,
    local_sem,
):
    greet_plane()
    core = lax.axis_index("tensor")
    m, width = x_ref.shape
    blocks = width // LANES

    def body(r, carry):
        acc = jnp.zeros((ROW_STEP, LANES), jnp.float32)
        for k in range(blocks):
            source = lanes(seq_major_block(k))
            v = tokens_ref[core, r, source]
            x_ref[r, lanes(k)] = v
            cot_own_ref[r, lanes(k)] = cot_ref[core, r, source]
            v = v.astype(jnp.float32)
            acc += v * v
        scale = lax.rsqrt(mean_of(acc, width) + norm_epsilon)
        for k in range(blocks):
            v = x_ref[r, lanes(k)].astype(jnp.float32)
            normed_ref[r, lanes(k)] = (v * scale * small_ref[k, 0:1, :]).astype(jnp.bfloat16)
        return carry

    row_blocks(m, ROW_STEP, body)(0)
    gather = gather_steps(normed_ref, all_ref, Sender(sems), local_sem)
    next(gather)
    plane, z = lax.axis_size("dp"), lax.axis_index("seq")
    rows, _, length = row_ref.shape
    pieces = length // LANES
    starts = []
    for chip in range(plane):
        block = small_ref[z * plane + chip]
        for r in range(rows // plane):
            first = 2 + r * pieces
            starts.append(
                jnp.concatenate([block[first + p : first + p + 1] for p in range(pieces)], axis=1)
            )
    starts = jnp.concatenate(starts).astype(jnp.bfloat16)
    down = lax.broadcasted_iota(jnp.int32, (length, length), 0)
    across = lax.broadcasted_iota(jnp.int32, (length, length), 1)
    counts = nn_dot(starts, jnp.where(down <= across, 1.0, 0.0).astype(jnp.bfloat16))
    turned = nt_dot(jnp.where(across <= down, 1.0, 0.0).astype(jnp.bfloat16), starts)
    for b in range(rows):
        row_ref[b] = counts[b : b + 1]
        column_ref[b] = turned[:, b : b + 1]
    run(gather)


def entry(tokens, cot, small, length, cid):
    cores, m, width = tokens.shape
    rows = 4 * cores * m // length
    whole = pltpu.VMEM
    gathered, x, cot_own, seg_col, seg_row = kernel_call(
        entry_kernel,
        "entry",
        cid,
        [
            ((4, cores, m, width), jnp.bfloat16, pl.ANY),
            ((m, width), jnp.bfloat16, whole),
            ((m, width), jnp.bfloat16, whole),
            ((rows, length, 1), jnp.float32, whole),
            ((rows, 1, length), jnp.float32, whole),
        ],
        [(tokens, whole), (cot, whole), (small, whole)],
        [pltpu.VMEM((m, width), jnp.bfloat16), copies(GATHER_COPIES), pltpu.SemaphoreType.DMA],
        moved=tokens.size * 40,
    )
    return gathered.reshape(-1, width), x, cot_own, seg_col, seg_row


FEATURES = 256
STATE_ROWS = 160
PIECES = 1
CHUNKS = 8
EARLY = 192


def feature_pairs():
    first = np.full(FEATURES, -4096, np.int32)
    second = np.full(FEATURES, -4096, np.int32)
    pairs = [(i, j) for i in range(FDIM + 1) for j in range(i, FDIM + 1)]
    for f, (i, j) in enumerate(pairs):
        first[f], second[f] = i, j
    return jnp.asarray(np.stack([first, second] + [first] * 6))


def feature_scale(pairs_ref):
    i, j = pairs_ref[0:1, :], pairs_ref[1:2, :]
    square = jnp.where(i == j, 1.0 / 32.0, 1.0 / 16.0)
    return jnp.where(j == FDIM, jnp.where(i == FDIM, 1.0, 0.25), square)


def fill_selectors(pairs_ref, pick_ref, qcols):
    kinds, heads = pick_ref.shape[:2]
    lane = lax.broadcasted_iota(jnp.int32, (LANES, FEATURES), 0)
    for kind in range(kinds):
        for h in range(heads):
            for side in range(2):
                index = pairs_ref[side : side + 1, :]
                source = jnp.where(
                    index == FDIM, 2 * qcols, index + (kind * qcols + h * FDIM)
                )
                pick_ref[kind, h, side] = jnp.where(lane == source, 1.0, 0.0).astype(jnp.bfloat16)


def factors(tile, pick_ref, kind, h):
    return nn_dot(tile, pick_ref[kind, h, 0]), nn_dot(tile, pick_ref[kind, h, 1])


def keys_in_place(tile, qcols):
    return pltpu.roll(tile.astype(jnp.float32), LANES - qcols, axis=1).astype(jnp.bfloat16)


def head_mask(rows, head):
    lane = lax.broadcasted_iota(jnp.int32, (rows, LANES), 1)
    return (lane >= head * FDIM) & (lane < (head + 1) * FDIM)


def masked_weights(query, key, column, row):
    length = query.shape[0]
    a = nt_dot(query, key) * 0.25
    t = lax.broadcasted_iota(jnp.int32, (length, length), 0)
    s = lax.broadcasted_iota(jnp.int32, (length, length), 1)
    keep = (s <= t) & (column == row)
    return a, jnp.where(keep, 1.0 + a + 0.5 * a * a, 0.0), keep


class Segments:
    def __init__(self, col_ref, row_ref, b):
        self.column, self.row = col_ref[b], row_ref[b]
        last = self.row[:, -1:]
        self.head = self.column == 0.0
        self.tail = self.column == last
        self.keep = jnp.where(last == 0.0, 1.0, 0.0)


class Chain:
    def __init__(self, forward, col_ref, row_ref, state_ref, sums_ref, scratch, copy_sems):
        span, z = lax.axis_size("seq"), lax.axis_index("seq")
        self.span = span
        self.to = {"seq": lax.rem(z + (1 if forward else span - 1), span)}
        self.distance = z if forward else span - 1 - z
        self.gets, self.gives = self.distance > 0, self.distance < span - 1
        self.segments = (col_ref, row_ref)
        self.state_ref, self.sums_ref = state_ref, sums_ref
        self.own_ref, self.own_sums_ref, self.out_ref, self.out_sums_ref = scratch
        self.sems = copy_sems
        self.rows = state_ref.shape[0] // CHUNKS

    def pieces(self, g):
        some = STATE_ROWS // PIECES
        return [
            (g * self.rows + i, h, k * some)
            for i in range(self.rows)
            for h in range(self.state_ref.shape[1])
            for k in range(PIECES)
        ]

    def move(self, g, n, source, target):
        count = self.rows * self.state_ref.shape[1] * PIECES + 1
        return pltpu.make_async_remote_copy(
            src_ref=source,
            dst_ref=target,
            send_sem=self.sems.at[0, count * g + n],
            recv_sem=self.sems.at[1, count * g + n],
            device_id=self.to,
            device_id_type=MESH_ID,
        )

    def moves(self, g):
        part = pl.ds(g * self.rows, self.rows)
        found = [self.move(g, 0, self.out_sums_ref.at[part], self.sums_ref.at[part])]
        for n, (b, h, first) in enumerate(self.pieces(g)):
            used = pl.ds(first, STATE_ROWS // PIECES)
            found.append(
                self.move(g, n + 1, self.out_ref.at[b, h, used], self.state_ref.at[b, h, used])
            )
        return found

    def step(self, n):
        g = n - self.distance

        @pl.when((g >= 0) & (g < CHUNKS))
        def _():
            moves = self.moves(g)

            def take(move):
                @pl.when(self.gets)
                def _():
                    move.wait_recv()

            def give(move):
                @pl.when(self.gives)
                def _():
                    move.start()

            for (b, h, first), move in zip(self.pieces(g), moves[1:]):
                take(move)
                used = pl.ds(first, STATE_ROWS // PIECES)
                keep = Segments(*self.segments, b).keep
                before = self.state_ref[b, h, used].astype(jnp.float32)
                self.out_ref[b, h, used] = (self.own_ref[b, h, used] + keep * before).astype(
                    jnp.bfloat16
                )
                give(move)
            take(moves[0])
            for i in range(self.rows):
                b = g * self.rows + i
                keep = Segments(*self.segments, b).keep
                self.out_sums_ref[b] = self.own_sums_ref[b] + keep * self.sums_ref[b]
            give(moves[0])

    def run(self, work, between=()):
        def body(n, carry):
            for at, piece in enumerate(between):
                if piece is None:
                    continue

                @pl.when(n == at)
                def _():
                    piece()

            work(n, self.step)
            return carry

        lax.fori_loop(0, CHUNKS + self.span - 1, body, 0)

    def close(self):
        @pl.when(self.gives)
        def _():
            for g in range(CHUNKS):
                for c in self.moves(g):
                    c.wait_send()


def states_kernel(
    heads,
    normed_ref,
    pack_ref,
    col_ref,
    row_ref,
    pairs_ref,
    late_ref,
    qkv_ref,
    state_ref,
    sums_ref,
    late_all_ref,
    pick_ref,
    own_ref,
    own_sums_ref,
    out_ref,
    out_sums_ref,
    sems,
    shard_sems,
    shard_local_sems,
):
    parts, _, depth = pack_ref.shape
    rows, length = col_ref.shape[0], col_ref.shape[1]
    vcols, qcols = heads * VHEAD, heads * FDIM
    plane, span = lax.axis_size("dp"), lax.axis_size("seq")
    at, z = lax.axis_index("dp"), lax.axis_index("seq")
    chips = [lax.rem(at + k, plane) for k in range(1, plane)]
    state_ref[...] = jnp.zeros_like(state_ref)
    sums_ref[...] = jnp.zeros_like(sums_ref)
    greet(
        [{"dp": p} for p in chips] + [{"seq": lax.rem(z + k, span)} for k in (1, span - 1)]
    )
    shards = swap_shards(
        (late_ref,),
        (late_all_ref,),
        chips,
        at,
        block_of,
        columns_of,
        Sender(shard_sems),
        shard_local_sems,
    )
    chain = Chain(
        True,
        col_ref,
        row_ref,
        state_ref,
        sums_ref,
        (own_ref, own_sums_ref, out_ref, out_sums_ref),
        sems,
    )
    fill_selectors(pairs_ref, pick_ref, qcols)
    scale = feature_scale(pairs_ref)

    def tokens_of(b):
        return pl.ds(pl.multiple_of(b * length, length), length)

    def first(b, carry):
        t = tokens_of(b)
        value = jnp.zeros((length, vcols), jnp.float32)
        tile = jnp.zeros((length, LANES), jnp.float32)
        for s in range(parts):
            piece = normed_ref[t, pl.ds(s * depth, depth)]
            value += nt_dot(piece, pack_ref[s, pl.ds(0, vcols)])
            tile += nt_dot(piece, pack_ref[s, pl.ds(vcols, LANES)])
        lane = lax.broadcasted_iota(jnp.int32, (length, LANES), 1)
        tile = jnp.where(lane < 2 * qcols, tile, jnp.where(lane == 2 * qcols, 1.0, 0.0))
        value, tile = value.astype(jnp.bfloat16), tile.astype(jnp.bfloat16)
        qkv_ref[t, pl.ds(0, vcols)] = value
        qkv_ref[t, pl.ds(vcols, LANES)] = tile
        tail = Segments(col_ref, row_ref, b).tail
        for h in range(heads):
            one, two = factors(tile, pick_ref, 1, h)
            lifted = jnp.where(tail, one * two * scale, 0.0)
            own_ref[b, h] = tn_dot(
                lifted.astype(jnp.bfloat16), value[:, h * VHEAD : (h + 1) * VHEAD]
            )
            own_sums_ref[b, h : h + 1] = jnp.sum(lifted, axis=0, keepdims=True)
        return carry

    own_sums_ref[...] = jnp.zeros_like(own_sums_ref)
    each = rows // CHUNKS

    def work(n, step):
        @pl.when(n < CHUNKS)
        def _():
            lax.fori_loop(n * each, (n + 1) * each, first, 0)

        step(n)

    chain.run(work)
    for c in shards:
        c.wait()
    chain.close()


def mix_kernel(
    heads,
    qkv_ref,
    col_ref,
    row_ref,
    pairs_ref,
    state_ref,
    sums_ref,
    cot_ref,
    mixed_ref,
    exact_ref,
    den_ref,
    cot_all_ref,
    pick_ref,
    cot_sems,
    local_sem,
):
    rows, length = col_ref.shape[0], col_ref.shape[1]
    vcols, qcols = heads * VHEAD, heads * FDIM
    greet_plane()
    gather = gather_steps(cot_ref, cot_all_ref, Sender(cot_sems), local_sem)
    next(gather)
    fill_selectors(pairs_ref, pick_ref, qcols)

    def tokens_of(b):
        return pl.ds(pl.multiple_of(b * length, length), length)

    lane = lax.broadcasted_iota(jnp.int32, (length, LANES), 1)

    def here(b, carry):
        t = tokens_of(b)
        seg = Segments(col_ref, row_ref, b)
        tile = qkv_ref[t, pl.ds(vcols, LANES)]
        key = keys_in_place(tile, qcols)
        dens = jnp.zeros((length, LANES), jnp.float32)
        for h in range(heads):
            v = pl.ds(h * VHEAD, VHEAD)
            query = jnp.where(head_mask(length, h), tile, jnp.zeros_like(tile))
            _, w, _ = masked_weights(query, key, seg.column, seg.row)
            exact_ref[t, v] = nn_dot(w.astype(jnp.bfloat16), qkv_ref[t, v])
            dens = jnp.where(lane == h, jnp.sum(w, axis=1, keepdims=True), dens)
        den_ref[t] = dens
        return carry

    def before(b, carry):
        t = tokens_of(b)
        head = Segments(col_ref, row_ref, b).head
        tile = qkv_ref[t, pl.ds(vcols, LANES)]
        dens = den_ref[t]
        for h in range(heads):
            v = pl.ds(h * VHEAD, VHEAD)
            one, two = factors(tile, pick_ref, 0, h)
            lifted = jnp.where(head, one * two, 0.0)
            num = exact_ref[t, v] + nn_dot(lifted.astype(jnp.bfloat16), state_ref[b, h])
            den = dens[:, h : h + 1]
            den += jnp.sum(lifted * sums_ref[b, h : h + 1], axis=1, keepdims=True)
            value = num / den
            exact_ref[t, v] = value
            mixed_ref[t, v] = value.astype(jnp.bfloat16)
            dens = jnp.where(lane == h, den, dens)
        den_ref[t] = dens
        return carry

    def row(b, carry):
        for at in range(1, 6):

            @pl.when(b == at)
            def _():
                next(gather)

        here(b, 0)
        before(b, 0)
        return carry

    lax.fori_loop(0, rows, row, 0)
    run(gather)


def state_scratch(rows, heads):
    return [
        pltpu.VMEM((2, heads, 2, LANES, FEATURES), jnp.bfloat16),
        pltpu.VMEM((rows, heads, FEATURES, VHEAD), jnp.float32),
        pltpu.VMEM((rows, 8, FEATURES), jnp.float32),
        pltpu.VMEM((rows, heads, FEATURES, VHEAD), jnp.bfloat16),
        pltpu.VMEM((rows, 8, FEATURES), jnp.float32),
    ]


def states(normed, pack, seg_col, seg_row, pairs, shards, heads, cid):
    tokens = normed.shape[0]
    rows = seg_col.shape[0]
    vcols = heads * VHEAD
    plane = lax.axis_size("dp")
    whole = pltpu.VMEM
    return kernel_call(
        partial(states_kernel, heads),
        "states",
        cid,
        [
            ((tokens, vcols + LANES), jnp.bfloat16, whole),
            ((rows, heads, FEATURES, VHEAD), jnp.bfloat16, whole),
            ((rows, 8, FEATURES), jnp.float32, whole),
        ]
        + [((p.shape[1], plane * p.shape[2]), p.dtype, pl.ANY) for p in shards],
        [(a, whole) for a in (normed, pack, seg_col, seg_row, pairs)]
        + [(p, pl.ANY) for p in shards],
        state_scratch(rows, heads)
        + [
            copies(rows * heads * PIECES + CHUNKS),
            copies(len(shards) * (plane - 1)),
            pltpu.SemaphoreType.DMA((len(shards),)),
        ],
        moved=normed.size * 20,
    )


def mix(qkv, seg_col, seg_row, pairs, state, sums, cot_own, heads, cid):
    tokens = qkv.shape[0]
    vcols = heads * VHEAD
    m, width = cot_own.shape
    whole = pltpu.VMEM
    mixed, exact, den, cot = kernel_call(
        partial(mix_kernel, heads),
        "mix",
        cid,
        [
            ((tokens, vcols), jnp.bfloat16, whole),
            ((tokens, vcols), jnp.float32, whole),
            ((tokens, LANES), jnp.float32, whole),
            ((4, 2, m, width), jnp.bfloat16, pl.ANY),
        ],
        [(a, whole) for a in (qkv, seg_col, seg_row, pairs, state, sums, cot_own)],
        [
            pltpu.VMEM((2, heads, 2, LANES, FEATURES), jnp.bfloat16),
            copies(GATHER_COPIES),
            pltpu.SemaphoreType.DMA,
        ],
        moved=cot_own.size * 80,
    )
    return mixed, exact, den, cot.reshape(-1, width)


def branch_kernel(
    mixed_ref,
    pack_ref,
    x_ref,
    small_ref,
    residual_ref,
    normed_ref,
    part_ref,
    pair_ref,
    sum_ref,
    got_ref,
    sems,
):
    greet_plane()
    parts, _, depth = pack_ref.shape
    m, width = x_ref.shape
    vcols = mixed_ref.shape[1]
    first = pack_ref.shape[1] - vcols

    def block(chip, core):
        left = mixed_ref[pl.ds(pl.multiple_of((chip * 2 + core) * m, m), m)]
        for s in range(parts):
            part_ref[chip, core, :, pl.ds(s * depth, depth)] = nn_dot(
                left, pack_ref[s, pl.ds(first, vcols)]
            ).astype(jnp.bfloat16)

    scatter = scatter_steps(
        part_ref, residual_ref, pair_ref, sum_ref, got_ref, Sender(sems), start=False
    )
    produce_parts(block, next(scatter))
    run(scatter)

    def body(r, carry):
        acc = jnp.zeros((ROW_STEP, LANES), jnp.float32)
        for k in range(width // LANES):
            v = residual_ref[r, lanes(k)] + x_ref[r, lanes(k)].astype(jnp.float32)
            residual_ref[r, lanes(k)] = v
            acc += v * v
        scale = lax.rsqrt(mean_of(acc, width) + norm_epsilon)
        for k in range(width // LANES):
            normed_ref[r, lanes(k)] = (
                residual_ref[r, lanes(k)] * scale * small_ref[k, 1:2, :]
            ).astype(jnp.bfloat16)
        return carry

    row_blocks(m, ROW_STEP, body)(0)


def scatter_scratch(m, width):
    return [
        pltpu.VMEM((4, m, width), jnp.bfloat16),
        pltpu.VMEM((3, m, width), jnp.bfloat16),
        pltpu.VMEM((3, m, width), jnp.bfloat16),
    ]


def branch(mixed, pack, x, small, cid):
    m, width = x.shape
    whole = pltpu.VMEM
    return kernel_call(
        branch_kernel,
        "branch",
        cid,
        [((m, width), jnp.float32, whole), ((m, width), jnp.bfloat16, whole)],
        [(mixed, whole), (pack, whole), (x, whole), (small, whole)],
        [pltpu.VMEM((4, 2, m, width), jnp.bfloat16)]
        + scatter_scratch(m, width)
        + [copies(SCATTER_COPIES)],
        moved=x.size * 80,
    )


def parity(i):
    return i % 2 if isinstance(i, int) else lax.rem(i, 2)


def choose(test, a, b):
    if isinstance(test, bool):
        return a if test else b
    return jnp.where(test, a, b)


def project(at, w_ref, rows):
    parts, _, depth = w_ref.shape
    total = nt_dot(at(pl.ds(0, depth)), w_ref[0, rows])
    for s in range(1, parts):
        total += nt_dot(at(pl.ds(s * depth, depth)), w_ref[s, rows])
    return total


def arrivals(i, half):
    at, x_at, y_at, d_at, core = plane_places()
    k = choose(parity(i) == 0, core, 1 - core)
    one = choose(i < 2, at, choose(i < 6, x_at, d_at))
    two = choose(i < 2, at, choose(i < 6, y_at, d_at))
    late = (i >= 4) & (i < 6)
    late = int(late) if isinstance(late, bool) else late.astype(jnp.int32)
    first, second = late * half, (1 - late) * half
    if not isinstance(i, int):
        first, second = pl.multiple_of(first, half), pl.multiple_of(second, half)
    return (one, k, first), (two, k, second)


def stacked_copies(early, late, out, sems):
    rows = pl.ds(early.shape[1] - EARLY, EARLY)
    return [
        pltpu.make_async_copy(early.at[:, rows], out.at[:, pl.ds(0, EARLY)], sems.at[0]),
        pltpu.make_async_copy(late, out.at[:, pl.ds(EARLY, late.shape[1])], sems.at[1]),
    ]


def expand_kernel(
    own_ref,
    early_hbm,
    late_hbm,
    normed_hbm,
    gate_hbm,
    up_hbm,
    hidden_hbm,
    normed_ref,
    w_ref,
    gate_ref,
    up_ref,
    hidden_ref,
    sems,
    local_sem,
    w_sems,
    store_sems,
    keep_sem,
):
    greet_plane()
    half = own_ref.shape[0] // 2
    units = gate_ref.shape[2]
    gather = gather_steps(own_ref, normed_ref, Sender(sems), local_sem)
    next(gather)
    weights = stacked_copies(early_hbm, late_hbm, w_ref, w_sems)
    for c in weights:
        c.start()

    def store_copies(i):
        slot = parity(i)
        found = []
        for n, (c, k, r) in enumerate(arrivals(i, half)):
            rows = pl.ds(n * half, half)
            column = (c * 2 + k) * (2 * half) + r
            pairs = (
                (gate_ref.at[slot, rows], gate_hbm.at[c, k, pl.ds(r, half)]),
                (up_ref.at[slot, rows], up_hbm.at[c, k, pl.ds(r, half)]),
                (
                    hidden_ref.at[slot, :, rows],
                    hidden_hbm.at[:, pl.ds(pl.multiple_of(column, half), half)],
                ),
            )
            for q, (a, b) in enumerate(pairs):
                found.append(pltpu.make_async_copy(a, b, store_sems.at[slot, 3 * n + q]))
        return found

    next(gather)
    for c in weights:
        c.wait()

    def body(i, carry):
        for step in range(1, 8):

            @pl.when(i == step)
            def _():
                next(gather)

        @pl.when(i >= 2)
        def _():
            for c in store_copies(i - 2):
                c.wait()

        slot = parity(i)
        pieces = arrivals(i, half)

        def columns(cols):
            return jnp.concatenate([normed_ref[c, k, pl.ds(r, half), cols] for c, k, r in pieces])

        gate = project(columns, w_ref, pl.ds(0, units))
        up = project(columns, w_ref, pl.ds(units, units))
        gate_ref[slot], up_ref[slot] = gate, up
        hidden_ref[slot] = (gate * jax.nn.sigmoid(gate) * up).astype(jnp.bfloat16).T
        for c in store_copies(i):
            c.start()
        return carry

    lax.fori_loop(0, 8, body, 0)
    keep = pltpu.make_async_copy(normed_ref, normed_hbm, keep_sem)
    keep.start()
    for i in (6, 7):
        for c in store_copies(i):
            c.wait()
    keep.wait()
    run(gather)


def expand(own, early, late, cid):
    m, width = own.shape
    weights = (early.shape[0], EARLY + late.shape[1], early.shape[2])
    units = weights[1] // 2
    low = jnp.bfloat16
    thin = ((4, 2, m, units), jnp.float32, pl.ANY)
    normed, gate, up, hidden = kernel_call(
        expand_kernel,
        "expand",
        cid,
        [((4, 2, m, width), low, pl.ANY), thin, thin, ((units, 8 * m), low, pl.ANY)],
        [(own, pltpu.VMEM), (early, pl.ANY), (late, pl.ANY)],
        [
            pltpu.VMEM((4, 2, m, width), low),
            pltpu.VMEM(weights, low),
            pltpu.VMEM((2, m, units), jnp.float32),
            pltpu.VMEM((2, m, units), jnp.float32),
            pltpu.VMEM((2, units, m), low),
            copies(GATHER_COPIES),
            pltpu.SemaphoreType.DMA,
            pltpu.SemaphoreType.DMA((2,)),
            pltpu.SemaphoreType.DMA((2, 6)),
            pltpu.SemaphoreType.DMA,
        ],
        flops=32 * m * width * units,
        moved=1 << 27,
    )
    return normed.reshape(8 * m, width), gate, up, hidden


def hidden_kernel(
    gate_hbm,
    up_hbm,
    cot_hbm,
    early_hbm,
    late_hbm,
    down_hbm,
    normed_hbm,
    out_hbm,
    total_ref,
    grads_hbm,
    gate_ref,
    up_ref,
    cot_ref,
    out_ref,
    w_ref,
    down_w_ref,
    part_ref,
    pair_ref,
    sum_ref,
    got_ref,
    turned_ref,
    normed_ref,
    grad_ref,
    sems,
    w_sems,
    load_sems,
    store_sems,
    normed_sem,
    grad_sems,
):
    greet_plane()
    at, x_at, y_at, d_at, core = plane_places()
    parts, units, depth = down_w_ref.shape
    m = cot_ref.shape[1]
    scatter = scatter_steps(
        part_ref, total_ref, pair_ref, sum_ref, got_ref, Sender(sems), start=False
    )
    pairs = next(scatter)
    weights = stacked_copies(early_hbm, late_hbm, w_ref, w_sems)
    weights.append(pltpu.make_async_copy(down_hbm, down_w_ref, w_sems.at[2]))
    normed_copy = pltpu.make_async_copy(normed_hbm, normed_ref, normed_sem)

    def loads(i):
        slot, (c, k) = parity(i), leaving(i)
        return [
            pltpu.make_async_copy(a.at[c, k], b.at[slot], load_sems.at[slot, n])
            for n, (a, b) in enumerate(
                ((gate_hbm, gate_ref), (up_hbm, up_ref), (cot_hbm, cot_ref))
            )
        ]

    def store(i):
        slot, (c, k) = parity(i), leaving(i)
        return pltpu.make_async_copy(out_ref.at[slot], out_hbm.at[c, k], store_sems.at[slot])

    for c in weights + loads(0):
        c.start()
    normed_copy.start()
    for c in weights:
        c.wait()

    def body(i, carry):
        for step in (2, 4, 6):

            @pl.when(i == step)
            def _():
                next(scatter)

        @pl.when(i < 7)
        def _():
            for c in loads(i + 1):
                c.start()

        for c in loads(i):
            c.wait()

        @pl.when(i >= 2)
        def _():
            store(i - 2).wait()

        slot, (chip, k) = parity(i), leaving(i)
        gate, up = gate_ref[slot], up_ref[slot]
        dhidden = project(lambda cols: cot_ref[slot, :, cols], down_w_ref, pl.ds(0, units))
        sig = jax.nn.sigmoid(gate)
        silu = gate * sig
        hidden = (silu * up).astype(jnp.bfloat16)
        dgate = (dhidden * up * sig * (1.0 + gate * (1.0 - sig))).astype(jnp.bfloat16)
        dup = (dhidden * silu).astype(jnp.bfloat16)
        for s in range(parts):
            cols = pl.ds(s * depth, depth)
            part_ref[chip, k, :, cols] = (
                nn_dot(dgate, w_ref[s, pl.ds(0, units)])
                + nn_dot(dup, w_ref[s, pl.ds(units, units)])
            ).astype(jnp.bfloat16)
            out_ref[slot, :, cols] = nn_dot(hidden, down_w_ref[s]).astype(jnp.bfloat16)
        store(i).start()
        for j in range(4):

            @pl.when(i == 2 * j)
            def _():
                pairs[j].start()

        column = pl.ds(pl.multiple_of((chip * 2 + k) * m, m), m)
        turned_ref[0, :, column], turned_ref[1, :, column] = dgate.T, dup.T
        return carry

    lax.fori_loop(0, 8, body, 0)
    next(scatter)
    store(6).wait()
    store(7).wait()
    normed_copy.wait()
    width = grad_ref.shape[2]
    blocks = normed_ref.shape[1] // width

    def gradients(which):
        rows = pl.ds(which * units, units)

        def stored(i):
            column = pl.ds(pl.multiple_of(i * width, width), width)
            slot = parity(i)
            return pltpu.make_async_copy(
                grad_ref.at[slot], grads_hbm.at[rows, column], grad_sems.at[slot]
            )

        def body(i, carry):
            column = pl.ds(pl.multiple_of(i * width, width), width)

            @pl.when(i >= 2)
            def _():
                stored(i - 2).wait()

            grad_ref[parity(i)] = nn_dot(turned_ref[which], normed_ref[:, column]).astype(
                jnp.bfloat16
            )
            stored(i).start()
            return carry

        lax.fori_loop(0, blocks, body, 0)
        for i in (blocks - 2, blocks - 1):
            stored(i).wait()

    gradients(0)
    gradients(1)
    run(scatter)


def hidden_units(gate, up, cot, early, late, down_w, normed, cid):
    _, _, m, units = gate.shape
    tokens, width = normed.shape
    low = jnp.bfloat16
    stacked = (early.shape[0], EARLY + late.shape[1], early.shape[2])
    ins = (gate, up, cot.reshape(4, 2, m, width), early, late, down_w, normed)
    return kernel_call(
        hidden_kernel,
        "hidden_units",
        cid,
        [
            ((4, 2, m, width), low, pl.ANY),
            ((m, width), jnp.float32, pltpu.VMEM),
            ((2 * units, width), low, pl.ANY),
        ],
        [(a, pl.ANY) for a in ins],
        [
            pltpu.VMEM((2, m, units), jnp.float32),
            pltpu.VMEM((2, m, units), jnp.float32),
            pltpu.VMEM((2, m, width), low),
            pltpu.VMEM((2, m, width), low),
            pltpu.VMEM(stacked, low),
            pltpu.VMEM(down_w.shape, low),
            pltpu.VMEM((4, 2, m, width), low),
        ]
        + scatter_scratch(m, width)
        + [
            pltpu.VMEM((2, units, tokens), low),
            pltpu.VMEM((tokens, width), low),
            pltpu.VMEM((2, units, 2 * LANES), low),
            copies(SCATTER_COPIES),
            pltpu.SemaphoreType.DMA((3,)),
            pltpu.SemaphoreType.DMA((2, 3)),
            pltpu.SemaphoreType.DMA((2,)),
            pltpu.SemaphoreType.DMA,
            pltpu.SemaphoreType.DMA((2,)),
        ],
        flops=12 * tokens * width * units,
        moved=1 << 27,
    )


def norm_gradient(r, value_at, grad_ref, gain_at, gain_grad, finish, width):
    squares = jnp.zeros((ROW_STEP, LANES), jnp.float32)
    cross = jnp.zeros((ROW_STEP, LANES), jnp.float32)
    for k in range(width // LANES):
        v = value_at(r, k)
        squares += v * v
        cross += v * grad_ref[r, lanes(k)] * gain_at(k)
    scale = lax.rsqrt(mean_of(squares, width) + norm_epsilon)
    pull = mean_of(cross, width) * scale * scale * scale
    for k in range(width // LANES):
        v, g = value_at(r, k), grad_ref[r, lanes(k)]
        gain_grad[:, lanes(k)] += jnp.sum(
            (g * v * scale).reshape(ROW_STEP // 8, 8, LANES), axis=0
        )
        finish(r, k, scale * g * gain_at(k) - v * pull)


def mixer_cotangents(dmixed, exact, den, h):
    v = slice(h * VHEAD, (h + 1) * VHEAD)
    dn = dmixed[:, v].astype(jnp.float32) / den[:, h : h + 1]
    dd = -jnp.sum(dn * exact[:, v], axis=1, keepdims=True)
    return dn.astype(jnp.bfloat16), dd


def turn_kernel(
    heads,
    total_ref,
    residual_ref,
    cot_ref,
    small_ref,
    pack_ref,
    mixed_ref,
    col_ref,
    row_ref,
    pairs_ref,
    qkv_ref,
    exact_ref,
    den_ref,
    dresid_ref,
    gain_ref,
    dmixed_ref,
    grad_ref,
    own_ref,
    own_sums_ref,
    all_ref,
    low_ref,
    sum_ref,
    pick_ref,
    gather_sems,
    local_sem,
):
    greet_plane()
    m, width = residual_ref.shape
    half = m // 2
    parts, _, depth = pack_ref.shape
    vcols = mixed_ref.shape[3]
    first_row = pack_ref.shape[1] - vcols
    gain_ref[...] = jnp.zeros_like(gain_ref)

    def finish(r, k, v):
        v += cot_ref[r, lanes(k)].astype(jnp.float32)
        dresid_ref[r, lanes(k)] = v
        low_ref[r, lanes(k)] = v.astype(jnp.bfloat16)

    def body(r, carry):
        norm_gradient(
            r,
            lambda r, k: residual_ref[r, lanes(k)],
            total_ref,
            lambda k: small_ref[k, 1:2, :],
            gain_ref,
            finish,
            width,
        )
        return carry

    row_blocks(m, ROW_STEP, body)(0)
    gather = gather_steps(low_ref, all_ref, Sender(gather_sems), local_sem)
    next(gather)
    sum_ref[...] = jnp.zeros_like(sum_ref)
    own_sums_ref[...] = jnp.zeros_like(own_sums_ref)
    fill_selectors(pairs_ref, pick_ref, heads * FDIM)
    next(gather)

    def first(chip, k):
        b = chip * 2 + k
        head = Segments(col_ref, row_ref, b).head
        t = pl.ds(pl.multiple_of(b * m, m), m)
        tile = qkv_ref[t, pl.ds(vcols, LANES)]
        for h in range(heads):
            dn, dd = mixer_cotangents(dmixed_ref[chip, k], exact_ref[t], den_ref[t], h)
            one, two = factors(tile, pick_ref, 0, h)
            lifted = jnp.where(head, one * two, 0.0)
            own_ref[b, h] = tn_dot(lifted.astype(jnp.bfloat16), dn)
            own_sums_ref[b, h : h + 1] = jnp.sum(lifted * dd, axis=0, keepdims=True)

    def block(i, carry):
        for step in range(1, 8):

            @pl.when(i == step)
            def _():
                next(gather)

        pieces = arrivals(i, half)

        def columns(cols):
            return jnp.concatenate([all_ref[c, k, pl.ds(r, half), cols] for c, k, r in pieces])

        left = jnp.concatenate([mixed_ref[c, k, pl.ds(r, half)] for c, k, r in pieces])
        dmixed = project(columns, pack_ref, pl.ds(first_row, vcols)).astype(jnp.bfloat16)
        for n, (c, k, r) in enumerate(pieces):
            dmixed_ref[c, k, pl.ds(r, half)] = dmixed[n * half : (n + 1) * half]
        for s in range(parts):
            cols = pl.ds(s * depth, depth)
            sum_ref[:, cols] += tn_dot(left, columns(cols))
        (one, k, _), (two, _, _) = pieces

        def rows_done(n, carry):
            first(jnp.where(n == 0, one, two), k)
            return carry

        both = ((i >= 4) & (i < 6)).astype(jnp.int32)
        whole = ((i < 2) | (i >= 4)).astype(jnp.int32)
        lax.fori_loop(0, whole + both, rows_done, 0)
        return carry

    lax.fori_loop(0, 8, block, 0)
    grad_ref[...] = sum_ref[...].astype(jnp.bfloat16)
    run(gather)


def turn(total, residual, cot_own, small, pack, mixed, segments, pairs, kept, heads, cid):
    m, width = residual.shape
    vcols = mixed.shape[1]
    rows = segments[0].shape[0]
    whole, low = pltpu.VMEM, jnp.bfloat16
    dresid, gain, dmixed, grad, own, own_sums = kernel_call(
        partial(turn_kernel, heads),
        "turn",
        cid,
        [
            ((m, width), jnp.float32, whole),
            ((8, width), jnp.float32, whole),
            ((4, 2, m, vcols), low, whole),
            ((vcols, width), low, whole),
            ((rows, heads, FEATURES, VHEAD), jnp.float32, whole),
            ((rows, 8, FEATURES), jnp.float32, whole),
        ],
        [(a, whole) for a in (total, residual, cot_own, small, pack)]
        + [(mixed.reshape(4, 2, m, vcols), whole)]
        + [(a, whole) for a in (*segments, pairs, *kept)],
        [
            pltpu.VMEM((4, 2, m, width), low),
            pltpu.VMEM((m, width), low),
            pltpu.VMEM((vcols, width), jnp.float32),
            pltpu.VMEM((2, heads, 2, LANES, FEATURES), low),
            copies(GATHER_COPIES),
            pltpu.SemaphoreType.DMA,
        ],
        moved=residual.size * 80,
    )
    return dresid, gain, dmixed.reshape(8 * m, vcols), grad, own, own_sums


def unmix_kernel(
    heads,
    count,
    dmixed_ref,
    normed_hbm,
    output_grad_ref,
    part_ref,
    residual_ref,
    col_ref,
    row_ref,
    pairs_ref,
    qkv_ref,
    exact_ref,
    den_ref,
    state_ref,
    sums_ref,
    own_ref,
    own_sums_ref,
    *refs,
):
    ins, dqkv_ref, block_ref, grad_ref = refs[:count], *refs[count : count + 3]
    outs = refs[count + 3 : 2 * count + 3]
    (
        normed_ref,
        early_ref,
        turned_ref,
        dvalue_ref,
        dtile_ref,
        back_ref,
        back_sums_ref,
        pick_ref,
        out_ref,
        out_sums_ref,
        total_ref,
        held_ref,
        pair_ref,
        sum_ref,
        got_ref,
        sems,
        shard_sems,
        local_sems,
        scatter_sems,
        held_sems,
        normed_sem,
    ) = refs[2 * count + 3 :]
    rows, length = col_ref.shape[0], col_ref.shape[1]
    vcols, qcols = heads * VHEAD, heads * FDIM
    at, x_at, y_at, _, core = plane_places()
    plane, span, z = lax.axis_size("dp"), lax.axis_size("seq"), lax.axis_index("seq")
    chips = [lax.rem(at + k, plane) for k in range(1, plane)]
    normed_copy = pltpu.make_async_copy(normed_hbm, normed_ref, normed_sem)
    normed_copy.start()
    back_ref[...] = jnp.zeros_like(back_ref)
    back_sums_ref[...] = jnp.zeros_like(back_sums_ref)
    greet(
        [{"dp": p} for p in chips]
        + [{"tensor": 1 - core}]
        + [{"seq": lax.rem(z + k, span)} for k in (1, span - 1)]
    )
    scatter = scatter_steps(
        part_ref,
        total_ref,
        pair_ref,
        sum_ref,
        got_ref,
        Sender(scatter_sems),
        (held_ref, held_sems),
    )
    next(scatter)
    chain = Chain(
        False,
        col_ref,
        row_ref,
        back_ref,
        back_sums_ref,
        (own_ref, own_sums_ref, out_ref, out_sums_ref),
        sems,
    )
    fill_selectors(pairs_ref, pick_ref, qcols)
    scale = feature_scale(pairs_ref)

    def tokens_of(b):
        return pl.ds(pl.multiple_of(b * length, length), length)

    def cotangents(t, h):
        return mixer_cotangents(dmixed_ref[t], exact_ref[t], den_ref[t], h)

    shards = swap_shards(ins, outs, chips, at, columns_of, block_of, Sender(shard_sems), local_sems)

    def lowered(dlifted, kind, h, one, two):
        return nt_dot((dlifted * two).astype(jnp.bfloat16), pick_ref[kind, h, 0]) + nt_dot(
            (dlifted * one).astype(jnp.bfloat16), pick_ref[kind, h, 1]
        )

    def here(b, carry):
        t = tokens_of(b)
        seg = Segments(col_ref, row_ref, b)
        tile = qkv_ref[t, pl.ds(vcols, LANES)]
        key = keys_in_place(tile, qcols)
        dtile = jnp.zeros((length, LANES), jnp.float32)
        dkey = jnp.zeros((length, LANES), jnp.float32)
        for h in range(heads):
            inside = head_mask(length, h)
            v = pl.ds(h * VHEAD, VHEAD)
            query = jnp.where(inside, tile, jnp.zeros_like(tile))
            dn, dd = cotangents(t, h)
            a, w, keep = masked_weights(query, key, seg.column, seg.row)
            dw = jnp.where(keep, nt_dot(dn, qkv_ref[t, v]) + dd, 0.0)
            da = (dw * (1.0 + a) * 0.25).astype(jnp.bfloat16)
            dvalue_ref[t, v] = tn_dot(w.astype(jnp.bfloat16), dn)
            dtile += jnp.where(inside, nn_dot(da, key), 0.0)
            dkey += jnp.where(inside, tn_dot(da, query), 0.0)
            one, two = factors(tile, pick_ref, 0, h)
            dlifted = nt_dot(dn, state_ref[b, h]) + dd * sums_ref[b, h : h + 1]
            dtile += lowered(jnp.where(seg.head, dlifted, 0.0), 0, h, one, two)
        dtile_ref[t] = dtile + pltpu.roll(dkey, qcols, axis=1)
        return carry

    def after(b, carry):
        t = tokens_of(b)
        tail = Segments(col_ref, row_ref, b).tail
        tile = qkv_ref[t, pl.ds(vcols, LANES)]
        dtile = dtile_ref[t]
        for h in range(heads):
            v = pl.ds(h * VHEAD, VHEAD)
            one, two = factors(tile, pick_ref, 1, h)
            lifted = jnp.where(tail, one * two * scale, 0.0)
            dlifted = nt_dot(qkv_ref[t, v], back_ref[b, h]) + back_sums_ref[b, h : h + 1]
            dtile += lowered(jnp.where(tail, dlifted * scale, 0.0), 1, h, one, two)
            dvalue = dvalue_ref[t, v] + nn_dot(lifted.astype(jnp.bfloat16), back_ref[b, h])
            dqkv_ref[t, v] = dvalue.astype(jnp.bfloat16)
        lane = lax.broadcasted_iota(jnp.int32, (length, LANES), 1)
        dqkv_ref[t, pl.ds(vcols, LANES)] = jnp.where(lane < 2 * qcols, dtile, 0.0).astype(
            jnp.bfloat16
        )
        turned_ref[:, t] = dqkv_ref[t].T
        return carry

    each = rows // CHUNKS

    def work(n, step):
        step(n)

        @pl.when(n < CHUNKS)
        def _():
            lax.fori_loop(n * each, (n + 1) * each, here, 0)

        done = n - chain.distance

        @pl.when((done >= 0) & (done < CHUNKS))
        def _():
            lax.fori_loop(done * each, (done + 1) * each, after, 0)

    def finish(r, carry):
        block_ref[r] = (residual_ref[r] + total_ref[r]).astype(jnp.bfloat16)
        return carry

    def output():
        run(scatter)
        row_blocks(block_ref.shape[0], ROW_STEP, finish)(0)

    wide = 4 * LANES
    qkv_rows = grad_ref.shape[0] - vcols
    early = (rows - each) * length

    def gradient(t, put):
        def body(i, carry):
            cols = pl.ds(pl.multiple_of(i * wide, wide), wide)
            put(cols, nn_dot(turned_ref[pl.ds(0, qkv_rows), t], normed_ref[t, cols]))
            return carry

        lax.fori_loop(0, normed_ref.shape[1] // wide, body, 0)

    def keep(cols, value):
        early_ref[:, cols] = value

    def close(cols, value):
        grad_ref[pl.ds(0, qkv_rows), cols] = (early_ref[:, cols] + value).astype(jnp.bfloat16)

    def most():
        normed_copy.wait()
        gradient(pl.ds(0, early), keep)

    steps = [None] * (CHUNKS + span - 1)
    steps[2] = lambda: advance(scatter, 3)
    steps[6] = lambda: advance(scatter)
    steps[-2], steps[-1] = output, most
    chain.run(work, steps)
    gradient(pl.ds(early, each * length), close)
    grad_ref[pl.ds(qkv_rows, vcols)] = output_grad_ref[...]
    for c in shards:
        c.wait()
    chain.close()


def unmix(
    dmixed, normed, output_grad, part, residual, segments, pairs, kept, own, shards, heads, cid
):
    seg_col, seg_row = segments
    tokens, vcols = dmixed.shape
    plane, rows = lax.axis_size("dp"), seg_col.shape[0]
    grad_rows = 2 * vcols + 2 * heads * FDIM
    m, width = residual.shape
    count = len(shards)
    whole, low = pltpu.VMEM, jnp.bfloat16
    dqkv, block, grad, *swapped = kernel_call(
        partial(unmix_kernel, heads, count),
        "unmix",
        cid,
        [
            ((tokens, vcols + LANES), low, whole),
            ((m, width), low, whole),
            ((grad_rows, width), low, whole),
        ]
        + [((plane, p.shape[0], p.shape[1] // plane), p.dtype, pl.ANY) for p in shards],
        [
            (dmixed, whole),
            (normed, pl.ANY),
            (output_grad, whole),
            (part, pl.ANY),
            (residual, whole),
            (seg_col, whole),
            (seg_row, whole),
            (pairs, whole),
        ]
        + [(a, whole) for a in (*kept, *own)]
        + [(p, pl.ANY) for p in shards],
        [
            pltpu.VMEM((tokens, width), low),
            pltpu.VMEM((grad_rows - vcols, width), jnp.float32),
            pltpu.VMEM((vcols + LANES, tokens), low),
            pltpu.VMEM((tokens, vcols), jnp.float32),
            pltpu.VMEM((tokens, LANES), jnp.float32),
            pltpu.VMEM((rows, heads, FEATURES, VHEAD), low),
            pltpu.VMEM((rows, 8, FEATURES), jnp.float32),
        ]
        + [
            pltpu.VMEM((2, heads, 2, LANES, FEATURES), low),
            pltpu.VMEM((rows, heads, FEATURES, VHEAD), low),
            pltpu.VMEM((rows, 8, FEATURES), jnp.float32),
        ]
        + [pltpu.VMEM((m, width), jnp.float32), pltpu.VMEM((4, m, width), low)]
        + scatter_scratch(m, width)
        + [
            copies(rows * heads * PIECES + CHUNKS),
            copies(count * (plane - 1)),
            pltpu.SemaphoreType.DMA((count,)),
            copies(SCATTER_COPIES),
            pltpu.SemaphoreType.DMA((4,)),
            pltpu.SemaphoreType.DMA,
        ],
        moved=residual.size * 120,
    )
    return dqkv, block, grad, swapped


def last_kernel(count, *refs):
    ins, gain_ref, outs, sum_ref = (
        refs[:count],
        refs[count],
        refs[count + 1 : 2 * count + 1],
        refs[2 * count + 1],
    )
    got_gain, sems, gain_sems, local_sems = refs[2 * count + 2 :]
    plane, at = lax.axis_size("dp"), lax.axis_index("dp")
    others, me = everyone()
    greet(others)
    copy_gain = Sender(gain_sems)
    gains = [
        copy_gain(gain_ref.at[p["seq"] * plane + p["dp"]], got_gain.at[me], p) for p in others
    ]
    for c in gains:
        c.start()
    chips = [lax.rem(at + k, plane) for k in range(1, plane)]
    shards = swap_shards(ins, outs, chips, at, columns_of, block_of, Sender(sems), local_sems)
    got_gain[me] = gain_ref[lax.axis_index("seq") * plane + at]
    for c in gains:
        c.wait()
    total = got_gain[0]
    for k in range(1, len(others) + 1):
        total += got_gain[k]
    sum_ref[...] = total
    for c in shards:
        c.wait()


def last(shards, gains, cid):
    plane = lax.axis_size("dp")
    count = len(shards)
    devices = lax.axis_size(("dp", "seq", "tensor"))
    *swapped, total = kernel_call(
        partial(last_kernel, count),
        "last",
        cid,
        [((plane, p.shape[0], p.shape[1] // plane), p.dtype, pl.ANY) for p in shards]
        + [(gains.shape[1:], jnp.float32, pltpu.VMEM)],
        [(p, pl.ANY) for p in shards] + [(gains, pltpu.VMEM)],
        [
            pltpu.VMEM((devices,) + gains.shape[1:], jnp.float32),
            copies(count * (plane - 1)),
            copies(devices - 1),
            pltpu.SemaphoreType.DMA((count,)),
        ],
        moved=1 << 26,
    )
    return swapped, total


def everyone():
    plane, span, cores = (lax.axis_size(a) for a in ("dp", "seq", "tensor"))
    at, z, core = (lax.axis_index(a) for a in ("dp", "seq", "tensor"))
    others = [
        {
            "dp": lax.rem(at + i, plane),
            "seq": lax.rem(z + k, span),
            "tensor": lax.rem(core + c, cores),
        }
        for k in range(span)
        for i in range(plane)
        for c in range(cores)
        if i or k or c
    ]
    return others, (at * span + z) * cores + core


def exit_kernel(
    dqkv_ref,
    pack_ref,
    x_ref,
    dresid_ref,
    block_ref,
    small_ref,
    gain_two_ref,
    shards_ref,
    grad_ref,
    out_ref,
    gains_ref,
    shards_all_ref,
    gain_ref,
    part_ref,
    total_ref,
    ordered_ref,
    low_ref,
    pair_ref,
    sum_ref,
    got_ref,
    sems,
    pair_sems,
    local_sems,
    shard_sems,
    shard_local_sems,
):
    plane, at = lax.axis_size("dp"), lax.axis_index("dp")
    core = lax.axis_index("tensor")
    chips = [lax.rem(at + k, plane) for k in range(1, plane)]
    greet([{"dp": p} for p in chips] + [{"tensor": 1 - core}])
    shard_copy = Sender(shard_sems)

    half = shards_ref.shape[0] // 2

    def swap(n):
        rows = pl.ds(n * half, half)
        return swap_shards(
            (shards_ref,),
            (shards_all_ref,),
            chips,
            at,
            lambda ref, p: columns_of(ref, p, rows),
            lambda ref, p: ref.at[p, rows],
            shard_copy,
            shard_local_sems.at[pl.ds(n, 1)],
        )

    shards = swap(0)
    parts, _, depth = pack_ref.shape
    m, width = x_ref.shape
    wide = dqkv_ref.shape[1] - LANES + 2 * FDIM * ((dqkv_ref.shape[1] - LANES) // VHEAD)
    blocks = width // LANES
    copy = Sender(pair_sems)

    def block(chip, core):
        left = dqkv_ref[pl.ds(pl.multiple_of((chip * 2 + core) * m, m), m), pl.ds(0, wide)]
        for s in range(parts):
            part_ref[chip, core, :, pl.ds(s * depth, depth)] = nn_dot(
                left, pack_ref[s, pl.ds(0, wide)]
            ).astype(jnp.bfloat16)

    scatter = scatter_steps(
        part_ref, total_ref, pair_ref, sum_ref, got_ref, Sender(sems), start=False
    )
    produce_parts(block, next(scatter))

    def order(r, carry):
        for k in range(blocks):
            low_ref[r, lanes(seq_major_block(k))] = block_ref[r, lanes(k)]
        return carry

    row_blocks(m, ROW_STEP, order)(0)
    to_pair = [copy(low_ref, out_ref.at[core], {"tensor": 1 - core})]
    local = [pltpu.make_async_copy(low_ref, out_ref.at[core], local_sems.at[0])]
    to_pair[0].start()
    local[0].start()
    advance(scatter, 4)
    shards += swap(1)
    run(scatter)
    gain_ref[...] = jnp.zeros_like(gain_ref)

    def finish(r, k, v):
        ordered_ref[r, lanes(seq_major_block(k))] = v + dresid_ref[r, lanes(k)]

    def body(r, carry):
        norm_gradient(
            r,
            lambda r, k: x_ref[r, lanes(k)].astype(jnp.float32),
            total_ref,
            lambda k: small_ref[k, 0:1, :],
            gain_ref,
            finish,
            width,
        )
        return carry

    row_blocks(m, ROW_STEP, body)(0)
    to_pair.append(copy(ordered_ref, grad_ref.at[core], {"tensor": 1 - core}))
    local.append(pltpu.make_async_copy(ordered_ref, grad_ref.at[core], local_sems.at[1]))
    to_pair[1].start()
    local[1].start()
    gains_ref[...] = jnp.zeros_like(gains_ref)
    for k in range(blocks):
        for row, ref in enumerate((gain_ref, gain_two_ref)):
            gains_ref[k, row : row + 1] = jnp.sum(ref[:, lanes(k)], axis=0, keepdims=True)
    for c in to_pair + local + shards:
        c.wait()


def leave(dqkv, pack, x, dresid, block, small, gain_two, shards, cid):
    m, width = x.shape
    plane = lax.axis_size("dp")
    whole = pltpu.VMEM
    return kernel_call(
        exit_kernel,
        "leave",
        cid,
        [
            ((2, m, width), jnp.float32, pl.ANY),
            ((2, m, width), jnp.bfloat16, pl.ANY),
            ((width // LANES, 8, LANES), jnp.float32, whole),
        ]
        + [((plane, p.shape[0], p.shape[1] // plane), p.dtype, pl.ANY) for p in shards],
        [(a, whole) for a in (dqkv, pack, x, dresid, block, small, gain_two)]
        + [(p, pl.ANY) for p in shards],
        [
            pltpu.VMEM((8, width), jnp.float32),
            pltpu.VMEM((4, 2, m, width), jnp.bfloat16),
            pltpu.VMEM((m, width), jnp.float32),
            pltpu.VMEM((m, width), jnp.float32),
            pltpu.VMEM((m, width), jnp.bfloat16),
        ]
        + scatter_scratch(m, width)
        + [
            copies(SCATTER_COPIES),
            copies(2),
            pltpu.SemaphoreType.DMA((2,)),
            copies(2 * (plane - 1)),
            pltpu.SemaphoreType.DMA((2,)),
        ],
        moved=x.size * 120,
    )


def plane_local(
    tokens,
    doc_starts,
    attn_gain,
    mlp_gain,
    query_weight,
    key_weight,
    value_weight,
    output_weight,
    gate_weight,
    up_weight,
    down_weight,
    cotangent,
):
    plane, span, cores = (lax.axis_size("dp"), lax.axis_size("seq"), lax.axis_size("tensor"))
    rows, length, width = tokens.shape
    chunk = width // (plane * span)
    own = rows * length // cores
    heads = query_weight.shape[1] // FDIM // plane
    hidden_part = gate_weight.shape[1] // plane
    vcols, qcols = heads * VHEAD, heads * FDIM

    def over_seq(pack):
        return lax.all_gather(pack, "seq", axis=0, tiled=False)

    def summed(grads):
        return lax.psum_scatter(
            grads.astype(jnp.bfloat16), "seq", scatter_dimension=1, tiled=True
        )

    def split(w):
        return w.reshape(plane, -1, chunk)

    gate_w = split(gate_weight.T)
    pack = weights_exchange(
        value_weight, query_weight, key_weight, output_weight, gate_w[:, :EARLY], 1
    )
    attn_gain, mlp_gain, doc_starts, pack = lax.optimization_barrier(
        (attn_gain, mlp_gain, doc_starts, pack)
    )
    small = jnp.concatenate(
        [
            attn_gain.astype(jnp.float32)[None],
            mlp_gain.astype(jnp.float32)[None],
            doc_starts.astype(jnp.float32).reshape(-1, chunk),
            jnp.zeros((2, chunk), jnp.float32),
        ]
    )
    small, down_w = small_exchange(small, split(down_weight), 2)
    pack = over_seq(pack)
    late_w = jnp.concatenate([gate_w[:, EARLY:], split(up_weight.T)], axis=1)
    qkv_rows = vcols + 2 * qcols
    pairs = feature_pairs()
    normed_one, x, cot_own, seg_col, seg_row = entry(
        tokens.reshape(cores, own, width), cotangent.reshape(cores, own, width), small, length, 3
    )
    into, out_of = Rows(pack, 0, vcols + LANES), Rows(pack, qkv_rows, vcols)
    qkv, state, sums, late_w = states(
        normed_one,
        into,
        seg_col,
        seg_row,
        pairs,
        [late_w],
        heads,
        4,
    )
    late_w, down_w = lax.optimization_barrier((late_w, down_w))
    late_w, down_w = over_seq(late_w), over_seq(down_w)
    mixed, exact, den, cot = mix(
        qkv, seg_col, seg_row, pairs, state, sums, cot_own, heads, 13
    )
    residual, normed_own = branch(mixed, out_of, x, small, 5)
    normed_two, gate, up, hidden = expand(normed_own, pack, late_w, 11)
    down_grad = nn_dot(hidden, cot).astype(jnp.bfloat16)
    gate, down_grad = lax.optimization_barrier((gate, down_grad))
    down_grad = summed(down_grad)
    out_part, dnormed_two, gate_up_grad = hidden_units(
        gate, up, cot, pack, late_w, down_w, normed_two, 6
    )
    gate_up_grad = summed(gate_up_grad)
    segments = (seg_col, seg_row)
    dresid, gain_two_grad, dmixed, out_grad, *sums_own = turn(
        dnormed_two,
        residual,
        cot_own,
        small,
        out_of,
        mixed,
        segments,
        pairs,
        (qkv, exact, den),
        heads,
        12,
    )
    dmixed, down_grad = lax.optimization_barrier((dmixed, down_grad))
    dqkv, block_own, attn_grad, (down_grad,) = unmix(
        dmixed,
        normed_one,
        out_grad,
        out_part,
        residual,
        segments,
        pairs,
        (qkv, exact, den, state, sums),
        sums_own,
        [down_grad],
        heads,
        8,
    )
    attn_grad = summed(attn_grad)
    dtokens, block_out, gains, gate_up_grad = leave(
        dqkv, into, x, dresid, block_own, small, gain_two_grad, [gate_up_grad], 9
    )
    down_grad, gains = lax.optimization_barrier((down_grad, gains))
    (attn_grad,), gain_grads = last([attn_grad], gains, 10)

    def stacked(a, start, size):
        return a[:, start : start + size].reshape(plane * size, chunk).astype(jnp.float32)

    h = hidden_part
    return (
        block_out.reshape(rows, length, width),
        dtokens.reshape(rows, length, width),
        gain_grads[0],
        gain_grads[1],
        stacked(attn_grad, vcols, qcols).T,
        stacked(attn_grad, vcols + qcols, qcols).T,
        stacked(attn_grad, 0, vcols).T,
        stacked(attn_grad, qkv_rows, vcols),
        stacked(gate_up_grad, 0, h).T,
        stacked(gate_up_grad, h, h).T,
        stacked(down_grad, 0, h),
    )


def fits_plane(mesh, tokens, query_weight, gate_weight):
    plane, span, cores = (mesh.shape[a] for a in ("dp", "seq", "tensor"))
    heads = query_weight.shape[1] // FDIM // cores
    return (
        plane == 4
        and cores == 2
        and heads % plane == 0
        and (gate_weight.shape[1] // cores) % (16 * plane) == 0
        and gate_weight.shape[1] // cores // plane > EARLY
        and tokens.shape[0] % CHUNKS == 0
    )


def solution(mesh):
    def step(*args):
        use = fits_plane(mesh, args[0], args[4], args[8])
        return sharded(mesh, plane_local if use else local)(*args)

    return step


def sharded(mesh, body):
    return jax.shard_map(
        body,
        mesh=mesh,
        in_specs=(
            P("dp", "seq", None),
            P("dp", "seq"),
            P(("dp", "seq")),
            P(("dp", "seq")),
            P(("dp", "seq"), "tensor"),
            P(("dp", "seq"), "tensor"),
            P(("dp", "seq"), "tensor"),
            P("tensor", ("dp", "seq")),
            P(("dp", "seq"), "tensor"),
            P(("dp", "seq"), "tensor"),
            P("tensor", ("dp", "seq")),
            P("dp", "seq", None),
        ),
        out_specs=(
            P("dp", "seq", None),
            P("dp", "seq", None),
            P(("dp", "seq")),
            P(("dp", "seq")),
            P(("dp", "seq"), "tensor"),
            P(("dp", "seq"), "tensor"),
            P(("dp", "seq"), "tensor"),
            P("tensor", ("dp", "seq")),
            P(("dp", "seq"), "tensor"),
            P(("dp", "seq"), "tensor"),
            P("tensor", ("dp", "seq")),
        ),
        check_vma=False,
    )
```
